32 devices in a mesh: ctx: 8 (over z, x), fsdp: 4 (over y, core).
Axes of the slice: x: 2, y: 2, z: 4, core: 2. Of those that a mesh axis runs over, the one named last changes fastest.
Arguments:
- tokens: bfloat16 [4, 1024, 768], P('fsdp', 'ctx'), may hold values from -6 to 6
- segment_ids: int32 [4, 1024], P('fsdp', 'ctx'), may hold values from 0 to 1023, as said below
- ln1_gain: bfloat16 [768], P('fsdp'), may hold values from 0.5 to 1.5
- ln1_bias: bfloat16 [768], P('fsdp'), may hold values from -1.5 to 1.5
- attn_weight: bfloat16 [768, 2304], P('fsdp'), may hold values from -0.21875 to 0.21875
- attn_bias: bfloat16 [1536], P('fsdp'), may hold values from -1.5 to 1.5
- proj_weight: bfloat16 [768, 768], P('fsdp'), may hold values from -1.25 to 1.25
- proj_bias: bfloat16 [768], P('fsdp'), may hold values from -1.5 to 1.5
- ln2_gain: bfloat16 [768], P('fsdp'), may hold values from 0.5 to 1.5
- ln2_bias: bfloat16 [768], P('fsdp'), may hold values from -1.5 to 1.5
- fc_weight: bfloat16 [768, 3072], P('fsdp'), may hold values from -0.21875 to 0.21875
- fc_bias: bfloat16 [3072], P('fsdp'), may hold values from -1.5 to 1.5
- out_weight: bfloat16 [3072, 768], P('fsdp'), may hold values from -0.109375 to 0.109375
- out_bias: bfloat16 [768], P('fsdp'), may hold values from -1.5 to 1.5
- out_cotangent: bfloat16 [4, 1024, 768], P('fsdp', 'ctx'), may hold values from -6 to 6
Outputs:
- output: bfloat16 [4, 1024, 768], P('fsdp', 'ctx')
- tokens_grad: bfloat16 [4, 1024, 768], P('fsdp', 'ctx')
- ln1_gain_grad: float32 [768], P('fsdp')
- ln1_bias_grad: float32 [768], P('fsdp')
- attn_weight_grad: float32 [768, 2304], P('fsdp')
- attn_bias_grad: float32 [1536], P('fsdp')
- proj_weight_grad: float32 [768, 768], P('fsdp')
- proj_bias_grad: float32 [768], P('fsdp')
- ln2_gain_grad: float32 [768], P('fsdp')
- ln2_bias_grad: float32 [768], P('fsdp')
- fc_weight_grad: float32 [768, 3072], P('fsdp')
- fc_bias_grad: float32 [3072], P('fsdp')
- out_weight_grad: float32 [3072, 768], P('fsdp')
- out_bias_grad: float32 [768], P('fsdp')
The draws below stay inside these ranges and needn't reach their ends.
Inputs may be any that keep to these rules, and one draw needn't show every extreme that they name: `segment_ids`: along each sequence the id is 0 at the first token and never falls; equal ids mark one document. Every sequence's last document has the id 1024 - 1. In every aligned group of 4 sequences one, placed by the seed, keeps a single id from token 63 to token 959.
All inputs are finite; a program needn't handle non-finite values.
Results may differ from the reference program's by a relative error of at most 0.023.
Values may be sent and summed in bfloat16 or wider, within the bound.
A program may use at most 256 MiB of HBM per device.

```python
import math
import jax
import jax.numpy as jnp
from jax import lax

D = 768
HEADS = 12
FF = 3072
HDIM = 64
SEQ_DEV = 128
SEQS = 4
LEN = 1024


def draw_segment_ids(key, part):
    key_pick, key_rate, key_mark = jax.random.split(key, 3)
    groups = SEQS // 4
    picks = jax.random.randint(key_pick, (groups, 1), 0, 4)
    spanning = (jnp.arange(4, dtype=jnp.int32)[None, :] == picks).reshape(SEQS, 1)
    regions = LEN // 64
    exponents = jax.random.randint(key_rate, (SEQS, regions, 1), 2, 11)
    periods = jnp.left_shift(jnp.ones_like(exponents), exponents)
    marks = jax.random.randint(key_mark, (SEQS, regions, 64), 0, 1 << 20)
    boundary = (jnp.remainder(marks, periods) == 0).reshape(SEQS, LEN)
    places = jnp.arange(LEN, dtype=jnp.int32)[None, :]
    edges = (places < SEQ_DEV // 2) | (places >= LEN - SEQ_DEV // 2)
    boundary = boundary & (places > 0) & (edges | jnp.logical_not(spanning))
    boundary = boundary | (places == LEN - 1)
    counted = jnp.cumsum(boundary.astype(jnp.int32), axis=1).astype(jnp.int32)
    final = counted[:, LEN - 1:LEN]
    return jnp.where(counted == final, jnp.int32(LEN - 1), counted).astype(jnp.int32)


def levels(rng, extent, shards, smallest, high):
    level = 1.0
    for dim, parts in shards:
        heights = jax.random.uniform(jax.random.fold_in(jax.random.fold_in(rng, 6), dim), (parts,), jnp.float32, smallest / len(shards), high / len(shards))
        level = level * jnp.repeat(jnp.exp(heights), extent[dim] // parts).reshape((-1,) + (1,) * (len(extent) - 1 - dim))
    return level


def noise(key, dims, spread, bound, cuts=(), held_as=jnp.bfloat16):
    entries = jax.random.normal(key, dims, jnp.float32) * spread
    if len(cuts) > 0:
        entries = levels(key, dims, cuts, -0.22, 0.18) * entries
    return jnp.clip(entries, min=-bound, max=bound).astype(held_as)


def setup_inputs(seed: int = 0) -> dict:
    arg_keys = jax.random.split(jax.random.key(seed), 16)
    return {
        "tokens": noise(arg_keys[0], (SEQS, LEN, D), 1.0, 6.0, ((0, 4), (1, 8))),
        "segment_ids": draw_segment_ids(jax.random.fold_in(arg_keys[15], 71), 0),
        "ln1_gain": jnp.clip(1.0 + 0.1 * jax.random.normal(arg_keys[2], (D,), jnp.float32), 0.5, 1.5).astype(jnp.bfloat16),
        "ln1_bias": noise(arg_keys[3], (D,), 0.25, 1.5, ((0, 4),)),
        "attn_weight": noise(arg_keys[4], (D, 3 * D), D ** -0.5, 0.21875, ((0, 4),)),
        "attn_bias": noise(arg_keys[5], (2 * D,), 0.25, 1.5, ((0, 4),)),
        "proj_weight": noise(arg_keys[6], (D, D), (D // 32) ** -0.5, 1.25, ((0, 4),)),
        "proj_bias": noise(arg_keys[7], (D,), 0.25, 1.5, ((0, 4),)),
        "ln2_gain": jnp.clip(1.0 + 0.1 * jax.random.normal(arg_keys[8], (D,), jnp.float32), 0.5, 1.5).astype(jnp.bfloat16),
        "ln2_bias": noise(arg_keys[9], (D,), 0.25, 1.5, ((0, 4),)),
        "fc_weight": noise(arg_keys[10], (D, FF), D ** -0.5, 0.21875, ((0, 4),)),
        "fc_bias": noise(arg_keys[11], (FF,), 0.25, 1.5, ((0, 4),)),
        "out_weight": noise(arg_keys[12], (FF, D), FF ** -0.5, 0.109375, ((0, 4),)),
        "out_bias": noise(arg_keys[13], (D,), 0.25, 1.5, ((0, 4),)),
        "out_cotangent": noise(arg_keys[14], (SEQS, LEN, D), 1.0, 6.0, ((0, 4), (1, 8))),
    }


@jax.custom_vjp
def low(v):
    return lax.optimization_barrier(v.astype(jnp.bfloat16)).astype(jnp.float32)

@jax.custom_vjp
def low_back(v):
    return v

def low_keep(v):
    return (low(v), None)

def low_pass(kept, grad):
    return (grad,)

def back_keep(v):
    return (v, None)

def back_low(kept, grad):
    return (low(grad),)
low.defvjp(low_keep, low_pass)
low_back.defvjp(back_keep, back_low)
PRECISE = lax.Precision.HIGHEST
EPSILON = 1e-05
NEGATIVE = -1e+30

def project(left_rows, matrix):
    return jnp.dot(left_rows, matrix, precision=PRECISE, preferred_element_type=jnp.float32)

def norm_rows(resid, gain_row, bias_row):
    average = lax.optimization_barrier(jnp.mean(resid, axis=-1, keepdims=True))
    centred = resid - average
    variance = lax.optimization_barrier(jnp.mean(centred * centred, axis=-1, keepdims=True))
    return centred * lax.rsqrt(variance + EPSILON) * gain_row + bias_row

def attend_sequence(queries, key_rows, value_rows, segments):
    block_rows = math.gcd(LEN, 512)
    starts = jnp.arange(LEN // block_rows, dtype=jnp.int32) * block_rows
    query_blocks = queries.reshape(LEN // block_rows, block_rows, HEADS, HDIM)
    key_heads = key_rows.reshape(LEN, HEADS, HDIM)
    value_heads = value_rows.reshape(LEN, HEADS, HDIM)

    def one_block(packed):
        query_rows, first_row = packed
        scores = jnp.einsum('qhd,khd->hqk', query_rows, key_heads, precision=PRECISE) * HDIM ** (-0.5)
        scores = low_back(scores)
        places = jnp.arange(LEN, dtype=jnp.int32)
        row_places = first_row + jnp.arange(block_rows, dtype=jnp.int32)
        row_segments = lax.dynamic_slice_in_dim(segments, first_row, block_rows)
        allowed = (row_segments[:, None] == segments[None, :]) & (places[None, :] <= row_places[:, None])
        scores = jnp.where(allowed[None], scores, NEGATIVE)
        attention = low(jax.nn.softmax(scores, axis=-1))
        return jnp.einsum('hqk,khd->qhd', attention, value_heads, precision=PRECISE)
    attended = lax.map(jax.checkpoint(one_block), (query_blocks, starts))
    return attended.reshape(LEN, D)

def one_layer(resid, segments, params):
    gain_one, bias_one, weight_qkv, bias_qv, weight_proj, bias_proj, gain_two, bias_two, weight_fc, bias_fc, weight_out, bias_out = params
    normed_one = low(norm_rows(resid, gain_one, bias_one))
    projected = project(normed_one, weight_qkv)
    queries = low(low_back(projected[:, :D] + bias_qv[:D]))
    key_rows = low(low_back(projected[:, D:2 * D]))
    value_rows = low(low_back(projected[:, 2 * D:] + bias_qv[D:]))
    attended = low(low_back(attend_sequence(queries, key_rows, value_rows, segments)))
    middle = resid + low_back(project(attended, weight_proj) + bias_proj)
    normed_two = low(norm_rows(middle, gain_two, bias_two))
    hidden = low_back(project(normed_two, weight_fc) + bias_fc)
    activated = low(jax.nn.gelu(hidden, approximate=True))
    return middle + low_back(project(activated, weight_out) + bias_out)

def reference(tokens, segment_ids, ln1_gain, ln1_bias, attn_weight, attn_bias, proj_weight, proj_bias, ln2_gain, ln2_bias, fc_weight, fc_bias, out_weight, out_bias, out_cotangent):
    params = tuple((item.astype(jnp.float32) for item in (ln1_gain, ln1_bias, attn_weight, attn_bias, proj_weight, proj_bias, ln2_gain, ln2_bias, fc_weight, fc_bias, out_weight, out_bias)))

    def forward(resid, weights):

        def one_sequence(packed):
            sequence_rows, segments = packed
            for layer_index in range(2):
                sequence_rows = one_layer(sequence_rows, segments, weights)
            return sequence_rows
        return lax.map(jax.checkpoint(one_sequence), (resid, segment_ids))
    output, pullback = jax.vjp(forward, tokens.astype(jnp.float32), params)
    grad_tokens, grad_params = pullback(out_cotangent.astype(jnp.float32))
    return (output.astype(jnp.bfloat16), grad_tokens.astype(jnp.bfloat16), grad_params[0], grad_params[1], grad_params[2], grad_params[3], grad_params[4], grad_params[5], grad_params[6], grad_params[7], grad_params[8], grad_params[9], grad_params[10], grad_params[11])
```

```python
from functools import partial

import jax
import jax.numpy as jnp
from jax import lax
from jax.experimental import pallas as pl
from jax.experimental.pallas import tpu as pltpu
from jax.sharding import PartitionSpec as P

D = 768
HEADS = 12
HDIM = 64
PAIRS = HEADS // 2
LANES = 128
EPSILON = 1e-05
NEGATIVE = -1e30
SCALE = HDIM ** (-0.5)
MESH = pl.DeviceIdType.MESH
F32 = jnp.float32
BF16 = jnp.bfloat16


def norm_forward(resid, gain_row, bias_row):
    average = jnp.mean(resid, axis=-1, keepdims=True)
    centred = resid - average
    variance = jnp.mean(centred * centred, axis=-1, keepdims=True)
    inverse = lax.rsqrt(variance + EPSILON)
    normal = centred * inverse
    return ((normal * gain_row + bias_row).astype(BF16), normal, inverse)


def norm_backward(grad_normed, normal, inverse, gain_row):
    scaled = grad_normed * gain_row
    mean_term = jnp.mean(scaled, axis=-1, keepdims=True)
    second = jnp.mean(scaled * normal, axis=-1, keepdims=True)
    grad_input = inverse * (scaled - mean_term - normal * second)
    return (grad_input, jnp.sum(grad_normed * normal, axis=0), jnp.sum(grad_normed, axis=0))


def two_heads(rows):
    lane = lax.broadcasted_iota(jnp.int32, rows.shape, 1)
    zero = jnp.zeros_like(rows)
    first = jnp.where(lane < HDIM, rows, zero)
    second = jnp.where(lane < HDIM, zero, rows)
    return jnp.concatenate([first, second], axis=0)


def one_pair(stacked):
    half = stacked.shape[0] // 2
    lane = lax.broadcasted_iota(jnp.int32, (half, LANES), 1)
    return jnp.where(lane < HDIM, stacked[:half], stacked[half:])


def dot_rows(left, right):
    return lax.dot_general(left, right, (((1,), (1,)), ((), ())), preferred_element_type=F32)


def pick_lanes(columns, pair):
    lane = lax.broadcasted_iota(jnp.int32, columns.shape, 1)
    first = jnp.sum(jnp.where(lane == 2 * pair, columns, 0.0), axis=1, keepdims=True)
    second = jnp.sum(jnp.where(lane == 2 * pair + 1, columns, 0.0), axis=1, keepdims=True)
    return jnp.concatenate([first, second], axis=0)


def mask_columns(bias_ref, own_segs, all_segs_ref, start, own_is_query):
    rows, columns = bias_ref.shape
    step = min(1024, columns)
    own_place = start + lax.broadcasted_iota(jnp.int32, (rows, step), 0)
    for offset in range(0, columns, step):
        place = offset + lax.broadcasted_iota(jnp.int32, (rows, step), 1)
        causal = (place <= own_place) if own_is_query else (own_place <= place)
        same = own_segs == all_segs_ref[:, offset : offset + step]
        bias_ref[:, offset : offset + step] = jnp.where(causal & same, 0.0, NEGATIVE)


def attention_forward_kernel(
    start_ref, q_ref, k_ref, v_ref, own_segs_ref, all_segs_ref, out_ref, lse_ref, lse_rows_ref, bias_ref
):
    pair = pl.program_id(0)
    rows, keys = bias_ref.shape

    @pl.when(pair == 0)
    def _():
        mask_columns(bias_ref, own_segs_ref[...], all_segs_ref, start_ref[0], True)
        lse_ref[...] = jnp.zeros_like(lse_ref)

    queries = two_heads(q_ref[...] * jnp.asarray(SCALE, BF16))
    step = min(1024, keys)

    def scores_of(offset):
        scores = dot_rows(queries, k_ref[pl.ds(offset, step), :])
        bias = bias_ref[:, pl.ds(offset, step)]
        return scores + jnp.concatenate([bias, bias], axis=0)

    if step == keys:
        scores = scores_of(0)
        top = jnp.max(scores, axis=1, keepdims=True)
        weights = jnp.exp(scores - top)
        total = jnp.sum(weights, axis=1, keepdims=True)
        mixed = jnp.dot(weights.astype(BF16), v_ref[...], preferred_element_type=F32)
    else:

        def visit(index, carried):
            top, total, mixed = carried
            offset = pl.multiple_of(index * step, step)
            scores = scores_of(offset)
            new_top = jnp.maximum(top, jnp.max(scores, axis=1, keepdims=True))
            weights = jnp.exp(scores - new_top)
            factor = jnp.exp(top - new_top)
            total = total * factor + jnp.sum(weights, axis=1, keepdims=True)
            more = jnp.dot(
                weights.astype(BF16), v_ref[pl.ds(offset, step), :], preferred_element_type=F32
            )
            return new_top, total, mixed * factor + more

        top, total, mixed = lax.fori_loop(
            0,
            (start_ref[0] + rows + step - 1) // step,
            visit,
            (
                jnp.full((2 * rows, 1), NEGATIVE, F32),
                jnp.zeros((2 * rows, 1), F32),
                jnp.zeros((2 * rows, LANES), F32),
            ),
        )
    out_ref[...] = one_pair(mixed / total).astype(BF16)
    lse = top + jnp.log(total)
    lane = lax.broadcasted_iota(jnp.int32, (rows, LANES), 1)
    kept = lse_ref[...]
    kept = jnp.where(lane == 2 * pair, lse[:rows], kept)
    kept = jnp.where(lane == 2 * pair + 1, lse[rows:], kept)
    lse_ref[...] = kept

    @pl.when(pair == PAIRS - 1)
    def _():
        lse_rows_ref[...] = kept.T[:16]


def attention_forward(start, queries, kv, own_segs, all_segs):
    rows = queries.shape[0]
    keys = kv.shape[0]
    whole = lambda shape: pl.BlockSpec(shape, lambda p: (0, 0))
    return pl.pallas_call(
        attention_forward_kernel,
        grid=(PAIRS,),
        in_specs=[
            pl.BlockSpec(memory_space=pltpu.SMEM),
            pl.BlockSpec((rows, LANES), lambda p: (0, p)),
            pl.BlockSpec((keys, LANES), lambda p: (0, p)),
            pl.BlockSpec((keys, LANES), lambda p: (0, PAIRS + p)),
            whole((rows, 1)),
            whole((1, keys)),
        ],
        out_specs=[
            pl.BlockSpec((rows, LANES), lambda p: (0, p)),
            whole((rows, LANES)),
            whole((16, rows)),
        ],
        out_shape=[
            jax.ShapeDtypeStruct((rows, D), BF16),
            jax.ShapeDtypeStruct((rows, LANES), F32),
            jax.ShapeDtypeStruct((16, rows), F32),
        ],
        scratch_shapes=[pltpu.VMEM((rows, keys), F32)],
        compiler_params=pltpu.CompilerParams(vmem_limit_bytes=40 << 20),
        cost_estimate=pl.CostEstimate(
            flops=8 * rows * keys * D, bytes_accessed=4 * keys * D, transcendentals=rows * keys * HEADS
        ),
        name="attention_forward",
    )(start, queries, kv, kv, own_segs, all_segs)


def attention_backward_kernel(
    start_ref,
    q_ref,
    grad_ref,
    k_own_ref,
    v_own_ref,
    lse_ref,
    delta_ref,
    k_ref,
    v_ref,
    q_all_ref,
    grad_all_ref,
    stats_ref,
    own_segs_ref,
    all_segs_ref,
    out_ref,
    query_bias_ref,
    key_bias_ref,
):
    pair = pl.program_id(0)
    rows, tokens = query_bias_ref.shape
    start = start_ref[0]

    @pl.when(pair == 0)
    def _():
        mask_columns(query_bias_ref, own_segs_ref[...], all_segs_ref, start, True)
        mask_columns(key_bias_ref, own_segs_ref[...], all_segs_ref, start, False)

    step = min(256, tokens)
    blocks = step // rows
    scale = jnp.asarray(SCALE, BF16)

    def doubled(bias):
        return jnp.concatenate([bias, bias], axis=0)

    queries = two_heads(q_ref[...] * scale)
    grads = two_heads(grad_ref[...])
    lse = pick_lanes(lse_ref[...], pair)
    delta = pick_lanes(delta_ref[...], pair)

    def visit_keys(index, grad_query):
        offset = pl.multiple_of(index * step, step)
        keys = k_ref[pl.ds(offset, step), :]
        values = v_ref[pl.ds(offset, step), :]
        bias = doubled(query_bias_ref[:, pl.ds(offset, step)])
        attention = jnp.exp(dot_rows(queries, keys) + bias - lse)
        grad_attention = dot_rows(grads, values)
        grad_scores = (attention * (grad_attention - delta)).astype(BF16)
        return grad_query + jnp.dot(grad_scores, keys, preferred_element_type=F32)

    zeros = jnp.zeros((2 * rows, LANES), F32)
    grad_query = lax.fori_loop(0, (start + rows + step - 1) // step, visit_keys, zeros)

    own_keys = two_heads(k_own_ref[...] * scale)
    own_values = two_heads(v_own_ref[...])

    def row_of(block, row):
        return jnp.broadcast_to(stats_ref[block, pl.ds(row, 1), :], (rows, rows))

    def stat_rows(index, row):
        first = [row_of(index * blocks + b, row + 2 * pair) for b in range(blocks)]
        second = [row_of(index * blocks + b, row + 2 * pair + 1) for b in range(blocks)]
        return jnp.concatenate(
            [jnp.concatenate(first, axis=1), jnp.concatenate(second, axis=1)], axis=0
        )

    def visit_queries(index, carried):
        grad_keys, grad_values = carried
        offset = pl.multiple_of(index * step, step)
        later = q_all_ref[pl.ds(offset, step), :]
        later_grads = grad_all_ref[pl.ds(offset, step), :]
        bias = doubled(key_bias_ref[:, pl.ds(offset, step)])
        attention = jnp.exp(dot_rows(own_keys, later) + bias - stat_rows(index, 0))
        grad_attention = dot_rows(own_values, later_grads)
        grad_scores = (attention * (grad_attention - stat_rows(index, 16))).astype(BF16)
        grad_keys = grad_keys + jnp.dot(grad_scores, later, preferred_element_type=F32)
        grad_values = grad_values + jnp.dot(
            attention.astype(BF16), later_grads, preferred_element_type=F32
        )
        return grad_keys, grad_values

    grad_keys, grad_values = lax.fori_loop(
        start // step, tokens // step, visit_queries, (zeros, zeros)
    )
    base = pl.multiple_of(pair * LANES, LANES)
    out_ref[:, pl.ds(base, LANES)] = (one_pair(grad_query) * SCALE).astype(BF16)
    out_ref[:, pl.ds(D + base, LANES)] = (one_pair(grad_keys) * SCALE).astype(BF16)
    out_ref[:, pl.ds(2 * D + base, LANES)] = one_pair(grad_values).astype(BF16)


def attention_backward(
    start, queries, grads, kv_own, lse, delta, kv, q_all, grad_all, stats, own_segs, all_segs
):
    rows = queries.shape[0]
    tokens = kv.shape[0]
    whole = lambda shape: pl.BlockSpec(shape, lambda p: (0,) * len(shape))
    own = pl.BlockSpec((rows, LANES), lambda p: (0, p))
    every = pl.BlockSpec((tokens, LANES), lambda p: (0, p))
    return pl.pallas_call(
        attention_backward_kernel,
        grid=(PAIRS,),
        in_specs=[
            pl.BlockSpec(memory_space=pltpu.SMEM),
            own,
            own,
            own,
            pl.BlockSpec((rows, LANES), lambda p: (0, PAIRS + p)),
            whole((rows, LANES)),
            whole((rows, LANES)),
            every,
            pl.BlockSpec((tokens, LANES), lambda p: (0, PAIRS + p)),
            every,
            every,
            whole(stats.shape),
            whole((rows, 1)),
            whole((1, tokens)),
        ],
        out_specs=whole((rows, 3 * D)),
        out_shape=jax.ShapeDtypeStruct((rows, 3 * D), BF16),
        scratch_shapes=[pltpu.VMEM((rows, tokens), F32), pltpu.VMEM((rows, tokens), F32)],
        compiler_params=pltpu.CompilerParams(vmem_limit_bytes=44 << 20),
        cost_estimate=pl.CostEstimate(
            flops=16 * rows * tokens * D,
            bytes_accessed=8 * tokens * D,
            transcendentals=rows * tokens * HEADS,
        ),
        name="attention_backward",
    )(
        start,
        queries,
        grads,
        kv_own,
        kv_own,
        lse,
        delta,
        kv,
        kv,
        q_all,
        grad_all,
        stats,
        own_segs,
        all_segs,
    )


def place_bits():
    ctx, fsdp = lax.axis_index("ctx"), lax.axis_index("fsdp")
    return lax.rem(ctx, 2), ctx // 2, fsdp // 2, lax.rem(fsdp, 2)


def greet(devices):
    barrier = pltpu.get_barrier_semaphore()
    for device in devices:
        pl.semaphore_signal(barrier, inc=1, device_id=device, device_id_type=MESH)
    pl.semaphore_wait(barrier, len(devices))


WEIGHT_COPIES = 11


def gather_weights_kernel(count, *refs):
    shares, fulls = refs[:count], refs[count : 2 * count]
    send_sems, recv_sems, local_sems = refs[2 * count :]
    x, z, y, core = place_bits()
    low = lax.rem(z, 2)
    z_next = z + 1 - 2 * low
    sibling = (2 * z + x, 2 * y + 1 - core)
    over_y = (2 * z + x, 2 * (1 - y) + core)
    over_x = (2 * z + 1 - x, 2 * y + core)
    over_z = (2 * z_next + x, 2 * y + core)
    own = 2 * y + core
    other = 2 * (1 - y) + core
    greet((sibling, over_y, over_x, over_z))

    def copy(index, which, src, dst, device):
        slot = which * WEIGHT_COPIES + index
        return pltpu.make_async_remote_copy(
            src_ref=src,
            dst_ref=dst,
            send_sem=send_sems.at[slot],
            recv_sem=recv_sems.at[slot],
            device_id=device,
            device_id_type=MESH,
        )

    started = []
    locals_started = []
    plans = []
    for which in range(count):
        share, full = shares[which], fulls[which]
        rows, columns = share.shape
        part = rows // 4
        half = columns // 2

        def piece(ref, x_bit, low_bit, part=part):
            return ref.at[pl.ds((2 * low_bit + x_bit) * part, part), :]

        def piece_half(ref, x_bit, low_bit, side, part=part, half=half):
            return ref.at[pl.ds((2 * low_bit + x_bit) * part, part), pl.ds(side * half, half)]

        theirs = full.at[other]
        same = lambda index, view, device, which=which: copy(index, which, view, view, device)
        mine = piece(theirs, x, low)
        from_x = piece(theirs, 1 - x, low)
        from_z = piece(theirs, x, 1 - low)
        plan = {
            0: copy(0, which, piece(share, x, low), piece(full.at[own], x, low), over_y),
            1: same(1, mine, over_x),
            2: same(2, mine, over_z),
            3: same(3, mine, sibling),
            4: same(4, piece_half(theirs, 1 - x, low, 0), over_z),
            5: same(5, from_x, sibling),
            6: same(6, piece_half(theirs, x, 1 - low, 1), over_x),
            7: same(7, from_z, sibling),
            8: same(8, piece_half(theirs, 1 - x, 1 - low, 0), sibling),
            9: same(9, piece_half(theirs, 1 - x, 1 - low, 1), sibling),
            10: copy(10, which, share, full.at[own], sibling),
        }
        plans.append(plan)
        plan[0].start()
        plan[10].start()
        local = pltpu.make_async_copy(share, full.at[own], local_sems.at[which])
        local.start()
        locals_started.append(local)

    for step in range(count + 2):
        if step < count:
            plan = plans[step]
            plan[0].wait_recv()
            plan[1].start()
            plan[2].start()
            plan[3].start()
        if 0 <= step - 1 < count:
            plan = plans[step - 1]
            plan[1].wait_recv()
            plan[4].start()
            plan[5].start()
            plan[2].wait_recv()
            plan[6].start()
            plan[7].start()
        if 0 <= step - 2 < count:
            plan = plans[step - 2]
            plan[4].wait_recv()
            plan[8].start()
            plan[6].wait_recv()
            plan[9].start()
    for plan in plans:
        for index in (3, 5, 7, 8, 9, 10):
            plan[index].wait_recv()
        for index in range(WEIGHT_COPIES):
            plan[index].wait_send()
    for local in locals_started:
        local.wait()


def gather_weights(shares, collective_id):
    count = len(shares)
    copies = count * WEIGHT_COPIES
    anywhere = pl.BlockSpec(memory_space=pl.ANY)
    fulls = pl.pallas_call(
        partial(gather_weights_kernel, count),
        in_specs=[anywhere] * count,
        out_specs=[anywhere] * count,
        out_shape=[jax.ShapeDtypeStruct((4, *share.shape), share.dtype) for share in shares],
        scratch_shapes=[
            pltpu.SemaphoreType.DMA((copies,)),
            pltpu.SemaphoreType.DMA((copies,)),
            pltpu.SemaphoreType.DMA((count,)),
        ],
        compiler_params=pltpu.CompilerParams(collective_id=collective_id, has_side_effects=True),
        name="gather_weights",
    )(*shares)
    return fulls


BLOCK_COPIES = 13


def gather_blocks_kernel(count, *refs):
    blocks, fulls = refs[:count], refs[count : 2 * count]
    send_sems, recv_sems, local_sems = refs[2 * count :]
    x, z, y, core = place_bits()
    sibling = (2 * z + x, 2 * y + 1 - core)
    over_x = (2 * z + 1 - x, 2 * y + core)
    over_y = (2 * z + x, 2 * (1 - y) + core)
    greet((sibling, over_x, over_y))

    plans = []
    locals_started = []
    for which in range(count):
        block, full = blocks[which], fulls[which]
        half = block.shape[0] // 2

        def copy(index, src, dst, device, which=which):
            slot = which * BLOCK_COPIES + index
            return pltpu.make_async_remote_copy(
                src_ref=src,
                dst_ref=dst,
                send_sem=send_sems.at[slot],
                recv_sem=recv_sems.at[slot],
                device_id=device,
                device_id_type=MESH,
            )

        def part(ref, side, half=half):
            return ref.at[pl.ds(side * half, half), :]

        def slot_of(x_bit, y_bit, full=full):
            return full.at[4 * y_bit + 2 * core + x_bit]

        same = lambda index, view, device, copy=copy: copy(index, view, view, device)
        mine = slot_of(x, y)
        from_x, from_y, from_both = slot_of(1 - x, y), slot_of(x, 1 - y), slot_of(1 - x, 1 - y)
        plan = {
            0: copy(0, block, mine, sibling),
            1: copy(1, part(block, 0), part(mine, 0), over_x),
            2: copy(2, part(block, 1), part(mine, 1), over_y),
            3: copy(3, part(block, 1), part(mine, 1), over_x),
            4: copy(4, part(block, 0), part(mine, 0), over_y),
            5: same(5, part(from_x, 0), over_y),
            6: same(6, part(from_x, 0), sibling),
            7: same(7, part(from_y, 1), over_x),
            8: same(8, part(from_y, 1), sibling),
            9: same(9, part(from_x, 1), sibling),
            10: same(10, part(from_y, 0), sibling),
            11: same(11, part(from_both, 0), sibling),
            12: same(12, part(from_both, 1), sibling),
        }
        plans.append(plan)
        for index in (1, 2, 3, 4, 0):
            plan[index].start()
        local = pltpu.make_async_copy(block, mine, local_sems.at[which])
        local.start()
        locals_started.append(local)

    for plan in plans:
        plan[1].wait_recv()
        plan[5].start()
        plan[6].start()
        plan[2].wait_recv()
        plan[7].start()
        plan[8].start()
    for plan in plans:
        plan[3].wait_recv()
        plan[9].start()
        plan[4].wait_recv()
        plan[10].start()
    for plan in plans:
        plan[5].wait_recv()
        plan[11].start()
        plan[7].wait_recv()
        plan[12].start()
    for plan in plans:
        for index in (0, 6, 8, 9, 10, 11, 12):
            plan[index].wait_recv()
        for index in range(BLOCK_COPIES):
            plan[index].wait_send()
    for local in locals_started:
        local.wait()


def gather_blocks(blocks, collective_id):
    count = len(blocks)
    copies = count * BLOCK_COPIES
    anywhere = pl.BlockSpec(memory_space=pl.ANY)
    return pl.pallas_call(
        partial(gather_blocks_kernel, count),
        in_specs=[anywhere] * count,
        out_specs=[anywhere] * count,
        out_shape=[jax.ShapeDtypeStruct((8, *block.shape), block.dtype) for block in blocks],
        scratch_shapes=[
            pltpu.SemaphoreType.DMA((copies,)),
            pltpu.SemaphoreType.DMA((copies,)),
            pltpu.SemaphoreType.DMA((count,)),
        ],
        compiler_params=pltpu.CompilerParams(collective_id=collective_id, has_side_effects=True),
        name="gather_blocks",
    )(*blocks)


class PlaneLinks:
    def __init__(self):
        self.x, self.z, self.y, self.core = place_bits()
        self.block = 2 * lax.axis_index("fsdp") + self.x
        self.count = 8

    def permute(self, value, target):
        pairs = [(c * 4 + f, target(c, f)) for c in range(8) for f in range(4)]
        return lax.ppermute(value, ("ctx", "fsdp"), pairs)

    def swap(self, value):
        return self.permute(value, lambda c, f: (2 * f + c % 2) * 4 + c // 2)

    enter = swap
    leave = swap

    def across(self, value, axis):
        target = {
            "core": lambda c, f: c * 4 + (f ^ 1),
            "y": lambda c, f: c * 4 + (f ^ 2),
            "x": lambda c, f: (c ^ 1) * 4 + f,
            "z": lambda c, f: (c ^ 2) * 4 + f,
            "zz": lambda c, f: (c ^ 4) * 4 + f,
        }[axis]
        return self.permute(value, target)

    def weights(self, shares):
        return gather_weights(shares, 0)

    def blocks(self, blocks, collective_id):
        return gather_blocks(blocks, collective_id)

    def halve(self, total, bit, axis):
        rows = total.shape[0] // 2
        sent = lax.dynamic_slice_in_dim(total, (1 - bit) * rows, rows, 0).astype(BF16)
        kept = lax.dynamic_slice_in_dim(total, bit * rows, rows, 0)
        return kept + self.across(sent, axis).astype(F32)

    def double(self, rows, bit, axis):
        got = self.across(rows, axis)
        low = jnp.where(bit == 0, rows, got)
        high = jnp.where(bit == 0, got, rows)
        return jnp.concatenate([low, high], axis=0)

    def weight_sum(self, left, right):
        tokens, rows = left.shape
        quarter = rows // 4
        columns = left.reshape(tokens, 2, 2, quarter)

        def term(part):
            return lax.dot_general(
                part, right, (((0,), (0,)), ((), ())), preferred_element_type=F32
            )

        pick = lambda array, index, axis: lax.dynamic_index_in_dim(array, index, axis, keepdims=False)
        sent = term(pick(columns, 1 - self.core, 2).reshape(tokens, 2 * quarter)).astype(BF16)
        got = self.across(sent, "core").reshape(2, quarter, right.shape[1])
        mine = pick(columns, self.core, 2)
        sent = (term(pick(mine, 1 - self.y, 1)) + pick(got, 1 - self.y, 0).astype(F32)).astype(BF16)
        got_y = self.across(sent, "y")
        kept = term(pick(mine, self.y, 1)) + pick(got, self.y, 0).astype(F32)
        total = kept + got_y.astype(F32)
        low, high = lax.rem(self.z, 2), self.z // 2
        total = self.halve(total, self.x, "x")
        total = self.halve(total, low, "z")
        total = self.halve(total, high, "zz").astype(BF16)
        total = self.double(total, high, "zz")
        total = self.double(total, low, "z")
        return self.double(total, self.x, "x").astype(F32)

    def vector_sum(self, packed):
        for axis in ("core", "y", "x", "z", "zz"):
            packed = packed + self.across(packed, axis)
        return lax.dynamic_index_in_dim(packed, 2 * self.y + self.core, 0, keepdims=False)


class PlainLinks:
    def __init__(self, ctx_size, fsdp_size):
        self.block = lax.axis_index("ctx")
        self.count = ctx_size
        self.fsdp_size = fsdp_size

    def enter(self, value):
        return value

    leave = enter

    def weights(self, shares):
        return [lax.all_gather(share, "fsdp", axis=0) for share in shares]

    def blocks(self, blocks, collective_id):
        return [lax.all_gather(block, "ctx", axis=0) for block in blocks]

    def weight_sum(self, left, right):
        term = lax.dot_general(left, right, (((0,), (0,)), ((), ())), preferred_element_type=F32)
        share = lax.psum_scatter(term.astype(BF16), "fsdp", scatter_dimension=0, tiled=True)
        return lax.psum(share.astype(F32), "ctx")

    def vector_sum(self, packed):
        share = lax.psum_scatter(packed, "fsdp", scatter_dimension=0, tiled=False)
        return lax.psum(share, "ctx")


def layer_forward(resid, weights, links, start, own_segs, segs, layer_index):
    (
        gain_one,
        bias_one,
        weight_qkv,
        bias_qv,
        weight_proj,
        bias_proj,
        gain_two,
        bias_two,
        weight_fc,
        bias_fc,
        weight_out,
        bias_out,
    ) = weights
    normed_one, normal_one, inverse_one = norm_forward(resid, gain_one, bias_one)
    projected = jnp.dot(normed_one, weight_qkv, preferred_element_type=F32)
    biases = jnp.concatenate([bias_qv[:D], jnp.zeros((D,), F32), bias_qv[D:]])
    projected = (projected + biases).astype(BF16)
    queries, kv_own = projected[:, :D], projected[:, D:]
    if layer_index == 0:
        kv, segs = links.blocks([kv_own, segs], 1)
        segs = segs[:, 0, :].reshape(1, -1)
    else:
        (kv,) = links.blocks([kv_own], 2)
    kv = kv.reshape(-1, 2 * D)
    attended, lse, lse_rows = attention_forward(start, queries, kv, own_segs, segs)
    middle = resid + jnp.dot(attended, weight_proj, preferred_element_type=F32) + bias_proj
    normed_two, normal_two, inverse_two = norm_forward(middle, gain_two, bias_two)
    hidden = jnp.dot(normed_two, weight_fc, preferred_element_type=F32) + bias_fc
    activated = jax.nn.gelu(hidden, approximate=True).astype(BF16)
    result_rows = middle + jnp.dot(activated, weight_out, preferred_element_type=F32) + bias_out
    saved = (
        normed_one,
        normal_one,
        inverse_one,
        queries,
        kv_own,
        kv,
        attended,
        lse,
        lse_rows,
        normed_two,
        normal_two,
        inverse_two,
        hidden,
        activated,
    )
    return result_rows, saved, segs


def layer_backward(gradient, weights, saved, links, start, own_segs, segs):
    (
        gain_one,
        _,
        weight_qkv,
        _,
        weight_proj,
        _,
        gain_two,
        _,
        weight_fc,
        _,
        weight_out,
        _,
    ) = weights
    (
        normed_one,
        normal_one,
        inverse_one,
        queries,
        kv_own,
        kv,
        attended,
        lse,
        lse_rows,
        normed_two,
        normal_two,
        inverse_two,
        hidden,
        activated,
    ) = saved
    rows = gradient.shape[0]
    total = lambda value: jnp.sum(value.astype(F32), axis=0)
    grad_branch = gradient.astype(BF16)
    grad_activated = dot_rows(grad_branch, weight_out)
    gelu_pull = jax.vjp(partial(jax.nn.gelu, approximate=True), hidden)[1]
    grad_hidden = gelu_pull(grad_activated)[0].astype(BF16)
    grad_normed_two = dot_rows(grad_hidden, weight_fc)
    grad_in_two, grad_gain_two, grad_bias_two = norm_backward(
        grad_normed_two, normal_two, inverse_two, gain_two
    )
    grad_middle = gradient + grad_in_two
    grad_proj = grad_middle.astype(BF16)
    grad_attended = dot_rows(grad_proj, weight_proj).astype(BF16)
    products = grad_attended.astype(F32) * attended.astype(F32)
    head_of = jnp.arange(D, dtype=jnp.int32) // HDIM
    by_lane = (head_of[:, None] == jnp.arange(LANES, dtype=jnp.int32)[None, :]).astype(F32)
    by_row = (jnp.arange(16, dtype=jnp.int32)[:, None] == head_of[None, :]).astype(F32)
    delta = jnp.dot(products, by_lane, precision=lax.Precision.HIGHEST, preferred_element_type=F32)
    delta_rows = lax.dot_general(
        by_row,
        products,
        (((1,), (1,)), ((), ())),
        precision=lax.Precision.HIGHEST,
        preferred_element_type=F32,
    )
    stats = jnp.concatenate([lse_rows, delta_rows], axis=0)
    q_all, grad_all, stats = links.blocks([queries, grad_attended, stats], 3)
    grad_projected = attention_backward(
        start,
        queries,
        grad_attended,
        kv_own,
        lse,
        delta,
        kv,
        q_all.reshape(-1, D),
        grad_all.reshape(-1, D),
        stats,
        own_segs,
        segs,
    )
    grad_normed_one = dot_rows(grad_projected, weight_qkv)
    grad_in_one, grad_gain_one, grad_bias_one = norm_backward(
        grad_normed_one, normal_one, inverse_one, gain_one
    )
    grad_input = grad_middle + grad_in_one
    matrices = (
        (activated, grad_branch),
        (normed_two, grad_hidden),
        (attended, grad_proj),
        (normed_one, grad_projected),
    )
    vectors = (
        grad_gain_one,
        grad_bias_one,
        jnp.concatenate([total(grad_projected[:, :D]), total(grad_projected[:, 2 * D :])]),
        total(grad_proj),
        grad_gain_two,
        grad_bias_two,
        total(grad_hidden),
        total(grad_branch),
    )
    return grad_input, matrices, vectors


def body(
    links_of,
    tokens,
    segment_ids,
    ln1_gain,
    ln1_bias,
    attn_weight,
    attn_bias,
    proj_weight,
    proj_bias,
    ln2_gain,
    ln2_bias,
    fc_weight,
    fc_bias,
    out_weight,
    out_bias,
    out_cotangent,
):
    members, seq_dev, features = tokens.shape
    links = links_of()
    start = (links.block * seq_dev).reshape(1).astype(jnp.int32)
    resid = links.enter(tokens[0])
    segs_row = links.enter(segment_ids)
    gradient = links.enter(out_cotangent[0])
    own_segs = segs_row.reshape(seq_dev, 1)
    segs = jnp.broadcast_to(segs_row, (16, seq_dev))

    vectors = (ln1_gain, ln1_bias, attn_bias, proj_bias, ln2_gain, ln2_bias, fc_bias, out_bias)
    sizes = [vector.shape[0] for vector in vectors]
    packed = jnp.concatenate(vectors)
    padding = -packed.shape[0] % (64 * 2 * LANES)
    packed = jnp.pad(packed, (0, padding)).reshape(-1, 2 * LANES)
    qkv_full, packed, proj_full, fc_full, out_full = links.weights(
        [attn_weight, packed, proj_weight, fc_weight, out_weight]
    )
    matrix = lambda full: full.reshape(-1, full.shape[-1])
    packed = packed.reshape(packed.shape[0], -1).astype(F32)
    pieces = []
    offset = 0
    for size in sizes:
        pieces.append(packed[:, offset : offset + size].reshape(-1))
        offset += size
    gain_one, bias_one, bias_qv, bias_proj, gain_two, bias_two, bias_fc, bias_out = pieces
    weights = (
        gain_one,
        bias_one,
        matrix(qkv_full),
        bias_qv,
        matrix(proj_full),
        bias_proj,
        gain_two,
        bias_two,
        matrix(fc_full),
        bias_fc,
        matrix(out_full),
        bias_out,
    )

    resid = resid.astype(F32)
    saved_layers = []
    for layer_index in range(2):
        resid, saved, segs = layer_forward(
            resid, weights, links, start, own_segs, segs, layer_index
        )
        saved_layers.append(saved)
    output = links.leave(resid.astype(BF16))
    gradient = gradient.astype(F32)
    collected = []
    for layer_index in (1, 0):
        gradient, matrices, terms = layer_backward(
            gradient, weights, saved_layers[layer_index], links, start, own_segs, segs
        )
        collected.append((matrices, terms))
    tokens_grad = links.leave(gradient.astype(BF16))

    sums = []
    for second, first in zip(collected[0][0], collected[1][0]):
        left = jnp.concatenate([second[0], first[0]], axis=0)
        right = jnp.concatenate([second[1], first[1]], axis=0)
        sums.append(links.weight_sum(left, right))
    out_grad, fc_grad, proj_grad, qkv_grad = sums
    shares = packed.shape[0]
    added = [a + b for a, b in zip(collected[0][1], collected[1][1])]
    rows = jnp.concatenate([vector.reshape(shares, -1) for vector in added], axis=1)
    summed = links.vector_sum(rows.reshape(shares, -1, LANES)).reshape(-1)
    small = []
    offset = 0
    for size in sizes:
        small.append(summed[offset : offset + size])
        offset += size
    g_gain_one, g_bias_one, g_bias_qv, g_bias_proj, g_gain_two, g_bias_two, g_bias_fc, g_bias_out = small
    return (
        output[None],
        tokens_grad[None],
        g_gain_one,
        g_bias_one,
        qkv_grad,
        g_bias_qv,
        proj_grad,
        g_bias_proj,
        g_gain_two,
        g_bias_two,
        fc_grad,
        g_bias_fc,
        out_grad,
        g_bias_out,
    )


def solution(mesh):
    ctx_size, fsdp_size = mesh.shape["ctx"], mesh.shape["fsdp"]
    if (ctx_size, fsdp_size) == (8, 4):
        links_of = PlaneLinks
    else:
        links_of = partial(PlainLinks, ctx_size, fsdp_size)
    rows = P("fsdp", "ctx", None)
    vector, matrix = P("fsdp"), P("fsdp", None)
    in_specs = (
        rows,
        P("fsdp", "ctx"),
        vector,
        vector,
        matrix,
        vector,
        matrix,
        vector,
        vector,
        vector,
        matrix,
        vector,
        matrix,
        vector,
        rows,
    )
    out_specs = (
        rows,
        rows,
        vector,
        vector,
        matrix,
        vector,
        matrix,
        vector,
        vector,
        vector,
        matrix,
        vector,
        matrix,
        vector,
    )
    return jax.shard_map(
        partial(body, links_of), mesh=mesh, in_specs=in_specs, out_specs=out_specs, check_vma=False
    )
```

```python
from functools import partial

import jax
import jax.numpy as jnp
from jax import lax
from jax.experimental import pallas as pl
from jax.experimental.pallas import tpu as pltpu
from jax.sharding import PartitionSpec as P

D = 768
HEADS = 12
HDIM = 64
PAIRS = HEADS // 2
LANES = 128
EPSILON = 1e-05
NEGATIVE = -1e30
SCALE = HDIM ** (-0.5)
MESH = pl.DeviceIdType.MESH
F32 = jnp.float32
BF16 = jnp.bfloat16


def norm_forward(resid, gain_row, bias_row):
    average = jnp.mean(resid, axis=-1, keepdims=True)
    centred = resid - average
    variance = jnp.mean(centred * centred, axis=-1, keepdims=True)
    inverse = lax.rsqrt(variance + EPSILON)
    normal = centred * inverse
    return ((normal * gain_row + bias_row).astype(BF16), normal, inverse)


def norm_backward(grad_normed, normal, inverse, gain_row):
    scaled = grad_normed * gain_row
    mean_term = jnp.mean(scaled, axis=-1, keepdims=True)
    second = jnp.mean(scaled * normal, axis=-1, keepdims=True)
    grad_input = inverse * (scaled - mean_term - normal * second)
    return (grad_input, jnp.sum(grad_normed * normal, axis=0), jnp.sum(grad_normed, axis=0))


def two_heads(rows):
    lane = lax.broadcasted_iota(jnp.int32, rows.shape, 1)
    zero = jnp.zeros_like(rows)
    first = jnp.where(lane < HDIM, rows, zero)
    second = jnp.where(lane < HDIM, zero, rows)
    return jnp.concatenate([first, second], axis=0)


def one_pair(stacked):
    half = stacked.shape[0] // 2
    lane = lax.broadcasted_iota(jnp.int32, (half, LANES), 1)
    return jnp.where(lane < HDIM, stacked[:half], stacked[half:])


def dot_rows(left, right):
    return lax.dot_general(left, right, (((1,), (1,)), ((), ())), preferred_element_type=F32)


def column_products(left, right):
    return lax.dot_general(left, right, (((0,), (0,)), ((), ())), preferred_element_type=F32)


def pick_lanes(columns, pair):
    lane = lax.broadcasted_iota(jnp.int32, columns.shape, 1)
    first = jnp.sum(jnp.where(lane == 2 * pair, columns, 0.0), axis=1, keepdims=True)
    second = jnp.sum(jnp.where(lane == 2 * pair + 1, columns, 0.0), axis=1, keepdims=True)
    return jnp.concatenate([first, second], axis=0)


def mask_columns(bias_ref, own_segs, all_segs_ref, start, own_is_query):
    rows, columns = bias_ref.shape
    step = min(1024, columns)
    own_place = start + lax.broadcasted_iota(jnp.int32, (rows, step), 0)
    for offset in range(0, columns, step):
        place = offset + lax.broadcasted_iota(jnp.int32, (rows, step), 1)
        causal = (place <= own_place) if own_is_query else (own_place <= place)
        same = own_segs == all_segs_ref[:, offset : offset + step]
        bias_ref[:, offset : offset + step] = jnp.where(causal & same, 0.0, NEGATIVE)


def attention_forward_kernel(
    start_ref, q_ref, k_ref, v_ref, own_segs_ref, all_segs_ref, out_ref, lse_ref, lse_rows_ref, bias_ref
):
    pair = pl.program_id(0)
    rows, keys = bias_ref.shape

    @pl.when(pair == 0)
    def _():
        mask_columns(bias_ref, own_segs_ref[...], all_segs_ref, start_ref[0], True)
        lse_ref[...] = jnp.zeros_like(lse_ref)

    queries = two_heads(q_ref[...] * jnp.asarray(SCALE, BF16))
    step = min(1024, keys)

    def scores_of(offset):
        scores = dot_rows(queries, k_ref[pl.ds(offset, step), :])
        bias = bias_ref[:, pl.ds(offset, step)]
        return scores + jnp.concatenate([bias, bias], axis=0)

    if step == keys:
        scores = scores_of(0)
        top = jnp.max(scores, axis=1, keepdims=True)
        weights = jnp.exp(scores - top)
        total = jnp.sum(weights, axis=1, keepdims=True)
        mixed = jnp.dot(weights.astype(BF16), v_ref[...], preferred_element_type=F32)
    else:

        def visit(index, carried):
            top, total, mixed = carried
            offset = pl.multiple_of(index * step, step)
            scores = scores_of(offset)
            new_top = jnp.maximum(top, jnp.max(scores, axis=1, keepdims=True))
            weights = jnp.exp(scores - new_top)
            factor = jnp.exp(top - new_top)
            total = total * factor + jnp.sum(weights, axis=1, keepdims=True)
            more = jnp.dot(
                weights.astype(BF16), v_ref[pl.ds(offset, step), :], preferred_element_type=F32
            )
            return new_top, total, mixed * factor + more

        top, total, mixed = lax.fori_loop(
            0,
            (start_ref[0] + rows + step - 1) // step,
            visit,
            (
                jnp.full((2 * rows, 1), NEGATIVE, F32),
                jnp.zeros((2 * rows, 1), F32),
                jnp.zeros((2 * rows, LANES), F32),
            ),
        )
    out_ref[...] = one_pair(mixed / total).astype(BF16)
    lse = top + jnp.log(total)
    lane = lax.broadcasted_iota(jnp.int32, (rows, LANES), 1)
    kept = lse_ref[...]
    kept = jnp.where(lane == 2 * pair, lse[:rows], kept)
    kept = jnp.where(lane == 2 * pair + 1, lse[rows:], kept)
    lse_ref[...] = kept

    @pl.when(pair == PAIRS - 1)
    def _():
        lse_rows_ref[...] = kept.T[:16]


def attention_forward(start, queries, kv, own_segs, all_segs):
    rows = queries.shape[0]
    keys = kv.shape[0]
    whole = lambda shape: pl.BlockSpec(shape, lambda p: (0, 0))
    return pl.pallas_call(
        attention_forward_kernel,
        grid=(PAIRS,),
        in_specs=[
            pl.BlockSpec(memory_space=pltpu.SMEM),
            pl.BlockSpec((rows, LANES), lambda p: (0, p)),
            pl.BlockSpec((keys, LANES), lambda p: (0, p)),
            pl.BlockSpec((keys, LANES), lambda p: (0, PAIRS + p)),
            whole((rows, 1)),
            whole((1, keys)),
        ],
        out_specs=[
            pl.BlockSpec((rows, LANES), lambda p: (0, p)),
            whole((rows, LANES)),
            whole((16, rows)),
        ],
        out_shape=[
            jax.ShapeDtypeStruct((rows, D), BF16),
            jax.ShapeDtypeStruct((rows, LANES), F32),
            jax.ShapeDtypeStruct((16, rows), F32),
        ],
        scratch_shapes=[pltpu.VMEM((rows, keys), F32)],
        compiler_params=pltpu.CompilerParams(vmem_limit_bytes=40 << 20),
        cost_estimate=pl.CostEstimate(
            flops=8 * rows * keys * D, bytes_accessed=4 * keys * D, transcendentals=rows * keys * HEADS
        ),
        name="attention_forward",
    )(start, queries, kv, kv, own_segs, all_segs)


def attention_backward_kernel(
    start_ref,
    q_ref,
    grad_ref,
    k_own_ref,
    v_own_ref,
    lse_ref,
    delta_ref,
    k_ref,
    v_ref,
    q_all_ref,
    grad_all_ref,
    stats_ref,
    own_segs_ref,
    all_segs_ref,
    out_ref,
    query_bias_ref,
    key_bias_ref,
):
    pair = pl.program_id(0)
    rows, tokens = query_bias_ref.shape
    start = start_ref[0]

    @pl.when(pair == 0)
    def _():
        mask_columns(query_bias_ref, own_segs_ref[...], all_segs_ref, start, True)
        mask_columns(key_bias_ref, own_segs_ref[...], all_segs_ref, start, False)

    step = min(256, tokens)
    blocks = step // rows
    scale = jnp.asarray(SCALE, BF16)

    def doubled(bias):
        return jnp.concatenate([bias, bias], axis=0)

    queries = two_heads(q_ref[...] * scale)
    grads = two_heads(grad_ref[...])
    lse = pick_lanes(lse_ref[...], pair)
    delta = pick_lanes(delta_ref[...], pair)

    def visit_keys(index, grad_query):
        offset = pl.multiple_of(index * step, step)
        keys = k_ref[pl.ds(offset, step), :]
        values = v_ref[pl.ds(offset, step), :]
        bias = doubled(query_bias_ref[:, pl.ds(offset, step)])
        attention = jnp.exp(dot_rows(queries, keys) + bias - lse)
        grad_attention = dot_rows(grads, values)
        grad_scores = (attention * (grad_attention - delta)).astype(BF16)
        return grad_query + jnp.dot(grad_scores, keys, preferred_element_type=F32)

    zeros = jnp.zeros((2 * rows, LANES), F32)
    grad_query = lax.fori_loop(0, (start + rows + step - 1) // step, visit_keys, zeros)

    own_keys = two_heads(k_own_ref[...] * scale)
    own_values = two_heads(v_own_ref[...])

    def row_of(block, row):
        return jnp.broadcast_to(stats_ref[block, pl.ds(row, 1), :], (rows, rows))

    def stat_rows(index, row):
        first = [row_of(index * blocks + b, row + 2 * pair) for b in range(blocks)]
        second = [row_of(index * blocks + b, row + 2 * pair + 1) for b in range(blocks)]
        return jnp.concatenate(
            [jnp.concatenate(first, axis=1), jnp.concatenate(second, axis=1)], axis=0
        )

    def visit_queries(index, carried):
        grad_keys, grad_values = carried
        offset = pl.multiple_of(index * step, step)
        later = q_all_ref[pl.ds(offset, step), :]
        later_grads = grad_all_ref[pl.ds(offset, step), :]
        bias = doubled(key_bias_ref[:, pl.ds(offset, step)])
        attention = jnp.exp(dot_rows(own_keys, later) + bias - stat_rows(index, 0))
        grad_attention = dot_rows(own_values, later_grads)
        grad_scores = (attention * (grad_attention - stat_rows(index, 16))).astype(BF16)
        grad_keys = grad_keys + jnp.dot(grad_scores, later, preferred_element_type=F32)
        grad_values = grad_values + jnp.dot(
            attention.astype(BF16), later_grads, preferred_element_type=F32
        )
        return grad_keys, grad_values

    grad_keys, grad_values = lax.fori_loop(
        start // step, tokens // step, visit_queries, (zeros, zeros)
    )
    base = pl.multiple_of(pair * LANES, LANES)
    out_ref[:, pl.ds(base, LANES)] = (one_pair(grad_query) * SCALE).astype(BF16)
    out_ref[:, pl.ds(D + base, LANES)] = (one_pair(grad_keys) * SCALE).astype(BF16)
    out_ref[:, pl.ds(2 * D + base, LANES)] = one_pair(grad_values).astype(BF16)


def attention_backward(
    start, queries, grads, kv_own, lse, delta, kv, q_all, grad_all, stats, own_segs, all_segs
):
    rows = queries.shape[0]
    tokens = kv.shape[0]
    whole = lambda shape: pl.BlockSpec(shape, lambda p: (0,) * len(shape))
    own = pl.BlockSpec((rows, LANES), lambda p: (0, p))
    every = pl.BlockSpec((tokens, LANES), lambda p: (0, p))
    return pl.pallas_call(
        attention_backward_kernel,
        grid=(PAIRS,),
        in_specs=[
            pl.BlockSpec(memory_space=pltpu.SMEM),
            own,
            own,
            own,
            pl.BlockSpec((rows, LANES), lambda p: (0, PAIRS + p)),
            whole((rows, LANES)),
            whole((rows, LANES)),
            every,
            pl.BlockSpec((tokens, LANES), lambda p: (0, PAIRS + p)),
            every,
            every,
            whole(stats.shape),
            whole((rows, 1)),
            whole((1, tokens)),
        ],
        out_specs=whole((rows, 3 * D)),
        out_shape=jax.ShapeDtypeStruct((rows, 3 * D), BF16),
        scratch_shapes=[pltpu.VMEM((rows, tokens), F32), pltpu.VMEM((rows, tokens), F32)],
        compiler_params=pltpu.CompilerParams(vmem_limit_bytes=44 << 20),
        cost_estimate=pl.CostEstimate(
            flops=16 * rows * tokens * D,
            bytes_accessed=8 * tokens * D,
            transcendentals=rows * tokens * HEADS,
        ),
        name="attention_backward",
    )(
        start,
        queries,
        grads,
        kv_own,
        kv_own,
        lse,
        delta,
        kv,
        kv,
        q_all,
        grad_all,
        stats,
        own_segs,
        all_segs,
    )


def place_bits():
    ctx, fsdp = lax.axis_index("ctx"), lax.axis_index("fsdp")
    return lax.rem(ctx, 2), ctx // 2, fsdp // 2, lax.rem(fsdp, 2)


def greet(devices):
    barrier = pltpu.get_barrier_semaphore()
    for device in devices:
        pl.semaphore_signal(barrier, inc=1, device_id=device, device_id_type=MESH)
    pl.semaphore_wait(barrier, len(devices))


WEIGHT_COPIES = 11


def gather_weights_kernel(count, *refs):
    shares, fulls = refs[:count], refs[count : 2 * count]
    send_sems, recv_sems, local_sems = refs[2 * count : 2 * count + 3]
    stages = refs[2 * count + 3 :]
    x, z, y, core = place_bits()
    low = lax.rem(z, 2)
    z_next = z + 1 - 2 * low
    sibling = (2 * z + x, 2 * y + 1 - core)
    over_y = (2 * z + x, 2 * (1 - y) + core)
    over_x = (2 * z + 1 - x, 2 * y + core)
    over_z = (2 * z_next + x, 2 * y + core)
    own = 2 * y + core
    other = 2 * (1 - y) + core
    greet((sibling, over_y, over_x, over_z))

    def copy(index, which, src, dst, device):
        slot = which * WEIGHT_COPIES + index
        return pltpu.make_async_remote_copy(
            src_ref=src,
            dst_ref=dst,
            send_sem=send_sems.at[slot],
            recv_sem=recv_sems.at[slot],
            device_id=device,
            device_id_type=MESH,
        )

    started = []
    locals_started = []
    plans = []
    for which in range(count):
        share, full = shares[which], fulls[which]
        rows, columns = share.shape
        part = rows // 4
        half = columns // 2

        def piece(ref, x_bit, low_bit, part=part):
            return ref.at[pl.ds((2 * low_bit + x_bit) * part, part), :]

        def piece_half(ref, x_bit, low_bit, side, part=part, half=half):
            return ref.at[pl.ds((2 * low_bit + x_bit) * part, part), pl.ds(side * half, half)]

        theirs = full.at[other]
        same = lambda index, view, device, which=which: copy(index, which, view, view, device)
        mine = piece(theirs, x, low)
        from_x = piece(theirs, 1 - x, low)
        from_z = piece(theirs, x, 1 - low)
        plan = {
            0: copy(0, which, piece(share, x, low), piece(full.at[own], x, low), over_y),
            1: same(1, mine, over_x),
            2: same(2, mine, over_z),
            3: same(3, mine, sibling),
            4: same(4, piece_half(theirs, 1 - x, low, 0), over_z),
            5: same(5, from_x, sibling),
            6: same(6, piece_half(theirs, x, 1 - low, 1), over_x),
            7: same(7, from_z, sibling),
            8: same(8, piece_half(theirs, 1 - x, 1 - low, 0), sibling),
            9: same(9, piece_half(theirs, 1 - x, 1 - low, 1), sibling),
            10: copy(10, which, share, full.at[own], sibling),
        }
        plans.append(plan)
        plan[0].start()
        plan[10].start()
        pltpu.make_async_copy(share, stages[which], local_sems.at[which]).start()
        locals_started.append(
            (
                pltpu.make_async_copy(share, stages[which], local_sems.at[which]),
                pltpu.make_async_copy(stages[which], full.at[own], local_sems.at[which]),
            )
        )

    for into, out in locals_started:
        into.wait()
        out.start()

    for step in range(count + 2):
        if step < count:
            plan = plans[step]
            plan[0].wait_recv()
            plan[1].start()
            plan[2].start()
            plan[3].start()
        if 0 <= step - 1 < count:
            plan = plans[step - 1]
            plan[1].wait_recv()
            plan[4].start()
            plan[5].start()
            plan[2].wait_recv()
            plan[6].start()
            plan[7].start()
        if 0 <= step - 2 < count:
            plan = plans[step - 2]
            plan[4].wait_recv()
            plan[8].start()
            plan[6].wait_recv()
            plan[9].start()
    for plan in plans:
        for index in (3, 5, 7, 8, 9, 10):
            plan[index].wait_recv()
        for index in range(WEIGHT_COPIES):
            plan[index].wait_send()
    for _, out in locals_started:
        out.wait()


def gather_weights(shares, collective_id):
    count = len(shares)
    copies = count * WEIGHT_COPIES
    anywhere = pl.BlockSpec(memory_space=pl.ANY)
    fulls = pl.pallas_call(
        partial(gather_weights_kernel, count),
        in_specs=[anywhere] * count,
        out_specs=[anywhere] * count,
        out_shape=[jax.ShapeDtypeStruct((4, *share.shape), share.dtype) for share in shares],
        scratch_shapes=[
            pltpu.SemaphoreType.DMA((copies,)),
            pltpu.SemaphoreType.DMA((copies,)),
            pltpu.SemaphoreType.DMA((count,)),
        ]
        + [pltpu.VMEM(share.shape, share.dtype) for share in shares],
        compiler_params=pltpu.CompilerParams(collective_id=collective_id, has_side_effects=True),
        name="gather_weights",
    )(*shares)
    return fulls


BLOCK_COPIES = 13


def gather_blocks_kernel(count, *refs):
    blocks, fulls = refs[:count], refs[count : 2 * count]
    send_sems, recv_sems, local_sems = refs[2 * count :]
    x, z, y, core = place_bits()
    sibling = (2 * z + x, 2 * y + 1 - core)
    over_x = (2 * z + 1 - x, 2 * y + core)
    over_y = (2 * z + x, 2 * (1 - y) + core)
    greet((sibling, over_x, over_y))

    plans = []
    locals_started = []
    for which in range(count):
        block, full = blocks[which], fulls[which]
        half = block.shape[0] // 2

        def copy(index, src, dst, device, which=which):
            slot = which * BLOCK_COPIES + index
            return pltpu.make_async_remote_copy(
                src_ref=src,
                dst_ref=dst,
                send_sem=send_sems.at[slot],
                recv_sem=recv_sems.at[slot],
                device_id=device,
                device_id_type=MESH,
            )

        def part(ref, side, half=half):
            return ref.at[pl.ds(side * half, half), :]

        def slot_of(x_bit, y_bit, full=full):
            return full.at[4 * y_bit + 2 * core + x_bit]

        same = lambda index, view, device, copy=copy: copy(index, view, view, device)
        mine = slot_of(x, y)
        from_x, from_y, from_both = slot_of(1 - x, y), slot_of(x, 1 - y), slot_of(1 - x, 1 - y)
        plan = {
            0: copy(0, block, mine, sibling),
            1: copy(1, part(block, 0), part(mine, 0), over_x),
            2: copy(2, part(block, 1), part(mine, 1), over_y),
            3: copy(3, part(block, 1), part(mine, 1), over_x),
            4: copy(4, part(block, 0), part(mine, 0), over_y),
            5: same(5, part(from_x, 0), over_y),
            6: same(6, part(from_x, 0), sibling),
            7: same(7, part(from_y, 1), over_x),
            8: same(8, part(from_y, 1), sibling),
            9: same(9, part(from_x, 1), sibling),
            10: same(10, part(from_y, 0), sibling),
            11: same(11, part(from_both, 0), sibling),
            12: same(12, part(from_both, 1), sibling),
        }
        plans.append(plan)
        for index in (1, 2, 3, 4, 0):
            plan[index].start()
        local = pltpu.make_async_copy(block, mine, local_sems.at[which])
        local.start()
        locals_started.append(local)

    for plan in plans:
        plan[1].wait_recv()
        plan[5].start()
        plan[6].start()
        plan[2].wait_recv()
        plan[7].start()
        plan[8].start()
    for plan in plans:
        plan[3].wait_recv()
        plan[9].start()
        plan[4].wait_recv()
        plan[10].start()
    for plan in plans:
        plan[5].wait_recv()
        plan[11].start()
        plan[7].wait_recv()
        plan[12].start()
    for plan in plans:
        for index in (0, 6, 8, 9, 10, 11, 12):
            plan[index].wait_recv()
        for index in range(BLOCK_COPIES):
            plan[index].wait_send()
    for local in locals_started:
        local.wait()


def gather_blocks(blocks, collective_id):
    count = len(blocks)
    copies = count * BLOCK_COPIES
    anywhere = pl.BlockSpec(memory_space=pl.ANY)
    return pl.pallas_call(
        partial(gather_blocks_kernel, count),
        in_specs=[pl.BlockSpec(memory_space=pltpu.VMEM)] * count,
        out_specs=[anywhere] * count,
        out_shape=[jax.ShapeDtypeStruct((8, *block.shape), block.dtype) for block in blocks],
        scratch_shapes=[
            pltpu.SemaphoreType.DMA((copies,)),
            pltpu.SemaphoreType.DMA((copies,)),
            pltpu.SemaphoreType.DMA((count,)),
        ],
        compiler_params=pltpu.CompilerParams(collective_id=collective_id, has_side_effects=True),
        name="gather_blocks",
    )(*blocks)


CHUNK_ROWS, CHUNK_COLUMNS = 192, 768
REDUCE_COPIES = 9
VECTOR_AXES = 5


def chunk_places(shapes):
    return [
        (which, row, column)
        for which, (rows, columns) in enumerate(shapes)
        for row in range(0, rows, CHUNK_ROWS)
        for column in range(0, columns, CHUNK_COLUMNS)
    ]


def reduce_gradients_kernel(places, count, *refs):
    partials, vector = refs[:count], refs[count]
    sums, vector_out = refs[count + 1 : 2 * count + 1], refs[2 * count + 1]
    (
        own,
        got_core,
        got_y,
        to_x,
        got_x,
        to_z,
        got_z,
        to_zz,
        got_zz,
        vector_got,
        send_sems,
        recv_sems,
        local_sems,
    ) = refs[2 * count + 2 :]
    x, z, y, core = place_bits()
    low, high = lax.rem(z, 2), z // 2
    fsdp = 2 * y + core
    sibling = (2 * z + x, 2 * y + 1 - core)
    over_y = (2 * z + x, 2 * (1 - y) + core)
    over_x = (2 * z + 1 - x, fsdp)
    over_z = (2 * (z + 1 - 2 * low) + x, fsdp)
    over_zz = (2 * (z + 2 - 4 * high) + x, fsdp)
    greet((sibling, over_y, over_x, over_z, over_zz))

    def copy(slot, src, dst, device):
        return pltpu.make_async_remote_copy(
            src_ref=src,
            dst_ref=dst,
            send_sem=send_sems.at[slot],
            recv_sem=recv_sems.at[slot],
            device_id=device,
            device_id_type=MESH,
        )

    x_rows, z_rows, zz_columns = CHUNK_ROWS // 2, CHUNK_ROWS // 4, CHUNK_COLUMNS // 2
    chunks = len(places)

    def add_up(store, loads, rows):
        step = z_rows

        def visit(index, carried):
            offset = pl.multiple_of(index * step, 16)
            total = loads[0](offset, step).astype(F32)
            for load in loads[1:]:
                total = total + load(offset, step).astype(F32)
            store(offset, step, total.astype(BF16))
            return carried

        if rows == step:
            visit(0, 0)
        else:
            lax.fori_loop(0, rows // step, visit, 0)

    vector_devices = (over_y, sibling, over_x, over_z, over_zz)
    vector_copies = [
        copy(chunks * REDUCE_COPIES + i, vector_out, vector_got.at[i], vector_devices[i])
        for i in range(VECTOR_AXES)
    ]
    vector_out[...] = vector[...]
    vector_copies[0].start()

    plans = []
    loads = []
    for k, (which, row, column) in enumerate(places):
        partial_sum, out = partials[which], sums[which]

        def term(quarter, partial_sum=partial_sum, row=row, column=column):
            return partial_sum.at[quarter, pl.ds(row, CHUNK_ROWS), pl.ds(column, CHUNK_COLUMNS)]

        def piece(first, rows, start, width, out=out, row=row, column=column):
            return out.at[
                pl.ds(pl.multiple_of(row + first, 16), rows),
                pl.ds(pl.multiple_of(column + start, LANES), width),
            ]

        final = piece(x * x_rows + low * z_rows, z_rows, high * zz_columns, zz_columns)
        wide = piece(x * x_rows + low * z_rows, z_rows, 0, CHUNK_COLUMNS)
        tall = piece(x * x_rows, x_rows, 0, CHUNK_COLUMNS)
        base = k * REDUCE_COPIES
        plans.append(
            {
                "core0": copy(base, term(1 - core), got_core.at[k, 0], sibling),
                "core1": copy(base + 1, term(3 - core), got_core.at[k, 1], sibling),
                "y": copy(base + 2, own.at[k, 1 - y], got_y.at[k], over_y),
                "x": copy(base + 3, to_x.at[k], got_x.at[k], over_x),
                "z": copy(base + 4, to_z.at[k], got_z.at[k], over_z),
                "zz": copy(base + 5, to_zz.at[k], got_zz.at[k], over_zz),
                "zz_back": copy(base + 6, final, final, over_zz),
                "z_back": copy(base + 7, wide, wide, over_z),
                "x_back": copy(base + 8, tall, tall, over_x),
                "final": final,
            }
        )
        loads.append(
            [
                pltpu.make_async_copy(term(2 * i + core), own.at[k, i], local_sems.at[2 * k + i])
                for i in range(2)
            ]
        )
        plans[k]["core0"].start()
        plans[k]["core1"].start()
        loads[k][0].start()
        loads[k][1].start()

    def slab(ref, *index, first=0, start=None, width=None):
        def load(offset, rows):
            place = pl.ds(pl.multiple_of(first + offset, 16), rows)
            if width is None:
                return ref[(*index, place)]
            return ref[(*index, place, pl.ds(pl.multiple_of(start, LANES), width))]

        return load

    def stage_y(k):
        plan = plans[k]
        for load in loads[k]:
            load.wait()
        plan["core0"].wait_recv()
        plan["core1"].wait_recv()

        def store(offset, rows, value):
            own[k, 1 - y, pl.ds(offset, rows)] = value

        add_up(store, [slab(own, k, 1 - y), slab(got_core, k, 1 - y)], CHUNK_ROWS)
        plan["y"].start()

    def stage_x(k):
        plan = plans[k]
        plan["y"].wait_recv()
        first = (1 - x) * x_rows

        def store(offset, rows, value):
            to_x[k, pl.ds(offset, rows)] = value

        add_up(
            store,
            [slab(own, k, y, first=first), slab(got_core, k, y, first=first), slab(got_y, k, first=first)],
            x_rows,
        )
        plan["x"].start()

    def stage_z(k):
        plan = plans[k]
        plan["x"].wait_recv()
        inner = (1 - low) * z_rows
        first = x * x_rows + inner

        def store(offset, rows, value):
            to_z[k] = value

        add_up(
            store,
            [
                slab(own, k, y, first=first),
                slab(got_core, k, y, first=first),
                slab(got_y, k, first=first),
                slab(got_x, k, first=inner),
            ],
            z_rows,
        )
        plan["z"].start()

    def last_loads(k, start):
        inner = low * z_rows
        first = x * x_rows + inner
        part = {"start": start, "width": zz_columns}
        return [
            slab(own, k, y, first=first, **part),
            slab(got_core, k, y, first=first, **part),
            slab(got_y, k, first=first, **part),
            slab(got_x, k, first=inner, **part),
            slab(got_z, k, **part),
        ]

    def stage_zz(k):
        plan = plans[k]
        plan["z"].wait_recv()

        def store(offset, rows, value):
            to_zz[k] = value

        add_up(store, last_loads(k, (1 - high) * zz_columns), z_rows)
        plan["zz"].start()

    def stage_final(k):
        plan = plans[k]
        plan["zz"].wait_recv()

        def store(offset, rows, value):
            plan["final"][...] = value

        add_up(store, last_loads(k, high * zz_columns) + [slab(got_zz, k)], z_rows)
        plan["zz_back"].start()

    def stage_z_back(k):
        plans[k]["zz_back"].wait_recv()
        plans[k]["z_back"].start()

    def stage_x_back(k):
        plans[k]["z_back"].wait_recv()
        plans[k]["x_back"].start()

    def vector_step(index):
        vector_copies[index].wait()
        vector_out[...] = vector_out[...] + vector_got[index]
        if index + 1 < VECTOR_AXES:
            vector_copies[index + 1].start()

    for k in range(chunks):
        stage_y(k)
    stages = (stage_x, stage_z, stage_zz, stage_final, stage_z_back, stage_x_back)
    for tick in range(chunks + len(stages) - 1):
        if tick < VECTOR_AXES:
            vector_step(tick)
        for lag, stage in enumerate(stages):
            if 0 <= tick - lag < chunks:
                stage(tick - lag)
    for plan in plans:
        plan["x_back"].wait_recv()
        for name in ("core0", "core1", "y", "x", "z", "zz", "zz_back", "z_back", "x_back"):
            plan[name].wait_send()


def reduce_gradients(partials, vector, collective_id):
    count = len(partials)
    places = chunk_places([partial_sum.shape[1:] for partial_sum in partials])
    chunks = len(places)
    slots = chunks * REDUCE_COPIES + VECTOR_AXES
    rows, columns = CHUNK_ROWS, CHUNK_COLUMNS
    buffers = [
        (2, rows, columns),
        (2, rows, columns),
        (rows, columns),
        (rows // 2, columns),
        (rows // 2, columns),
        (rows // 4, columns),
        (rows // 4, columns),
        (rows // 4, columns // 2),
        (rows // 4, columns // 2),
    ]
    vmem = pl.BlockSpec(memory_space=pltpu.VMEM)
    return pl.pallas_call(
        partial(reduce_gradients_kernel, places, count),
        in_specs=[pl.BlockSpec(memory_space=pl.ANY)] * count + [vmem],
        out_specs=[vmem] * (count + 1),
        out_shape=[jax.ShapeDtypeStruct(p.shape[1:], BF16) for p in partials]
        + [jax.ShapeDtypeStruct(vector.shape, F32)],
        scratch_shapes=[pltpu.VMEM((chunks, *shape), BF16) for shape in buffers]
        + [
            pltpu.VMEM((VECTOR_AXES, *vector.shape), F32),
            pltpu.SemaphoreType.DMA((slots,)),
            pltpu.SemaphoreType.DMA((slots,)),
            pltpu.SemaphoreType.DMA((2 * chunks,)),
        ],
        compiler_params=pltpu.CompilerParams(
            collective_id=collective_id, has_side_effects=True, vmem_limit_bytes=48 << 20
        ),
        name="reduce_gradients",
    )(*partials, vector)


class PlaneLinks:
    def __init__(self):
        self.x, self.z, self.y, self.core = place_bits()
        self.block = 2 * lax.axis_index("fsdp") + self.x
        self.count = 8

    def permute(self, value, target):
        pairs = [(c * 4 + f, target(c, f)) for c in range(8) for f in range(4)]
        return lax.ppermute(value, ("ctx", "fsdp"), pairs)

    def swap(self, value):
        return self.permute(value, lambda c, f: (2 * f + c % 2) * 4 + c // 2)

    enter = swap
    leave = swap

    def weights(self, shares):
        return gather_weights(shares, 0)

    def blocks(self, blocks, collective_id):
        return gather_blocks(blocks, collective_id)

    def sum_gradients(self, factors, packed):
        terms = []
        for left, right in factors:
            term = column_products(left, right).astype(BF16)
            terms.append(term.reshape(4, term.shape[0] // 4, term.shape[1]))
        *sums, vector = reduce_gradients(terms, packed.reshape(-1, LANES), 4)
        vector = vector.reshape(packed.shape)
        mine = lax.dynamic_index_in_dim(vector, 2 * self.y + self.core, 0, keepdims=False)
        return [total.astype(F32) for total in sums], mine


class PlainLinks:
    def __init__(self, ctx_size, fsdp_size):
        self.block = lax.axis_index("ctx")
        self.count = ctx_size
        self.fsdp_size = fsdp_size

    def enter(self, value):
        return value

    leave = enter

    def weights(self, shares):
        return [lax.all_gather(share, "fsdp", axis=0) for share in shares]

    def blocks(self, blocks, collective_id):
        return [lax.all_gather(block, "ctx", axis=0) for block in blocks]

    def sum_gradients(self, factors, packed):
        sums = []
        for left, right in factors:
            term = column_products(left, right).astype(BF16)
            share = lax.psum_scatter(term, "fsdp", scatter_dimension=0, tiled=True)
            sums.append(lax.psum(share.astype(F32), "ctx"))
        share = lax.psum_scatter(packed, "fsdp", scatter_dimension=0, tiled=False)
        return sums, lax.psum(share, "ctx")


def layer_forward(resid, weights, links, start, own_segs, segs, layer_index):
    (
        gain_one,
        bias_one,
        weight_qkv,
        bias_qv,
        weight_proj,
        bias_proj,
        gain_two,
        bias_two,
        weight_fc,
        bias_fc,
        weight_out,
        bias_out,
    ) = weights
    normed_one, normal_one, inverse_one = norm_forward(resid, gain_one, bias_one)
    projected = jnp.dot(normed_one, weight_qkv, preferred_element_type=F32)
    biases = jnp.concatenate([bias_qv[:D], jnp.zeros((D,), F32), bias_qv[D:]])
    projected = (projected + biases).astype(BF16)
    queries, kv_own = projected[:, :D], projected[:, D:]
    if layer_index == 0:
        kv, segs = links.blocks([kv_own, segs], 1)
        segs = segs[:, 0, :].reshape(1, -1)
    else:
        (kv,) = links.blocks([kv_own], 2)
    kv = kv.reshape(-1, 2 * D)
    attended, lse, lse_rows = attention_forward(start, queries, kv, own_segs, segs)
    middle = resid + jnp.dot(attended, weight_proj, preferred_element_type=F32) + bias_proj
    normed_two, normal_two, inverse_two = norm_forward(middle, gain_two, bias_two)
    hidden = jnp.dot(normed_two, weight_fc, preferred_element_type=F32) + bias_fc
    activated = jax.nn.gelu(hidden, approximate=True).astype(BF16)
    result_rows = middle + jnp.dot(activated, weight_out, preferred_element_type=F32) + bias_out
    saved = (
        normed_one,
        normal_one,
        inverse_one,
        queries,
        kv_own,
        kv,
        attended,
        lse,
        lse_rows,
        normed_two,
        normal_two,
        inverse_two,
        hidden,
        activated,
    )
    return result_rows, saved, segs


def layer_backward(gradient, weights, saved, links, start, own_segs, segs):
    (
        gain_one,
        _,
        weight_qkv,
        _,
        weight_proj,
        _,
        gain_two,
        _,
        weight_fc,
        _,
        weight_out,
        _,
    ) = weights
    (
        normed_one,
        normal_one,
        inverse_one,
        queries,
        kv_own,
        kv,
        attended,
        lse,
        lse_rows,
        normed_two,
        normal_two,
        inverse_two,
        hidden,
        activated,
    ) = saved
    rows = gradient.shape[0]
    total = lambda value: jnp.sum(value.astype(F32), axis=0)
    grad_branch = gradient.astype(BF16)
    grad_activated = dot_rows(grad_branch, weight_out)
    gelu_pull = jax.vjp(partial(jax.nn.gelu, approximate=True), hidden)[1]
    grad_hidden = gelu_pull(grad_activated)[0].astype(BF16)
    grad_normed_two = dot_rows(grad_hidden, weight_fc)
    grad_in_two, grad_gain_two, grad_bias_two = norm_backward(
        grad_normed_two, normal_two, inverse_two, gain_two
    )
    grad_middle = gradient + grad_in_two
    grad_proj = grad_middle.astype(BF16)
    grad_attended = dot_rows(grad_proj, weight_proj).astype(BF16)
    products = grad_attended.astype(F32) * attended.astype(F32)
    head_of = jnp.arange(D, dtype=jnp.int32) // HDIM
    by_lane = (head_of[:, None] == jnp.arange(LANES, dtype=jnp.int32)[None, :]).astype(F32)
    by_row = (jnp.arange(16, dtype=jnp.int32)[:, None] == head_of[None, :]).astype(F32)
    delta = jnp.dot(products, by_lane, precision=lax.Precision.HIGHEST, preferred_element_type=F32)
    delta_rows = lax.dot_general(
        by_row,
        products,
        (((1,), (1,)), ((), ())),
        precision=lax.Precision.HIGHEST,
        preferred_element_type=F32,
    )
    stats = jnp.concatenate([lse_rows, delta_rows], axis=0)
    q_all, grad_all, stats = links.blocks([queries, grad_attended, stats], 3)
    grad_projected = attention_backward(
        start,
        queries,
        grad_attended,
        kv_own,
        lse,
        delta,
        kv,
        q_all.reshape(-1, D),
        grad_all.reshape(-1, D),
        stats,
        own_segs,
        segs,
    )
    grad_normed_one = dot_rows(grad_projected, weight_qkv)
    grad_in_one, grad_gain_one, grad_bias_one = norm_backward(
        grad_normed_one, normal_one, inverse_one, gain_one
    )
    grad_input = grad_middle + grad_in_one
    matrices = (
        (activated, grad_branch),
        (normed_two, grad_hidden),
        (attended, grad_proj),
        (normed_one, grad_projected),
    )
    vectors = (
        grad_gain_one,
        grad_bias_one,
        jnp.concatenate([total(grad_projected[:, :D]), total(grad_projected[:, 2 * D :])]),
        total(grad_proj),
        grad_gain_two,
        grad_bias_two,
        total(grad_hidden),
        total(grad_branch),
    )
    return grad_input, matrices, vectors


def body(
    links_of,
    tokens,
    segment_ids,
    ln1_gain,
    ln1_bias,
    attn_weight,
    attn_bias,
    proj_weight,
    proj_bias,
    ln2_gain,
    ln2_bias,
    fc_weight,
    fc_bias,
    out_weight,
    out_bias,
    out_cotangent,
):
    members, seq_dev, features = tokens.shape
    links = links_of()
    start = (links.block * seq_dev).reshape(1).astype(jnp.int32)
    resid = links.enter(tokens[0])
    segs_row = links.enter(segment_ids)
    gradient = links.enter(out_cotangent[0])
    own_segs = segs_row.reshape(seq_dev, 1)
    segs = jnp.broadcast_to(segs_row, (16, seq_dev))

    vectors = (ln1_gain, ln1_bias, attn_bias, proj_bias, ln2_gain, ln2_bias, fc_bias, out_bias)
    sizes = [vector.shape[0] for vector in vectors]
    packed = jnp.concatenate(vectors)
    padding = -packed.shape[0] % (64 * 2 * LANES)
    packed = jnp.pad(packed, (0, padding)).reshape(-1, 2 * LANES)
    qkv_full, packed, proj_full, fc_full, out_full = links.weights(
        [attn_weight, packed, proj_weight, fc_weight, out_weight]
    )
    matrix = lambda full: full.reshape(-1, full.shape[-1])
    packed = packed.reshape(packed.shape[0], -1).astype(F32)
    pieces = []
    offset = 0
    for size in sizes:
        pieces.append(packed[:, offset : offset + size].reshape(-1))
        offset += size
    gain_one, bias_one, bias_qv, bias_proj, gain_two, bias_two, bias_fc, bias_out = pieces
    weights = (
        gain_one,
        bias_one,
        matrix(qkv_full),
        bias_qv,
        matrix(proj_full),
        bias_proj,
        gain_two,
        bias_two,
        matrix(fc_full),
        bias_fc,
        matrix(out_full),
        bias_out,
    )

    resid = resid.astype(F32)
    saved_layers = []
    for layer_index in range(2):
        resid, saved, segs = layer_forward(
            resid, weights, links, start, own_segs, segs, layer_index
        )
        saved_layers.append(saved)
    output = links.leave(resid.astype(BF16))
    gradient = gradient.astype(F32)
    collected = []
    for layer_index in (1, 0):
        gradient, matrices, terms = layer_backward(
            gradient, weights, saved_layers[layer_index], links, start, own_segs, segs
        )
        collected.append((matrices, terms))
    tokens_grad = links.leave(gradient.astype(BF16))

    factors = []
    for second, first in zip(collected[0][0], collected[1][0]):
        left = jnp.concatenate([second[0], first[0]], axis=0)
        right = jnp.concatenate([second[1], first[1]], axis=0)
        factors.append((left, right))
    shares = packed.shape[0]
    added = [a + b for a, b in zip(collected[0][1], collected[1][1])]
    rows = jnp.concatenate([vector.reshape(shares, -1) for vector in added], axis=1)
    sums, summed = links.sum_gradients(factors, rows.reshape(shares, -1, LANES))
    out_grad, fc_grad, proj_grad, qkv_grad = sums
    summed = summed.reshape(-1)
    small = []
    offset = 0
    for size in sizes:
        small.append(summed[offset : offset + size])
        offset += size
    g_gain_one, g_bias_one, g_bias_qv, g_bias_proj, g_gain_two, g_bias_two, g_bias_fc, g_bias_out = small
    return (
        output[None],
        tokens_grad[None],
        g_gain_one,
        g_bias_one,
        qkv_grad,
        g_bias_qv,
        proj_grad,
        g_bias_proj,
        g_gain_two,
        g_bias_two,
        fc_grad,
        g_bias_fc,
        out_grad,
        g_bias_out,
    )


def solution(mesh):
    ctx_size, fsdp_size = mesh.shape["ctx"], mesh.shape["fsdp"]
    if (ctx_size, fsdp_size) == (8, 4):
        links_of = PlaneLinks
    else:
        links_of = partial(PlainLinks, ctx_size, fsdp_size)
    rows = P("fsdp", "ctx", None)
    vector, matrix = P("fsdp"), P("fsdp", None)
    in_specs = (
        rows,
        P("fsdp", "ctx"),
        vector,
        vector,
        matrix,
        vector,
        matrix,
        vector,
        vector,
        vector,
        matrix,
        vector,
        matrix,
        vector,
        rows,
    )
    out_specs = (
        rows,
        rows,
        vector,
        vector,
        matrix,
        vector,
        matrix,
        vector,
        vector,
        vector,
        matrix,
        vector,
        matrix,
        vector,
    )
    return jax.shard_map(
        partial(body, links_of), mesh=mesh, in_specs=in_specs, out_specs=out_specs, check_vma=False
    )
```

```python
from functools import partial

import jax
import jax.numpy as jnp
from jax import lax
from jax.experimental import pallas as pl
from jax.experimental.pallas import tpu as pltpu
from jax.sharding import PartitionSpec as P

D = 768
HEADS = 12
HDIM = 64
PAIRS = HEADS // 2
LANES = 128
EPSILON = 1e-05
NEGATIVE = -1e30
SCALE = HDIM ** (-0.5)
MESH = pl.DeviceIdType.MESH
F32 = jnp.float32
BF16 = jnp.bfloat16


def norm_forward(resid, gain_row, bias_row):
    average = jnp.mean(resid, axis=-1, keepdims=True)
    centred = resid - average
    variance = jnp.mean(centred * centred, axis=-1, keepdims=True)
    inverse = lax.rsqrt(variance + EPSILON)
    normal = centred * inverse
    return ((normal * gain_row + bias_row).astype(BF16), normal, inverse)


def norm_backward(grad_normed, normal, inverse, gain_row):
    scaled = grad_normed * gain_row
    mean_term = jnp.mean(scaled, axis=-1, keepdims=True)
    second = jnp.mean(scaled * normal, axis=-1, keepdims=True)
    grad_input = inverse * (scaled - mean_term - normal * second)
    return (grad_input, jnp.sum(grad_normed * normal, axis=0), jnp.sum(grad_normed, axis=0))


def two_heads(rows):
    lane = lax.broadcasted_iota(jnp.int32, rows.shape, 1)
    zero = jnp.zeros_like(rows)
    first = jnp.where(lane < HDIM, rows, zero)
    second = jnp.where(lane < HDIM, zero, rows)
    return jnp.concatenate([first, second], axis=0)


def one_pair(stacked):
    half = stacked.shape[0] // 2
    lane = lax.broadcasted_iota(jnp.int32, (half, LANES), 1)
    return jnp.where(lane < HDIM, stacked[:half], stacked[half:])


def dot_rows(left, right):
    return lax.dot_general(left, right, (((1,), (1,)), ((), ())), preferred_element_type=F32)


def column_products(left, right):
    return lax.dot_general(left, right, (((0,), (0,)), ((), ())), preferred_element_type=F32)


def pick_lanes(columns, pair):
    lane = lax.broadcasted_iota(jnp.int32, columns.shape, 1)
    first = jnp.sum(jnp.where(lane == 2 * pair, columns, 0.0), axis=1, keepdims=True)
    second = jnp.sum(jnp.where(lane == 2 * pair + 1, columns, 0.0), axis=1, keepdims=True)
    return jnp.concatenate([first, second], axis=0)


def mask_columns(bias_ref, own_segs, all_segs_ref, start, own_is_query):
    rows, columns = bias_ref.shape
    step = min(1024, columns)
    own_place = start + lax.broadcasted_iota(jnp.int32, (rows, step), 0)
    for offset in range(0, columns, step):
        place = offset + lax.broadcasted_iota(jnp.int32, (rows, step), 1)
        causal = (place <= own_place) if own_is_query else (own_place <= place)
        same = own_segs == all_segs_ref[:, offset : offset + step]
        bias_ref[:, offset : offset + step] = jnp.where(causal & same, 0.0, NEGATIVE)


def attention_forward_kernel(
    start_ref, q_ref, k_ref, v_ref, own_segs_ref, all_segs_ref, out_ref, lse_ref, lse_rows_ref, bias_ref
):
    pair = pl.program_id(0)
    rows, keys = bias_ref.shape

    @pl.when(pair == 0)
    def _():
        mask_columns(bias_ref, own_segs_ref[...], all_segs_ref, start_ref[0], True)
        lse_ref[...] = jnp.zeros_like(lse_ref)

    queries = two_heads(q_ref[...] * jnp.asarray(SCALE, BF16))
    step = min(1024, keys)

    def scores_of(offset):
        scores = dot_rows(queries, k_ref[pl.ds(offset, step), :])
        bias = bias_ref[:, pl.ds(offset, step)]
        return scores + jnp.concatenate([bias, bias], axis=0)

    if step == keys:
        scores = scores_of(0)
        top = jnp.max(scores, axis=1, keepdims=True)
        weights = jnp.exp(scores - top)
        total = jnp.sum(weights, axis=1, keepdims=True)
        mixed = jnp.dot(weights.astype(BF16), v_ref[...], preferred_element_type=F32)
    else:

        def visit(index, carried):
            top, total, mixed = carried
            offset = pl.multiple_of(index * step, step)
            scores = scores_of(offset)
            new_top = jnp.maximum(top, jnp.max(scores, axis=1, keepdims=True))
            weights = jnp.exp(scores - new_top)
            factor = jnp.exp(top - new_top)
            total = total * factor + jnp.sum(weights, axis=1, keepdims=True)
            more = jnp.dot(
                weights.astype(BF16), v_ref[pl.ds(offset, step), :], preferred_element_type=F32
            )
            return new_top, total, mixed * factor + more

        top, total, mixed = lax.fori_loop(
            0,
            (start_ref[0] + rows + step - 1) // step,
            visit,
            (
                jnp.full((2 * rows, 1), NEGATIVE, F32),
                jnp.zeros((2 * rows, 1), F32),
                jnp.zeros((2 * rows, LANES), F32),
            ),
        )
    out_ref[...] = one_pair(mixed / total).astype(BF16)
    lse = top + jnp.log(total)
    lane = lax.broadcasted_iota(jnp.int32, (rows, LANES), 1)
    kept = lse_ref[...]
    kept = jnp.where(lane == 2 * pair, lse[:rows], kept)
    kept = jnp.where(lane == 2 * pair + 1, lse[rows:], kept)
    lse_ref[...] = kept

    @pl.when(pair == PAIRS - 1)
    def _():
        lse_rows_ref[...] = kept.T[:16]


def attention_forward(start, queries, kv, own_segs, all_segs):
    rows = queries.shape[0]
    keys = kv.shape[0]
    whole = lambda shape: pl.BlockSpec(shape, lambda p: (0, 0))
    return pl.pallas_call(
        attention_forward_kernel,
        grid=(PAIRS,),
        in_specs=[
            pl.BlockSpec(memory_space=pltpu.SMEM),
            pl.BlockSpec((rows, LANES), lambda p: (0, p)),
            pl.BlockSpec((keys, LANES), lambda p: (0, p)),
            pl.BlockSpec((keys, LANES), lambda p: (0, PAIRS + p)),
            whole((rows, 1)),
            whole((1, keys)),
        ],
        out_specs=[
            pl.BlockSpec((rows, LANES), lambda p: (0, p)),
            whole((rows, LANES)),
            whole((16, rows)),
        ],
        out_shape=[
            jax.ShapeDtypeStruct((rows, D), BF16),
            jax.ShapeDtypeStruct((rows, LANES), F32),
            jax.ShapeDtypeStruct((16, rows), F32),
        ],
        scratch_shapes=[pltpu.VMEM((rows, keys), F32)],
        compiler_params=pltpu.CompilerParams(vmem_limit_bytes=40 << 20),
        cost_estimate=pl.CostEstimate(
            flops=8 * rows * keys * D, bytes_accessed=4 * keys * D, transcendentals=rows * keys * HEADS
        ),
        name="attention_forward",
    )(start, queries, kv, kv, own_segs, all_segs)


def attention_backward_kernel(
    start_ref,
    q_ref,
    grad_ref,
    k_own_ref,
    v_own_ref,
    lse_ref,
    delta_ref,
    k_ref,
    v_ref,
    q_all_ref,
    grad_all_ref,
    stats_ref,
    own_segs_ref,
    all_segs_ref,
    out_ref,
    query_bias_ref,
    key_bias_ref,
):
    pair = pl.program_id(0)
    rows, tokens = query_bias_ref.shape
    start = start_ref[0]

    @pl.when(pair == 0)
    def _():
        mask_columns(query_bias_ref, own_segs_ref[...], all_segs_ref, start, True)
        mask_columns(key_bias_ref, own_segs_ref[...], all_segs_ref, start, False)

    step = min(256, tokens)
    blocks = step // rows
    scale = jnp.asarray(SCALE, BF16)

    def doubled(bias):
        return jnp.concatenate([bias, bias], axis=0)

    queries = two_heads(q_ref[...] * scale)
    grads = two_heads(grad_ref[...])
    lse = pick_lanes(lse_ref[...], pair)
    delta = pick_lanes(delta_ref[...], pair)

    def visit_keys(index, grad_query):
        offset = pl.multiple_of(index * step, step)
        keys = k_ref[pl.ds(offset, step), :]
        values = v_ref[pl.ds(offset, step), :]
        bias = doubled(query_bias_ref[:, pl.ds(offset, step)])
        attention = jnp.exp(dot_rows(queries, keys) + bias - lse)
        grad_attention = dot_rows(grads, values)
        grad_scores = (attention * (grad_attention - delta)).astype(BF16)
        return grad_query + jnp.dot(grad_scores, keys, preferred_element_type=F32)

    zeros = jnp.zeros((2 * rows, LANES), F32)
    grad_query = lax.fori_loop(0, (start + rows + step - 1) // step, visit_keys, zeros)

    own_keys = two_heads(k_own_ref[...] * scale)
    own_values = two_heads(v_own_ref[...])

    def row_of(block, row):
        return jnp.broadcast_to(stats_ref[block, pl.ds(row, 1), :], (rows, rows))

    def stat_rows(index, row):
        first = [row_of(index * blocks + b, row + 2 * pair) for b in range(blocks)]
        second = [row_of(index * blocks + b, row + 2 * pair + 1) for b in range(blocks)]
        return jnp.concatenate(
            [jnp.concatenate(first, axis=1), jnp.concatenate(second, axis=1)], axis=0
        )

    def visit_queries(index, carried):
        grad_keys, grad_values = carried
        offset = pl.multiple_of(index * step, step)
        later = q_all_ref[pl.ds(offset, step), :]
        later_grads = grad_all_ref[pl.ds(offset, step), :]
        bias = doubled(key_bias_ref[:, pl.ds(offset, step)])
        attention = jnp.exp(dot_rows(own_keys, later) + bias - stat_rows(index, 0))
        grad_attention = dot_rows(own_values, later_grads)
        grad_scores = (attention * (grad_attention - stat_rows(index, 16))).astype(BF16)
        grad_keys = grad_keys + jnp.dot(grad_scores, later, preferred_element_type=F32)
        grad_values = grad_values + jnp.dot(
            attention.astype(BF16), later_grads, preferred_element_type=F32
        )
        return grad_keys, grad_values

    grad_keys, grad_values = lax.fori_loop(
        start // step, tokens // step, visit_queries, (zeros, zeros)
    )
    base = pl.multiple_of(pair * LANES, LANES)
    out_ref[:, pl.ds(base, LANES)] = (one_pair(grad_query) * SCALE).astype(BF16)
    out_ref[:, pl.ds(D + base, LANES)] = (one_pair(grad_keys) * SCALE).astype(BF16)
    out_ref[:, pl.ds(2 * D + base, LANES)] = one_pair(grad_values).astype(BF16)


def attention_backward(
    start, queries, grads, kv_own, lse, delta, kv, q_all, grad_all, stats, own_segs, all_segs
):
    rows = queries.shape[0]
    tokens = kv.shape[0]
    whole = lambda shape: pl.BlockSpec(shape, lambda p: (0,) * len(shape))
    own = pl.BlockSpec((rows, LANES), lambda p: (0, p))
    every = pl.BlockSpec((tokens, LANES), lambda p: (0, p))
    return pl.pallas_call(
        attention_backward_kernel,
        grid=(PAIRS,),
        in_specs=[
            pl.BlockSpec(memory_space=pltpu.SMEM),
            own,
            own,
            own,
            pl.BlockSpec((rows, LANES), lambda p: (0, PAIRS + p)),
            whole((rows, LANES)),
            whole((rows, LANES)),
            every,
            pl.BlockSpec((tokens, LANES), lambda p: (0, PAIRS + p)),
            every,
            every,
            whole(stats.shape),
            whole((rows, 1)),
            whole((1, tokens)),
        ],
        out_specs=whole((rows, 3 * D)),
        out_shape=jax.ShapeDtypeStruct((rows, 3 * D), BF16),
        scratch_shapes=[pltpu.VMEM((rows, tokens), F32), pltpu.VMEM((rows, tokens), F32)],
        compiler_params=pltpu.CompilerParams(vmem_limit_bytes=44 << 20),
        cost_estimate=pl.CostEstimate(
            flops=16 * rows * tokens * D,
            bytes_accessed=8 * tokens * D,
            transcendentals=rows * tokens * HEADS,
        ),
        name="attention_backward",
    )(
        start,
        queries,
        grads,
        kv_own,
        kv_own,
        lse,
        delta,
        kv,
        kv,
        q_all,
        grad_all,
        stats,
        own_segs,
        all_segs,
    )


def place_bits():
    ctx, fsdp = lax.axis_index("ctx"), lax.axis_index("fsdp")
    return lax.rem(ctx, 2), ctx // 2, fsdp // 2, lax.rem(fsdp, 2)


class Place:
    def __init__(self):
        self.x, self.z, self.y, self.core = x, z, y, core = place_bits()
        self.low, self.high = low, high = lax.rem(z, 2), z // 2
        self.fsdp = fsdp = 2 * y + core
        self.block = 2 * fsdp + x
        self.sibling = (2 * z + x, 2 * y + 1 - core)
        self.over_y = (2 * z + x, 2 * (1 - y) + core)
        self.over_x = (2 * z + 1 - x, fsdp)
        self.over_z = (2 * (z + 1 - 2 * low) + x, fsdp)
        self.over_zz = (2 * (z + 2 - 4 * high) + x, fsdp)
        self.partner = (2 * fsdp + x, z)
        self.has_partner = fsdp != z


class Copies:
    def __init__(self, send_sems, recv_sems):
        self.send_sems, self.recv_sems = send_sems, recv_sems
        self.used = 0

    def make(self, src, dst, device):
        slot = self.used
        self.used += 1
        return pltpu.make_async_remote_copy(
            src_ref=src,
            dst_ref=dst,
            send_sem=self.send_sems.at[slot],
            recv_sem=self.recv_sems.at[slot],
            device_id=device,
            device_id_type=MESH,
        )


def greet(devices):
    barrier = pltpu.get_barrier_semaphore()
    for device in devices:
        pl.semaphore_signal(barrier, inc=1, device_id=device, device_id_type=MESH)
    pl.semaphore_wait(barrier, len(devices))


WEIGHT_COPIES = 11


class WeightGather:
    def __init__(self, place, copies, shares, fulls, stages, local_sems):
        x, low = place.x, place.low
        own, other = place.fsdp, 2 * (1 - place.y) + place.core
        self.plans = []
        self.locals = []
        for which, (share, full) in enumerate(zip(shares, fulls)):
            rows, columns = share.shape
            part, half = rows // 4, columns // 2

            def piece(ref, x_bit, low_bit, part=part):
                return ref.at[pl.ds((2 * low_bit + x_bit) * part, part), :]

            def side(ref, x_bit, low_bit, index, part=part, half=half):
                place_of = pl.ds((2 * low_bit + x_bit) * part, part)
                return ref.at[place_of, pl.ds(index * half, half)]

            theirs = full.at[other]
            same = lambda view, device: copies.make(view, view, device)
            mine = piece(theirs, x, low)
            from_x, from_z = piece(theirs, 1 - x, low), piece(theirs, x, 1 - low)
            self.plans.append(
                [
                    copies.make(piece(share, x, low), piece(full.at[own], x, low), place.over_y),
                    same(mine, place.over_x),
                    same(mine, place.over_z),
                    same(mine, place.sibling),
                    same(side(theirs, 1 - x, low, 0), place.over_z),
                    same(from_x, place.sibling),
                    same(side(theirs, x, 1 - low, 1), place.over_x),
                    same(from_z, place.sibling),
                    same(side(theirs, 1 - x, 1 - low, 0), place.sibling),
                    same(side(theirs, 1 - x, 1 - low, 1), place.sibling),
                    copies.make(share, full.at[own], place.sibling),
                ]
            )
            sem = local_sems.at[which]
            self.locals.append(
                (
                    pltpu.make_async_copy(share, stages[which], sem),
                    pltpu.make_async_copy(stages[which], full.at[own], sem),
                )
            )

    def begin(self):
        for plan, (into, _) in zip(self.plans, self.locals):
            plan[0].start()
            plan[10].start()
            into.start()

    def keep_own(self):
        for into, out in self.locals:
            into.wait()
            out.start()

    def steps(self):
        count = len(self.plans)
        for step in range(count + 2):
            yield step

    def step(self, step):
        count = len(self.plans)
        if step < count:
            plan = self.plans[step]
            plan[0].wait_recv()
            plan[1].start()
            plan[2].start()
            plan[3].start()
        if 0 <= step - 1 < count:
            plan = self.plans[step - 1]
            plan[1].wait_recv()
            plan[4].start()
            plan[5].start()
            plan[2].wait_recv()
            plan[6].start()
            plan[7].start()
        if 0 <= step - 2 < count:
            plan = self.plans[step - 2]
            plan[4].wait_recv()
            plan[8].start()
            plan[6].wait_recv()
            plan[9].start()

    def finish(self):
        for plan in self.plans:
            for index in (3, 5, 7, 8, 9, 10):
                plan[index].wait_recv()
            for copy in plan:
                copy.wait_send()
        for _, out in self.locals:
            out.wait()


BLOCK_COPIES = 13


class BlockGather:
    def __init__(self, place, copies, blocks, fulls):
        self.own = place.block
        self.pairs = list(zip(blocks, fulls))
        self.plans = []
        for block, full in self.pairs:
            half = block.shape[0] // 2

            def part(ref, side, half=half):
                return ref.at[pl.ds(side * half, half), :]

            def slot_of(x_bit, y_bit, full=full):
                return full.at[4 * y_bit + 2 * place.core + x_bit]

            same = lambda view, device: copies.make(view, view, device)
            x, y = place.x, place.y
            mine, from_x = slot_of(x, y), slot_of(1 - x, y)
            from_y, from_both = slot_of(x, 1 - y), slot_of(1 - x, 1 - y)
            self.plans.append(
                [
                    copies.make(block, mine, place.sibling),
                    copies.make(part(block, 0), part(mine, 0), place.over_x),
                    copies.make(part(block, 1), part(mine, 1), place.over_y),
                    copies.make(part(block, 1), part(mine, 1), place.over_x),
                    copies.make(part(block, 0), part(mine, 0), place.over_y),
                    same(part(from_x, 0), place.over_y),
                    same(part(from_x, 0), place.sibling),
                    same(part(from_y, 1), place.over_x),
                    same(part(from_y, 1), place.sibling),
                    same(part(from_x, 1), place.sibling),
                    same(part(from_y, 0), place.sibling),
                    same(part(from_both, 0), place.sibling),
                    same(part(from_both, 1), place.sibling),
                ]
            )

    def begin(self):
        for index in (1, 2, 3, 4, 0):
            for plan in self.plans:
                plan[index].start()
        for block, full in self.pairs:
            full[self.own] = block[...]

    def relay(self, *pairs):
        for arrived, followers in pairs:
            for plan in self.plans:
                plan[arrived].wait_recv()
                for index in followers:
                    plan[index].start()

    def first_halves(self):
        self.relay((1, (5, 6)), (2, (7, 8)))

    def second_halves(self):
        self.relay((3, (9,)), (4, (10,)))

    def corners(self):
        self.relay((5, (11,)), (7, (12,)))

    def wait(self, *indices):
        for plan in self.plans:
            for index in indices:
                plan[index].wait_recv()

    def wait_near(self):
        self.wait(0, 6, 9)

    def wait_far(self):
        self.wait(8, 10, 11, 12)

    def finish(self):
        for plan in self.plans:
            for copy in plan:
                copy.wait_send()


def opening_kernel(
    tokens_ref,
    segs_ref,
    cotangent_ref,
    vectors_ref,
    weight_ref,
    tokens_out,
    segs_out,
    cotangent_out,
    vectors_out,
    weight_out,
    vectors_all,
    segs_own,
    stage,
    send_sems,
    recv_sems,
    local_sems,
):
    place = Place()
    others = (place.sibling, place.over_x, place.over_y, place.over_z)
    barrier = pltpu.get_barrier_semaphore()
    for device in others:
        pl.semaphore_signal(barrier, inc=1, device_id=device, device_id_type=MESH)

    @pl.when(place.has_partner)
    def _():
        pl.semaphore_signal(barrier, inc=1, device_id=place.partner, device_id_type=MESH)
        pl.semaphore_wait(barrier, len(others) + 1)

    @pl.when(jnp.logical_not(place.has_partner))
    def _():
        pl.semaphore_wait(barrier, len(others))

    copies = Copies(send_sems, recv_sems)
    swaps = [
        copies.make(segs_ref, segs_own, place.partner),
        copies.make(tokens_ref, tokens_out, place.partner),
        copies.make(cotangent_ref, cotangent_out, place.partner),
    ]
    own, other = place.fsdp, 2 * (1 - place.y) + place.core
    vector_copies = [
        copies.make(vectors_ref, vectors_all.at[own], place.over_y),
        copies.make(vectors_ref, vectors_all.at[own], place.sibling),
        copies.make(vectors_all.at[other], vectors_all.at[other], place.sibling),
    ]
    gather = WeightGather(place, copies, [weight_ref], [weight_out], [stage], local_sems)
    segs = BlockGather(place, copies, [segs_own], [segs_out])

    @pl.when(place.has_partner)
    def _():
        for swap in swaps:
            swap.start()

    vector_copies[0].start()
    vector_copies[1].start()
    vectors_all[own] = vectors_ref[...]
    gather.begin()

    @pl.when(jnp.logical_not(place.has_partner))
    def _():
        segs_own[...] = segs_ref[...]
        tokens_out[...] = tokens_ref[...]
        cotangent_out[...] = cotangent_ref[...]

    @pl.when(place.has_partner)
    def _():
        swaps[0].wait_recv()

    segs.begin()
    vector_copies[0].wait_recv()
    vector_copies[2].start()
    segs.first_halves()
    segs.second_halves()
    segs.corners()
    gather.keep_own()
    for step in gather.steps():
        gather.step(step)
    segs.wait_near()
    segs.wait_far()
    segs.finish()
    vector_copies[1].wait_recv()
    vector_copies[2].wait_recv()
    for copy in vector_copies:
        copy.wait_send()
    vectors_out[...] = assemble_vectors([vectors_all[i] for i in range(4)])

    @pl.when(place.has_partner)
    def _():
        for swap in swaps[1:]:
            swap.wait_recv()
        for swap in swaps:
            swap.wait_send()

    gather.finish()


def pack_vectors(ln1_gain, ln1_bias, ln2_gain, ln2_bias, proj_bias, out_bias, attn_bias, fc_bias):
    rows = (ln1_gain, ln1_bias, ln2_gain, ln2_bias, proj_bias, out_bias, attn_bias, fc_bias)
    return jnp.stack([jnp.pad(row.astype(F32), (0, D - row.shape[0])) for row in rows])


def assemble_vectors(shares):
    quarter = D // 4
    small = jnp.concatenate([share[:6, :quarter] for share in shares], axis=1)
    query = jnp.concatenate([shares[0][6:7, : 2 * quarter], shares[1][6:7, : 2 * quarter]], axis=1)
    value = jnp.concatenate([shares[2][6:7, : 2 * quarter], shares[3][6:7, : 2 * quarter]], axis=1)
    hidden = [share[7:8] for share in shares]
    return jnp.concatenate([small, query, value, *hidden, jnp.zeros((4, D), F32)], axis=0)


def opening(tokens, segs, cotangent, vectors, weight, collective_id):
    rows, columns = tokens.shape
    copies = 3 + 3 + WEIGHT_COPIES + BLOCK_COPIES
    vmem = pl.BlockSpec(memory_space=pltpu.VMEM)
    anywhere = pl.BlockSpec(memory_space=pl.ANY)
    return pl.pallas_call(
        opening_kernel,
        in_specs=[vmem, vmem, vmem, vmem, anywhere],
        out_specs=[vmem, vmem, vmem, vmem, anywhere],
        out_shape=[
            jax.ShapeDtypeStruct((rows, columns), tokens.dtype),
            jax.ShapeDtypeStruct((8, *segs.shape), segs.dtype),
            jax.ShapeDtypeStruct((rows, columns), cotangent.dtype),
            jax.ShapeDtypeStruct((16, D), F32),
            jax.ShapeDtypeStruct((4, *weight.shape), weight.dtype),
        ],
        scratch_shapes=[
            pltpu.VMEM((4, *vectors.shape), F32),
            pltpu.VMEM(segs.shape, segs.dtype),
            pltpu.VMEM(weight.shape, weight.dtype),
            pltpu.SemaphoreType.DMA((copies,)),
            pltpu.SemaphoreType.DMA((copies,)),
            pltpu.SemaphoreType.DMA((1,)),
        ],
        compiler_params=pltpu.CompilerParams(
            collective_id=collective_id, has_side_effects=True, vmem_limit_bytes=32 << 20
        ),
        name="opening",
    )(tokens, segs, cotangent, vectors, weight)


def mask_block(own_segs, segs_ref, block, start, own_is_query):
    rows = own_segs.shape[0]
    own_place = start + lax.broadcasted_iota(jnp.int32, (rows, rows), 0)
    place = block * rows + lax.broadcasted_iota(jnp.int32, (rows, rows), 1)
    causal = (place <= own_place) if own_is_query else (own_place <= place)
    same = own_segs == segs_ref[block, 0:1, :]
    return jnp.where(causal & same, 0.0, NEGATIVE)


def own_columns(segs_ref, block):
    rows = segs_ref.shape[2]
    return jnp.broadcast_to(segs_ref[block, 0:1, :], (rows, rows)).T


def attend_kernel(count, *refs):
    q_ref, kv_ref, segs_ref = refs[:3]
    shares = refs[3 : 3 + count]
    out_ref, lse_ref, lse_rows_ref, kv_out = refs[3 + count : 7 + count]
    fulls = refs[7 + count : 7 + 2 * count]
    rest = refs[7 + 2 * count :]
    kv_all, near_bias, far_bias, top_ref, total_ref, mixed_ref, send_sems, recv_sems, local_sems = rest[:9]
    stages = rest[9:]
    place = Place()
    devices = [place.sibling, place.over_x, place.over_y] + ([place.over_z] if count else [])
    greet(devices)
    copies = Copies(send_sems, recv_sems)
    gather = BlockGather(place, copies, [kv_ref], [kv_all])
    weights = WeightGather(place, copies, shares, fulls, stages, local_sems)
    gather.begin()

    rows = q_ref.shape[0]
    start = place.block * rows
    near, far = 4 * place.y, 4 * (1 - place.y)
    own_segs = own_columns(segs_ref, place.block)
    for i in range(4):
        near_bias[:, i * rows : (i + 1) * rows] = mask_block(own_segs, segs_ref, near + i, start, True)
        far_bias[:, i * rows : (i + 1) * rows] = mask_block(own_segs, segs_ref, far + i, start, True)
    lse_ref[...] = jnp.zeros_like(lse_ref)
    gather.first_halves()
    if count:
        weights.begin()
        weights.keep_own()
    gather.second_halves()

    def blocks_of(first, pair, side):
        lanes = pl.ds(pl.multiple_of(side * D + pair * LANES, LANES), LANES)
        return kv_all[pl.ds(first, 4), :, lanes].reshape(4 * rows, LANES)

    def queries_of(pair):
        lanes = pl.ds(pl.multiple_of(pair * LANES, LANES), LANES)
        return two_heads(q_ref[:, lanes] * jnp.asarray(SCALE, BF16))

    def part(first, bias_ref, pair):
        bias = bias_ref[...]
        scores = dot_rows(queries_of(pair), blocks_of(first, pair, 0))
        scores = scores + jnp.concatenate([bias, bias], axis=0)
        top = jnp.max(scores, axis=1, keepdims=True)
        weights_here = jnp.exp(scores - top)
        total = jnp.sum(weights_here, axis=1, keepdims=True)
        mixed = jnp.dot(
            weights_here.astype(BF16), blocks_of(first, pair, 1), preferred_element_type=F32
        )
        return top, total, mixed

    def visit_near(pair, carried):
        top_ref[pair], total_ref[pair], mixed_ref[pair] = part(near, near_bias, pair)
        return carried

    def visit_far(pair, carried):
        top, total, mixed = part(far, far_bias, pair)
        old_top, old_total, old_mixed = top_ref[pair], total_ref[pair], mixed_ref[pair]
        new_top = jnp.maximum(top, old_top)
        new, old = jnp.exp(top - new_top), jnp.exp(old_top - new_top)
        top_ref[pair] = new_top
        total_ref[pair] = total * new + old_total * old
        mixed_ref[pair] = mixed * new + old_mixed * old
        return carried

    def visit_last(pair, carried):
        top, total, mixed = top_ref[pair], total_ref[pair], mixed_ref[pair]
        lanes = pl.ds(pl.multiple_of(pair * LANES, LANES), LANES)
        out_ref[:, lanes] = one_pair(mixed / total).astype(BF16)
        lse = top + jnp.log(total)
        lane = lax.broadcasted_iota(jnp.int32, (rows, LANES), 1)
        kept = jnp.where(lane == 2 * pair, lse[:rows], lse_ref[...])
        lse_ref[...] = jnp.where(lane == 2 * pair + 1, lse[rows:], kept)
        return carried

    gather.wait_near()
    near_out = pltpu.make_async_copy(
        kv_all.at[pl.ds(near, 4)], kv_out.at[pl.ds(near, 4)], local_sems.at[count]
    )
    near_out.start()
    lax.fori_loop(0, PAIRS, visit_near, 0)
    gather.corners()
    if count:
        weights.step(0)
    gather.wait_far()
    far_out = pltpu.make_async_copy(
        kv_all.at[pl.ds(far, 4)], kv_out.at[pl.ds(far, 4)], local_sems.at[count + 1]
    )
    far_out.start()

    @pl.when(place.y == 1)
    def _():
        lax.fori_loop(0, PAIRS, visit_far, 0)

    lax.fori_loop(0, PAIRS, visit_last, 0)
    lse_rows_ref[...] = lse_ref[...].T[:16]
    for step in weights.steps():
        if count and step > 0:
            weights.step(step)
    weights.finish()
    gather.finish()
    near_out.wait()
    far_out.wait()


def attend(queries, kv_own, segs, shares, collective_id):
    rows = queries.shape[0]
    count = len(shares)
    slots = BLOCK_COPIES + count * WEIGHT_COPIES
    vmem = pl.BlockSpec(memory_space=pltpu.VMEM)
    anywhere = pl.BlockSpec(memory_space=pl.ANY)
    return pl.pallas_call(
        partial(attend_kernel, count),
        in_specs=[vmem, vmem, vmem] + [anywhere] * count,
        out_specs=[vmem, vmem, vmem, anywhere] + [anywhere] * count,
        out_shape=[
            jax.ShapeDtypeStruct((rows, D), BF16),
            jax.ShapeDtypeStruct((rows, LANES), F32),
            jax.ShapeDtypeStruct((16, rows), F32),
            jax.ShapeDtypeStruct((8, rows, 2 * D), BF16),
        ]
        + [jax.ShapeDtypeStruct((4, *share.shape), share.dtype) for share in shares],
        scratch_shapes=[
            pltpu.VMEM((8, rows, 2 * D), BF16),
            pltpu.VMEM((rows, 4 * rows), F32),
            pltpu.VMEM((rows, 4 * rows), F32),
            pltpu.VMEM((PAIRS, 2 * rows, 1), F32),
            pltpu.VMEM((PAIRS, 2 * rows, 1), F32),
            pltpu.VMEM((PAIRS, 2 * rows, LANES), F32),
            pltpu.SemaphoreType.DMA((slots,)),
            pltpu.SemaphoreType.DMA((slots,)),
            pltpu.SemaphoreType.DMA((count + 2,)),
        ]
        + [pltpu.VMEM(share.shape, share.dtype) for share in shares],
        compiler_params=pltpu.CompilerParams(
            collective_id=collective_id, has_side_effects=True, vmem_limit_bytes=40 << 20
        ),
        name="attend",
    )(queries, kv_own, segs, *shares)


class AttentionGrads:
    def __init__(self, place, q_ref, grad_ref, lse_ref, delta_ref, segs_ref, kv_all, q_all, grad_all, stats_all, biases, sums):
        self.place = place
        self.q_ref, self.grad_ref, self.lse_ref, self.delta_ref = q_ref, grad_ref, lse_ref, delta_ref
        self.segs_ref, self.kv_all, self.q_all, self.grad_all = segs_ref, kv_all, q_all, grad_all
        self.stats_all = stats_all
        self.query_bias, self.key_bias = biases
        self.query_sum, self.key_sum, self.value_sum = sums
        self.rows = q_ref.shape[0]

    def masks(self):
        rows, place = self.rows, self.place
        start = place.block * rows
        own_segs = own_columns(self.segs_ref, place.block)
        for i in range(8):
            at = slice(i * rows, (i + 1) * rows)
            self.query_bias[:, at] = mask_block(own_segs, self.segs_ref, i, start, True)
            self.key_bias[:, at] = mask_block(own_segs, self.segs_ref, i, start, False)

    def lanes(self, pair, side=0):
        return pl.ds(pl.multiple_of(side * D + pair * LANES, LANES), LANES)

    def two_blocks(self, ref, index, lanes):
        return ref[pl.ds(2 * index, 2), :, lanes].reshape(2 * self.rows, LANES)

    def bias(self, ref, index):
        step = 2 * self.rows
        bias = ref[:, pl.ds(pl.multiple_of(index * step, step), step)]
        return jnp.concatenate([bias, bias], axis=0)

    def query_grads(self, first_pair, last_pair):
        scale = jnp.asarray(SCALE, BF16)
        count = self.place.block // 2 + 1

        def visit_pair(pair, carried):
            lanes = self.lanes(pair)
            queries = two_heads(self.q_ref[:, lanes] * scale)
            grads = two_heads(self.grad_ref[:, lanes])
            lse = pick_lanes(self.lse_ref[...], pair)
            delta = pick_lanes(self.delta_ref[...], pair)

            def visit(index, total):
                keys = self.two_blocks(self.kv_all, index, lanes)
                values = self.two_blocks(self.kv_all, index, self.lanes(pair, 1))
                scores = dot_rows(queries, keys) + self.bias(self.query_bias, index)
                attention = jnp.exp(scores - lse)
                grad_attention = dot_rows(grads, values)
                grad_scores = (attention * (grad_attention - delta)).astype(BF16)
                return total + jnp.dot(grad_scores, keys, preferred_element_type=F32)

            zeros = jnp.zeros((2 * self.rows, LANES), F32)
            self.query_sum[pair] = lax.fori_loop(0, count, visit, zeros)
            return carried

        lax.fori_loop(first_pair, last_pair, visit_pair, 0)

    def key_grads(self, first, last, fresh):
        rows = self.rows
        scale = jnp.asarray(SCALE, BF16)
        own = self.place.block

        def visit_pair(pair, carried):
            lanes = self.lanes(pair)
            own_keys = two_heads(self.kv_all[own, :, lanes] * scale)
            own_values = two_heads(self.kv_all[own, :, self.lanes(pair, 1)])

            def stat_rows(index, row):
                def spread(block, head):
                    line = self.stats_all[2 * index + block, pl.ds(row + 2 * pair + head, 1), :]
                    return jnp.broadcast_to(line, (rows, rows))

                heads = [
                    jnp.concatenate([spread(0, head), spread(1, head)], axis=1) for head in range(2)
                ]
                return jnp.concatenate(heads, axis=0)

            def visit(index, totals):
                key_total, value_total = totals
                later = self.two_blocks(self.q_all, index, lanes)
                later_grads = self.two_blocks(self.grad_all, index, lanes)
                scores = dot_rows(own_keys, later) + self.bias(self.key_bias, index)
                attention = jnp.exp(scores - stat_rows(index, 0))
                grad_attention = dot_rows(own_values, later_grads)
                grad_scores = attention * (grad_attention - stat_rows(index, 16))
                key_total = key_total + jnp.dot(
                    grad_scores.astype(BF16), later, preferred_element_type=F32
                )
                value_total = value_total + jnp.dot(
                    attention.astype(BF16), later_grads, preferred_element_type=F32
                )
                return key_total, value_total

            if fresh:
                zeros = jnp.zeros((2 * rows, LANES), F32)
                totals = (zeros, zeros)
            else:
                totals = (self.key_sum[pair], self.value_sum[pair])
            self.key_sum[pair], self.value_sum[pair] = lax.fori_loop(first, last, visit, totals)
            return carried

        lax.fori_loop(0, PAIRS, visit_pair, 0)

    def near_keys(self):
        self.key_grads(self.place.block // 2, 2 * self.place.y + 2, True)

    def far_keys(self):
        @pl.when(self.place.y == 0)
        def _():
            self.key_grads(2, 4, False)

    def store(self, out_ref):
        def visit(pair, carried):
            out_ref[:, self.lanes(pair)] = (one_pair(self.query_sum[pair]) * SCALE).astype(BF16)
            out_ref[:, self.lanes(pair, 1)] = (one_pair(self.key_sum[pair]) * SCALE).astype(BF16)
            out_ref[:, self.lanes(pair, 2)] = one_pair(self.value_sum[pair]).astype(BF16)
            return carried

        lax.fori_loop(0, PAIRS, visit, 0)


def attention_scratch(rows):
    return [
        pltpu.VMEM((8, rows, 2 * D), BF16),
        pltpu.VMEM((8, rows, D), BF16),
        pltpu.VMEM((8, rows, D), BF16),
        pltpu.VMEM((8, 32, rows), F32),
        pltpu.VMEM((rows, 8 * rows), F32),
        pltpu.VMEM((rows, 8 * rows), F32),
        pltpu.VMEM((PAIRS, 2 * rows, LANES), F32),
        pltpu.VMEM((PAIRS, 2 * rows, LANES), F32),
        pltpu.VMEM((PAIRS, 2 * rows, LANES), F32),
    ]


ATTENTION_SCRATCH = 9


def attend_back_kernel(
    q_ref, grad_ref, stats_ref, lse_ref, delta_ref, segs_ref, kv_ref, out_ref, *scratch
):
    kv_all, q_all, grad_all, stats_all = scratch[:4]
    biases, sums = scratch[4:6], scratch[6:9]
    send_sems, recv_sems, local_sem = scratch[9:]
    place = Place()
    greet((place.sibling, place.over_x, place.over_y))
    copies = Copies(send_sems, recv_sems)
    gather = BlockGather(
        place, copies, [q_ref, grad_ref, stats_ref], [q_all, grad_all, stats_all]
    )
    load = pltpu.make_async_copy(kv_ref, kv_all, local_sem)
    load.start()
    gather.begin()
    grads = AttentionGrads(
        place, q_ref, grad_ref, lse_ref, delta_ref, segs_ref, kv_all, q_all, grad_all, stats_all, biases, sums
    )
    grads.masks()
    load.wait()
    grads.query_grads(0, 2)
    gather.first_halves()
    grads.query_grads(2, PAIRS)
    gather.second_halves()
    gather.wait_near()
    grads.near_keys()
    gather.corners()
    gather.wait_far()
    grads.far_keys()
    grads.store(out_ref)
    gather.finish()


def attend_back(queries, grads, stats, lse, delta, segs, kv, collective_id):
    rows = queries.shape[0]
    slots = 3 * BLOCK_COPIES
    vmem = pl.BlockSpec(memory_space=pltpu.VMEM)
    return pl.pallas_call(
        attend_back_kernel,
        in_specs=[vmem] * 6 + [pl.BlockSpec(memory_space=pl.ANY)],
        out_specs=vmem,
        out_shape=jax.ShapeDtypeStruct((rows, 3 * D), BF16),
        scratch_shapes=attention_scratch(rows)
        + [
            pltpu.SemaphoreType.DMA((slots,)),
            pltpu.SemaphoreType.DMA((slots,)),
            pltpu.SemaphoreType.DMA,
        ],
        compiler_params=pltpu.CompilerParams(
            collective_id=collective_id, has_side_effects=True, vmem_limit_bytes=40 << 20
        ),
        name="attend_back",
    )(queries, grads, stats, lse, delta, segs, kv)


CHUNK_ROWS, CHUNK_COLUMNS = 192, 768
REDUCE_COPIES = 9
VECTOR_AXES = 5


def chunk_places(shapes):
    return [
        (which, row, column)
        for which, (rows, columns) in enumerate(shapes)
        for row in range(0, rows, CHUNK_ROWS)
        for column in range(0, columns, CHUNK_COLUMNS)
    ]


def reduce_gradients_kernel(places, count, *refs):
    partials, vector = refs[:count], refs[count]
    sums, vector_out = refs[count + 1 : 2 * count + 1], refs[2 * count + 1]
    (
        own,
        got_core,
        got_y,
        to_x,
        got_x,
        to_z,
        got_z,
        to_zz,
        got_zz,
        vector_got,
        send_sems,
        recv_sems,
        local_sems,
    ) = refs[2 * count + 2 :]
    x, z, y, core = place_bits()
    low, high = lax.rem(z, 2), z // 2
    fsdp = 2 * y + core
    sibling = (2 * z + x, 2 * y + 1 - core)
    over_y = (2 * z + x, 2 * (1 - y) + core)
    over_x = (2 * z + 1 - x, fsdp)
    over_z = (2 * (z + 1 - 2 * low) + x, fsdp)
    over_zz = (2 * (z + 2 - 4 * high) + x, fsdp)
    greet((sibling, over_y, over_x, over_z, over_zz))

    def copy(slot, src, dst, device):
        return pltpu.make_async_remote_copy(
            src_ref=src,
            dst_ref=dst,
            send_sem=send_sems.at[slot],
            recv_sem=recv_sems.at[slot],
            device_id=device,
            device_id_type=MESH,
        )

    x_rows, z_rows, zz_columns = CHUNK_ROWS // 2, CHUNK_ROWS // 4, CHUNK_COLUMNS // 2
    chunks = len(places)

    def add_up(store, loads, rows):
        step = z_rows

        def visit(index, carried):
            offset = pl.multiple_of(index * step, 16)
            total = loads[0](offset, step).astype(F32)
            for load in loads[1:]:
                total = total + load(offset, step).astype(F32)
            store(offset, step, total.astype(BF16))
            return carried

        if rows == step:
            visit(0, 0)
        else:
            lax.fori_loop(0, rows // step, visit, 0)

    vector_devices = (over_y, sibling, over_x, over_z, over_zz)
    vector_copies = [
        copy(chunks * REDUCE_COPIES + i, vector_out, vector_got.at[i], vector_devices[i])
        for i in range(VECTOR_AXES)
    ]
    vector_out[...] = vector[...]
    vector_copies[0].start()

    plans = []
    loads = []
    for k, (which, row, column) in enumerate(places):
        partial_sum, out = partials[which], sums[which]

        def term(quarter, partial_sum=partial_sum, row=row, column=column):
            return partial_sum.at[quarter, pl.ds(row, CHUNK_ROWS), pl.ds(column, CHUNK_COLUMNS)]

        def piece(first, rows, start, width, out=out, row=row, column=column):
            return out.at[
                pl.ds(pl.multiple_of(row + first, 16), rows),
                pl.ds(pl.multiple_of(column + start, LANES), width),
            ]

        final = piece(x * x_rows + low * z_rows, z_rows, high * zz_columns, zz_columns)
        wide = piece(x * x_rows + low * z_rows, z_rows, 0, CHUNK_COLUMNS)
        tall = piece(x * x_rows, x_rows, 0, CHUNK_COLUMNS)
        base = k * REDUCE_COPIES
        plans.append(
            {
                "core0": copy(base, term(1 - core), got_core.at[k, 0], sibling),
                "core1": copy(base + 1, term(3 - core), got_core.at[k, 1], sibling),
                "y": copy(base + 2, own.at[k, 1 - y], got_y.at[k], over_y),
                "x": copy(base + 3, to_x.at[k], got_x.at[k], over_x),
                "z": copy(base + 4, to_z.at[k], got_z.at[k], over_z),
                "zz": copy(base + 5, to_zz.at[k], got_zz.at[k], over_zz),
                "zz_back": copy(base + 6, final, final, over_zz),
                "z_back": copy(base + 7, wide, wide, over_z),
                "x_back": copy(base + 8, tall, tall, over_x),
                "final": final,
            }
        )
        loads.append(
            [
                pltpu.make_async_copy(term(2 * i + core), own.at[k, i], local_sems.at[2 * k + i])
                for i in range(2)
            ]
        )
        plans[k]["core0"].start()
        plans[k]["core1"].start()
        loads[k][0].start()
        loads[k][1].start()

    def slab(ref, *index, first=0, start=None, width=None):
        def load(offset, rows):
            place = pl.ds(pl.multiple_of(first + offset, 16), rows)
            if width is None:
                return ref[(*index, place)]
            return ref[(*index, place, pl.ds(pl.multiple_of(start, LANES), width))]

        return load

    def stage_y(k):
        plan = plans[k]
        for load in loads[k]:
            load.wait()
        plan["core0"].wait_recv()
        plan["core1"].wait_recv()

        def store(offset, rows, value):
            own[k, 1 - y, pl.ds(offset, rows)] = value

        add_up(store, [slab(own, k, 1 - y), slab(got_core, k, 1 - y)], CHUNK_ROWS)
        plan["y"].start()

    def stage_x(k):
        plan = plans[k]
        plan["y"].wait_recv()
        first = (1 - x) * x_rows

        def store(offset, rows, value):
            to_x[k, pl.ds(offset, rows)] = value

        add_up(
            store,
            [slab(own, k, y, first=first), slab(got_core, k, y, first=first), slab(got_y, k, first=first)],
            x_rows,
        )
        plan["x"].start()

    def stage_z(k):
        plan = plans[k]
        plan["x"].wait_recv()
        inner = (1 - low) * z_rows
        first = x * x_rows + inner

        def store(offset, rows, value):
            to_z[k] = value

        add_up(
            store,
            [
                slab(own, k, y, first=first),
                slab(got_core, k, y, first=first),
                slab(got_y, k, first=first),
                slab(got_x, k, first=inner),
            ],
            z_rows,
        )
        plan["z"].start()

    def last_loads(k, start):
        inner = low * z_rows
        first = x * x_rows + inner
        part = {"start": start, "width": zz_columns}
        return [
            slab(own, k, y, first=first, **part),
            slab(got_core, k, y, first=first, **part),
            slab(got_y, k, first=first, **part),
            slab(got_x, k, first=inner, **part),
            slab(got_z, k, **part),
        ]

    def stage_zz(k):
        plan = plans[k]
        plan["z"].wait_recv()

        def store(offset, rows, value):
            to_zz[k] = value

        add_up(store, last_loads(k, (1 - high) * zz_columns), z_rows)
        plan["zz"].start()

    def stage_final(k):
        plan = plans[k]
        plan["zz"].wait_recv()

        def store(offset, rows, value):
            plan["final"][...] = value

        add_up(store, last_loads(k, high * zz_columns) + [slab(got_zz, k)], z_rows)
        plan["zz_back"].start()

    def stage_z_back(k):
        plans[k]["zz_back"].wait_recv()
        plans[k]["z_back"].start()

    def stage_x_back(k):
        plans[k]["z_back"].wait_recv()
        plans[k]["x_back"].start()

    def vector_step(index):
        vector_copies[index].wait()
        vector_out[...] = vector_out[...] + vector_got[index]
        if index + 1 < VECTOR_AXES:
            vector_copies[index + 1].start()

    for k in range(chunks):
        stage_y(k)
    stages = (stage_x, stage_z, stage_zz, stage_final, stage_z_back, stage_x_back)
    for tick in range(chunks + len(stages) - 1):
        if tick < VECTOR_AXES:
            vector_step(tick)
        for lag, stage in enumerate(stages):
            if 0 <= tick - lag < chunks:
                stage(tick - lag)
    for plan in plans:
        plan["x_back"].wait_recv()
        for name in ("core0", "core1", "y", "x", "z", "zz", "zz_back", "z_back", "x_back"):
            plan[name].wait_send()


def reduce_gradients(partials, vector, collective_id):
    count = len(partials)
    places = chunk_places([partial_sum.shape[1:] for partial_sum in partials])
    chunks = len(places)
    slots = chunks * REDUCE_COPIES + VECTOR_AXES
    rows, columns = CHUNK_ROWS, CHUNK_COLUMNS
    buffers = [
        (2, rows, columns),
        (2, rows, columns),
        (rows, columns),
        (rows // 2, columns),
        (rows // 2, columns),
        (rows // 4, columns),
        (rows // 4, columns),
        (rows // 4, columns // 2),
        (rows // 4, columns // 2),
    ]
    vmem = pl.BlockSpec(memory_space=pltpu.VMEM)
    return pl.pallas_call(
        partial(reduce_gradients_kernel, places, count),
        in_specs=[pl.BlockSpec(memory_space=pl.ANY)] * count + [vmem],
        out_specs=[vmem] * (count + 1),
        out_shape=[jax.ShapeDtypeStruct(p.shape[1:], BF16) for p in partials]
        + [jax.ShapeDtypeStruct(vector.shape, F32)],
        scratch_shapes=[pltpu.VMEM((chunks, *shape), BF16) for shape in buffers]
        + [
            pltpu.VMEM((VECTOR_AXES, *vector.shape), F32),
            pltpu.SemaphoreType.DMA((slots,)),
            pltpu.SemaphoreType.DMA((slots,)),
            pltpu.SemaphoreType.DMA((2 * chunks,)),
        ],
        compiler_params=pltpu.CompilerParams(
            collective_id=collective_id, has_side_effects=True, vmem_limit_bytes=48 << 20
        ),
        name="reduce_gradients",
    )(*partials, vector)


class PlaneLinks:
    def leave(self, value):
        pairs = [(c * 4 + f, (2 * f + c % 2) * 4 + c // 2) for c in range(8) for f in range(4)]
        return lax.ppermute(value, ("ctx", "fsdp"), pairs)

    def open(self, tokens, segs_row, cotangent, vectors, weight):
        segs = jnp.broadcast_to(segs_row, (16, segs_row.shape[1]))
        return opening(tokens, segs, cotangent, vectors, weight, 0)

    def attend(self, queries, kv_own, segs, shares):
        attended, lse, lse_rows, kv, *fulls = attend(
            queries, kv_own, segs, shares, 1 if shares else 2
        )
        return attended, lse, lse_rows, kv, fulls

    def attend_back(self, queries, grads, stats, lse, delta, segs, kv, kv_own):
        return attend_back(queries, grads, stats, lse, delta, segs, kv, 3)

    def sum_gradients(self, factors, vectors):
        terms = []
        for left, right in factors:
            term = column_products(left, right).astype(BF16)
            terms.append(term.reshape(4, term.shape[0] // 4, term.shape[1]))
        *sums, vectors = reduce_gradients(terms, vectors, 4)
        return [total.astype(F32) for total in sums], vectors


class PlainLinks:
    def leave(self, value):
        return value

    def open(self, tokens, segs_row, cotangent, vectors, weight):
        segs = lax.all_gather(segs_row, "ctx", axis=1, tiled=True)
        shares = lax.all_gather(vectors, "fsdp", axis=0)
        vectors = assemble_vectors([shares[i] for i in range(4)])
        return tokens, (segs_row, segs), cotangent, vectors, lax.all_gather(weight, "fsdp", axis=0)

    def place(self, segs):
        own_segs, all_segs = segs
        rows = own_segs.shape[1]
        start = (lax.axis_index("ctx") * rows).reshape(1).astype(jnp.int32)
        return start, own_segs.reshape(rows, 1), all_segs

    def blocks(self, block):
        return lax.all_gather(block, "ctx", axis=0)

    def attend(self, queries, kv_own, segs, shares):
        start, own_segs, all_segs = self.place(segs)
        kv = self.blocks(kv_own).reshape(-1, 2 * D)
        attended, lse, lse_rows = attention_forward(start, queries, kv, own_segs, all_segs)
        fulls = [lax.all_gather(share, "fsdp", axis=0) for share in shares]
        return attended, lse, lse_rows, kv, fulls

    def attend_back(self, queries, grads, stats, lse, delta, segs, kv, kv_own):
        start, own_segs, all_segs = self.place(segs)
        q_all = self.blocks(queries).reshape(-1, D)
        grad_all = self.blocks(grads).reshape(-1, D)
        return attention_backward(
            start,
            queries,
            grads,
            kv_own,
            lse,
            delta,
            kv,
            q_all,
            grad_all,
            self.blocks(stats),
            own_segs,
            all_segs,
        )

    def sum_gradients(self, factors, vectors):
        sums = []
        for left, right in factors:
            term = column_products(left, right).astype(BF16)
            share = lax.psum_scatter(term, "fsdp", scatter_dimension=0, tiled=True)
            sums.append(lax.psum(share.astype(F32), "ctx"))
        return sums, lax.psum(vectors, ("ctx", "fsdp"))


def layer_forward(resid, weights, vectors, links, segs, shares):
    gain_one, bias_one, gain_two, bias_two, bias_proj, bias_out = (vectors[i : i + 1] for i in range(6))
    bias_qkv = jnp.concatenate([vectors[6:7], jnp.zeros((1, D), F32), vectors[7:8]], axis=1)
    bias_fc = vectors[8:12].reshape(1, 4 * D)
    normed_one, normal_one, inverse_one = norm_forward(resid, gain_one, bias_one)
    projected = jnp.dot(normed_one, weights[0], preferred_element_type=F32) + bias_qkv
    projected = projected.astype(BF16)
    queries, kv_own = projected[:, :D], projected[:, D:]
    attended, lse, lse_rows, kv, fulls = links.attend(queries, kv_own, segs, shares)
    weights = weights + tuple(full.reshape(-1, full.shape[-1]) for full in fulls)
    _, weight_proj, weight_fc, weight_out = weights
    middle = resid + jnp.dot(attended, weight_proj, preferred_element_type=F32) + bias_proj
    normed_two, normal_two, inverse_two = norm_forward(middle, gain_two, bias_two)
    hidden = jnp.dot(normed_two, weight_fc, preferred_element_type=F32) + bias_fc
    activated = jax.nn.gelu(hidden, approximate=True).astype(BF16)
    result_rows = middle + jnp.dot(activated, weight_out, preferred_element_type=F32) + bias_out
    saved = (
        normed_one,
        normal_one,
        inverse_one,
        queries,
        kv_own,
        kv,
        attended,
        lse,
        lse_rows,
        normed_two,
        normal_two,
        inverse_two,
        hidden,
        activated,
    )
    return result_rows, saved, weights


def layer_backward(gradient, weights, vectors, saved, links, segs):
    weight_qkv, weight_proj, weight_fc, weight_out = weights
    gain_one, gain_two = vectors[0:1], vectors[2:3]
    (
        normed_one,
        normal_one,
        inverse_one,
        queries,
        kv_own,
        kv,
        attended,
        lse,
        lse_rows,
        normed_two,
        normal_two,
        inverse_two,
        hidden,
        activated,
    ) = saved
    total = lambda value: jnp.sum(value.astype(F32), axis=0)
    grad_branch = gradient.astype(BF16)
    grad_activated = dot_rows(grad_branch, weight_out)
    gelu_pull = jax.vjp(partial(jax.nn.gelu, approximate=True), hidden)[1]
    grad_hidden = gelu_pull(grad_activated)[0].astype(BF16)
    grad_normed_two = dot_rows(grad_hidden, weight_fc)
    grad_in_two, grad_gain_two, grad_bias_two = norm_backward(
        grad_normed_two, normal_two, inverse_two, gain_two
    )
    grad_middle = gradient + grad_in_two
    grad_proj = grad_middle.astype(BF16)
    grad_attended = dot_rows(grad_proj, weight_proj).astype(BF16)
    products = grad_attended.astype(F32) * attended.astype(F32)
    head_of = jnp.arange(D, dtype=jnp.int32) // HDIM
    by_lane = (head_of[:, None] == jnp.arange(LANES, dtype=jnp.int32)[None, :]).astype(F32)
    by_row = (jnp.arange(16, dtype=jnp.int32)[:, None] == head_of[None, :]).astype(F32)
    delta = jnp.dot(products, by_lane, precision=lax.Precision.HIGHEST, preferred_element_type=F32)
    delta_rows = lax.dot_general(
        by_row,
        products,
        (((1,), (1,)), ((), ())),
        precision=lax.Precision.HIGHEST,
        preferred_element_type=F32,
    )
    stats = jnp.concatenate([lse_rows, delta_rows], axis=0)
    grad_projected = links.attend_back(
        queries, grad_attended, stats, lse, delta, segs, kv, kv_own
    )
    grad_normed_one = dot_rows(grad_projected, weight_qkv)
    grad_in_one, grad_gain_one, grad_bias_one = norm_backward(
        grad_normed_one, normal_one, inverse_one, gain_one
    )
    grad_input = grad_middle + grad_in_one
    matrices = (
        (activated, grad_branch),
        (normed_two, grad_hidden),
        (attended, grad_proj),
        (normed_one, grad_projected),
    )
    terms = (
        grad_gain_one,
        grad_bias_one,
        grad_gain_two,
        grad_bias_two,
        total(grad_proj),
        total(grad_branch),
        total(grad_projected[:, :D]),
        total(grad_projected[:, 2 * D :]),
        total(grad_hidden).reshape(4, D),
    )
    return grad_input, matrices, terms


def body(
    links,
    tokens,
    segment_ids,
    ln1_gain,
    ln1_bias,
    attn_weight,
    attn_bias,
    proj_weight,
    proj_bias,
    ln2_gain,
    ln2_bias,
    fc_weight,
    fc_bias,
    out_weight,
    out_bias,
    out_cotangent,
):
    vectors = pack_vectors(
        ln1_gain, ln1_bias, ln2_gain, ln2_bias, proj_bias, out_bias, attn_bias, fc_bias
    )
    resid, segs, gradient, vectors, qkv_full = links.open(
        tokens[0], segment_ids, out_cotangent[0], vectors, attn_weight
    )
    weights = (qkv_full.reshape(-1, qkv_full.shape[-1]),)
    shares = [proj_weight, fc_weight, out_weight]
    resid = resid.astype(F32)
    saved_layers = []
    for layer_index in range(2):
        resid, saved, weights = layer_forward(resid, weights, vectors, links, segs, shares)
        saved_layers.append(saved)
        shares = []
    output = links.leave(resid.astype(BF16))
    gradient = gradient.astype(F32)
    collected = []
    for layer_index in (1, 0):
        gradient, matrices, terms = layer_backward(
            gradient, weights, vectors, saved_layers[layer_index], links, segs
        )
        collected.append((matrices, terms))
    tokens_grad = links.leave(gradient.astype(BF16))

    factors = []
    for second, first in zip(collected[0][0], collected[1][0]):
        left = jnp.concatenate([second[0], first[0]], axis=0)
        right = jnp.concatenate([second[1], first[1]], axis=0)
        factors.append((left, right))
    added = [(a + b).reshape(-1, D) for a, b in zip(collected[0][1], collected[1][1])]
    packed = jnp.concatenate(added + [jnp.zeros((4, D), F32)], axis=0)
    (out_grad, fc_grad, proj_grad, qkv_grad), summed = links.sum_gradients(factors, packed)
    own = lax.axis_index("fsdp")
    pick = lambda value, axis: lax.dynamic_index_in_dim(value, own, axis, keepdims=False)
    small = pick(summed[:6].reshape(6, 4, -1), 1)
    bias_qv = pick(summed[6:8].reshape(4, -1), 0)
    bias_fc = pick(summed[8:12], 0)
    gain_one, bias_one, gain_two, bias_two, bias_proj, bias_out = (small[i] for i in range(6))
    return (
        output[None],
        tokens_grad[None],
        gain_one,
        bias_one,
        qkv_grad,
        bias_qv,
        proj_grad,
        bias_proj,
        gain_two,
        bias_two,
        fc_grad,
        bias_fc,
        out_grad,
        bias_out,
    )


def solution(mesh):
    links = PlaneLinks() if (mesh.shape["ctx"], mesh.shape["fsdp"]) == (8, 4) else PlainLinks()
    rows = P("fsdp", "ctx", None)
    vector, matrix = P("fsdp"), P("fsdp", None)
    in_specs = (
        rows,
        P("fsdp", "ctx"),
        vector,
        vector,
        matrix,
        vector,
        matrix,
        vector,
        vector,
        vector,
        matrix,
        vector,
        matrix,
        vector,
        rows,
    )
    out_specs = (
        rows,
        rows,
        vector,
        vector,
        matrix,
        vector,
        matrix,
        vector,
        vector,
        vector,
        matrix,
        vector,
        matrix,
        vector,
    )
    return jax.shard_map(
        partial(body, links), mesh=mesh, in_specs=in_specs, out_specs=out_specs, check_vma=False
    )
```

```python
from functools import partial

import jax
import jax.numpy as jnp
from jax import lax
from jax.experimental import pallas as pl
from jax.experimental.pallas import tpu as pltpu
from jax.sharding import PartitionSpec as P

D = 768
HEADS = 12
HDIM = 64
PAIRS = HEADS // 2
LANES = 128
EPSILON = 1e-05
NEGATIVE = -1e30
SCALE = HDIM ** (-0.5)
MESH = pl.DeviceIdType.MESH
F32 = jnp.float32
BF16 = jnp.bfloat16


def norm_forward(resid, gain_row, bias_row):
    average = jnp.mean(resid, axis=-1, keepdims=True)
    centred = resid - average
    variance = jnp.mean(centred * centred, axis=-1, keepdims=True)
    inverse = lax.rsqrt(variance + EPSILON)
    normal = centred * inverse
    return ((normal * gain_row + bias_row).astype(BF16), normal, inverse)


def norm_backward(grad_normed, normal, inverse, gain_row):
    scaled = grad_normed * gain_row
    mean_term = jnp.mean(scaled, axis=-1, keepdims=True)
    second = jnp.mean(scaled * normal, axis=-1, keepdims=True)
    grad_input = inverse * (scaled - mean_term - normal * second)
    return (grad_input, jnp.sum(grad_normed * normal, axis=0), jnp.sum(grad_normed, axis=0))


def two_heads(rows):
    lane = lax.broadcasted_iota(jnp.int32, rows.shape, 1)
    zero = jnp.zeros_like(rows)
    first = jnp.where(lane < HDIM, rows, zero)
    second = jnp.where(lane < HDIM, zero, rows)
    return jnp.concatenate([first, second], axis=0)


def one_pair(stacked):
    half = stacked.shape[0] // 2
    lane = lax.broadcasted_iota(jnp.int32, (half, LANES), 1)
    return jnp.where(lane < HDIM, stacked[:half], stacked[half:])


def dot_rows(left, right):
    return lax.dot_general(left, right, (((1,), (1,)), ((), ())), preferred_element_type=F32)


def column_products(left, right):
    return lax.dot_general(left, right, (((0,), (0,)), ((), ())), preferred_element_type=F32)


def pick_lanes(columns, pair):
    lane = lax.broadcasted_iota(jnp.int32, columns.shape, 1)
    first = jnp.sum(jnp.where(lane == 2 * pair, columns, 0.0), axis=1, keepdims=True)
    second = jnp.sum(jnp.where(lane == 2 * pair + 1, columns, 0.0), axis=1, keepdims=True)
    return jnp.concatenate([first, second], axis=0)


def mask_columns(bias_ref, own_segs, all_segs_ref, start, own_is_query):
    rows, columns = bias_ref.shape
    step = min(1024, columns)
    own_place = start + lax.broadcasted_iota(jnp.int32, (rows, step), 0)
    for offset in range(0, columns, step):
        place = offset + lax.broadcasted_iota(jnp.int32, (rows, step), 1)
        causal = (place <= own_place) if own_is_query else (own_place <= place)
        same = own_segs == all_segs_ref[:, offset : offset + step]
        bias_ref[:, offset : offset + step] = jnp.where(causal & same, 0.0, NEGATIVE)


def attention_forward_kernel(
    start_ref, q_ref, k_ref, v_ref, own_segs_ref, all_segs_ref, out_ref, lse_ref, lse_rows_ref, bias_ref
):
    pair = pl.program_id(0)
    rows, keys = bias_ref.shape

    @pl.when(pair == 0)
    def _():
        mask_columns(bias_ref, own_segs_ref[...], all_segs_ref, start_ref[0], True)
        lse_ref[...] = jnp.zeros_like(lse_ref)

    queries = two_heads(q_ref[...] * jnp.asarray(SCALE, BF16))
    step = min(1024, keys)

    def scores_of(offset):
        scores = dot_rows(queries, k_ref[pl.ds(offset, step), :])
        bias = bias_ref[:, pl.ds(offset, step)]
        return scores + jnp.concatenate([bias, bias], axis=0)

    if step == keys:
        scores = scores_of(0)
        top = jnp.max(scores, axis=1, keepdims=True)
        weights = jnp.exp(scores - top)
        total = jnp.sum(weights, axis=1, keepdims=True)
        mixed = jnp.dot(weights.astype(BF16), v_ref[...], preferred_element_type=F32)
    else:

        def visit(index, carried):
            top, total, mixed = carried
            offset = pl.multiple_of(index * step, step)
            scores = scores_of(offset)
            new_top = jnp.maximum(top, jnp.max(scores, axis=1, keepdims=True))
            weights = jnp.exp(scores - new_top)
            factor = jnp.exp(top - new_top)
            total = total * factor + jnp.sum(weights, axis=1, keepdims=True)
            more = jnp.dot(
                weights.astype(BF16), v_ref[pl.ds(offset, step), :], preferred_element_type=F32
            )
            return new_top, total, mixed * factor + more

        top, total, mixed = lax.fori_loop(
            0,
            (start_ref[0] + rows + step - 1) // step,
            visit,
            (
                jnp.full((2 * rows, 1), NEGATIVE, F32),
                jnp.zeros((2 * rows, 1), F32),
                jnp.zeros((2 * rows, LANES), F32),
            ),
        )
    out_ref[...] = one_pair(mixed / total).astype(BF16)
    lse = top + jnp.log(total)
    lane = lax.broadcasted_iota(jnp.int32, (rows, LANES), 1)
    kept = lse_ref[...]
    kept = jnp.where(lane == 2 * pair, lse[:rows], kept)
    kept = jnp.where(lane == 2 * pair + 1, lse[rows:], kept)
    lse_ref[...] = kept

    @pl.when(pair == PAIRS - 1)
    def _():
        lse_rows_ref[...] = kept.T[:16]


def attention_forward(start, queries, kv, own_segs, all_segs):
    rows = queries.shape[0]
    keys = kv.shape[0]
    whole = lambda shape: pl.BlockSpec(shape, lambda p: (0, 0))
    return pl.pallas_call(
        attention_forward_kernel,
        grid=(PAIRS,),
        in_specs=[
            pl.BlockSpec(memory_space=pltpu.SMEM),
            pl.BlockSpec((rows, LANES), lambda p: (0, p)),
            pl.BlockSpec((keys, LANES), lambda p: (0, p)),
            pl.BlockSpec((keys, LANES), lambda p: (0, PAIRS + p)),
            whole((rows, 1)),
            whole((1, keys)),
        ],
        out_specs=[
            pl.BlockSpec((rows, LANES), lambda p: (0, p)),
            whole((rows, LANES)),
            whole((16, rows)),
        ],
        out_shape=[
            jax.ShapeDtypeStruct((rows, D), BF16),
            jax.ShapeDtypeStruct((rows, LANES), F32),
            jax.ShapeDtypeStruct((16, rows), F32),
        ],
        scratch_shapes=[pltpu.VMEM((rows, keys), F32)],
        compiler_params=pltpu.CompilerParams(vmem_limit_bytes=60 << 20),
        cost_estimate=pl.CostEstimate(
            flops=8 * rows * keys * D, bytes_accessed=4 * keys * D, transcendentals=rows * keys * HEADS
        ),
        name="attention_forward",
    )(start, queries, kv, kv, own_segs, all_segs)


def attention_backward_kernel(
    start_ref,
    q_ref,
    grad_ref,
    k_own_ref,
    v_own_ref,
    lse_ref,
    delta_ref,
    k_ref,
    v_ref,
    q_all_ref,
    grad_all_ref,
    stats_ref,
    own_segs_ref,
    all_segs_ref,
    out_ref,
    query_bias_ref,
    key_bias_ref,
):
    pair = pl.program_id(0)
    rows, tokens = query_bias_ref.shape
    start = start_ref[0]

    @pl.when(pair == 0)
    def _():
        mask_columns(query_bias_ref, own_segs_ref[...], all_segs_ref, start, True)
        mask_columns(key_bias_ref, own_segs_ref[...], all_segs_ref, start, False)

    step = min(256, tokens)
    blocks = step // rows
    scale = jnp.asarray(SCALE, BF16)

    def doubled(bias):
        return jnp.concatenate([bias, bias], axis=0)

    queries = two_heads(q_ref[...] * scale)
    grads = two_heads(grad_ref[...])
    lse = pick_lanes(lse_ref[...], pair)
    delta = pick_lanes(delta_ref[...], pair)

    def visit_keys(index, grad_query):
        offset = pl.multiple_of(index * step, step)
        keys = k_ref[pl.ds(offset, step), :]
        values = v_ref[pl.ds(offset, step), :]
        bias = doubled(query_bias_ref[:, pl.ds(offset, step)])
        attention = jnp.exp(dot_rows(queries, keys) + bias - lse)
        grad_attention = dot_rows(grads, values)
        grad_scores = (attention * (grad_attention - delta)).astype(BF16)
        return grad_query + jnp.dot(grad_scores, keys, preferred_element_type=F32)

    zeros = jnp.zeros((2 * rows, LANES), F32)
    grad_query = lax.fori_loop(0, (start + rows + step - 1) // step, visit_keys, zeros)

    own_keys = two_heads(k_own_ref[...] * scale)
    own_values = two_heads(v_own_ref[...])

    def row_of(block, row):
        return jnp.broadcast_to(stats_ref[block, pl.ds(row, 1), :], (rows, rows))

    def stat_rows(index, row):
        first = [row_of(index * blocks + b, row + 2 * pair) for b in range(blocks)]
        second = [row_of(index * blocks + b, row + 2 * pair + 1) for b in range(blocks)]
        return jnp.concatenate(
            [jnp.concatenate(first, axis=1), jnp.concatenate(second, axis=1)], axis=0
        )

    def visit_queries(index, carried):
        grad_keys, grad_values = carried
        offset = pl.multiple_of(index * step, step)
        later = q_all_ref[pl.ds(offset, step), :]
        later_grads = grad_all_ref[pl.ds(offset, step), :]
        bias = doubled(key_bias_ref[:, pl.ds(offset, step)])
        attention = jnp.exp(dot_rows(own_keys, later) + bias - stat_rows(index, 0))
        grad_attention = dot_rows(own_values, later_grads)
        grad_scores = (attention * (grad_attention - stat_rows(index, 16))).astype(BF16)
        grad_keys = grad_keys + jnp.dot(grad_scores, later, preferred_element_type=F32)
        grad_values = grad_values + jnp.dot(
            attention.astype(BF16), later_grads, preferred_element_type=F32
        )
        return grad_keys, grad_values

    grad_keys, grad_values = lax.fori_loop(
        start // step, tokens // step, visit_queries, (zeros, zeros)
    )
    base = pl.multiple_of(pair * LANES, LANES)
    out_ref[:, pl.ds(base, LANES)] = (one_pair(grad_query) * SCALE).astype(BF16)
    out_ref[:, pl.ds(D + base, LANES)] = (one_pair(grad_keys) * SCALE).astype(BF16)
    out_ref[:, pl.ds(2 * D + base, LANES)] = one_pair(grad_values).astype(BF16)


def attention_backward(
    start, queries, grads, kv_own, lse, delta, kv, q_all, grad_all, stats, own_segs, all_segs
):
    rows = queries.shape[0]
    tokens = kv.shape[0]
    whole = lambda shape: pl.BlockSpec(shape, lambda p: (0,) * len(shape))
    own = pl.BlockSpec((rows, LANES), lambda p: (0, p))
    every = pl.BlockSpec((tokens, LANES), lambda p: (0, p))
    return pl.pallas_call(
        attention_backward_kernel,
        grid=(PAIRS,),
        in_specs=[
            pl.BlockSpec(memory_space=pltpu.SMEM),
            own,
            own,
            own,
            pl.BlockSpec((rows, LANES), lambda p: (0, PAIRS + p)),
            whole((rows, LANES)),
            whole((rows, LANES)),
            every,
            pl.BlockSpec((tokens, LANES), lambda p: (0, PAIRS + p)),
            every,
            every,
            whole(stats.shape),
            whole((rows, 1)),
            whole((1, tokens)),
        ],
        out_specs=whole((rows, 3 * D)),
        out_shape=jax.ShapeDtypeStruct((rows, 3 * D), BF16),
        scratch_shapes=[pltpu.VMEM((rows, tokens), F32), pltpu.VMEM((rows, tokens), F32)],
        compiler_params=pltpu.CompilerParams(vmem_limit_bytes=60 << 20),
        cost_estimate=pl.CostEstimate(
            flops=16 * rows * tokens * D,
            bytes_accessed=8 * tokens * D,
            transcendentals=rows * tokens * HEADS,
        ),
        name="attention_backward",
    )(
        start,
        queries,
        grads,
        kv_own,
        kv_own,
        lse,
        delta,
        kv,
        kv,
        q_all,
        grad_all,
        stats,
        own_segs,
        all_segs,
    )


def place_bits():
    ctx, fsdp = lax.axis_index("ctx"), lax.axis_index("fsdp")
    return lax.rem(ctx, 2), ctx // 2, fsdp // 2, lax.rem(fsdp, 2)


class Place:
    def __init__(self):
        self.x, self.z, self.y, self.core = x, z, y, core = place_bits()
        self.low, self.high = low, high = lax.rem(z, 2), z // 2
        self.fsdp = fsdp = 2 * y + core
        self.block = 2 * fsdp + x
        self.sibling = (2 * z + x, 2 * y + 1 - core)
        self.over_y = (2 * z + x, 2 * (1 - y) + core)
        self.over_x = (2 * z + 1 - x, fsdp)
        self.over_z = (2 * (z + 1 - 2 * low) + x, fsdp)
        self.over_zz = (2 * (z + 2 - 4 * high) + x, fsdp)
        self.partner = (2 * fsdp + x, z)
        self.has_partner = fsdp != z


class Copies:
    def __init__(self, send_sems, recv_sems):
        self.send_sems, self.recv_sems = send_sems, recv_sems
        self.used = 0

    def make(self, src, dst, device):
        slot = self.used
        self.used += 1
        return pltpu.make_async_remote_copy(
            src_ref=src,
            dst_ref=dst,
            send_sem=self.send_sems.at[slot],
            recv_sem=self.recv_sems.at[slot],
            device_id=device,
            device_id_type=MESH,
        )


def greet(devices):
    barrier = pltpu.get_barrier_semaphore()
    for device in devices:
        pl.semaphore_signal(barrier, inc=1, device_id=device, device_id_type=MESH)
    pl.semaphore_wait(barrier, len(devices))


WEIGHT_COPIES = 11


def weight_cuts(shape):
    rows, columns = shape
    if rows * columns <= 192 * 768:
        return [(0, columns)]
    return [(0, columns // 2), (columns // 2, columns // 2)]


class WeightGather:
    def __init__(self, place, copies, shares, fulls, stages, local_sems):
        x, low = place.x, place.low
        own, other = place.fsdp, 2 * (1 - place.y) + place.core
        self.plans = []
        self.locals = []
        for which, (share, full) in enumerate(zip(shares, fulls)):
            part = share.shape[0] // 4
            for first, width in weight_cuts(share.shape):
                columns = pl.ds(first, width)

                def piece(ref, x_bit, low_bit, part=part, columns=columns):
                    return ref.at[pl.ds((2 * low_bit + x_bit) * part, part), columns]

                def side(ref, x_bit, low_bit, index, part=part, first=first, width=width):
                    start = (2 * low_bit + x_bit) * part
                    if part % 32 == 0:
                        rows = pl.ds(start + index * (part // 2), part // 2)
                        return ref.at[rows, pl.ds(first, width)]
                    half = width // 2
                    return ref.at[pl.ds(start, part), pl.ds(first + index * half, half)]

                theirs = full.at[other]
                same = lambda view, device: copies.make(view, view, device)
                mine = piece(theirs, x, low)
                from_x, from_z = piece(theirs, 1 - x, low), piece(theirs, x, 1 - low)
                self.plans.append(
                    [
                        copies.make(piece(share, x, low), piece(full.at[own], x, low), place.over_y),
                        same(mine, place.over_x),
                        same(mine, place.over_z),
                        same(mine, place.sibling),
                        same(side(theirs, 1 - x, low, 0), place.over_z),
                        same(from_x, place.sibling),
                        same(side(theirs, x, 1 - low, 1), place.over_x),
                        same(from_z, place.sibling),
                        same(side(theirs, 1 - x, 1 - low, 0), place.sibling),
                        same(side(theirs, 1 - x, 1 - low, 1), place.sibling),
                        copies.make(share.at[:, columns], full.at[own, :, columns], place.sibling),
                    ]
                )
            sem = local_sems.at[which]
            self.locals.append(
                (
                    pltpu.make_async_copy(share, stages[which], sem),
                    pltpu.make_async_copy(stages[which], full.at[own], sem),
                )
            )

    def begin(self):
        for plan in self.plans:
            plan[0].start()
        for plan in self.plans:
            plan[10].start()
        for into, _ in self.locals:
            into.start()

    def keep_own(self):
        for into, out in self.locals:
            into.wait()
            out.start()

    def steps(self):
        count = len(self.plans)
        for step in range(count + 2):
            yield step

    def step(self, step):
        count = len(self.plans)
        if step < count:
            plan = self.plans[step]
            plan[0].wait_recv()
            plan[1].start()
            plan[2].start()
            plan[3].start()
        if 0 <= step - 1 < count:
            plan = self.plans[step - 1]
            plan[1].wait_recv()
            plan[4].start()
            plan[5].start()
            plan[2].wait_recv()
            plan[6].start()
            plan[7].start()
        if 0 <= step - 2 < count:
            plan = self.plans[step - 2]
            plan[4].wait_recv()
            plan[8].start()
            plan[6].wait_recv()
            plan[9].start()

    def finish(self):
        for plan in self.plans:
            for index in (3, 5, 7, 8, 9, 10):
                plan[index].wait_recv()
            for copy in plan:
                copy.wait_send()
        for _, out in self.locals:
            out.wait()


BLOCK_COPIES = 13


class BlockGather:
    def __init__(self, place, copies, blocks, fulls):
        self.own = place.block
        self.pairs = list(zip(blocks, fulls))
        self.plans = []
        for block, full in self.pairs:
            half = block.shape[0] // 2

            def part(ref, side, half=half):
                return ref.at[pl.ds(side * half, half), :]

            def slot_of(x_bit, y_bit, full=full):
                return full.at[4 * y_bit + 2 * place.core + x_bit]

            same = lambda view, device: copies.make(view, view, device)
            x, y = place.x, place.y
            mine, from_x = slot_of(x, y), slot_of(1 - x, y)
            from_y, from_both = slot_of(x, 1 - y), slot_of(1 - x, 1 - y)
            self.plans.append(
                [
                    copies.make(block, mine, place.sibling),
                    copies.make(part(block, 0), part(mine, 0), place.over_x),
                    copies.make(part(block, 1), part(mine, 1), place.over_y),
                    copies.make(part(block, 1), part(mine, 1), place.over_x),
                    copies.make(part(block, 0), part(mine, 0), place.over_y),
                    same(part(from_x, 0), place.over_y),
                    same(part(from_x, 0), place.sibling),
                    same(part(from_y, 1), place.over_x),
                    same(part(from_y, 1), place.sibling),
                    same(part(from_x, 1), place.sibling),
                    same(part(from_y, 0), place.sibling),
                    same(part(from_both, 0), place.sibling),
                    same(part(from_both, 1), place.sibling),
                ]
            )

    def begin(self):
        for index in (1, 2, 3, 4, 0):
            for plan in self.plans:
                plan[index].start()
        for block, full in self.pairs:
            full[self.own] = block[...]

    def relay(self, *pairs):
        for arrived, followers in pairs:
            for plan in self.plans:
                plan[arrived].wait_recv()
                for index in followers:
                    plan[index].start()

    def first_halves(self):
        self.relay((1, (5, 6)), (2, (7, 8)))

    def second_halves(self):
        self.relay((3, (9,)), (4, (10,)))

    def corners(self):
        self.relay((5, (11,)), (7, (12,)))

    def wait(self, *indices):
        for plan in self.plans:
            for index in indices:
                plan[index].wait_recv()

    def wait_near(self):
        self.wait(0, 6, 9)

    def wait_far(self):
        self.wait(8, 10, 11, 12)

    def finish(self):
        for plan in self.plans:
            for copy in plan:
                copy.wait_send()


VECTORS = 8


def pack_vectors(ln1_gain, ln1_bias, ln2_gain, ln2_bias, proj_bias, out_bias, attn_bias, fc_bias):
    rows = (ln1_gain, ln1_bias, ln2_gain, ln2_bias, proj_bias, out_bias, attn_bias, fc_bias)
    return jnp.stack([jnp.pad(row.astype(F32), (0, D - row.shape[0])) for row in rows])


def assemble_vectors(shares):
    quarter = D // 4
    small = jnp.concatenate([share[:6, :quarter] for share in shares], axis=1)
    query = jnp.concatenate([shares[0][6:7, : 2 * quarter], shares[1][6:7, : 2 * quarter]], axis=1)
    value = jnp.concatenate([shares[2][6:7, : 2 * quarter], shares[3][6:7, : 2 * quarter]], axis=1)
    hidden = [share[7:8] for share in shares]
    return jnp.concatenate([small, query, value, *hidden, jnp.zeros((4, D), F32)], axis=0)


def mask_block(own_segs, segs_ref, block, start, own_is_query):
    rows = own_segs.shape[0]
    own_place = start + lax.broadcasted_iota(jnp.int32, (rows, rows), 0)
    place = block * rows + lax.broadcasted_iota(jnp.int32, (rows, rows), 1)
    causal = (place <= own_place) if own_is_query else (own_place <= place)
    same = own_segs == segs_ref[block, 0:1, :]
    return jnp.where(causal & same, 0.0, NEGATIVE)


def own_columns(segs_ref, block):
    rows = segs_ref.shape[2]
    return jnp.broadcast_to(segs_ref[block, 0:1, :], (rows, rows)).T


class AttentionForward:
    def __init__(self, place, q_ref, segs_ref, kv_all, out_ref, lse_ref, lse_rows_ref, kv_out, scratch, sems):
        self.place = place
        self.q_ref, self.segs_ref, self.kv_all = q_ref, segs_ref, kv_all
        self.out_ref, self.lse_ref, self.lse_rows_ref = out_ref, lse_ref, lse_rows_ref
        self.near_bias, self.far_bias, self.top, self.total, self.mixed = scratch
        self.rows = q_ref.shape[0]
        self.near, self.far = 4 * place.y, 4 * (1 - place.y)
        self.saves = [
            pltpu.make_async_copy(kv_all.at[pl.ds(first, 4)], kv_out.at[pl.ds(first, 4)], sem)
            for first, sem in zip((self.near, self.far), sems)
        ]

    def masks(self, far):
        rows = self.rows
        start = self.place.block * rows
        own_segs = own_columns(self.segs_ref, self.place.block)
        first, bias = (self.far, self.far_bias) if far else (self.near, self.near_bias)
        for i in range(4):
            at = slice(i * rows, (i + 1) * rows)
            bias[:, at] = mask_block(own_segs, self.segs_ref, first + i, start, True)

    def lanes(self, pair, side=0):
        return pl.ds(pl.multiple_of(side * D + pair * LANES, LANES), LANES)

    def part(self, first, bias_ref, pair):
        rows = self.rows
        queries = two_heads(self.q_ref[:, self.lanes(pair)] * jnp.asarray(SCALE, BF16))
        keys = self.kv_all[pl.ds(first, 4), :, self.lanes(pair)].reshape(4 * rows, LANES)
        values = self.kv_all[pl.ds(first, 4), :, self.lanes(pair, 1)].reshape(4 * rows, LANES)
        bias = bias_ref[...]
        scores = dot_rows(queries, keys) + jnp.concatenate([bias, bias], axis=0)
        top = jnp.max(scores, axis=1, keepdims=True)
        shares = jnp.exp(scores - top)
        total = jnp.sum(shares, axis=1, keepdims=True)
        return top, total, jnp.dot(shares.astype(BF16), values, preferred_element_type=F32)

    def near_part(self):
        self.saves[0].start()
        self.lse_ref[...] = jnp.zeros_like(self.lse_ref)

        def visit(pair, carried):
            self.top[pair], self.total[pair], self.mixed[pair] = self.part(
                self.near, self.near_bias, pair
            )
            return carried

        lax.fori_loop(0, PAIRS, visit, 0)

    def far_part(self):
        self.saves[1].start()

        def visit(pair, carried):
            top, total, mixed = self.part(self.far, self.far_bias, pair)
            old_top = self.top[pair]
            new_top = jnp.maximum(top, old_top)
            new, old = jnp.exp(top - new_top), jnp.exp(old_top - new_top)
            self.top[pair] = new_top
            self.total[pair] = total * new + self.total[pair] * old
            self.mixed[pair] = mixed * new + self.mixed[pair] * old
            return carried

        @pl.when(self.place.y == 1)
        def _():
            lax.fori_loop(0, PAIRS, visit, 0)

    def store(self):
        rows = self.rows

        def visit(pair, carried):
            total = self.total[pair]
            self.out_ref[:, self.lanes(pair)] = one_pair(self.mixed[pair] / total).astype(BF16)
            lse = self.top[pair] + jnp.log(total)
            lane = lax.broadcasted_iota(jnp.int32, (rows, LANES), 1)
            kept = jnp.where(lane == 2 * pair, lse[:rows], self.lse_ref[...])
            self.lse_ref[...] = jnp.where(lane == 2 * pair + 1, lse[rows:], kept)
            return carried

        lax.fori_loop(0, PAIRS, visit, 0)
        self.lse_rows_ref[...] = self.lse_ref[...].T[:16]

    def finish(self):
        for save in self.saves:
            save.wait()


def forward_scratch(rows):
    return [
        pltpu.VMEM((8, rows, 2 * D), BF16),
        pltpu.VMEM((rows, 4 * rows), F32),
        pltpu.VMEM((rows, 4 * rows), F32),
        pltpu.VMEM((PAIRS, 2 * rows, 1), F32),
        pltpu.VMEM((PAIRS, 2 * rows, 1), F32),
        pltpu.VMEM((PAIRS, 2 * rows, LANES), F32),
    ]


FORWARD_SCRATCH = 6


def forward_shapes(rows):
    return [
        jax.ShapeDtypeStruct((rows, D), BF16),
        jax.ShapeDtypeStruct((rows, LANES), F32),
        jax.ShapeDtypeStruct((16, rows), F32),
        jax.ShapeDtypeStruct((8, rows, 2 * D), BF16),
    ]


def greet_with_partner(place, others):
    barrier = pltpu.get_barrier_semaphore()
    for device in others:
        pl.semaphore_signal(barrier, inc=1, device_id=device, device_id_type=MESH)

    @pl.when(place.has_partner)
    def _():
        pl.semaphore_signal(barrier, inc=1, device_id=place.partner, device_id_type=MESH)
        pl.semaphore_wait(barrier, len(others) + 1)

    @pl.when(jnp.logical_not(place.has_partner))
    def _():
        pl.semaphore_wait(barrier, len(others))


def attend_kernel(
    q_ref, kv_ref, segs_ref, cotangent_ref, out_ref, lse_ref, lse_rows_ref, kv_out, cotangent_out, *scratch
):
    kv_all, send_sems, recv_sems, local_sems = scratch[0], *scratch[FORWARD_SCRATCH:]
    place = Place()
    greet_with_partner(place, (place.sibling, place.over_x, place.over_y))
    copies = Copies(send_sems, recv_sems)
    gather = BlockGather(place, copies, [kv_ref], [kv_all])
    swap = copies.make(cotangent_ref, cotangent_out, place.partner)
    keep = pltpu.make_async_copy(cotangent_ref, cotangent_out, local_sems.at[2])
    gather.begin()

    @pl.when(place.has_partner)
    def _():
        swap.start()

    @pl.when(jnp.logical_not(place.has_partner))
    def _():
        keep.start()

    attention = AttentionForward(
        place,
        q_ref,
        segs_ref,
        kv_all,
        out_ref,
        lse_ref,
        lse_rows_ref,
        kv_out,
        scratch[1:FORWARD_SCRATCH],
        (local_sems.at[0], local_sems.at[1]),
    )
    attention.masks(False)
    attention.masks(True)
    gather.first_halves()
    gather.second_halves()
    gather.wait_near()
    attention.near_part()
    gather.corners()
    gather.wait_far()
    attention.far_part()
    attention.store()
    attention.finish()
    gather.finish()

    @pl.when(place.has_partner)
    def _():
        swap.wait()

    @pl.when(jnp.logical_not(place.has_partner))
    def _():
        keep.wait()


def attend(queries, kv_own, segs, cotangent, collective_id):
    rows = queries.shape[0]
    vmem = pl.BlockSpec(memory_space=pltpu.VMEM)
    anywhere = pl.BlockSpec(memory_space=pl.ANY)
    return pl.pallas_call(
        attend_kernel,
        in_specs=[vmem, vmem, vmem, anywhere],
        out_specs=[vmem, vmem, vmem, anywhere, vmem],
        out_shape=forward_shapes(rows) + [jax.ShapeDtypeStruct((rows, D), BF16)],
        scratch_shapes=forward_scratch(rows)
        + [
            pltpu.SemaphoreType.DMA((BLOCK_COPIES + 1,)),
            pltpu.SemaphoreType.DMA((BLOCK_COPIES + 1,)),
            pltpu.SemaphoreType.DMA((3,)),
        ],
        compiler_params=pltpu.CompilerParams(
            collective_id=collective_id, has_side_effects=True, vmem_limit_bytes=32 << 20
        ),
        name="attend",
    )(queries, kv_own, segs, cotangent)


class FirstWeightGather:
    def __init__(self, place, copies, share, full, columns, part, sem):
        x = place.x
        own, other = place.fsdp, 2 * (1 - place.y) + place.core
        half = share.shape[0] // 2
        self.steps = []
        for index in range(half // part):
            mine = pl.ds(pl.multiple_of(x * half + index * part, 16), part)
            theirs = pl.ds(pl.multiple_of((1 - x) * half + index * part, 16), part)
            got, from_x = full.at[other, mine, columns], full.at[other, theirs, columns]
            self.steps.append(
                [
                    copies.make(share.at[mine, columns], full.at[own, mine, columns], place.over_y),
                    copies.make(got, got, place.over_x),
                    copies.make(got, got, place.sibling),
                    copies.make(from_x, from_x, place.sibling),
                ]
            )
        whole = full.at[own, :, columns]
        self.to_sibling = copies.make(share.at[:, columns], whole, place.sibling)
        self.load = pltpu.make_async_copy(share.at[:, columns], whole, sem)

    def begin(self):
        for step in self.steps:
            step[0].start()
        self.to_sibling.start()
        self.load.start()

    def relay_y(self):
        for step in self.steps:
            step[0].wait_recv()
            step[1].start()
            step[2].start()

    def relay_x(self):
        for step in self.steps:
            step[1].wait_recv()
            step[3].start()

    def wait_near(self):
        self.load.wait()
        self.to_sibling.wait_recv()

    def wait_far(self):
        for step in self.steps:
            step[2].wait_recv()
            step[3].wait_recv()

    def finish(self):
        self.to_sibling.wait_send()
        for step in self.steps:
            for copy in step:
                copy.wait_send()


def opening_kernel(count, *refs):
    tokens_ref, segs_ref, first_ref = refs[:3]
    vector_refs = refs[3 : 3 + VECTORS]
    shares = refs[3 + VECTORS : 3 + VECTORS + count]
    refs = refs[3 + VECTORS + count :]
    (
        tokens_out,
        segs_out,
        vectors_out,
        normed_out,
        normal_out,
        inverse_out,
        q_out,
        kv_own_out,
        attended_out,
        lse_out,
        lse_rows_out,
        kv_out,
        first_out,
    ) = refs[:13]
    fulls = refs[13 : 13 + count]
    refs = refs[13 + count :]
    kv_all = refs[0]
    forward = refs[1:FORWARD_SCRATCH]
    vectors_own, vectors_all, segs_row, segs_sent, segs_own = refs[FORWARD_SCRATCH : FORWARD_SCRATCH + 5]
    refs = refs[FORWARD_SCRATCH + 5 :]
    first_full, projected, send_sems, recv_sems, local_sems = refs[:5]
    stages, vector_rows = refs[5 : 5 + count], refs[5 + count :]
    place = Place()
    own, other = place.fsdp, 2 * (1 - place.y) + place.core
    loads = [
        pltpu.make_async_copy(src, dst, local_sems.at[count + 6 + i])
        for i, (src, dst) in enumerate(zip((segs_ref, *vector_refs), (segs_row, *vector_rows)))
    ]
    for load in loads:
        load.start()
    for load in loads:
        load.wait()
    vectors_own[...] = jnp.zeros_like(vectors_own)
    for i, row in enumerate(vector_rows):
        size = row.shape[0]
        vectors_own[i : i + 1, :size] = row[...].astype(F32).reshape(1, size)
    segs_sent[...] = jnp.broadcast_to(segs_row[...], segs_sent.shape)
    greet_with_partner(place, (place.sibling, place.over_x, place.over_y, place.over_z))
    copies = Copies(send_sems, recv_sems)
    swap_tokens = copies.make(tokens_ref, tokens_out, place.partner)
    swap_segs = copies.make(segs_sent, segs_own, place.partner)
    vector_copies = [
        copies.make(vectors_own, vectors_all.at[own], place.over_y),
        copies.make(vectors_own, vectors_all.at[own], place.sibling),
        copies.make(vectors_all.at[other], vectors_all.at[other], place.sibling),
    ]
    keys = FirstWeightGather(
        place, copies, first_ref, first_full, pl.ds(D, 2 * D), 32, local_sems.at[count]
    )
    queries = FirstWeightGather(
        place, copies, first_ref, first_full, pl.ds(0, D), 48, local_sems.at[count + 5]
    )
    weights = WeightGather(place, copies, shares, fulls, stages, local_sems)
    gather = BlockGather(place, copies, [kv_own_out, segs_own], [kv_all, segs_out])
    save_first = pltpu.make_async_copy(first_full, first_out, local_sems.at[count + 1])
    attention = AttentionForward(
        place,
        q_out,
        segs_out,
        kv_all,
        attended_out,
        lse_out,
        lse_rows_out,
        kv_out,
        forward,
        (local_sems.at[count + 2], local_sems.at[count + 3]),
    )

    keep_tokens = pltpu.make_async_copy(tokens_ref, tokens_out, local_sems.at[count + 7 + VECTORS])
    vector_copies[0].start()
    vector_copies[1].start()

    @pl.when(place.has_partner)
    def _():
        swap_segs.start()

    keys.begin()

    @pl.when(place.has_partner)
    def _():
        swap_tokens.start()

    @pl.when(jnp.logical_not(place.has_partner))
    def _():
        keep_tokens.start()

    queries.begin()
    weights.begin()
    vectors_all[own] = vectors_own[...]

    @pl.when(jnp.logical_not(place.has_partner))
    def _():
        segs_own[...] = segs_sent[...]

    vector_copies[0].wait_recv()
    vector_copies[2].start()
    keys.relay_y()
    vector_copies[1].wait_recv()
    vector_copies[2].wait_recv()
    vectors_out[...] = assemble_vectors([vectors_all[i] for i in range(4)])

    @pl.when(place.has_partner)
    def _():
        swap_tokens.wait_recv()
        swap_segs.wait_recv()

    @pl.when(jnp.logical_not(place.has_partner))
    def _():
        keep_tokens.wait()

    normed, normal, inverse = norm_forward(
        tokens_out[...].astype(F32), vectors_out[0:1, :], vectors_out[1:2, :]
    )
    normed_out[...] = normed
    normal_out[...] = normal
    inverse_out[...] = inverse

    def half_product(y_bit, start, width):
        depth = D // 2
        rows = normed_out[:, pl.ds(pl.multiple_of(y_bit * depth, LANES), depth)]
        weight = first_full[pl.ds(2 * y_bit, 2), :, start : start + width].reshape(depth, width)
        return jnp.dot(rows, weight, preferred_element_type=F32)

    keys.wait_near()
    projected[...] = half_product(place.y, D, 2 * D)
    keys.relay_x()
    keys.wait_far()
    total = projected[...] + half_product(1 - place.y, D, 2 * D)
    kv_own_out[:, :D] = total[:, :D].astype(BF16)
    kv_own_out[:, D:] = (total[:, D:] + vectors_out[7:8, :]).astype(BF16)
    gather.begin()
    queries.relay_y()
    weights.step(0)
    weights.step(1)
    queries.relay_x()
    queries.wait_near()
    queries.wait_far()
    total = half_product(place.y, 0, D) + half_product(1 - place.y, 0, D)
    q_out[...] = (total + vectors_out[6:7, :]).astype(BF16)
    save_first.start()
    gather.first_halves()
    weights.keep_own()
    weights.step(2)
    gather.second_halves()
    gather.wait_near()
    attention.masks(False)
    weights.step(3)
    attention.near_part()
    gather.corners()
    weights.step(4)
    gather.wait_far()
    attention.masks(True)
    attention.far_part()
    weights.step(5)
    weights.step(6)
    attention.store()
    save_first.wait()
    attention.finish()
    keys.finish()
    queries.finish()
    gather.finish()
    for copy in vector_copies:
        copy.wait_send()

    @pl.when(place.has_partner)
    def _():
        swap_segs.wait_send()
        swap_tokens.wait_send()

    weights.finish()


def opening(tokens, segs_row, vectors, first, shares, collective_id):
    rows, columns = tokens.shape
    count = len(shares)
    slots = 2 + 3 + (3 + 2) * 4 + 2 + sum(len(weight_cuts(share.shape)) for share in shares) * WEIGHT_COPIES + 2 * BLOCK_COPIES
    vmem = pl.BlockSpec(memory_space=pltpu.VMEM)
    anywhere = pl.BlockSpec(memory_space=pl.ANY)
    shape = jax.ShapeDtypeStruct
    segs_shape = (16, segs_row.shape[1])
    return pl.pallas_call(
        partial(opening_kernel, count),
        in_specs=[anywhere] * (3 + VECTORS + count),
        out_specs=[vmem] * 11 + [anywhere] * (2 + count),
        out_shape=[
            shape((rows, columns), tokens.dtype),
            shape((8, *segs_shape), segs_row.dtype),
            shape((16, D), F32),
            shape((rows, D), BF16),
            shape((rows, D), F32),
            shape((rows, 1), F32),
            shape((rows, D), BF16),
            shape((rows, 2 * D), BF16),
        ]
        + forward_shapes(rows)
        + [shape((4, *share.shape), share.dtype) for share in [first, *shares]],
        scratch_shapes=forward_scratch(rows)
        + [
            pltpu.VMEM((8, D), F32),
            pltpu.VMEM((4, 8, D), F32),
            pltpu.VMEM(segs_row.shape, segs_row.dtype),
            pltpu.VMEM(segs_shape, segs_row.dtype),
            pltpu.VMEM(segs_shape, segs_row.dtype),
            pltpu.VMEM((4, *first.shape), first.dtype),
            pltpu.VMEM((rows, 2 * D), F32),
            pltpu.SemaphoreType.DMA((slots,)),
            pltpu.SemaphoreType.DMA((slots,)),
            pltpu.SemaphoreType.DMA((count + 8 + VECTORS,)),
        ]
        + [pltpu.VMEM(share.shape, share.dtype) for share in shares]
        + [pltpu.VMEM(vector.shape, vector.dtype) for vector in vectors],
        compiler_params=pltpu.CompilerParams(
            collective_id=collective_id, has_side_effects=True, vmem_limit_bytes=60 << 20
        ),
        name="opening",
    )(tokens, segs_row, first, *vectors, *shares)


class AttentionGrads:
    def __init__(self, place, q_ref, grad_ref, lse_ref, delta_ref, segs_ref, kv_all, q_all, grad_all, stats_all, biases, sums):
        self.place = place
        self.q_ref, self.grad_ref, self.lse_ref, self.delta_ref = q_ref, grad_ref, lse_ref, delta_ref
        self.segs_ref, self.kv_all, self.q_all, self.grad_all = segs_ref, kv_all, q_all, grad_all
        self.stats_all = stats_all
        self.query_bias, self.key_bias = biases
        self.query_sum, self.key_sum, self.value_sum = sums
        self.rows = q_ref.shape[0]

    def masks(self):
        rows, place = self.rows, self.place
        start = place.block * rows
        own_segs = own_columns(self.segs_ref, place.block)
        for i in range(8):
            at = slice(i * rows, (i + 1) * rows)
            self.query_bias[:, at] = mask_block(own_segs, self.segs_ref, i, start, True)
            self.key_bias[:, at] = mask_block(own_segs, self.segs_ref, i, start, False)

    def lanes(self, pair, side=0):
        return pl.ds(pl.multiple_of(side * D + pair * LANES, LANES), LANES)

    def two_blocks(self, ref, index, lanes):
        return ref[pl.ds(2 * index, 2), :, lanes].reshape(2 * self.rows, LANES)

    def bias(self, ref, index):
        step = 2 * self.rows
        bias = ref[:, pl.ds(pl.multiple_of(index * step, step), step)]
        return jnp.concatenate([bias, bias], axis=0)

    def query_grads(self, first_pair, last_pair):
        scale = jnp.asarray(SCALE, BF16)
        count = self.place.block // 2 + 1

        def visit_pair(pair, carried):
            lanes = self.lanes(pair)
            queries = two_heads(self.q_ref[:, lanes] * scale)
            grads = two_heads(self.grad_ref[:, lanes])
            lse = pick_lanes(self.lse_ref[...], pair)
            delta = pick_lanes(self.delta_ref[...], pair)

            def visit(index, total):
                keys = self.two_blocks(self.kv_all, index, lanes)
                values = self.two_blocks(self.kv_all, index, self.lanes(pair, 1))
                scores = dot_rows(queries, keys) + self.bias(self.query_bias, index)
                attention = jnp.exp(scores - lse)
                grad_attention = dot_rows(grads, values)
                grad_scores = (attention * (grad_attention - delta)).astype(BF16)
                return total + jnp.dot(grad_scores, keys, preferred_element_type=F32)

            zeros = jnp.zeros((2 * self.rows, LANES), F32)
            self.query_sum[pair] = lax.fori_loop(0, count, visit, zeros)
            return carried

        lax.fori_loop(first_pair, last_pair, visit_pair, 0)

    def key_grads(self, first, last, fresh):
        rows = self.rows
        scale = jnp.asarray(SCALE, BF16)
        own = self.place.block

        def visit_pair(pair, carried):
            lanes = self.lanes(pair)
            own_keys = two_heads(self.kv_all[own, :, lanes] * scale)
            own_values = two_heads(self.kv_all[own, :, self.lanes(pair, 1)])

            def stat_rows(index, row):
                def spread(block, head):
                    line = self.stats_all[2 * index + block, pl.ds(row + 2 * pair + head, 1), :]
                    return jnp.broadcast_to(line, (rows, rows))

                heads = [
                    jnp.concatenate([spread(0, head), spread(1, head)], axis=1) for head in range(2)
                ]
                return jnp.concatenate(heads, axis=0)

            def visit(index, totals):
                key_total, value_total = totals
                later = self.two_blocks(self.q_all, index, lanes)
                later_grads = self.two_blocks(self.grad_all, index, lanes)
                scores = dot_rows(own_keys, later) + self.bias(self.key_bias, index)
                attention = jnp.exp(scores - stat_rows(index, 0))
                grad_attention = dot_rows(own_values, later_grads)
                grad_scores = attention * (grad_attention - stat_rows(index, 16))
                key_total = key_total + jnp.dot(
                    grad_scores.astype(BF16), later, preferred_element_type=F32
                )
                value_total = value_total + jnp.dot(
                    attention.astype(BF16), later_grads, preferred_element_type=F32
                )
                return key_total, value_total

            if fresh:
                zeros = jnp.zeros((2 * rows, LANES), F32)
                totals = (zeros, zeros)
            else:
                totals = (self.key_sum[pair], self.value_sum[pair])
            self.key_sum[pair], self.value_sum[pair] = lax.fori_loop(first, last, visit, totals)
            return carried

        lax.fori_loop(0, PAIRS, visit_pair, 0)

    def near_keys(self):
        self.key_grads(self.place.block // 2, 2 * self.place.y + 2, True)

    def far_keys(self):
        @pl.when(self.place.y == 0)
        def _():
            self.key_grads(2, 4, False)

    def store(self, out_ref):
        def visit(pair, carried):
            out_ref[:, self.lanes(pair)] = (one_pair(self.query_sum[pair]) * SCALE).astype(BF16)
            out_ref[:, self.lanes(pair, 1)] = (one_pair(self.key_sum[pair]) * SCALE).astype(BF16)
            out_ref[:, self.lanes(pair, 2)] = one_pair(self.value_sum[pair]).astype(BF16)
            return carried

        lax.fori_loop(0, PAIRS, visit, 0)


def attention_scratch(rows):
    return [
        pltpu.VMEM((8, rows, 2 * D), BF16),
        pltpu.VMEM((8, rows, D), BF16),
        pltpu.VMEM((8, rows, D), BF16),
        pltpu.VMEM((8, 32, rows), F32),
        pltpu.VMEM((rows, 8 * rows), F32),
        pltpu.VMEM((rows, 8 * rows), F32),
        pltpu.VMEM((PAIRS, 2 * rows, LANES), F32),
        pltpu.VMEM((PAIRS, 2 * rows, LANES), F32),
        pltpu.VMEM((PAIRS, 2 * rows, LANES), F32),
    ]


ATTENTION_SCRATCH = 9


def attend_back_kernel(
    q_ref, grad_ref, stats_ref, lse_ref, delta_ref, segs_ref, kv_ref, out_ref, *scratch
):
    kv_all, q_all, grad_all, stats_all = scratch[:4]
    biases, sums = scratch[4:6], scratch[6:9]
    send_sems, recv_sems, local_sem = scratch[9:]
    place = Place()
    greet((place.sibling, place.over_x, place.over_y))
    copies = Copies(send_sems, recv_sems)
    gather = BlockGather(
        place, copies, [q_ref, grad_ref, stats_ref], [q_all, grad_all, stats_all]
    )
    load = pltpu.make_async_copy(kv_ref, kv_all, local_sem)
    load.start()
    gather.begin()
    grads = AttentionGrads(
        place, q_ref, grad_ref, lse_ref, delta_ref, segs_ref, kv_all, q_all, grad_all, stats_all, biases, sums
    )
    grads.masks()
    load.wait()
    grads.query_grads(0, 2)
    gather.first_halves()
    grads.query_grads(2, PAIRS)
    gather.second_halves()
    gather.wait_near()
    grads.near_keys()
    gather.corners()
    gather.wait_far()
    grads.far_keys()
    grads.store(out_ref)
    gather.finish()


def attend_back(queries, grads, stats, lse, delta, segs, kv, collective_id):
    rows = queries.shape[0]
    slots = 3 * BLOCK_COPIES
    vmem = pl.BlockSpec(memory_space=pltpu.VMEM)
    return pl.pallas_call(
        attend_back_kernel,
        in_specs=[vmem] * 6 + [pl.BlockSpec(memory_space=pl.ANY)],
        out_specs=vmem,
        out_shape=jax.ShapeDtypeStruct((rows, 3 * D), BF16),
        scratch_shapes=attention_scratch(rows)
        + [
            pltpu.SemaphoreType.DMA((slots,)),
            pltpu.SemaphoreType.DMA((slots,)),
            pltpu.SemaphoreType.DMA,
        ],
        compiler_params=pltpu.CompilerParams(
            collective_id=collective_id, has_side_effects=True, vmem_limit_bytes=32 << 20
        ),
        name="attend_back",
    )(queries, grads, stats, lse, delta, segs, kv)


CHUNK_ROWS, CHUNK_COLUMNS = 192, 768
REDUCE_COPIES = 9
VECTOR_AXES = 5


def chunk_places(shapes):
    return [
        (which, row, column)
        for which, (rows, columns) in enumerate(shapes)
        for row in range(0, rows, CHUNK_ROWS)
        for column in range(0, columns, CHUNK_COLUMNS)
    ]


REDUCE_STAGES = ("core0", "core1", "y", "x", "z", "zz", "zz_back", "z_back", "x_back")


class GradientSum:
    def __init__(self, place, copies, places, terms, sums, buffers, local_sems):
        self.place = place
        (
            self.own,
            self.got_core,
            self.got_y,
            self.to_x,
            self.got_x,
            self.to_z,
            self.got_z,
            self.to_zz,
            self.got_zz,
            to_core,
        ) = buffers
        self.to_core = to_core
        self.x_rows, self.z_rows = CHUNK_ROWS // 2, CHUNK_ROWS // 4
        self.zz_columns = CHUNK_COLUMNS // 2
        x, y, core, low, high = place.x, place.y, place.core, place.low, place.high
        self.plans = []
        self.finals = []
        self.loads = []
        self.filled = []
        for k, (which, row, column) in enumerate(places):
            term, out = terms[which], sums[which]

            def piece(first, rows, start, width, out=out, row=row, column=column):
                return out.at[
                    pl.ds(pl.multiple_of(row + first, 16), rows),
                    pl.ds(pl.multiple_of(column + start, LANES), width),
                ]

            def quarter(index, term=term, row=row, column=column):
                return term.at[index, pl.ds(row, CHUNK_ROWS), pl.ds(column, CHUNK_COLUMNS)]

            if term is None:
                sent = [to_core.at[len(self.filled), i] for i in range(2)]
                self.filled.append((k, column))
                loads = []
            else:
                sent = [quarter(1 - core), quarter(3 - core)]
                loads = [
                    pltpu.make_async_copy(
                        quarter(2 * i + core), self.own.at[k, i], local_sems.at[2 * k + i]
                    )
                    for i in range(2)
                ]
            final = piece(
                x * self.x_rows + low * self.z_rows, self.z_rows, high * self.zz_columns, self.zz_columns
            )
            wide = piece(x * self.x_rows + low * self.z_rows, self.z_rows, 0, CHUNK_COLUMNS)
            tall = piece(x * self.x_rows, self.x_rows, 0, CHUNK_COLUMNS)
            moves = (
                (sent[0], self.got_core.at[k, 0], place.sibling),
                (sent[1], self.got_core.at[k, 1], place.sibling),
                (self.own.at[k, 1 - y], self.got_y.at[k], place.over_y),
                (self.to_x.at[k], self.got_x.at[k], place.over_x),
                (self.to_z.at[k], self.got_z.at[k], place.over_z),
                (self.to_zz.at[k], self.got_zz.at[k], place.over_zz),
                (final, final, place.over_zz),
                (wide, wide, place.over_z),
                (tall, tall, place.over_x),
            )
            self.plans.append(
                {name: copies.make(*move) for name, move in zip(REDUCE_STAGES, moves)}
            )
            self.finals.append(final)
            self.loads.append(loads)
        self.stages = (
            self.stage_x,
            self.stage_z,
            self.stage_zz,
            self.stage_final,
            self.stage_z_back,
            self.stage_x_back,
        )

    def begin(self, k):
        self.plans[k]["core0"].start()
        self.plans[k]["core1"].start()
        for load in self.loads[k]:
            load.start()

    def add_up(self, store, loads, rows):
        step = self.z_rows

        def visit(index, carried):
            offset = pl.multiple_of(index * step, 16)
            total = loads[0](offset, step).astype(F32)
            for load in loads[1:]:
                total = total + load(offset, step).astype(F32)
            store(offset, step, total.astype(BF16))
            return carried

        if rows == step:
            visit(0, 0)
        else:
            lax.fori_loop(0, rows // step, visit, 0)

    def slab(self, ref, *index, first=0, start=None, width=None):
        def load(offset, rows):
            place = pl.ds(pl.multiple_of(first + offset, 16), rows)
            if width is None:
                return ref[(*index, place)]
            return ref[(*index, place, pl.ds(pl.multiple_of(start, LANES), width))]

        return load

    def stage_y(self, k):
        plan, y = self.plans[k], self.place.y
        for load in self.loads[k]:
            load.wait()
        plan["core0"].wait_recv()
        plan["core1"].wait_recv()

        def store(offset, rows, value):
            self.own[k, 1 - y, pl.ds(offset, rows)] = value

        loads = [self.slab(self.own, k, 1 - y), self.slab(self.got_core, k, 1 - y)]
        self.add_up(store, loads, CHUNK_ROWS)
        plan["y"].start()

    def terms_at(self, k, first, depth, inner=0, **part):
        y = self.place.y
        loads = [
            self.slab(self.own, k, y, first=first, **part),
            self.slab(self.got_core, k, y, first=first, **part),
            self.slab(self.got_y, k, first=first, **part),
        ]
        if depth > 0:
            loads.append(self.slab(self.got_x, k, first=inner, **part))
        if depth > 1:
            loads.append(self.slab(self.got_z, k, **part))
        return loads

    def stage_x(self, k):
        plan = self.plans[k]
        plan["y"].wait_recv()

        def store(offset, rows, value):
            self.to_x[k, pl.ds(offset, rows)] = value

        self.add_up(store, self.terms_at(k, (1 - self.place.x) * self.x_rows, 0), self.x_rows)
        plan["x"].start()

    def stage_z(self, k):
        plan = self.plans[k]
        plan["x"].wait_recv()
        inner = (1 - self.place.low) * self.z_rows

        def store(offset, rows, value):
            self.to_z[k] = value

        first = self.place.x * self.x_rows + inner
        self.add_up(store, self.terms_at(k, first, 1, inner), self.z_rows)
        plan["z"].start()

    def last_terms(self, k, start):
        inner = self.place.low * self.z_rows
        first = self.place.x * self.x_rows + inner
        return self.terms_at(k, first, 2, inner, start=start, width=self.zz_columns)

    def stage_zz(self, k):
        plan = self.plans[k]
        plan["z"].wait_recv()

        def store(offset, rows, value):
            self.to_zz[k] = value

        self.add_up(store, self.last_terms(k, (1 - self.place.high) * self.zz_columns), self.z_rows)
        plan["zz"].start()

    def stage_final(self, k):
        plan = self.plans[k]
        plan["zz"].wait_recv()

        def store(offset, rows, value):
            self.finals[k][...] = value

        terms = self.last_terms(k, self.place.high * self.zz_columns)
        self.add_up(store, terms + [self.slab(self.got_zz, k)], self.z_rows)
        plan["zz_back"].start()

    def stage_z_back(self, k):
        self.plans[k]["zz_back"].wait_recv()
        self.plans[k]["z_back"].start()

    def stage_x_back(self, k):
        self.plans[k]["z_back"].wait_recv()
        self.plans[k]["x_back"].start()

    def ticks(self):
        return len(self.plans) + len(self.stages) - 1

    def tick(self, tick):
        for lag, stage in enumerate(self.stages):
            if 0 <= tick - lag < len(self.plans):
                stage(tick - lag)

    def finish(self):
        for plan in self.plans:
            plan["x_back"].wait_recv()
            for name in REDUCE_STAGES:
                plan[name].wait_send()


def reduce_scratch(chunks, filled):
    rows, columns = CHUNK_ROWS, CHUNK_COLUMNS
    shapes = [
        (chunks, 2, rows, columns),
        (chunks, 2, rows, columns),
        (chunks, rows, columns),
        (chunks, rows // 2, columns),
        (chunks, rows // 2, columns),
        (chunks, rows // 4, columns),
        (chunks, rows // 4, columns),
        (chunks, rows // 4, columns // 2),
        (chunks, rows // 4, columns // 2),
        (filled, 2, rows, columns),
    ]
    return [pltpu.VMEM(shape, BF16) for shape in shapes]


REDUCE_SCRATCH = 10
CLOSING_INPUTS = 14


def closing_kernel(places, count, *refs):
    (
        q_ref,
        grad_ref,
        stats_ref,
        lse_ref,
        delta_ref,
        segs_ref,
        normal_ref,
        inverse_ref,
        gain_ref,
        middle_ref,
        left_ref,
        later_ref,
        terms_ref,
    ) = refs[: CLOSING_INPUTS - 1]
    kv_ref, weight_ref = refs[CLOSING_INPUTS - 1 : CLOSING_INPUTS + 1]
    partials = refs[CLOSING_INPUTS + 1 : CLOSING_INPUTS + 1 + count]
    refs = refs[CLOSING_INPUTS + 1 + count :]
    sums, vector_out, tokens_out = refs[: count + 1], refs[count + 1], refs[count + 2]
    refs = refs[count + 3 :]
    kv_all, q_all, grad_all, stats_all = refs[:4]
    biases, attention_sums = refs[4:6], refs[6:9]
    refs = refs[ATTENTION_SCRATCH:]
    buffers = refs[:REDUCE_SCRATCH]
    grads_ref, weight, turned, vector_got, tokens_own, send_sems, recv_sems, local_sems = refs[REDUCE_SCRATCH:]

    place = Place()
    greet_with_partner(
        place, (place.sibling, place.over_x, place.over_y, place.over_z, place.over_zz)
    )
    copies = Copies(send_sems, recv_sems)
    gather = BlockGather(
        place, copies, [q_ref, grad_ref, stats_ref], [q_all, grad_all, stats_all]
    )
    swap = copies.make(tokens_own, tokens_out, place.partner)
    reduce = GradientSum(
        place, copies, places, list(partials) + [None], sums, buffers, local_sems
    )
    chunks = len(places)
    filled = len(reduce.filled)
    early = chunks - filled
    vector_devices = (place.over_x, place.over_z, place.over_zz, place.sibling, place.over_y)
    vector_copies = [
        copies.make(vector_out, vector_got.at[i], device)
        for i, device in enumerate(vector_devices)
    ]
    load_kv = pltpu.make_async_copy(kv_ref, kv_all, local_sems.at[2 * chunks])
    load_weight = pltpu.make_async_copy(weight_ref, weight, local_sems.at[2 * chunks + 1])

    load_kv.start()
    gather.begin()
    for k in range(early):
        reduce.begin(k)
    load_weight.start()
    grads = AttentionGrads(
        place,
        q_ref,
        grad_ref,
        lse_ref,
        delta_ref,
        segs_ref,
        kv_all,
        q_all,
        grad_all,
        stats_all,
        biases,
        attention_sums,
    )
    grads.masks()
    turned[...] = left_ref[...].T
    load_kv.wait()
    grads.query_grads(0, 2)
    gather.first_halves()
    reduce.stage_y(0)
    grads.query_grads(2, PAIRS)
    gather.second_halves()
    for k in range(1, 4):
        reduce.stage_y(k)
    gather.wait_near()
    grads.near_keys()
    gather.corners()
    for k in range(4, early):
        reduce.stage_y(k)
    gather.wait_far()
    reduce.tick(0)
    grads.far_keys()
    grads.store(grads_ref)
    reduce.tick(1)

    own_grads = grads_ref[...]
    right = jnp.concatenate([later_ref[...], own_grads], axis=0)
    for index, (k, column) in enumerate(reduce.filled):
        columns = right[:, column : column + CHUNK_COLUMNS]

        def term(quarter):
            rows = turned[pl.ds(pl.multiple_of(quarter * CHUNK_ROWS, 16), CHUNK_ROWS), :]
            return jnp.dot(rows, columns, preferred_element_type=F32).astype(BF16)

        for i in range(2):
            reduce.to_core[index, i] = term(2 * i + 1 - place.core)
            reduce.own[k, i] = term(2 * i + place.core)
        reduce.begin(k)
    reduce.tick(2)
    load_weight.wait()
    grad_normed = dot_rows(own_grads, weight[...])
    grad_input, grad_gain, grad_bias = norm_backward(
        grad_normed, normal_ref[...], inverse_ref[...], gain_ref[...]
    )
    swapped = (middle_ref[...] + grad_input).astype(BF16)
    tokens_own[...] = swapped

    @pl.when(place.has_partner)
    def _():
        swap.start()

    @pl.when(jnp.logical_not(place.has_partner))
    def _():
        tokens_out[...] = swapped

    vector_out[...] = terms_ref[...]
    query_bias = jnp.sum(own_grads[:, :D].astype(F32), axis=0, keepdims=True)
    value_bias = jnp.sum(own_grads[:, 2 * D :].astype(F32), axis=0, keepdims=True)
    for row, value in ((0, grad_gain[None]), (1, grad_bias[None]), (6, query_bias), (7, value_bias)):
        vector_out[row : row + 1, :] = vector_out[row : row + 1, :] + value
    vector_copies[0].start()
    for k in range(early, chunks):
        reduce.stage_y(k)

    def vector_step(index):
        vector_copies[index].wait()
        vector_out[...] = vector_out[...] + vector_got[index]
        if index + 1 < VECTOR_AXES:
            vector_copies[index + 1].start()

    for tick in range(3, reduce.ticks()):
        reduce.tick(tick)
        if tick - 3 < VECTOR_AXES - 1:
            vector_step(tick - 3)
    vector_step(VECTOR_AXES - 1)
    reduce.finish()
    gather.finish()

    @pl.when(place.has_partner)
    def _():
        swap.wait_recv()
        swap.wait_send()


def closing(
    queries,
    grads,
    stats,
    lse,
    delta,
    segs,
    normal,
    inverse,
    gain,
    middle,
    left,
    later,
    terms,
    kv,
    weight,
    partials,
    collective_id,
):
    rows = queries.shape[0]
    count = len(partials)
    shapes = [term.shape[1:] for term in partials] + [(weight.shape[0] // 4, weight.shape[1])]
    places = chunk_places(shapes)
    chunks = len(places)
    filled = len(chunk_places(shapes[-1:]))
    slots = chunks * REDUCE_COPIES + VECTOR_AXES + 3 * BLOCK_COPIES + 1
    vmem = pl.BlockSpec(memory_space=pltpu.VMEM)
    anywhere = pl.BlockSpec(memory_space=pl.ANY)
    return pl.pallas_call(
        partial(closing_kernel, places, count),
        in_specs=[vmem] * (CLOSING_INPUTS - 1) + [anywhere] * (2 + count),
        out_specs=[vmem] * (count + 3),
        out_shape=[jax.ShapeDtypeStruct(shape, BF16) for shape in shapes]
        + [jax.ShapeDtypeStruct(terms.shape, F32), jax.ShapeDtypeStruct((rows, D), BF16)],
        scratch_shapes=attention_scratch(rows)
        + reduce_scratch(chunks, filled)
        + [
            pltpu.VMEM((rows, 3 * D), BF16),
            pltpu.VMEM(weight.shape, BF16),
            pltpu.VMEM(left.shape[::-1], BF16),
            pltpu.VMEM((VECTOR_AXES, *terms.shape), F32),
            pltpu.VMEM((rows, D), BF16),
            pltpu.SemaphoreType.DMA((slots,)),
            pltpu.SemaphoreType.DMA((slots,)),
            pltpu.SemaphoreType.DMA((2 * chunks + 2,)),
        ],
        compiler_params=pltpu.CompilerParams(
            collective_id=collective_id, has_side_effects=True, vmem_limit_bytes=60 << 20
        ),
        name="closing",
    )(
        queries,
        grads,
        stats,
        lse,
        delta,
        segs,
        normal,
        inverse,
        gain,
        middle,
        left,
        later,
        terms,
        kv,
        weight,
        *partials,
    )


class PlaneLinks:
    def leave(self, value):
        pairs = [(c * 4 + f, (2 * f + c % 2) * 4 + c // 2) for c in range(8) for f in range(4)]
        return lax.ppermute(value, ("ctx", "fsdp"), pairs)

    def open(self, tokens, segs_row, vectors, shares):
        tokens, segs, vectors, *results = opening(tokens, segs_row, vectors, shares[0], shares[1:], 0)
        return tokens.astype(F32), segs, vectors, as_matrices(results[9:]), results[:9]

    def attend(self, queries, kv_own, segs, cotangent):
        *results, cotangent = attend(queries, kv_own, segs, cotangent, 2)
        return results, cotangent

    def attend_back(self, queries, grads, stats, lse, delta, segs, kv, kv_own):
        return attend_back(queries, grads, stats, lse, delta, segs, kv, 3)

    def close(self, attention, norm, factors, later, vectors, weight):
        queries, grads, stats, lse, delta, segs, kv, _ = attention
        normal, inverse, gain, middle = norm
        terms = []
        for left, right in factors[:-1]:
            term = column_products(left, right).astype(BF16)
            terms.append(term.reshape(4, term.shape[0] // 4, term.shape[1]))
        *sums, vectors, tokens_grad = closing(
            queries,
            grads,
            stats,
            lse,
            delta,
            segs,
            normal,
            inverse,
            gain,
            middle,
            factors[-1],
            later,
            vectors,
            kv,
            weight,
            terms,
            4,
        )
        return [total.astype(F32) for total in sums], vectors, tokens_grad


class PlainLinks:
    def leave(self, value):
        return value

    def open(self, tokens, segs_row, vectors, shares):
        segs = (segs_row, lax.all_gather(segs_row, "ctx", axis=1, tiled=True))
        gathered = lax.all_gather(pack_vectors(*vectors), "fsdp", axis=0)
        vectors = assemble_vectors([gathered[i] for i in range(4)])
        weights = as_matrices([lax.all_gather(share, "fsdp", axis=0) for share in shares])
        resid = tokens.astype(F32)
        first = project_rows(resid, vectors, weights[0])
        first = first + self.attend(*first[3:], segs, None)[0]
        return resid, segs, vectors, weights, first

    def place(self, segs):
        own_segs, all_segs = segs
        rows = own_segs.shape[1]
        start = (lax.axis_index("ctx") * rows).reshape(1).astype(jnp.int32)
        return start, own_segs.reshape(rows, 1), all_segs

    def blocks(self, block):
        return lax.all_gather(block, "ctx", axis=0)

    def attend(self, queries, kv_own, segs, cotangent):
        start, own_segs, all_segs = self.place(segs)
        kv = self.blocks(kv_own).reshape(-1, 2 * D)
        return (*attention_forward(start, queries, kv, own_segs, all_segs), kv), cotangent

    def attend_back(self, queries, grads, stats, lse, delta, segs, kv, kv_own):
        start, own_segs, all_segs = self.place(segs)
        q_all = self.blocks(queries).reshape(-1, D)
        grad_all = self.blocks(grads).reshape(-1, D)
        return attention_backward(
            start,
            queries,
            grads,
            kv_own,
            lse,
            delta,
            kv,
            q_all,
            grad_all,
            self.blocks(stats),
            own_segs,
            all_segs,
        )

    def close(self, attention, norm, factors, later, vectors, weight):
        grad_projected = self.attend_back(*attention)
        grad_input, terms = input_gradient(grad_projected, weight, *norm)
        vectors = vectors + jnp.concatenate(
            [terms[:2], jnp.zeros((4, D), F32), terms[2:], jnp.zeros((8, D), F32)], axis=0
        )
        right = jnp.concatenate([later, grad_projected], axis=0)
        sums = []
        for left, right in factors[:-1] + [(factors[-1], right)]:
            term = column_products(left, right).astype(BF16)
            share = lax.psum_scatter(term, "fsdp", scatter_dimension=0, tiled=True)
            sums.append(lax.psum(share.astype(F32), "ctx"))
        return sums, lax.psum(vectors, ("ctx", "fsdp")), grad_input.astype(BF16)


def as_matrices(fulls):
    return tuple(full.reshape(-1, full.shape[-1]) for full in fulls)


def project_rows(resid, vectors, weight_qkv):
    bias = jnp.concatenate([vectors[6:7], jnp.zeros((1, D), F32), vectors[7:8]], axis=1)
    normed, normal, inverse = norm_forward(resid, vectors[0:1], vectors[1:2])
    projected = (jnp.dot(normed, weight_qkv, preferred_element_type=F32) + bias).astype(BF16)
    return normed, normal, inverse, projected[:, :D], projected[:, D:]


def layer_forward(resid, weights, vectors, first):
    gain_two, bias_two, bias_proj, bias_out = (vectors[i : i + 1] for i in range(2, 6))
    bias_fc = vectors[8:12].reshape(1, 4 * D)
    _, weight_proj, weight_fc, weight_out = weights
    normed_one, normal_one, inverse_one, queries, kv_own, attended, lse, lse_rows, kv = first
    middle = resid + jnp.dot(attended, weight_proj, preferred_element_type=F32) + bias_proj
    normed_two, normal_two, inverse_two = norm_forward(middle, gain_two, bias_two)
    hidden = jnp.dot(normed_two, weight_fc, preferred_element_type=F32) + bias_fc
    activated = jax.nn.gelu(hidden, approximate=True).astype(BF16)
    result_rows = middle + jnp.dot(activated, weight_out, preferred_element_type=F32) + bias_out
    saved = (
        normed_one,
        normal_one,
        inverse_one,
        queries,
        kv_own,
        kv,
        attended,
        lse,
        lse_rows,
        normed_two,
        normal_two,
        inverse_two,
        hidden,
        activated,
    )
    return result_rows, saved


def layer_backward(gradient, weights, vectors, saved, links, segs):
    weight_qkv, weight_proj, weight_fc, weight_out = weights
    gain_one, gain_two = vectors[0:1], vectors[2:3]
    (
        normed_one,
        normal_one,
        inverse_one,
        queries,
        kv_own,
        kv,
        attended,
        lse,
        lse_rows,
        normed_two,
        normal_two,
        inverse_two,
        hidden,
        activated,
    ) = saved
    total = lambda value: jnp.sum(value.astype(F32), axis=0)
    grad_branch = gradient.astype(BF16)
    grad_activated = dot_rows(grad_branch, weight_out)
    gelu_pull = jax.vjp(partial(jax.nn.gelu, approximate=True), hidden)[1]
    grad_hidden = gelu_pull(grad_activated)[0].astype(BF16)
    grad_normed_two = dot_rows(grad_hidden, weight_fc)
    grad_in_two, grad_gain_two, grad_bias_two = norm_backward(
        grad_normed_two, normal_two, inverse_two, gain_two
    )
    grad_middle = gradient + grad_in_two
    grad_proj = grad_middle.astype(BF16)
    grad_attended = dot_rows(grad_proj, weight_proj).astype(BF16)
    products = grad_attended.astype(F32) * attended.astype(F32)
    head_of = jnp.arange(D, dtype=jnp.int32) // HDIM
    by_lane = (head_of[:, None] == jnp.arange(LANES, dtype=jnp.int32)[None, :]).astype(F32)
    by_row = (jnp.arange(16, dtype=jnp.int32)[:, None] == head_of[None, :]).astype(F32)
    delta = jnp.dot(products, by_lane, precision=lax.Precision.HIGHEST, preferred_element_type=F32)
    delta_rows = lax.dot_general(
        by_row,
        products,
        (((1,), (1,)), ((), ())),
        precision=lax.Precision.HIGHEST,
        preferred_element_type=F32,
    )
    stats = jnp.concatenate([lse_rows, delta_rows], axis=0)
    attention = (queries, grad_attended, stats, lse, delta, segs, kv, kv_own)
    norm = (normal_one, inverse_one, gain_one, grad_middle)
    matrices = ((activated, grad_branch), (normed_two, grad_hidden), (attended, grad_proj))
    upper = jnp.stack([grad_gain_two, grad_bias_two, total(grad_proj), total(grad_branch)])
    lower = total(grad_hidden).reshape(4, D)
    return attention, norm, matrices, (upper, lower)


def input_gradient(grad_projected, weight_qkv, normal, inverse, gain, middle):
    total = lambda value: jnp.sum(value.astype(F32), axis=0)
    grad_normed = dot_rows(grad_projected, weight_qkv)
    grad_in, grad_gain, grad_bias = norm_backward(grad_normed, normal, inverse, gain)
    terms = [
        grad_gain,
        grad_bias,
        total(grad_projected[:, :D]),
        total(grad_projected[:, 2 * D :]),
    ]
    return middle + grad_in, jnp.stack(terms)


def body(
    links,
    tokens,
    segment_ids,
    ln1_gain,
    ln1_bias,
    attn_weight,
    attn_bias,
    proj_weight,
    proj_bias,
    ln2_gain,
    ln2_bias,
    fc_weight,
    fc_bias,
    out_weight,
    out_bias,
    out_cotangent,
):
    vectors = (
        ln1_gain,
        ln1_bias,
        ln2_gain,
        ln2_bias,
        proj_bias,
        out_bias,
        attn_bias,
        fc_bias,
    )
    shares = [attn_weight, proj_weight, fc_weight, out_weight]
    resid, segs, vectors, weights, first = links.open(tokens[0], segment_ids, vectors, shares)
    resid, saved = layer_forward(resid, weights, vectors, first)
    saved_layers = [saved]
    first = project_rows(resid, vectors, weights[0])
    attended, gradient = links.attend(*first[3:], segs, out_cotangent[0])
    resid, saved = layer_forward(resid, weights, vectors, first + tuple(attended))
    saved_layers.append(saved)
    output = links.leave(resid.astype(BF16))
    gradient = gradient.astype(F32)
    attention, norm, later, (upper, lower) = layer_backward(
        gradient, weights, vectors, saved_layers[1], links, segs
    )
    later_projected = links.attend_back(*attention)
    gradient, terms = input_gradient(later_projected, weights[0], *norm)
    attention, norm, first, (more_upper, more_lower) = layer_backward(
        gradient, weights, vectors, saved_layers[0], links, segs
    )
    both = lambda a, b: jnp.concatenate([a, b], axis=0)
    factors = [(both(a[0], b[0]), both(a[1], b[1])) for a, b in zip(later, first)]
    factors.append(both(saved_layers[1][0], saved_layers[0][0]))
    packed = jnp.concatenate(
        [terms[:2], upper + more_upper, terms[2:], lower + more_lower, jnp.zeros((4, D), F32)], axis=0
    )
    (out_grad, fc_grad, proj_grad, qkv_grad), summed, tokens_grad = links.close(
        attention, norm, factors, later_projected, packed, weights[0]
    )
    own = lax.axis_index("fsdp")
    pick = lambda value, axis: lax.dynamic_index_in_dim(value, own, axis, keepdims=False)
    small = pick(summed[:6].reshape(6, 4, -1), 1)
    bias_qv = pick(summed[6:8].reshape(4, -1), 0)
    bias_fc = pick(summed[8:12], 0)
    gain_one, bias_one, gain_two, bias_two, bias_proj, bias_out = (small[i] for i in range(6))
    return (
        output[None],
        tokens_grad[None],
        gain_one,
        bias_one,
        qkv_grad,
        bias_qv,
        proj_grad,
        bias_proj,
        gain_two,
        bias_two,
        fc_grad,
        bias_fc,
        out_grad,
        bias_out,
    )


def solution(mesh):
    links = PlaneLinks() if (mesh.shape["ctx"], mesh.shape["fsdp"]) == (8, 4) else PlainLinks()
    rows = P("fsdp", "ctx", None)
    vector, matrix = P("fsdp"), P("fsdp", None)
    in_specs = (
        rows,
        P("fsdp", "ctx"),
        vector,
        vector,
        matrix,
        vector,
        matrix,
        vector,
        vector,
        vector,
        matrix,
        vector,
        matrix,
        vector,
        rows,
    )
    out_specs = (
        rows,
        rows,
        vector,
        vector,
        matrix,
        vector,
        matrix,
        vector,
        vector,
        vector,
        matrix,
        vector,
        matrix,
        vector,
    )
    return jax.shard_map(
        partial(body, links), mesh=mesh, in_specs=in_specs, out_specs=out_specs, check_vma=False
    )
```

```python
from functools import partial

import jax
import jax.numpy as jnp
from jax import lax
from jax.experimental import pallas as pl
from jax.experimental.pallas import tpu as pltpu
from jax.sharding import PartitionSpec as P

D = 768
HEADS = 12
HDIM = 64
PAIRS = HEADS // 2
LANES = 128
EPSILON = 1e-05
NEGATIVE = -1e30
SCALE = HDIM ** (-0.5)
MESH = pl.DeviceIdType.MESH
F32 = jnp.float32
BF16 = jnp.bfloat16


def norm_forward(resid, gain_row, bias_row):
    average = jnp.mean(resid, axis=-1, keepdims=True)
    centred = resid - average
    variance = jnp.mean(centred * centred, axis=-1, keepdims=True)
    inverse = lax.rsqrt(variance + EPSILON)
    normal = centred * inverse
    return ((normal * gain_row + bias_row).astype(BF16), normal, inverse)


def norm_backward(grad_normed, normal, inverse, gain_row):
    scaled = grad_normed * gain_row
    mean_term = jnp.mean(scaled, axis=-1, keepdims=True)
    second = jnp.mean(scaled * normal, axis=-1, keepdims=True)
    grad_input = inverse * (scaled - mean_term - normal * second)
    return (grad_input, jnp.sum(grad_normed * normal, axis=0), jnp.sum(grad_normed, axis=0))


def two_heads(rows):
    lane = lax.broadcasted_iota(jnp.int32, rows.shape, 1)
    zero = jnp.zeros_like(rows)
    first = jnp.where(lane < HDIM, rows, zero)
    second = jnp.where(lane < HDIM, zero, rows)
    return jnp.concatenate([first, second], axis=0)


def one_pair(stacked):
    half = stacked.shape[0] // 2
    lane = lax.broadcasted_iota(jnp.int32, (half, LANES), 1)
    return jnp.where(lane < HDIM, stacked[:half], stacked[half:])


def dot_rows(left, right):
    return lax.dot_general(left, right, (((1,), (1,)), ((), ())), preferred_element_type=F32)


def column_products(left, right):
    return lax.dot_general(left, right, (((0,), (0,)), ((), ())), preferred_element_type=F32)


def pick_lanes(columns, pair):
    lane = lax.broadcasted_iota(jnp.int32, columns.shape, 1)
    first = jnp.sum(jnp.where(lane == 2 * pair, columns, 0.0), axis=1, keepdims=True)
    second = jnp.sum(jnp.where(lane == 2 * pair + 1, columns, 0.0), axis=1, keepdims=True)
    return jnp.concatenate([first, second], axis=0)


def mask_columns(bias_ref, own_segs, all_segs_ref, start, own_is_query):
    rows, columns = bias_ref.shape
    step = min(1024, columns)
    own_place = start + lax.broadcasted_iota(jnp.int32, (rows, step), 0)
    for offset in range(0, columns, step):
        place = offset + lax.broadcasted_iota(jnp.int32, (rows, step), 1)
        causal = (place <= own_place) if own_is_query else (own_place <= place)
        same = own_segs == all_segs_ref[:, offset : offset + step]
        bias_ref[:, offset : offset + step] = jnp.where(causal & same, 0.0, NEGATIVE)


def attention_forward_kernel(
    start_ref, q_ref, k_ref, v_ref, own_segs_ref, all_segs_ref, out_ref, lse_ref, lse_rows_ref, bias_ref
):
    pair = pl.program_id(0)
    rows, keys = bias_ref.shape

    @pl.when(pair == 0)
    def _():
        mask_columns(bias_ref, own_segs_ref[...], all_segs_ref, start_ref[0], True)
        lse_ref[...] = jnp.zeros_like(lse_ref)

    queries = two_heads(q_ref[...] * jnp.asarray(SCALE, BF16))
    step = min(1024, keys)

    def scores_of(offset):
        scores = dot_rows(queries, k_ref[pl.ds(offset, step), :])
        bias = bias_ref[:, pl.ds(offset, step)]
        return scores + jnp.concatenate([bias, bias], axis=0)

    if step == keys:
        scores = scores_of(0)
        top = jnp.max(scores, axis=1, keepdims=True)
        weights = jnp.exp(scores - top)
        total = jnp.sum(weights, axis=1, keepdims=True)
        mixed = jnp.dot(weights.astype(BF16), v_ref[...], preferred_element_type=F32)
    else:

        def visit(index, carried):
            top, total, mixed = carried
            offset = pl.multiple_of(index * step, step)
            scores = scores_of(offset)
            new_top = jnp.maximum(top, jnp.max(scores, axis=1, keepdims=True))
            weights = jnp.exp(scores - new_top)
            factor = jnp.exp(top - new_top)
            total = total * factor + jnp.sum(weights, axis=1, keepdims=True)
            more = jnp.dot(
                weights.astype(BF16), v_ref[pl.ds(offset, step), :], preferred_element_type=F32
            )
            return new_top, total, mixed * factor + more

        top, total, mixed = lax.fori_loop(
            0,
            (start_ref[0] + rows + step - 1) // step,
            visit,
            (
                jnp.full((2 * rows, 1), NEGATIVE, F32),
                jnp.zeros((2 * rows, 1), F32),
                jnp.zeros((2 * rows, LANES), F32),
            ),
        )
    out_ref[...] = one_pair(mixed / total).astype(BF16)
    lse = top + jnp.log(total)
    lane = lax.broadcasted_iota(jnp.int32, (rows, LANES), 1)
    kept = lse_ref[...]
    kept = jnp.where(lane == 2 * pair, lse[:rows], kept)
    kept = jnp.where(lane == 2 * pair + 1, lse[rows:], kept)
    lse_ref[...] = kept

    @pl.when(pair == PAIRS - 1)
    def _():
        lse_rows_ref[...] = kept.T[:16]


def attention_forward(start, queries, kv, own_segs, all_segs):
    rows = queries.shape[0]
    keys = kv.shape[0]
    whole = lambda shape: pl.BlockSpec(shape, lambda p: (0, 0))
    return pl.pallas_call(
        attention_forward_kernel,
        grid=(PAIRS,),
        in_specs=[
            pl.BlockSpec(memory_space=pltpu.SMEM),
            pl.BlockSpec((rows, LANES), lambda p: (0, p)),
            pl.BlockSpec((keys, LANES), lambda p: (0, p)),
            pl.BlockSpec((keys, LANES), lambda p: (0, PAIRS + p)),
            whole((rows, 1)),
            whole((1, keys)),
        ],
        out_specs=[
            pl.BlockSpec((rows, LANES), lambda p: (0, p)),
            whole((rows, LANES)),
            whole((16, rows)),
        ],
        out_shape=[
            jax.ShapeDtypeStruct((rows, D), BF16),
            jax.ShapeDtypeStruct((rows, LANES), F32),
            jax.ShapeDtypeStruct((16, rows), F32),
        ],
        scratch_shapes=[pltpu.VMEM((rows, keys), F32)],
        compiler_params=pltpu.CompilerParams(vmem_limit_bytes=60 << 20),
        cost_estimate=pl.CostEstimate(
            flops=8 * rows * keys * D, bytes_accessed=4 * keys * D, transcendentals=rows * keys * HEADS
        ),
        name="attention_forward",
    )(start, queries, kv, kv, own_segs, all_segs)


def attention_backward_kernel(
    start_ref,
    q_ref,
    grad_ref,
    k_own_ref,
    v_own_ref,
    lse_ref,
    delta_ref,
    k_ref,
    v_ref,
    q_all_ref,
    grad_all_ref,
    stats_ref,
    own_segs_ref,
    all_segs_ref,
    out_ref,
    query_bias_ref,
    key_bias_ref,
):
    pair = pl.program_id(0)
    rows, tokens = query_bias_ref.shape
    start = start_ref[0]

    @pl.when(pair == 0)
    def _():
        mask_columns(query_bias_ref, own_segs_ref[...], all_segs_ref, start, True)
        mask_columns(key_bias_ref, own_segs_ref[...], all_segs_ref, start, False)

    step = min(256, tokens)
    blocks = step // rows
    scale = jnp.asarray(SCALE, BF16)

    def doubled(bias):
        return jnp.concatenate([bias, bias], axis=0)

    queries = two_heads(q_ref[...] * scale)
    grads = two_heads(grad_ref[...])
    lse = pick_lanes(lse_ref[...], pair)
    delta = pick_lanes(delta_ref[...], pair)

    def visit_keys(index, grad_query):
        offset = pl.multiple_of(index * step, step)
        keys = k_ref[pl.ds(offset, step), :]
        values = v_ref[pl.ds(offset, step), :]
        bias = doubled(query_bias_ref[:, pl.ds(offset, step)])
        attention = jnp.exp(dot_rows(queries, keys) + bias - lse)
        grad_attention = dot_rows(grads, values)
        grad_scores = (attention * (grad_attention - delta)).astype(BF16)
        return grad_query + jnp.dot(grad_scores, keys, preferred_element_type=F32)

    zeros = jnp.zeros((2 * rows, LANES), F32)
    grad_query = lax.fori_loop(0, (start + rows + step - 1) // step, visit_keys, zeros)

    own_keys = two_heads(k_own_ref[...] * scale)
    own_values = two_heads(v_own_ref[...])

    def row_of(block, row):
        return jnp.broadcast_to(stats_ref[block, pl.ds(row, 1), :], (rows, rows))

    def stat_rows(index, row):
        first = [row_of(index * blocks + b, row + 2 * pair) for b in range(blocks)]
        second = [row_of(index * blocks + b, row + 2 * pair + 1) for b in range(blocks)]
        return jnp.concatenate(
            [jnp.concatenate(first, axis=1), jnp.concatenate(second, axis=1)], axis=0
        )

    def visit_queries(index, carried):
        grad_keys, grad_values = carried
        offset = pl.multiple_of(index * step, step)
        later = q_all_ref[pl.ds(offset, step), :]
        later_grads = grad_all_ref[pl.ds(offset, step), :]
        bias = doubled(key_bias_ref[:, pl.ds(offset, step)])
        attention = jnp.exp(dot_rows(own_keys, later) + bias - stat_rows(index, 0))
        grad_attention = dot_rows(own_values, later_grads)
        grad_scores = (attention * (grad_attention - stat_rows(index, 16))).astype(BF16)
        grad_keys = grad_keys + jnp.dot(grad_scores, later, preferred_element_type=F32)
        grad_values = grad_values + jnp.dot(
            attention.astype(BF16), later_grads, preferred_element_type=F32
        )
        return grad_keys, grad_values

    grad_keys, grad_values = lax.fori_loop(
        start // step, tokens // step, visit_queries, (zeros, zeros)
    )
    base = pl.multiple_of(pair * LANES, LANES)
    out_ref[:, pl.ds(base, LANES)] = (one_pair(grad_query) * SCALE).astype(BF16)
    out_ref[:, pl.ds(D + base, LANES)] = (one_pair(grad_keys) * SCALE).astype(BF16)
    out_ref[:, pl.ds(2 * D + base, LANES)] = one_pair(grad_values).astype(BF16)


def attention_backward(
    start, queries, grads, kv_own, lse, delta, kv, q_all, grad_all, stats, own_segs, all_segs
):
    rows = queries.shape[0]
    tokens = kv.shape[0]
    whole = lambda shape: pl.BlockSpec(shape, lambda p: (0,) * len(shape))
    own = pl.BlockSpec((rows, LANES), lambda p: (0, p))
    every = pl.BlockSpec((tokens, LANES), lambda p: (0, p))
    return pl.pallas_call(
        attention_backward_kernel,
        grid=(PAIRS,),
        in_specs=[
            pl.BlockSpec(memory_space=pltpu.SMEM),
            own,
            own,
            own,
            pl.BlockSpec((rows, LANES), lambda p: (0, PAIRS + p)),
            whole((rows, LANES)),
            whole((rows, LANES)),
            every,
            pl.BlockSpec((tokens, LANES), lambda p: (0, PAIRS + p)),
            every,
            every,
            whole(stats.shape),
            whole((rows, 1)),
            whole((1, tokens)),
        ],
        out_specs=whole((rows, 3 * D)),
        out_shape=jax.ShapeDtypeStruct((rows, 3 * D), BF16),
        scratch_shapes=[pltpu.VMEM((rows, tokens), F32), pltpu.VMEM((rows, tokens), F32)],
        compiler_params=pltpu.CompilerParams(vmem_limit_bytes=60 << 20),
        cost_estimate=pl.CostEstimate(
            flops=16 * rows * tokens * D,
            bytes_accessed=8 * tokens * D,
            transcendentals=rows * tokens * HEADS,
        ),
        name="attention_backward",
    )(
        start,
        queries,
        grads,
        kv_own,
        kv_own,
        lse,
        delta,
        kv,
        kv,
        q_all,
        grad_all,
        stats,
        own_segs,
        all_segs,
    )


def place_bits():
    ctx, fsdp = lax.axis_index("ctx"), lax.axis_index("fsdp")
    return lax.rem(ctx, 2), ctx // 2, fsdp // 2, lax.rem(fsdp, 2)


class Place:
    def __init__(self):
        self.x, self.z, self.y, self.core = x, z, y, core = place_bits()
        self.low, self.high = low, high = lax.rem(z, 2), z // 2
        self.fsdp = fsdp = 2 * y + core
        self.block = 2 * fsdp + x
        self.sibling = (2 * z + x, 2 * y + 1 - core)
        self.over_y = (2 * z + x, 2 * (1 - y) + core)
        self.over_x = (2 * z + 1 - x, fsdp)
        self.over_z = (2 * (z + 1 - 2 * low) + x, fsdp)
        self.over_zz = (2 * (z + 2 - 4 * high) + x, fsdp)
        self.partner = (2 * fsdp + x, z)
        self.has_partner = fsdp != z


class Copies:
    def __init__(self, send_sems, recv_sems):
        self.send_sems, self.recv_sems = send_sems, recv_sems
        self.used = 0

    def make(self, src, dst, device):
        slot = self.used
        self.used += 1
        return pltpu.make_async_remote_copy(
            src_ref=src,
            dst_ref=dst,
            send_sem=self.send_sems.at[slot],
            recv_sem=self.recv_sems.at[slot],
            device_id=device,
            device_id_type=MESH,
        )


def greet(devices):
    barrier = pltpu.get_barrier_semaphore()
    for device in devices:
        pl.semaphore_signal(barrier, inc=1, device_id=device, device_id_type=MESH)
    pl.semaphore_wait(barrier, len(devices))


WEIGHT_COPIES = 11


def weight_cuts(shape):
    rows, columns = shape
    if rows * columns <= 192 * 768:
        return [(0, columns)]
    return [(0, columns // 2), (columns // 2, columns // 2)]


class WeightGather:
    def __init__(self, place, copies, shares, fulls, stages, local_sems):
        x, low = place.x, place.low
        own, other = place.fsdp, 2 * (1 - place.y) + place.core
        self.plans = []
        self.locals = []
        for which, (share, full) in enumerate(zip(shares, fulls)):
            part = share.shape[0] // 4
            for first, width in weight_cuts(share.shape):
                columns = pl.ds(first, width)

                def piece(ref, x_bit, low_bit, part=part, columns=columns):
                    return ref.at[pl.ds((2 * low_bit + x_bit) * part, part), columns]

                def side(ref, x_bit, low_bit, index, part=part, first=first, width=width):
                    start = (2 * low_bit + x_bit) * part
                    if part % 32 == 0:
                        rows = pl.ds(start + index * (part // 2), part // 2)
                        return ref.at[rows, pl.ds(first, width)]
                    half = width // 2
                    return ref.at[pl.ds(start, part), pl.ds(first + index * half, half)]

                theirs = full.at[other]
                same = lambda view, device: copies.make(view, view, device)
                mine = piece(theirs, x, low)
                from_x, from_z = piece(theirs, 1 - x, low), piece(theirs, x, 1 - low)
                self.plans.append(
                    [
                        copies.make(piece(share, x, low), piece(full.at[own], x, low), place.over_y),
                        same(mine, place.over_x),
                        same(mine, place.over_z),
                        same(mine, place.sibling),
                        same(side(theirs, 1 - x, low, 0), place.over_z),
                        same(from_x, place.sibling),
                        same(side(theirs, x, 1 - low, 1), place.over_x),
                        same(from_z, place.sibling),
                        same(side(theirs, 1 - x, 1 - low, 0), place.sibling),
                        same(side(theirs, 1 - x, 1 - low, 1), place.sibling),
                        copies.make(share.at[:, columns], full.at[own, :, columns], place.sibling),
                    ]
                )
            sem = local_sems.at[which]
            self.locals.append(
                (
                    pltpu.make_async_copy(share, stages[which], sem),
                    pltpu.make_async_copy(stages[which], full.at[own], sem),
                )
            )

    def begin(self):
        for plan in self.plans:
            plan[0].start()
        for plan in self.plans:
            plan[10].start()
        for into, _ in self.locals:
            into.start()

    def keep_own(self):
        for into, out in self.locals:
            into.wait()
            out.start()

    def steps(self):
        count = len(self.plans)
        for step in range(count + 2):
            yield step

    def step(self, step):
        count = len(self.plans)
        if step < count:
            plan = self.plans[step]
            plan[0].wait_recv()
            plan[1].start()
            plan[2].start()
            plan[3].start()
        if 0 <= step - 1 < count:
            plan = self.plans[step - 1]
            plan[1].wait_recv()
            plan[4].start()
            plan[5].start()
            plan[2].wait_recv()
            plan[6].start()
            plan[7].start()
        if 0 <= step - 2 < count:
            plan = self.plans[step - 2]
            plan[4].wait_recv()
            plan[8].start()
            plan[6].wait_recv()
            plan[9].start()

    def finish(self):
        for plan in self.plans:
            for index in (3, 5, 7, 8, 9, 10):
                plan[index].wait_recv()
            for copy in plan:
                copy.wait_send()
        for _, out in self.locals:
            out.wait()


BLOCK_COPIES = 13


class BlockGather:
    def __init__(self, place, copies, blocks, fulls):
        self.own = place.block
        self.pairs = list(zip(blocks, fulls))
        self.plans = []
        for block, full in self.pairs:
            half = block.shape[0] // 2

            def part(ref, side, half=half):
                return ref.at[pl.ds(side * half, half), :]

            def slot_of(x_bit, y_bit, full=full):
                return full.at[4 * y_bit + 2 * place.core + x_bit]

            same = lambda view, device: copies.make(view, view, device)
            x, y = place.x, place.y
            mine, from_x = slot_of(x, y), slot_of(1 - x, y)
            from_y, from_both = slot_of(x, 1 - y), slot_of(1 - x, 1 - y)
            self.plans.append(
                [
                    copies.make(block, mine, place.sibling),
                    copies.make(part(block, 0), part(mine, 0), place.over_x),
                    copies.make(part(block, 1), part(mine, 1), place.over_y),
                    copies.make(part(block, 1), part(mine, 1), place.over_x),
                    copies.make(part(block, 0), part(mine, 0), place.over_y),
                    same(part(from_x, 0), place.over_y),
                    same(part(from_x, 0), place.sibling),
                    same(part(from_y, 1), place.over_x),
                    same(part(from_y, 1), place.sibling),
                    same(part(from_x, 1), place.sibling),
                    same(part(from_y, 0), place.sibling),
                    same(part(from_both, 0), place.sibling),
                    same(part(from_both, 1), place.sibling),
                ]
            )

    def begin(self):
        for index in (1, 2, 3, 4, 0):
            for plan in self.plans:
                plan[index].start()
        for block, full in self.pairs:
            full[self.own] = block[...]

    def relay(self, *pairs):
        for arrived, followers in pairs:
            for plan in self.plans:
                plan[arrived].wait_recv()
                for index in followers:
                    plan[index].start()

    def first_halves(self):
        self.relay((1, (5, 6)), (2, (7, 8)))

    def second_halves(self):
        self.relay((3, (9,)), (4, (10,)))

    def corners(self):
        self.relay((5, (11,)), (7, (12,)))

    def wait(self, *indices):
        for plan in self.plans:
            for index in indices:
                plan[index].wait_recv()

    def wait_near(self):
        self.wait(0, 6, 9)

    def wait_far(self):
        self.wait(8, 10, 11, 12)

    def finish(self):
        for plan in self.plans:
            for copy in plan:
                copy.wait_send()


VECTORS = 8


def pack_vectors(ln1_gain, ln1_bias, ln2_gain, ln2_bias, proj_bias, out_bias, attn_bias, fc_bias):
    rows = (ln1_gain, ln1_bias, ln2_gain, ln2_bias, proj_bias, out_bias, attn_bias, fc_bias)
    return jnp.stack([jnp.pad(row.astype(F32), (0, D - row.shape[0])) for row in rows])


def assemble_vectors(shares):
    quarter = D // 4
    small = jnp.concatenate([share[:6, :quarter] for share in shares], axis=1)
    query = jnp.concatenate([shares[0][6:7, : 2 * quarter], shares[1][6:7, : 2 * quarter]], axis=1)
    value = jnp.concatenate([shares[2][6:7, : 2 * quarter], shares[3][6:7, : 2 * quarter]], axis=1)
    hidden = [share[7:8] for share in shares]
    return jnp.concatenate([small, query, value, *hidden, jnp.zeros((4, D), F32)], axis=0)


def mask_block(own_segs, segs_ref, block, start, own_is_query):
    rows = own_segs.shape[0]
    own_place = start + lax.broadcasted_iota(jnp.int32, (rows, rows), 0)
    place = block * rows + lax.broadcasted_iota(jnp.int32, (rows, rows), 1)
    causal = (place <= own_place) if own_is_query else (own_place <= place)
    same = own_segs == segs_ref[block, 0:1, :]
    return jnp.where(causal & same, 0.0, NEGATIVE)


def own_columns(segs_ref, block):
    rows = segs_ref.shape[2]
    return jnp.broadcast_to(segs_ref[block, 0:1, :], (rows, rows)).T


class AttentionForward:
    def __init__(self, place, q_ref, segs_ref, kv_all, out_ref, lse_ref, lse_rows_ref, kv_out, scratch, sems):
        self.place = place
        self.q_ref, self.segs_ref, self.kv_all = q_ref, segs_ref, kv_all
        self.out_ref, self.lse_ref, self.lse_rows_ref = out_ref, lse_ref, lse_rows_ref
        self.near_bias, self.far_bias, self.top, self.total, self.mixed = scratch
        self.rows = q_ref.shape[0]
        self.near, self.far = 4 * place.y, 4 * (1 - place.y)
        self.saves = [
            pltpu.make_async_copy(kv_all.at[pl.ds(first, 4)], kv_out.at[pl.ds(first, 4)], sem)
            for first, sem in zip((self.near, self.far), sems)
        ]

    def masks(self, far):
        rows = self.rows
        start = self.place.block * rows
        own_segs = own_columns(self.segs_ref, self.place.block)
        first, bias = (self.far, self.far_bias) if far else (self.near, self.near_bias)
        for i in range(4):
            at = slice(i * rows, (i + 1) * rows)
            bias[:, at] = mask_block(own_segs, self.segs_ref, first + i, start, True)

    def lanes(self, pair, side=0):
        return pl.ds(pl.multiple_of(side * D + pair * LANES, LANES), LANES)

    def part(self, first, bias_ref, pair):
        rows = self.rows
        queries = two_heads(self.q_ref[:, self.lanes(pair)] * jnp.asarray(SCALE, BF16))
        keys = self.kv_all[pl.ds(first, 4), :, self.lanes(pair)].reshape(4 * rows, LANES)
        values = self.kv_all[pl.ds(first, 4), :, self.lanes(pair, 1)].reshape(4 * rows, LANES)
        bias = bias_ref[...]
        scores = dot_rows(queries, keys) + jnp.concatenate([bias, bias], axis=0)
        top = jnp.max(scores, axis=1, keepdims=True)
        shares = jnp.exp(scores - top)
        total = jnp.sum(shares, axis=1, keepdims=True)
        return top, total, jnp.dot(shares.astype(BF16), values, preferred_element_type=F32)

    def near_part(self):
        self.saves[0].start()
        self.lse_ref[...] = jnp.zeros_like(self.lse_ref)

        def visit(pair, carried):
            self.top[pair], self.total[pair], self.mixed[pair] = self.part(
                self.near, self.near_bias, pair
            )
            return carried

        lax.fori_loop(0, PAIRS, visit, 0)

    def far_part(self):
        self.saves[1].start()

        def visit(pair, carried):
            top, total, mixed = self.part(self.far, self.far_bias, pair)
            old_top = self.top[pair]
            new_top = jnp.maximum(top, old_top)
            new, old = jnp.exp(top - new_top), jnp.exp(old_top - new_top)
            self.top[pair] = new_top
            self.total[pair] = total * new + self.total[pair] * old
            self.mixed[pair] = mixed * new + self.mixed[pair] * old
            return carried

        @pl.when(self.place.y == 1)
        def _():
            lax.fori_loop(0, PAIRS, visit, 0)

    def store(self):
        rows = self.rows

        def visit(pair, carried):
            total = self.total[pair]
            self.out_ref[:, self.lanes(pair)] = one_pair(self.mixed[pair] / total).astype(BF16)
            lse = self.top[pair] + jnp.log(total)
            lane = lax.broadcasted_iota(jnp.int32, (rows, LANES), 1)
            kept = jnp.where(lane == 2 * pair, lse[:rows], self.lse_ref[...])
            self.lse_ref[...] = jnp.where(lane == 2 * pair + 1, lse[rows:], kept)
            return carried

        lax.fori_loop(0, PAIRS, visit, 0)
        self.lse_rows_ref[...] = self.lse_ref[...].T[:16]

    def finish(self):
        for save in self.saves:
            save.wait()


def forward_scratch(rows):
    return [
        pltpu.VMEM((8, rows, 2 * D), BF16),
        pltpu.VMEM((rows, 4 * rows), F32),
        pltpu.VMEM((rows, 4 * rows), F32),
        pltpu.VMEM((PAIRS, 2 * rows, 1), F32),
        pltpu.VMEM((PAIRS, 2 * rows, 1), F32),
        pltpu.VMEM((PAIRS, 2 * rows, LANES), F32),
    ]


FORWARD_SCRATCH = 6


def forward_shapes(rows):
    return [
        jax.ShapeDtypeStruct((rows, D), BF16),
        jax.ShapeDtypeStruct((rows, LANES), F32),
        jax.ShapeDtypeStruct((16, rows), F32),
        jax.ShapeDtypeStruct((8, rows, 2 * D), BF16),
    ]


def greet_with_partner(place, others):
    barrier = pltpu.get_barrier_semaphore()
    for device in others:
        pl.semaphore_signal(barrier, inc=1, device_id=device, device_id_type=MESH)

    @pl.when(place.has_partner)
    def _():
        pl.semaphore_signal(barrier, inc=1, device_id=place.partner, device_id_type=MESH)
        pl.semaphore_wait(barrier, len(others) + 1)

    @pl.when(jnp.logical_not(place.has_partner))
    def _():
        pl.semaphore_wait(barrier, len(others))


def attend_kernel(
    q_ref, kv_ref, segs_ref, cotangent_ref, out_ref, lse_ref, lse_rows_ref, kv_out, cotangent_out, *scratch
):
    kv_all, send_sems, recv_sems, local_sems = scratch[0], *scratch[FORWARD_SCRATCH:]
    place = Place()
    greet_with_partner(place, (place.sibling, place.over_x, place.over_y))
    copies = Copies(send_sems, recv_sems)
    gather = BlockGather(place, copies, [kv_ref], [kv_all])
    swap = copies.make(cotangent_ref, cotangent_out, place.partner)
    keep = pltpu.make_async_copy(cotangent_ref, cotangent_out, local_sems.at[2])
    gather.begin()

    @pl.when(place.has_partner)
    def _():
        swap.start()

    @pl.when(jnp.logical_not(place.has_partner))
    def _():
        keep.start()

    attention = AttentionForward(
        place,
        q_ref,
        segs_ref,
        kv_all,
        out_ref,
        lse_ref,
        lse_rows_ref,
        kv_out,
        scratch[1:FORWARD_SCRATCH],
        (local_sems.at[0], local_sems.at[1]),
    )
    attention.masks(False)
    attention.masks(True)
    gather.first_halves()
    gather.second_halves()
    gather.wait_near()
    attention.near_part()
    gather.corners()
    gather.wait_far()
    attention.far_part()
    attention.store()
    attention.finish()
    gather.finish()

    @pl.when(place.has_partner)
    def _():
        swap.wait()

    @pl.when(jnp.logical_not(place.has_partner))
    def _():
        keep.wait()


def attend(queries, kv_own, segs, cotangent, collective_id):
    rows = queries.shape[0]
    vmem = pl.BlockSpec(memory_space=pltpu.VMEM)
    anywhere = pl.BlockSpec(memory_space=pl.ANY)
    return pl.pallas_call(
        attend_kernel,
        in_specs=[vmem, vmem, vmem, anywhere],
        out_specs=[vmem, vmem, vmem, anywhere, vmem],
        out_shape=forward_shapes(rows) + [jax.ShapeDtypeStruct((rows, D), BF16)],
        scratch_shapes=forward_scratch(rows)
        + [
            pltpu.SemaphoreType.DMA((BLOCK_COPIES + 1,)),
            pltpu.SemaphoreType.DMA((BLOCK_COPIES + 1,)),
            pltpu.SemaphoreType.DMA((3,)),
        ],
        compiler_params=pltpu.CompilerParams(
            collective_id=collective_id, has_side_effects=True, vmem_limit_bytes=32 << 20
        ),
        name="attend",
    )(queries, kv_own, segs, cotangent)


class FirstWeightGather:
    def __init__(self, place, copies, share, full, columns, part, sem):
        x = place.x
        own, other = place.fsdp, 2 * (1 - place.y) + place.core
        half = share.shape[0] // 2
        self.steps = []
        for index in range(half // part):
            mine = pl.ds(pl.multiple_of(x * half + index * part, 16), part)
            theirs = pl.ds(pl.multiple_of((1 - x) * half + index * part, 16), part)
            got, from_x = full.at[other, mine, columns], full.at[other, theirs, columns]
            self.steps.append(
                [
                    copies.make(share.at[mine, columns], full.at[own, mine, columns], place.over_y),
                    copies.make(got, got, place.over_x),
                    copies.make(got, got, place.sibling),
                    copies.make(from_x, from_x, place.sibling),
                ]
            )
        whole = full.at[own, :, columns]
        self.to_sibling = copies.make(share.at[:, columns], whole, place.sibling)
        self.load = pltpu.make_async_copy(share.at[:, columns], whole, sem)

    def begin(self):
        for step in self.steps:
            step[0].start()
        self.to_sibling.start()
        self.load.start()

    def relay_y(self):
        for step in self.steps:
            step[0].wait_recv()
            step[1].start()
            step[2].start()

    def relay_x(self):
        for step in self.steps:
            step[1].wait_recv()
            step[3].start()

    def wait_near(self):
        self.load.wait()
        self.to_sibling.wait_recv()

    def wait_far(self):
        for step in self.steps:
            step[2].wait_recv()
            step[3].wait_recv()

    def finish(self):
        self.to_sibling.wait_send()
        for step in self.steps:
            for copy in step:
                copy.wait_send()


def opening_kernel(count, *refs):
    tokens_ref, segs_ref, first_ref = refs[:3]
    vector_refs = refs[3 : 3 + VECTORS]
    shares = refs[3 + VECTORS : 3 + VECTORS + count]
    refs = refs[3 + VECTORS + count :]
    (
        tokens_out,
        segs_out,
        vectors_out,
        normed_out,
        normal_out,
        inverse_out,
        q_out,
        kv_own_out,
        attended_out,
        lse_out,
        lse_rows_out,
        kv_out,
        first_out,
    ) = refs[:13]
    fulls = refs[13 : 13 + count]
    refs = refs[13 + count :]
    kv_all = refs[0]
    forward = refs[1:FORWARD_SCRATCH]
    vectors_own, vectors_all, segs_row, segs_sent, segs_own = refs[FORWARD_SCRATCH : FORWARD_SCRATCH + 5]
    refs = refs[FORWARD_SCRATCH + 5 :]
    first_full, projected, send_sems, recv_sems, local_sems = refs[:5]
    stages, vector_rows = refs[5 : 5 + count], refs[5 + count :]
    place = Place()
    own, other = place.fsdp, 2 * (1 - place.y) + place.core
    loads = [
        pltpu.make_async_copy(src, dst, local_sems.at[count + 6 + i])
        for i, (src, dst) in enumerate(zip((segs_ref, *vector_refs), (segs_row, *vector_rows)))
    ]
    for load in loads:
        load.start()
    for load in loads:
        load.wait()
    vectors_own[...] = jnp.zeros_like(vectors_own)
    for i, row in enumerate(vector_rows):
        size = row.shape[0]
        vectors_own[i : i + 1, :size] = row[...].astype(F32).reshape(1, size)
    segs_sent[...] = jnp.broadcast_to(segs_row[...], segs_sent.shape)
    greet_with_partner(place, (place.sibling, place.over_x, place.over_y, place.over_z))
    copies = Copies(send_sems, recv_sems)
    swap_tokens = copies.make(tokens_ref, tokens_out, place.partner)
    swap_segs = copies.make(segs_sent, segs_own, place.partner)
    vector_copies = [
        copies.make(vectors_own, vectors_all.at[own], place.over_y),
        copies.make(vectors_own, vectors_all.at[own], place.sibling),
        copies.make(vectors_all.at[other], vectors_all.at[other], place.sibling),
    ]
    keys = FirstWeightGather(
        place, copies, first_ref, first_full, pl.ds(D, 2 * D), 32, local_sems.at[count]
    )
    queries = FirstWeightGather(
        place, copies, first_ref, first_full, pl.ds(0, D), 48, local_sems.at[count + 5]
    )
    weights = WeightGather(place, copies, shares, fulls, stages, local_sems)
    gather = BlockGather(place, copies, [kv_own_out, segs_own], [kv_all, segs_out])
    save_first = pltpu.make_async_copy(first_full, first_out, local_sems.at[count + 1])
    attention = AttentionForward(
        place,
        q_out,
        segs_out,
        kv_all,
        attended_out,
        lse_out,
        lse_rows_out,
        kv_out,
        forward,
        (local_sems.at[count + 2], local_sems.at[count + 3]),
    )

    keep_tokens = pltpu.make_async_copy(tokens_ref, tokens_out, local_sems.at[count + 7 + VECTORS])
    vector_copies[0].start()
    vector_copies[1].start()

    @pl.when(place.has_partner)
    def _():
        swap_segs.start()

    keys.begin()

    @pl.when(place.has_partner)
    def _():
        swap_tokens.start()

    @pl.when(jnp.logical_not(place.has_partner))
    def _():
        keep_tokens.start()

    queries.begin()
    weights.begin()
    vectors_all[own] = vectors_own[...]

    @pl.when(jnp.logical_not(place.has_partner))
    def _():
        segs_own[...] = segs_sent[...]

    vector_copies[0].wait_recv()
    vector_copies[2].start()
    keys.relay_y()
    vector_copies[1].wait_recv()
    vector_copies[2].wait_recv()
    vectors_out[...] = assemble_vectors([vectors_all[i] for i in range(4)])

    @pl.when(place.has_partner)
    def _():
        swap_tokens.wait_recv()
        swap_segs.wait_recv()

    @pl.when(jnp.logical_not(place.has_partner))
    def _():
        keep_tokens.wait()

    normed, normal, inverse = norm_forward(
        tokens_out[...].astype(F32), vectors_out[0:1, :], vectors_out[1:2, :]
    )
    normed_out[...] = normed
    normal_out[...] = normal
    inverse_out[...] = inverse

    def half_product(y_bit, start, width):
        depth = D // 2
        rows = normed_out[:, pl.ds(pl.multiple_of(y_bit * depth, LANES), depth)]
        weight = first_full[pl.ds(2 * y_bit, 2), :, start : start + width].reshape(depth, width)
        return jnp.dot(rows, weight, preferred_element_type=F32)

    keys.wait_near()
    projected[...] = half_product(place.y, D, 2 * D)
    keys.relay_x()
    keys.wait_far()
    total = projected[...] + half_product(1 - place.y, D, 2 * D)
    kv_own_out[:, :D] = total[:, :D].astype(BF16)
    kv_own_out[:, D:] = (total[:, D:] + vectors_out[7:8, :]).astype(BF16)
    gather.begin()
    queries.relay_y()
    weights.step(0)
    weights.step(1)
    queries.relay_x()
    queries.wait_near()
    queries.wait_far()
    total = half_product(place.y, 0, D) + half_product(1 - place.y, 0, D)
    q_out[...] = (total + vectors_out[6:7, :]).astype(BF16)
    save_first.start()
    gather.first_halves()
    weights.keep_own()
    weights.step(2)
    gather.second_halves()
    gather.wait_near()
    attention.masks(False)
    weights.step(3)
    attention.near_part()
    gather.corners()
    weights.step(4)
    gather.wait_far()
    attention.masks(True)
    attention.far_part()
    weights.step(5)
    weights.step(6)
    attention.store()
    save_first.wait()
    attention.finish()
    keys.finish()
    queries.finish()
    gather.finish()
    for copy in vector_copies:
        copy.wait_send()

    @pl.when(place.has_partner)
    def _():
        swap_segs.wait_send()
        swap_tokens.wait_send()

    weights.finish()


def opening(tokens, segs_row, vectors, first, shares, collective_id):
    rows, columns = tokens.shape
    count = len(shares)
    slots = 2 + 3 + (3 + 2) * 4 + 2 + sum(len(weight_cuts(share.shape)) for share in shares) * WEIGHT_COPIES + 2 * BLOCK_COPIES
    vmem = pl.BlockSpec(memory_space=pltpu.VMEM)
    anywhere = pl.BlockSpec(memory_space=pl.ANY)
    shape = jax.ShapeDtypeStruct
    segs_shape = (16, segs_row.shape[1])
    return pl.pallas_call(
        partial(opening_kernel, count),
        in_specs=[anywhere] * (3 + VECTORS + count),
        out_specs=[vmem] * 11 + [anywhere] * (2 + count),
        out_shape=[
            shape((rows, columns), tokens.dtype),
            shape((8, *segs_shape), segs_row.dtype),
            shape((16, D), F32),
            shape((rows, D), BF16),
            shape((rows, D), F32),
            shape((rows, 1), F32),
            shape((rows, D), BF16),
            shape((rows, 2 * D), BF16),
        ]
        + forward_shapes(rows)
        + [shape((4, *share.shape), share.dtype) for share in [first, *shares]],
        scratch_shapes=forward_scratch(rows)
        + [
            pltpu.VMEM((8, D), F32),
            pltpu.VMEM((4, 8, D), F32),
            pltpu.VMEM(segs_row.shape, segs_row.dtype),
            pltpu.VMEM(segs_shape, segs_row.dtype),
            pltpu.VMEM(segs_shape, segs_row.dtype),
            pltpu.VMEM((4, *first.shape), first.dtype),
            pltpu.VMEM((rows, 2 * D), F32),
            pltpu.SemaphoreType.DMA((slots,)),
            pltpu.SemaphoreType.DMA((slots,)),
            pltpu.SemaphoreType.DMA((count + 8 + VECTORS,)),
        ]
        + [pltpu.VMEM(share.shape, share.dtype) for share in shares]
        + [pltpu.VMEM(vector.shape, vector.dtype) for vector in vectors],
        compiler_params=pltpu.CompilerParams(
            collective_id=collective_id, has_side_effects=True, vmem_limit_bytes=60 << 20
        ),
        name="opening",
    )(tokens, segs_row, first, *vectors, *shares)


class AttentionGrads:
    def __init__(self, place, q_ref, grad_ref, lse_ref, delta_ref, segs_ref, kv_all, q_all, grad_all, stats_all, biases, sums):
        self.place = place
        self.q_ref, self.grad_ref, self.lse_ref, self.delta_ref = q_ref, grad_ref, lse_ref, delta_ref
        self.segs_ref, self.kv_all, self.q_all, self.grad_all = segs_ref, kv_all, q_all, grad_all
        self.stats_all = stats_all
        self.query_bias, self.key_bias = biases
        self.query_sum, self.key_sum, self.value_sum = sums
        self.rows = q_ref.shape[0]

    def masks(self):
        rows, place = self.rows, self.place
        start = place.block * rows
        own_segs = own_columns(self.segs_ref, place.block)
        for i in range(8):
            at = slice(i * rows, (i + 1) * rows)
            self.query_bias[:, at] = mask_block(own_segs, self.segs_ref, i, start, True)
            self.key_bias[:, at] = mask_block(own_segs, self.segs_ref, i, start, False)

    def lanes(self, pair, side=0):
        return pl.ds(pl.multiple_of(side * D + pair * LANES, LANES), LANES)

    def two_blocks(self, ref, index, lanes):
        return ref[pl.ds(2 * index, 2), :, lanes].reshape(2 * self.rows, LANES)

    def bias(self, ref, index):
        step = 2 * self.rows
        bias = ref[:, pl.ds(pl.multiple_of(index * step, step), step)]
        return jnp.concatenate([bias, bias], axis=0)

    def query_grads(self, first_pair, last_pair):
        scale = jnp.asarray(SCALE, BF16)
        count = self.place.block // 2 + 1

        def visit_pair(pair, carried):
            lanes = self.lanes(pair)
            queries = two_heads(self.q_ref[:, lanes] * scale)
            grads = two_heads(self.grad_ref[:, lanes])
            lse = pick_lanes(self.lse_ref[...], pair)
            delta = pick_lanes(self.delta_ref[...], pair)

            def visit(index, total):
                keys = self.two_blocks(self.kv_all, index, lanes)
                values = self.two_blocks(self.kv_all, index, self.lanes(pair, 1))
                scores = dot_rows(queries, keys) + self.bias(self.query_bias, index)
                attention = jnp.exp(scores - lse)
                grad_attention = dot_rows(grads, values)
                grad_scores = (attention * (grad_attention - delta)).astype(BF16)
                return total + jnp.dot(grad_scores, keys, preferred_element_type=F32)

            zeros = jnp.zeros((2 * self.rows, LANES), F32)
            self.query_sum[pair] = lax.fori_loop(0, count, visit, zeros)
            return carried

        lax.fori_loop(first_pair, last_pair, visit_pair, 0)

    def key_grads(self, first, last, fresh):
        rows = self.rows
        scale = jnp.asarray(SCALE, BF16)
        own = self.place.block

        def visit_pair(pair, carried):
            lanes = self.lanes(pair)
            own_keys = two_heads(self.kv_all[own, :, lanes] * scale)
            own_values = two_heads(self.kv_all[own, :, self.lanes(pair, 1)])

            def stat_rows(index, row):
                def spread(block, head):
                    line = self.stats_all[2 * index + block, pl.ds(row + 2 * pair + head, 1), :]
                    return jnp.broadcast_to(line, (rows, rows))

                heads = [
                    jnp.concatenate([spread(0, head), spread(1, head)], axis=1) for head in range(2)
                ]
                return jnp.concatenate(heads, axis=0)

            def visit(index, totals):
                key_total, value_total = totals
                later = self.two_blocks(self.q_all, index, lanes)
                later_grads = self.two_blocks(self.grad_all, index, lanes)
                scores = dot_rows(own_keys, later) + self.bias(self.key_bias, index)
                attention = jnp.exp(scores - stat_rows(index, 0))
                grad_attention = dot_rows(own_values, later_grads)
                grad_scores = attention * (grad_attention - stat_rows(index, 16))
                key_total = key_total + jnp.dot(
                    grad_scores.astype(BF16), later, preferred_element_type=F32
                )
                value_total = value_total + jnp.dot(
                    attention.astype(BF16), later_grads, preferred_element_type=F32
                )
                return key_total, value_total

            if fresh:
                zeros = jnp.zeros((2 * rows, LANES), F32)
                totals = (zeros, zeros)
            else:
                totals = (self.key_sum[pair], self.value_sum[pair])
            self.key_sum[pair], self.value_sum[pair] = lax.fori_loop(first, last, visit, totals)
            return carried

        lax.fori_loop(0, PAIRS, visit_pair, 0)

    def near_keys(self):
        self.key_grads(self.place.block // 2, 2 * self.place.y + 2, True)

    def far_keys(self):
        @pl.when(self.place.y == 0)
        def _():
            self.key_grads(2, 4, False)

    def store(self, out_ref):
        def visit(pair, carried):
            out_ref[:, self.lanes(pair)] = (one_pair(self.query_sum[pair]) * SCALE).astype(BF16)
            out_ref[:, self.lanes(pair, 1)] = (one_pair(self.key_sum[pair]) * SCALE).astype(BF16)
            out_ref[:, self.lanes(pair, 2)] = one_pair(self.value_sum[pair]).astype(BF16)
            return carried

        lax.fori_loop(0, PAIRS, visit, 0)


def attention_scratch(rows):
    return [
        pltpu.VMEM((8, rows, 2 * D), BF16),
        pltpu.VMEM((8, rows, D), BF16),
        pltpu.VMEM((8, rows, D), BF16),
        pltpu.VMEM((8, 32, rows), F32),
        pltpu.VMEM((rows, 8 * rows), F32),
        pltpu.VMEM((rows, 8 * rows), F32),
        pltpu.VMEM((PAIRS, 2 * rows, LANES), F32),
        pltpu.VMEM((PAIRS, 2 * rows, LANES), F32),
        pltpu.VMEM((PAIRS, 2 * rows, LANES), F32),
    ]


ATTENTION_SCRATCH = 9


def attend_back_kernel(
    q_ref,
    grad_ref,
    stats_ref,
    lse_ref,
    delta_ref,
    segs_ref,
    next_q_ref,
    kv_ref,
    out_ref,
    next_q_out,
    *scratch,
):
    kv_all, q_all, grad_all, stats_all = scratch[:4]
    biases, sums = scratch[4:6], scratch[6:9]
    next_q_all, send_sems, recv_sems, local_sems = scratch[ATTENTION_SCRATCH:]
    place = Place()
    greet((place.sibling, place.over_x, place.over_y))
    copies = Copies(send_sems, recv_sems)
    gather = BlockGather(
        place, copies, [q_ref, grad_ref, stats_ref], [q_all, grad_all, stats_all]
    )
    ahead = BlockGather(place, copies, [next_q_ref], [next_q_all])
    load = pltpu.make_async_copy(kv_ref, kv_all, local_sems.at[0])
    save = pltpu.make_async_copy(next_q_all, next_q_out, local_sems.at[1])
    load.start()
    gather.begin()
    grads = AttentionGrads(
        place, q_ref, grad_ref, lse_ref, delta_ref, segs_ref, kv_all, q_all, grad_all, stats_all, biases, sums
    )
    grads.masks()
    load.wait()
    grads.query_grads(0, 2)
    gather.first_halves()
    ahead.begin()
    grads.query_grads(2, PAIRS)
    gather.second_halves()
    gather.wait_near()
    grads.near_keys()
    gather.corners()
    gather.wait_far()
    ahead.first_halves()
    grads.far_keys()
    ahead.second_halves()
    ahead.corners()
    grads.store(out_ref)
    ahead.wait_near()
    ahead.wait_far()
    save.start()
    gather.finish()
    ahead.finish()
    save.wait()


def attend_back(queries, grads, stats, lse, delta, segs, next_queries, kv, collective_id):
    rows = queries.shape[0]
    slots = 4 * BLOCK_COPIES
    vmem = pl.BlockSpec(memory_space=pltpu.VMEM)
    anywhere = pl.BlockSpec(memory_space=pl.ANY)
    return pl.pallas_call(
        attend_back_kernel,
        in_specs=[vmem] * 7 + [anywhere],
        out_specs=[vmem, anywhere],
        out_shape=[
            jax.ShapeDtypeStruct((rows, 3 * D), BF16),
            jax.ShapeDtypeStruct((8, rows, D), BF16),
        ],
        scratch_shapes=attention_scratch(rows)
        + [
            pltpu.VMEM((8, rows, D), BF16),
            pltpu.SemaphoreType.DMA((slots,)),
            pltpu.SemaphoreType.DMA((slots,)),
            pltpu.SemaphoreType.DMA((2,)),
        ],
        compiler_params=pltpu.CompilerParams(
            collective_id=collective_id, has_side_effects=True, vmem_limit_bytes=32 << 20
        ),
        name="attend_back",
    )(queries, grads, stats, lse, delta, segs, next_queries, kv)


CHUNK_ROWS, CHUNK_COLUMNS = 192, 768
REDUCE_COPIES = 9
VECTOR_AXES = 5


def chunk_places(shapes):
    places = [
        (which, row, column, CHUNK_COLUMNS)
        for which, (rows, columns) in enumerate(shapes)
        for row in range(0, rows, CHUNK_ROWS)
        for column in range(0, columns, CHUNK_COLUMNS)
    ]
    which, row, column, width = places.pop()
    cut = 2 * width // 3
    return places + [(which, row, column, cut), (which, row, column + cut, width - cut)]


CORE_SLOTS = 4
REDUCE_STAGES = ("core0", "core1", "y", "x", "z", "zz", "zz_back", "z_back", "x_back")


class GradientSum:
    def __init__(self, place, copies, places, sums, buffers):
        self.place = place
        (
            self.own,
            self.got_core,
            self.got_y,
            self.to_x,
            self.got_x,
            self.to_z,
            self.got_z,
            self.to_zz,
            self.got_zz,
            self.to_core,
        ) = buffers
        self.places = places
        self.x_rows, self.z_rows = CHUNK_ROWS // 2, CHUNK_ROWS // 4
        x, y, low, high = place.x, place.y, place.low, place.high
        self.plans = []
        self.finals = []
        for k, (which, row, column, width) in enumerate(places):
            out = sums[which]
            half = width // 2

            def piece(first, rows, start, columns, out=out, row=row, column=column):
                return out.at[
                    pl.ds(pl.multiple_of(row + first, 16), rows),
                    pl.ds(pl.multiple_of(column + start, LANES), columns),
                ]

            def wide_part(ref, *index, columns=width):
                return ref.at[(*index, slice(None), pl.ds(0, columns))]

            final = piece(x * self.x_rows + low * self.z_rows, self.z_rows, high * half, half)
            wide = piece(x * self.x_rows + low * self.z_rows, self.z_rows, 0, width)
            tall = piece(x * self.x_rows, self.x_rows, 0, width)
            slot = k % CORE_SLOTS
            moves = (
                (wide_part(self.to_core, slot, 0), wide_part(self.got_core, k, 0), place.sibling),
                (wide_part(self.to_core, slot, 1), wide_part(self.got_core, k, 1), place.sibling),
                (wide_part(self.own, k, 1 - y), wide_part(self.got_y, k), place.over_y),
                (wide_part(self.to_x, k), wide_part(self.got_x, k), place.over_x),
                (wide_part(self.to_z, k), wide_part(self.got_z, k), place.over_z),
                (
                    wide_part(self.to_zz, k, columns=half),
                    wide_part(self.got_zz, k, columns=half),
                    place.over_zz,
                ),
                (final, final, place.over_zz),
                (wide, wide, place.over_z),
                (tall, tall, place.over_x),
            )
            self.plans.append(
                {name: copies.make(*move) for name, move in zip(REDUCE_STAGES, moves)}
            )
            self.finals.append(final)
        self.stages = (
            self.stage_x,
            self.stage_z,
            self.stage_zz,
            self.stage_final,
            self.stage_z_back,
            self.stage_x_back,
        )

    def make(self, which, left, right):
        core = self.place.core
        for k, (owner, row, column, width) in enumerate(self.places):
            if owner != which:
                continue
            quarter_rows = left.shape[0] // 4

            def term(quarter):
                first = pl.multiple_of(quarter * quarter_rows + row, 16)
                rows = left[pl.ds(first, CHUNK_ROWS), :]
                columns = right[:, column : column + width]
                return jnp.dot(rows, columns, preferred_element_type=F32).astype(BF16)

            if k >= CORE_SLOTS:
                for name in ("core0", "core1"):
                    self.plans[k - CORE_SLOTS][name].wait_send()
            for i in range(2):
                self.to_core[k % CORE_SLOTS, i, :, :width] = term(2 * i + 1 - core)
            self.plans[k]["core0"].start()
            self.plans[k]["core1"].start()
            for i in range(2):
                self.own[k, i, :, :width] = term(2 * i + core)

    def add_up(self, store, loads, rows):
        step = self.z_rows

        def visit(index, carried):
            offset = pl.multiple_of(index * step, 16)
            total = loads[0](offset, step).astype(F32)
            for load in loads[1:]:
                total = total + load(offset, step).astype(F32)
            store(offset, step, total.astype(BF16))
            return carried

        if rows == step:
            visit(0, 0)
        else:
            lax.fori_loop(0, rows // step, visit, 0)

    def slab(self, ref, *index, first=0, start=0, width=None):
        def load(offset, rows):
            place = pl.ds(pl.multiple_of(first + offset, 16), rows)
            return ref[(*index, place, pl.ds(pl.multiple_of(start, LANES), width))]

        return load

    def stage_y(self, k):
        plan, y, width = self.plans[k], self.place.y, self.places[k][3]
        plan["core0"].wait_recv()
        plan["core1"].wait_recv()

        def store(offset, rows, value):
            self.own[k, 1 - y, pl.ds(offset, rows), :width] = value

        loads = [
            self.slab(self.own, k, 1 - y, width=width),
            self.slab(self.got_core, k, 1 - y, width=width),
        ]
        self.add_up(store, loads, CHUNK_ROWS)
        plan["y"].start()

    def terms_at(self, k, first, depth, inner=0, start=0, width=None):
        y = self.place.y
        part = {"start": start, "width": self.places[k][3] if width is None else width}
        loads = [
            self.slab(self.own, k, y, first=first, **part),
            self.slab(self.got_core, k, y, first=first, **part),
            self.slab(self.got_y, k, first=first, **part),
        ]
        if depth > 0:
            loads.append(self.slab(self.got_x, k, first=inner, **part))
        if depth > 1:
            loads.append(self.slab(self.got_z, k, **part))
        return loads

    def stage_x(self, k):
        plan, width = self.plans[k], self.places[k][3]
        plan["y"].wait_recv()

        def store(offset, rows, value):
            self.to_x[k, pl.ds(offset, rows), :width] = value

        self.add_up(store, self.terms_at(k, (1 - self.place.x) * self.x_rows, 0), self.x_rows)
        plan["x"].start()

    def stage_z(self, k):
        plan, width = self.plans[k], self.places[k][3]
        plan["x"].wait_recv()
        inner = (1 - self.place.low) * self.z_rows

        def store(offset, rows, value):
            self.to_z[k, :, :width] = value

        first = self.place.x * self.x_rows + inner
        self.add_up(store, self.terms_at(k, first, 1, inner), self.z_rows)
        plan["z"].start()

    def last_terms(self, k, side):
        inner = self.place.low * self.z_rows
        first = self.place.x * self.x_rows + inner
        half = self.places[k][3] // 2
        return self.terms_at(k, first, 2, inner, side * half, half)

    def stage_zz(self, k):
        plan, half = self.plans[k], self.places[k][3] // 2
        plan["z"].wait_recv()

        def store(offset, rows, value):
            self.to_zz[k, :, :half] = value

        self.add_up(store, self.last_terms(k, 1 - self.place.high), self.z_rows)
        plan["zz"].start()

    def stage_final(self, k):
        plan, half = self.plans[k], self.places[k][3] // 2
        plan["zz"].wait_recv()

        def store(offset, rows, value):
            self.finals[k][...] = value

        terms = self.last_terms(k, self.place.high)
        self.add_up(store, terms + [self.slab(self.got_zz, k, width=half)], self.z_rows)
        plan["zz_back"].start()

    def stage_z_back(self, k):
        self.plans[k]["zz_back"].wait_recv()
        self.plans[k]["z_back"].start()

    def stage_x_back(self, k):
        self.plans[k]["z_back"].wait_recv()
        self.plans[k]["x_back"].start()

    def ticks(self):
        return len(self.plans) + len(self.stages) - 1

    def tick(self, tick):
        for lag, stage in enumerate(self.stages):
            if 0 <= tick - lag < len(self.plans):
                stage(tick - lag)

    def finish(self):
        for k, plan in enumerate(self.plans):
            plan["x_back"].wait_recv()
            waited = k + CORE_SLOTS < len(self.plans)
            for name in REDUCE_STAGES[2:] if waited else REDUCE_STAGES:
                plan[name].wait_send()


def reduce_scratch(chunks):
    rows, columns = CHUNK_ROWS, CHUNK_COLUMNS
    shapes = [
        (chunks, 2, rows, columns),
        (chunks, 2, rows, columns),
        (chunks, rows, columns),
        (chunks, rows // 2, columns),
        (chunks, rows // 2, columns),
        (chunks, rows // 4, columns),
        (chunks, rows // 4, columns),
        (chunks, rows // 4, columns // 2),
        (chunks, rows // 4, columns // 2),
        (CORE_SLOTS, 2, rows, columns),
    ]
    return [pltpu.VMEM(shape, BF16) for shape in shapes]


REDUCE_SCRATCH = 10
CLOSING_INPUTS = 10


def closing_kernel(places, count, *refs):
    (
        grad_ref,
        stats_ref,
        lse_ref,
        delta_ref,
        segs_ref,
        normal_ref,
        inverse_ref,
        gain_ref,
        middle_ref,
        terms_ref,
    ) = refs[:CLOSING_INPUTS]
    refs = refs[CLOSING_INPUTS:]
    factors = refs[: 4 * count - 1]
    q_ref, q_saved, kv_ref, weight_ref = refs[4 * count - 1 : 4 * count + 3]
    refs = refs[4 * count + 3 :]
    sums, vector_out, tokens_out = refs[:count], refs[count], refs[count + 1]
    refs = refs[count + 2 :]
    kv_all, q_all, grad_all, stats_all = refs[:4]
    biases, attention_sums = refs[4:6], refs[6:9]
    refs = refs[ATTENTION_SCRATCH:]
    buffers = refs[:REDUCE_SCRATCH]
    (
        grads_ref,
        weight,
        left,
        right,
        vector_got,
        tokens_own,
        send_sems,
        recv_sems,
        local_sems,
    ) = refs[REDUCE_SCRATCH:]

    place = Place()
    load_kv = pltpu.make_async_copy(kv_ref, kv_all, local_sems.at[0])
    load_weight = pltpu.make_async_copy(weight_ref, weight, local_sems.at[1])
    load_q = pltpu.make_async_copy(q_saved, q_all, local_sems.at[2])
    load_kv.start()
    load_q.start()
    load_weight.start()
    greet_with_partner(
        place, (place.sibling, place.over_x, place.over_y, place.over_z, place.over_zz)
    )
    copies = Copies(send_sems, recv_sems)
    gather = BlockGather(place, copies, [grad_ref, stats_ref], [grad_all, stats_all])
    swap = copies.make(tokens_own, tokens_out, place.partner)
    reduce = GradientSum(place, copies, places, sums, buffers)
    chunks = len(places)
    by_weight = [[k for k in range(chunks) if places[k][0] == which] for which in range(count)]
    vector_devices = (place.over_x, place.over_z, place.over_zz, place.sibling, place.over_y)
    vector_copies = [
        copies.make(vector_out, vector_got.at[i], device)
        for i, device in enumerate(vector_devices)
    ]
    tokens = grad_ref.shape[0]

    def make_terms(which, last_right=None):
        later_left, later_right, first_left = factors[4 * which : 4 * which + 3]
        rows, columns = later_left.shape[1], later_right.shape[1]
        left[:rows, :tokens] = later_left[...].T
        left[:rows, tokens:] = first_left[...].T
        right[:tokens, :columns] = later_right[...]
        if last_right is None:
            right[tokens:, :columns] = factors[4 * which + 3][...]
        else:
            right[tokens:, :columns] = last_right
        reduce.make(which, left.at[pl.ds(0, rows), :], right)

    gather.begin()
    make_terms(0)
    grads = AttentionGrads(
        place,
        q_ref,
        grad_ref,
        lse_ref,
        delta_ref,
        segs_ref,
        kv_all,
        q_all,
        grad_all,
        stats_all,
        biases,
        attention_sums,
    )
    gather.first_halves()
    for k in by_weight[0]:
        reduce.stage_y(k)
    gather.second_halves()
    grads.masks()
    load_kv.wait()
    grads.query_grads(0, PAIRS)
    gather.corners()
    load_q.wait()
    gather.wait_near()
    make_terms(1)
    for k in by_weight[1]:
        reduce.stage_y(k)
    reduce.tick(0)
    grads.near_keys()
    gather.wait_far()
    reduce.tick(1)
    grads.far_keys()
    grads.store(grads_ref)
    reduce.tick(2)
    make_terms(2)
    for k in by_weight[2]:
        reduce.stage_y(k)
    own_grads = grads_ref[...]
    make_terms(3, own_grads)
    reduce.tick(3)
    load_weight.wait()
    grad_normed = dot_rows(own_grads, weight[...])
    grad_input, grad_gain, grad_bias = norm_backward(
        grad_normed, normal_ref[...], inverse_ref[...], gain_ref[...]
    )
    swapped = (middle_ref[...] + grad_input).astype(BF16)
    tokens_own[...] = swapped

    @pl.when(place.has_partner)
    def _():
        swap.start()

    @pl.when(jnp.logical_not(place.has_partner))
    def _():
        tokens_out[...] = swapped

    vector_out[...] = terms_ref[...]
    query_bias = jnp.sum(own_grads[:, :D].astype(F32), axis=0, keepdims=True)
    value_bias = jnp.sum(own_grads[:, 2 * D :].astype(F32), axis=0, keepdims=True)
    for row, value in ((0, grad_gain[None]), (1, grad_bias[None]), (6, query_bias), (7, value_bias)):
        vector_out[row : row + 1, :] = vector_out[row : row + 1, :] + value
    vector_copies[0].start()
    for k in by_weight[3]:
        reduce.stage_y(k)

    def vector_step(index):
        vector_copies[index].wait()
        vector_out[...] = vector_out[...] + vector_got[index]
        if index + 1 < VECTOR_AXES:
            vector_copies[index + 1].start()

    for tick in range(4, reduce.ticks()):
        reduce.tick(tick)
        if tick - 4 < VECTOR_AXES - 1:
            vector_step(tick - 4)
    vector_step(VECTOR_AXES - 1)
    reduce.finish()
    gather.finish()

    @pl.when(place.has_partner)
    def _():
        swap.wait_recv()
        swap.wait_send()


def closing(attention, queries_saved, norm, terms, factors, weight, collective_id):
    queries, grads, stats, lse, delta, segs, kv, _ = attention
    rows = queries.shape[0]
    count = len(factors)
    shapes = [(group[0].shape[1] // 4, group[1].shape[1]) for group in factors]
    places = chunk_places(shapes)
    chunks = len(places)
    slots = chunks * REDUCE_COPIES + VECTOR_AXES + 2 * BLOCK_COPIES + 1
    flat = [factor for group in factors for factor in group]
    tallest = max(group[0].shape[1] for group in factors)
    widest = max(group[1].shape[1] for group in factors)
    vmem = pl.BlockSpec(memory_space=pltpu.VMEM)
    anywhere = pl.BlockSpec(memory_space=pl.ANY)
    return pl.pallas_call(
        partial(closing_kernel, places, count),
        in_specs=[vmem] * (CLOSING_INPUTS + len(flat) + 1) + [anywhere] * 3,
        out_specs=[vmem] * (count + 2),
        out_shape=[jax.ShapeDtypeStruct(shape, BF16) for shape in shapes]
        + [jax.ShapeDtypeStruct(terms.shape, F32), jax.ShapeDtypeStruct((rows, D), BF16)],
        scratch_shapes=attention_scratch(rows)
        + reduce_scratch(chunks)
        + [
            pltpu.VMEM((rows, 3 * D), BF16),
            pltpu.VMEM(weight.shape, BF16),
            pltpu.VMEM((tallest, 2 * rows), BF16),
            pltpu.VMEM((2 * rows, widest), BF16),
            pltpu.VMEM((VECTOR_AXES, *terms.shape), F32),
            pltpu.VMEM((rows, D), BF16),
            pltpu.SemaphoreType.DMA((slots,)),
            pltpu.SemaphoreType.DMA((slots,)),
            pltpu.SemaphoreType.DMA((3,)),
        ],
        compiler_params=pltpu.CompilerParams(
            collective_id=collective_id, has_side_effects=True, vmem_limit_bytes=60 << 20
        ),
        name="closing",
    )(grads, stats, lse, delta, segs, *norm, terms, *flat, queries, queries_saved, kv, weight)


class PlaneLinks:
    def leave(self, value):
        pairs = [(c * 4 + f, (2 * f + c % 2) * 4 + c // 2) for c in range(8) for f in range(4)]
        return lax.ppermute(value, ("ctx", "fsdp"), pairs)

    def open(self, tokens, segs_row, vectors, shares):
        tokens, segs, vectors, *results = opening(tokens, segs_row, vectors, shares[0], shares[1:], 0)
        return tokens.astype(F32), segs, vectors, as_matrices(results[9:]), results[:9]

    def attend(self, queries, kv_own, segs, cotangent):
        *results, cotangent = attend(queries, kv_own, segs, cotangent, 2)
        return results, cotangent

    def attend_back(self, attention, next_queries):
        return attend_back(*attention[:6], next_queries, attention[6], 3)

    def close(self, attention, queries_saved, norm, factors, vectors, weight):
        *sums, vectors, tokens_grad = closing(
            attention, queries_saved, norm, vectors, factors, weight, 4
        )
        return [total.astype(F32) for total in sums], vectors, tokens_grad


class PlainLinks:
    def leave(self, value):
        return value

    def open(self, tokens, segs_row, vectors, shares):
        segs = (segs_row, lax.all_gather(segs_row, "ctx", axis=1, tiled=True))
        gathered = lax.all_gather(pack_vectors(*vectors), "fsdp", axis=0)
        vectors = assemble_vectors([gathered[i] for i in range(4)])
        weights = as_matrices([lax.all_gather(share, "fsdp", axis=0) for share in shares])
        resid = tokens.astype(F32)
        first = project_rows(resid, vectors, weights[0])
        first = first + self.attend(*first[3:], segs, None)[0]
        return resid, segs, vectors, weights, first

    def place(self, segs):
        own_segs, all_segs = segs
        rows = own_segs.shape[1]
        start = (lax.axis_index("ctx") * rows).reshape(1).astype(jnp.int32)
        return start, own_segs.reshape(rows, 1), all_segs

    def blocks(self, block):
        return lax.all_gather(block, "ctx", axis=0)

    def attend(self, queries, kv_own, segs, cotangent):
        start, own_segs, all_segs = self.place(segs)
        kv = self.blocks(kv_own).reshape(-1, 2 * D)
        return (*attention_forward(start, queries, kv, own_segs, all_segs), kv), cotangent

    def attend_back(self, attention, next_queries):
        queries, grads, stats, lse, delta, segs, kv, kv_own = attention
        start, own_segs, all_segs = self.place(segs)
        q_all = self.blocks(queries).reshape(-1, D)
        grad_all = self.blocks(grads).reshape(-1, D)
        return attention_backward(
            start,
            queries,
            grads,
            kv_own,
            lse,
            delta,
            kv,
            q_all,
            grad_all,
            self.blocks(stats),
            own_segs,
            all_segs,
        ), None

    def close(self, attention, queries_saved, norm, factors, vectors, weight):
        grad_projected, _ = self.attend_back(attention, None)
        grad_input, terms = input_gradient(grad_projected, weight, *norm)
        vectors = vectors + jnp.concatenate(
            [terms[:2], jnp.zeros((4, D), F32), terms[2:], jnp.zeros((8, D), F32)], axis=0
        )
        sums = []
        for later_left, later_right, first_left, *first_right in factors:
            left = jnp.concatenate([later_left, first_left], axis=0)
            right = jnp.concatenate([later_right, *(first_right or [grad_projected])], axis=0)
            term = column_products(left, right).astype(BF16)
            share = lax.psum_scatter(term, "fsdp", scatter_dimension=0, tiled=True)
            sums.append(lax.psum(share.astype(F32), "ctx"))
        return sums, lax.psum(vectors, ("ctx", "fsdp")), grad_input.astype(BF16)


def as_matrices(fulls):
    return tuple(full.reshape(-1, full.shape[-1]) for full in fulls)


def project_rows(resid, vectors, weight_qkv):
    bias = jnp.concatenate([vectors[6:7], jnp.zeros((1, D), F32), vectors[7:8]], axis=1)
    normed, normal, inverse = norm_forward(resid, vectors[0:1], vectors[1:2])
    projected = (jnp.dot(normed, weight_qkv, preferred_element_type=F32) + bias).astype(BF16)
    return normed, normal, inverse, projected[:, :D], projected[:, D:]


def layer_forward(resid, weights, vectors, first):
    gain_two, bias_two, bias_proj, bias_out = (vectors[i : i + 1] for i in range(2, 6))
    bias_fc = vectors[8:12].reshape(1, 4 * D)
    _, weight_proj, weight_fc, weight_out = weights
    normed_one, normal_one, inverse_one, queries, kv_own, attended, lse, lse_rows, kv = first
    middle = resid + jnp.dot(attended, weight_proj, preferred_element_type=F32) + bias_proj
    normed_two, normal_two, inverse_two = norm_forward(middle, gain_two, bias_two)
    hidden = jnp.dot(normed_two, weight_fc, preferred_element_type=F32) + bias_fc
    activated = jax.nn.gelu(hidden, approximate=True).astype(BF16)
    result_rows = middle + jnp.dot(activated, weight_out, preferred_element_type=F32) + bias_out
    saved = (
        normed_one,
        normal_one,
        inverse_one,
        queries,
        kv_own,
        kv,
        attended,
        lse,
        lse_rows,
        normed_two,
        normal_two,
        inverse_two,
        hidden,
        activated,
    )
    return result_rows, saved


def layer_backward(gradient, weights, vectors, saved, links, segs):
    weight_qkv, weight_proj, weight_fc, weight_out = weights
    gain_one, gain_two = vectors[0:1], vectors[2:3]
    (
        normed_one,
        normal_one,
        inverse_one,
        queries,
        kv_own,
        kv,
        attended,
        lse,
        lse_rows,
        normed_two,
        normal_two,
        inverse_two,
        hidden,
        activated,
    ) = saved
    total = lambda value: jnp.sum(value.astype(F32), axis=0)
    grad_branch = gradient.astype(BF16)
    grad_activated = dot_rows(grad_branch, weight_out)
    gelu_pull = jax.vjp(partial(jax.nn.gelu, approximate=True), hidden)[1]
    grad_hidden = gelu_pull(grad_activated)[0].astype(BF16)
    grad_normed_two = dot_rows(grad_hidden, weight_fc)
    grad_in_two, grad_gain_two, grad_bias_two = norm_backward(
        grad_normed_two, normal_two, inverse_two, gain_two
    )
    grad_middle = gradient + grad_in_two
    grad_proj = grad_middle.astype(BF16)
    grad_attended = dot_rows(grad_proj, weight_proj).astype(BF16)
    products = grad_attended.astype(F32) * attended.astype(F32)
    head_of = jnp.arange(D, dtype=jnp.int32) // HDIM
    by_lane = (head_of[:, None] == jnp.arange(LANES, dtype=jnp.int32)[None, :]).astype(F32)
    by_row = (jnp.arange(16, dtype=jnp.int32)[:, None] == head_of[None, :]).astype(F32)
    delta = jnp.dot(products, by_lane, precision=lax.Precision.HIGHEST, preferred_element_type=F32)
    delta_rows = lax.dot_general(
        by_row,
        products,
        (((1,), (1,)), ((), ())),
        precision=lax.Precision.HIGHEST,
        preferred_element_type=F32,
    )
    stats = jnp.concatenate([lse_rows, delta_rows], axis=0)
    attention = (queries, grad_attended, stats, lse, delta, segs, kv, kv_own)
    norm = (normal_one, inverse_one, gain_one, grad_middle)
    matrices = ((activated, grad_branch), (normed_two, grad_hidden), (attended, grad_proj))
    upper = jnp.stack([grad_gain_two, grad_bias_two, total(grad_proj), total(grad_branch)])
    lower = total(grad_hidden).reshape(4, D)
    return attention, norm, matrices, (upper, lower)


def input_gradient(grad_projected, weight_qkv, normal, inverse, gain, middle):
    total = lambda value: jnp.sum(value.astype(F32), axis=0)
    grad_normed = dot_rows(grad_projected, weight_qkv)
    grad_in, grad_gain, grad_bias = norm_backward(grad_normed, normal, inverse, gain)
    terms = [
        grad_gain,
        grad_bias,
        total(grad_projected[:, :D]),
        total(grad_projected[:, 2 * D :]),
    ]
    return middle + grad_in, jnp.stack(terms)


def body(
    links,
    tokens,
    segment_ids,
    ln1_gain,
    ln1_bias,
    attn_weight,
    attn_bias,
    proj_weight,
    proj_bias,
    ln2_gain,
    ln2_bias,
    fc_weight,
    fc_bias,
    out_weight,
    out_bias,
    out_cotangent,
):
    vectors = (
        ln1_gain,
        ln1_bias,
        ln2_gain,
        ln2_bias,
        proj_bias,
        out_bias,
        attn_bias,
        fc_bias,
    )
    shares = [attn_weight, proj_weight, fc_weight, out_weight]
    resid, segs, vectors, weights, first = links.open(tokens[0], segment_ids, vectors, shares)
    resid, saved = layer_forward(resid, weights, vectors, first)
    saved_layers = [saved]
    first = project_rows(resid, vectors, weights[0])
    attended, gradient = links.attend(*first[3:], segs, out_cotangent[0])
    resid, saved = layer_forward(resid, weights, vectors, first + tuple(attended))
    saved_layers.append(saved)
    output = links.leave(resid.astype(BF16))
    gradient = gradient.astype(F32)
    attention, norm, later, (upper, lower) = layer_backward(
        gradient, weights, vectors, saved_layers[1], links, segs
    )
    later_projected, queries_saved = links.attend_back(attention, saved_layers[0][3])
    gradient, terms = input_gradient(later_projected, weights[0], *norm)
    attention, norm, first, (more_upper, more_lower) = layer_backward(
        gradient, weights, vectors, saved_layers[0], links, segs
    )
    factors = [(*a, *b) for a, b in zip(later, first)]
    factors.append((saved_layers[1][0], later_projected, saved_layers[0][0]))
    packed = jnp.concatenate(
        [terms[:2], upper + more_upper, terms[2:], lower + more_lower, jnp.zeros((4, D), F32)], axis=0
    )
    (out_grad, fc_grad, proj_grad, qkv_grad), summed, tokens_grad = links.close(
        attention, queries_saved, norm, factors, packed, weights[0]
    )
    own = lax.axis_index("fsdp")
    pick = lambda value, axis: lax.dynamic_index_in_dim(value, own, axis, keepdims=False)
    small = pick(summed[:6].reshape(6, 4, -1), 1)
    bias_qv = pick(summed[6:8].reshape(4, -1), 0)
    bias_fc = pick(summed[8:12], 0)
    gain_one, bias_one, gain_two, bias_two, bias_proj, bias_out = (small[i] for i in range(6))
    return (
        output[None],
        tokens_grad[None],
        gain_one,
        bias_one,
        qkv_grad,
        bias_qv,
        proj_grad,
        bias_proj,
        gain_two,
        bias_two,
        fc_grad,
        bias_fc,
        out_grad,
        bias_out,
    )


def solution(mesh):
    links = PlaneLinks() if (mesh.shape["ctx"], mesh.shape["fsdp"]) == (8, 4) else PlainLinks()
    rows = P("fsdp", "ctx", None)
    vector, matrix = P("fsdp"), P("fsdp", None)
    in_specs = (
        rows,
        P("fsdp", "ctx"),
        vector,
        vector,
        matrix,
        vector,
        matrix,
        vector,
        vector,
        vector,
        matrix,
        vector,
        matrix,
        vector,
        rows,
    )
    out_specs = (
        rows,
        rows,
        vector,
        vector,
        matrix,
        vector,
        matrix,
        vector,
        vector,
        vector,
        matrix,
        vector,
        matrix,
        vector,
    )
    return jax.shard_map(
        partial(body, links), mesh=mesh, in_specs=in_specs, out_specs=out_specs, check_vma=False
    )
```

```python
from functools import partial

import jax
import jax.numpy as jnp
from jax import lax
from jax.experimental import pallas as pl
from jax.experimental.pallas import tpu as pltpu
from jax.sharding import PartitionSpec as P

D = 768
HEADS = 12
HDIM = 64
PAIRS = HEADS // 2
LANES = 128
EPSILON = 1e-05
NEGATIVE = -1e30
SCALE = HDIM ** (-0.5)
MESH = pl.DeviceIdType.MESH
F32 = jnp.float32
BF16 = jnp.bfloat16


def norm_forward(resid, gain_row, bias_row):
    average = jnp.mean(resid, axis=-1, keepdims=True)
    centred = resid - average
    variance = jnp.mean(centred * centred, axis=-1, keepdims=True)
    inverse = lax.rsqrt(variance + EPSILON)
    normal = centred * inverse
    return ((normal * gain_row + bias_row).astype(BF16), normal, inverse)


def norm_backward(grad_normed, normal, inverse, gain_row):
    scaled = grad_normed * gain_row
    mean_term = jnp.mean(scaled, axis=-1, keepdims=True)
    second = jnp.mean(scaled * normal, axis=-1, keepdims=True)
    grad_input = inverse * (scaled - mean_term - normal * second)
    return (grad_input, jnp.sum(grad_normed * normal, axis=0), jnp.sum(grad_normed, axis=0))


def two_heads(rows):
    lane = lax.broadcasted_iota(jnp.int32, rows.shape, 1)
    zero = jnp.zeros_like(rows)
    first = jnp.where(lane < HDIM, rows, zero)
    second = jnp.where(lane < HDIM, zero, rows)
    return jnp.concatenate([first, second], axis=0)


def one_pair(stacked):
    half = stacked.shape[0] // 2
    lane = lax.broadcasted_iota(jnp.int32, (half, LANES), 1)
    return jnp.where(lane < HDIM, stacked[:half], stacked[half:])


def dot_rows(left, right):
    return lax.dot_general(left, right, (((1,), (1,)), ((), ())), preferred_element_type=F32)


def column_products(left, right):
    return lax.dot_general(left, right, (((0,), (0,)), ((), ())), preferred_element_type=F32)


def pick_lanes(columns, pair):
    lane = lax.broadcasted_iota(jnp.int32, columns.shape, 1)
    first = jnp.sum(jnp.where(lane == 2 * pair, columns, 0.0), axis=1, keepdims=True)
    second = jnp.sum(jnp.where(lane == 2 * pair + 1, columns, 0.0), axis=1, keepdims=True)
    return jnp.concatenate([first, second], axis=0)


def mask_columns(bias_ref, own_segs, all_segs_ref, start, own_is_query):
    rows, columns = bias_ref.shape
    step = min(1024, columns)
    own_place = start + lax.broadcasted_iota(jnp.int32, (rows, step), 0)
    for offset in range(0, columns, step):
        place = offset + lax.broadcasted_iota(jnp.int32, (rows, step), 1)
        causal = (place <= own_place) if own_is_query else (own_place <= place)
        same = own_segs == all_segs_ref[:, offset : offset + step]
        bias_ref[:, offset : offset + step] = jnp.where(causal & same, 0.0, NEGATIVE)


def attention_forward_kernel(
    start_ref, q_ref, k_ref, v_ref, own_segs_ref, all_segs_ref, out_ref, lse_ref, lse_rows_ref, bias_ref
):
    pair = pl.program_id(0)
    rows, keys = bias_ref.shape

    @pl.when(pair == 0)
    def _():
        mask_columns(bias_ref, own_segs_ref[...], all_segs_ref, start_ref[0], True)
        lse_ref[...] = jnp.zeros_like(lse_ref)

    queries = two_heads(q_ref[...] * jnp.asarray(SCALE, BF16))
    step = min(1024, keys)

    def scores_of(offset):
        scores = dot_rows(queries, k_ref[pl.ds(offset, step), :])
        bias = bias_ref[:, pl.ds(offset, step)]
        return scores + jnp.concatenate([bias, bias], axis=0)

    if step == keys:
        scores = scores_of(0)
        top = jnp.max(scores, axis=1, keepdims=True)
        weights = jnp.exp(scores - top)
        total = jnp.sum(weights, axis=1, keepdims=True)
        mixed = jnp.dot(weights.astype(BF16), v_ref[...], preferred_element_type=F32)
    else:

        def visit(index, carried):
            top, total, mixed = carried
            offset = pl.multiple_of(index * step, step)
            scores = scores_of(offset)
            new_top = jnp.maximum(top, jnp.max(scores, axis=1, keepdims=True))
            weights = jnp.exp(scores - new_top)
            factor = jnp.exp(top - new_top)
            total = total * factor + jnp.sum(weights, axis=1, keepdims=True)
            more = jnp.dot(
                weights.astype(BF16), v_ref[pl.ds(offset, step), :], preferred_element_type=F32
            )
            return new_top, total, mixed * factor + more

        top, total, mixed = lax.fori_loop(
            0,
            (start_ref[0] + rows + step - 1) // step,
            visit,
            (
                jnp.full((2 * rows, 1), NEGATIVE, F32),
                jnp.zeros((2 * rows, 1), F32),
                jnp.zeros((2 * rows, LANES), F32),
            ),
        )
    out_ref[...] = one_pair(mixed / total).astype(BF16)
    lse = top + jnp.log(total)
    lane = lax.broadcasted_iota(jnp.int32, (rows, LANES), 1)
    kept = lse_ref[...]
    kept = jnp.where(lane == 2 * pair, lse[:rows], kept)
    kept = jnp.where(lane == 2 * pair + 1, lse[rows:], kept)
    lse_ref[...] = kept

    @pl.when(pair == PAIRS - 1)
    def _():
        lse_rows_ref[...] = kept.T[:16]


def attention_forward(start, queries, kv, own_segs, all_segs):
    rows = queries.shape[0]
    keys = kv.shape[0]
    whole = lambda shape: pl.BlockSpec(shape, lambda p: (0, 0))
    return pl.pallas_call(
        attention_forward_kernel,
        grid=(PAIRS,),
        in_specs=[
            pl.BlockSpec(memory_space=pltpu.SMEM),
            pl.BlockSpec((rows, LANES), lambda p: (0, p)),
            pl.BlockSpec((keys, LANES), lambda p: (0, p)),
            pl.BlockSpec((keys, LANES), lambda p: (0, PAIRS + p)),
            whole((rows, 1)),
            whole((1, keys)),
        ],
        out_specs=[
            pl.BlockSpec((rows, LANES), lambda p: (0, p)),
            whole((rows, LANES)),
            whole((16, rows)),
        ],
        out_shape=[
            jax.ShapeDtypeStruct((rows, D), BF16),
            jax.ShapeDtypeStruct((rows, LANES), F32),
            jax.ShapeDtypeStruct((16, rows), F32),
        ],
        scratch_shapes=[pltpu.VMEM((rows, keys), F32)],
        compiler_params=pltpu.CompilerParams(vmem_limit_bytes=60 << 20),
        cost_estimate=pl.CostEstimate(
            flops=8 * rows * keys * D, bytes_accessed=4 * keys * D, transcendentals=rows * keys * HEADS
        ),
        name="attention_forward",
    )(start, queries, kv, kv, own_segs, all_segs)


def attention_backward_kernel(
    start_ref,
    q_ref,
    grad_ref,
    k_own_ref,
    v_own_ref,
    lse_ref,
    delta_ref,
    k_ref,
    v_ref,
    q_all_ref,
    grad_all_ref,
    stats_ref,
    own_segs_ref,
    all_segs_ref,
    out_ref,
    query_bias_ref,
    key_bias_ref,
):
    pair = pl.program_id(0)
    rows, tokens = query_bias_ref.shape
    start = start_ref[0]

    @pl.when(pair == 0)
    def _():
        mask_columns(query_bias_ref, own_segs_ref[...], all_segs_ref, start, True)
        mask_columns(key_bias_ref, own_segs_ref[...], all_segs_ref, start, False)

    step = min(256, tokens)
    blocks = step // rows
    scale = jnp.asarray(SCALE, BF16)

    def doubled(bias):
        return jnp.concatenate([bias, bias], axis=0)

    queries = two_heads(q_ref[...] * scale)
    grads = two_heads(grad_ref[...])
    lse = pick_lanes(lse_ref[...], pair)
    delta = pick_lanes(delta_ref[...], pair)

    def visit_keys(index, grad_query):
        offset = pl.multiple_of(index * step, step)
        keys = k_ref[pl.ds(offset, step), :]
        values = v_ref[pl.ds(offset, step), :]
        bias = doubled(query_bias_ref[:, pl.ds(offset, step)])
        attention = jnp.exp(dot_rows(queries, keys) + bias - lse)
        grad_attention = dot_rows(grads, values)
        grad_scores = (attention * (grad_attention - delta)).astype(BF16)
        return grad_query + jnp.dot(grad_scores, keys, preferred_element_type=F32)

    zeros = jnp.zeros((2 * rows, LANES), F32)
    grad_query = lax.fori_loop(0, (start + rows + step - 1) // step, visit_keys, zeros)

    own_keys = two_heads(k_own_ref[...] * scale)
    own_values = two_heads(v_own_ref[...])

    def row_of(block, row):
        return jnp.broadcast_to(stats_ref[block, pl.ds(row, 1), :], (rows, rows))

    def stat_rows(index, row):
        first = [row_of(index * blocks + b, row + 2 * pair) for b in range(blocks)]
        second = [row_of(index * blocks + b, row + 2 * pair + 1) for b in range(blocks)]
        return jnp.concatenate(
            [jnp.concatenate(first, axis=1), jnp.concatenate(second, axis=1)], axis=0
        )

    def visit_queries(index, carried):
        grad_keys, grad_values = carried
        offset = pl.multiple_of(index * step, step)
        later = q_all_ref[pl.ds(offset, step), :]
        later_grads = grad_all_ref[pl.ds(offset, step), :]
        bias = doubled(key_bias_ref[:, pl.ds(offset, step)])
        attention = jnp.exp(dot_rows(own_keys, later) + bias - stat_rows(index, 0))
        grad_attention = dot_rows(own_values, later_grads)
        grad_scores = (attention * (grad_attention - stat_rows(index, 16))).astype(BF16)
        grad_keys = grad_keys + jnp.dot(grad_scores, later, preferred_element_type=F32)
        grad_values = grad_values + jnp.dot(
            attention.astype(BF16), later_grads, preferred_element_type=F32
        )
        return grad_keys, grad_values

    grad_keys, grad_values = lax.fori_loop(
        start // step, tokens // step, visit_queries, (zeros, zeros)
    )
    base = pl.multiple_of(pair * LANES, LANES)
    out_ref[:, pl.ds(base, LANES)] = (one_pair(grad_query) * SCALE).astype(BF16)
    out_ref[:, pl.ds(D + base, LANES)] = (one_pair(grad_keys) * SCALE).astype(BF16)
    out_ref[:, pl.ds(2 * D + base, LANES)] = one_pair(grad_values).astype(BF16)


def attention_backward(
    start, queries, grads, kv_own, lse, delta, kv, q_all, grad_all, stats, own_segs, all_segs
):
    rows = queries.shape[0]
    tokens = kv.shape[0]
    whole = lambda shape: pl.BlockSpec(shape, lambda p: (0,) * len(shape))
    own = pl.BlockSpec((rows, LANES), lambda p: (0, p))
    every = pl.BlockSpec((tokens, LANES), lambda p: (0, p))
    return pl.pallas_call(
        attention_backward_kernel,
        grid=(PAIRS,),
        in_specs=[
            pl.BlockSpec(memory_space=pltpu.SMEM),
            own,
            own,
            own,
            pl.BlockSpec((rows, LANES), lambda p: (0, PAIRS + p)),
            whole((rows, LANES)),
            whole((rows, LANES)),
            every,
            pl.BlockSpec((tokens, LANES), lambda p: (0, PAIRS + p)),
            every,
            every,
            whole(stats.shape),
            whole((rows, 1)),
            whole((1, tokens)),
        ],
        out_specs=whole((rows, 3 * D)),
        out_shape=jax.ShapeDtypeStruct((rows, 3 * D), BF16),
        scratch_shapes=[pltpu.VMEM((rows, tokens), F32), pltpu.VMEM((rows, tokens), F32)],
        compiler_params=pltpu.CompilerParams(vmem_limit_bytes=60 << 20),
        cost_estimate=pl.CostEstimate(
            flops=16 * rows * tokens * D,
            bytes_accessed=8 * tokens * D,
            transcendentals=rows * tokens * HEADS,
        ),
        name="attention_backward",
    )(
        start,
        queries,
        grads,
        kv_own,
        kv_own,
        lse,
        delta,
        kv,
        kv,
        q_all,
        grad_all,
        stats,
        own_segs,
        all_segs,
    )


def place_bits():
    ctx, fsdp = lax.axis_index("ctx"), lax.axis_index("fsdp")
    return lax.rem(ctx, 2), ctx // 2, fsdp // 2, lax.rem(fsdp, 2)


class Place:
    def __init__(self):
        self.x, self.z, self.y, self.core = x, z, y, core = place_bits()
        self.low, self.high = low, high = lax.rem(z, 2), z // 2
        self.fsdp = fsdp = 2 * y + core
        self.block = 2 * fsdp + x
        self.sibling = (2 * z + x, 2 * y + 1 - core)
        self.over_y = (2 * z + x, 2 * (1 - y) + core)
        self.over_x = (2 * z + 1 - x, fsdp)
        self.over_z = (2 * (z + 1 - 2 * low) + x, fsdp)
        self.over_zz = (2 * (z + 2 - 4 * high) + x, fsdp)
        self.partner = (2 * fsdp + x, z)
        self.has_partner = fsdp != z


class Copies:
    def __init__(self, send_sems, recv_sems):
        self.send_sems, self.recv_sems = send_sems, recv_sems
        self.used = 0

    def make(self, src, dst, device):
        slot = self.used
        self.used += 1
        return pltpu.make_async_remote_copy(
            src_ref=src,
            dst_ref=dst,
            send_sem=self.send_sems.at[slot],
            recv_sem=self.recv_sems.at[slot],
            device_id=device,
            device_id_type=MESH,
        )


def greet(devices):
    barrier = pltpu.get_barrier_semaphore()
    for device in devices:
        pl.semaphore_signal(barrier, inc=1, device_id=device, device_id_type=MESH)
    pl.semaphore_wait(barrier, len(devices))


WEIGHT_COPIES = 11


def weight_cuts(shape):
    rows, columns = shape
    pieces = 1 if rows * columns <= 192 * 768 else 3 if columns == 3 * D else 2
    width = columns // pieces
    return [(i * width, width) for i in range(pieces)]


class WeightGather:
    def __init__(self, place, copies, shares, fulls, stages, local_sems):
        x, low = place.x, place.low
        own, other = place.fsdp, 2 * (1 - place.y) + place.core
        self.plans = []
        self.locals = []
        self.arrived = set()
        for which, (share, full) in enumerate(zip(shares, fulls)):
            part = share.shape[0] // 4
            for first, width in weight_cuts(share.shape):
                columns = pl.ds(first, width)

                def piece(ref, x_bit, low_bit, part=part, columns=columns):
                    return ref.at[pl.ds((2 * low_bit + x_bit) * part, part), columns]

                def side(ref, x_bit, low_bit, index, part=part, first=first, width=width):
                    start = (2 * low_bit + x_bit) * part
                    if part % 32 == 0:
                        rows = pl.ds(start + index * (part // 2), part // 2)
                        return ref.at[rows, pl.ds(first, width)]
                    half = width // 2
                    return ref.at[pl.ds(start, part), pl.ds(first + index * half, half)]

                theirs = full.at[other]
                same = lambda view, device: copies.make(view, view, device)
                mine = piece(theirs, x, low)
                from_x, from_z = piece(theirs, 1 - x, low), piece(theirs, x, 1 - low)
                self.plans.append(
                    [
                        copies.make(piece(share, x, low), piece(full.at[own], x, low), place.over_y),
                        same(mine, place.over_x),
                        same(mine, place.over_z),
                        same(mine, place.sibling),
                        same(side(theirs, 1 - x, low, 0), place.over_z),
                        same(from_x, place.sibling),
                        same(side(theirs, x, 1 - low, 1), place.over_x),
                        same(from_z, place.sibling),
                        same(side(theirs, 1 - x, 1 - low, 0), place.sibling),
                        same(side(theirs, 1 - x, 1 - low, 1), place.sibling),
                        copies.make(share.at[:, columns], full.at[own, :, columns], place.sibling),
                    ]
                )
            sem = local_sems.at[which]
            if stages[which] is None:
                self.locals.append((pltpu.make_async_copy(share, full.at[own], sem), None))
            else:
                self.locals.append(
                    (
                        pltpu.make_async_copy(share, stages[which], sem),
                        pltpu.make_async_copy(stages[which], full.at[own], sem),
                    )
                )

    def begin(self):
        for plan in self.plans:
            plan[0].start()
        for plan in self.plans:
            plan[10].start()
        for into, _ in self.locals:
            into.start()

    def keep_own(self):
        for into, out in self.locals:
            into.wait()
            if out is not None:
                out.start()

    def arrive(self, first, last):
        for index in range(first, last):
            if index not in self.arrived:
                self.arrived.add(index)
                for copy in (3, 5, 7, 8, 9, 10):
                    self.plans[index][copy].wait_recv()

    def steps(self):
        count = len(self.plans)
        for step in range(count + 2):
            yield step

    def step(self, step):
        count = len(self.plans)
        if step < count:
            plan = self.plans[step]
            plan[0].wait_recv()
            plan[1].start()
            plan[2].start()
            plan[3].start()
        if 0 <= step - 1 < count:
            plan = self.plans[step - 1]
            plan[1].wait_recv()
            plan[4].start()
            plan[5].start()
            plan[2].wait_recv()
            plan[6].start()
            plan[7].start()
        if 0 <= step - 2 < count:
            plan = self.plans[step - 2]
            plan[4].wait_recv()
            plan[8].start()
            plan[6].wait_recv()
            plan[9].start()

    def finish(self):
        self.arrive(0, len(self.plans))
        for plan in self.plans:
            for copy in plan:
                copy.wait_send()
        for _, out in self.locals:
            if out is not None:
                out.wait()


BLOCK_COPIES = 13


class BlockGather:
    def __init__(self, place, copies, blocks, fulls):
        self.own = place.block
        self.pairs = list(zip(blocks, fulls))
        self.plans = []
        for block, full in self.pairs:
            half = block.shape[0] // 2

            def part(ref, side, half=half):
                return ref.at[pl.ds(side * half, half), :]

            def slot_of(x_bit, y_bit, full=full):
                return full.at[4 * y_bit + 2 * place.core + x_bit]

            same = lambda view, device: copies.make(view, view, device)
            x, y = place.x, place.y
            mine, from_x = slot_of(x, y), slot_of(1 - x, y)
            from_y, from_both = slot_of(x, 1 - y), slot_of(1 - x, 1 - y)
            self.plans.append(
                [
                    copies.make(block, mine, place.sibling),
                    copies.make(part(block, 0), part(mine, 0), place.over_x),
                    copies.make(part(block, 1), part(mine, 1), place.over_y),
                    copies.make(part(block, 1), part(mine, 1), place.over_x),
                    copies.make(part(block, 0), part(mine, 0), place.over_y),
                    same(part(from_x, 0), place.over_y),
                    same(part(from_x, 0), place.sibling),
                    same(part(from_y, 1), place.over_x),
                    same(part(from_y, 1), place.sibling),
                    same(part(from_x, 1), place.sibling),
                    same(part(from_y, 0), place.sibling),
                    same(part(from_both, 0), place.sibling),
                    same(part(from_both, 1), place.sibling),
                ]
            )

    def begin(self):
        for index in (1, 2, 3, 4, 0):
            for plan in self.plans:
                plan[index].start()
        for block, full in self.pairs:
            full[self.own] = block[...]

    def relay(self, *pairs):
        for arrived, followers in pairs:
            for plan in self.plans:
                plan[arrived].wait_recv()
                for index in followers:
                    plan[index].start()

    def first_halves(self):
        self.relay((1, (5, 6)), (2, (7, 8)))

    def second_halves(self):
        self.relay((3, (9,)), (4, (10,)))

    def corners(self):
        self.relay((5, (11,)), (7, (12,)))

    def wait(self, *indices):
        for plan in self.plans:
            for index in indices:
                plan[index].wait_recv()

    def wait_near(self):
        self.wait(0, 6, 9)

    def wait_far(self):
        self.wait(8, 10, 11, 12)

    def finish(self):
        for plan in self.plans:
            for copy in plan:
                copy.wait_send()


VECTORS = 8


def pack_vectors(ln1_gain, ln1_bias, ln2_gain, ln2_bias, proj_bias, out_bias, attn_bias, fc_bias):
    rows = (ln1_gain, ln1_bias, ln2_gain, ln2_bias, proj_bias, out_bias, attn_bias, fc_bias)
    return jnp.stack([jnp.pad(row.astype(F32), (0, D - row.shape[0])) for row in rows])


def assemble_vectors(shares):
    quarter = D // 4
    small = jnp.concatenate([share[:6, :quarter] for share in shares], axis=1)
    query = jnp.concatenate([shares[0][6:7, : 2 * quarter], shares[1][6:7, : 2 * quarter]], axis=1)
    value = jnp.concatenate([shares[2][6:7, : 2 * quarter], shares[3][6:7, : 2 * quarter]], axis=1)
    hidden = [share[7:8] for share in shares]
    return jnp.concatenate([small, query, value, *hidden, jnp.zeros((4, D), F32)], axis=0)


def mask_block(own_segs, segs_ref, block, start, own_is_query):
    rows = own_segs.shape[0]
    own_place = start + lax.broadcasted_iota(jnp.int32, (rows, rows), 0)
    place = block * rows + lax.broadcasted_iota(jnp.int32, (rows, rows), 1)
    causal = (place <= own_place) if own_is_query else (own_place <= place)
    same = own_segs == segs_ref[block, 0:1, :]
    return jnp.where(causal & same, 0.0, NEGATIVE)


def own_columns(segs_ref, block):
    rows = segs_ref.shape[2]
    return jnp.broadcast_to(segs_ref[block, 0:1, :], (rows, rows)).T


def project_blocks(rows_all, first, weight_of, bias, out_ref, width):
    rows = rows_all[pl.ds(first, 4)].reshape(4 * rows_all.shape[1], D)
    for side in range(width // D):
        total = jnp.dot(rows, weight_of(side), preferred_element_type=F32)
        if bias[side] is not None:
            total = total + bias[side]
        out_ref[pl.ds(first, 4), :, side * D : (side + 1) * D] = total.astype(BF16).reshape(4, -1, D)


class AttentionForward:
    def __init__(
        self, place, q_ref, segs_ref, rows_all, kv_all, outs, scratch, sems, weight_of, vectors_ref
    ):
        self.place = place
        out_ref, lse_ref, lse_rows_ref, kv_out, rows_out = outs
        self.q_ref, self.segs_ref, self.kv_all = q_ref, segs_ref, kv_all
        self.rows_all, self.weight_of, self.vectors_ref = rows_all, weight_of, vectors_ref
        self.out_ref, self.lse_ref, self.lse_rows_ref = out_ref, lse_ref, lse_rows_ref
        self.near_bias, self.far_bias, self.top, self.total, self.mixed = scratch
        self.rows = q_ref.shape[0]
        self.near, self.far = 4 * place.y, 4 * (1 - place.y)
        moves = [
            (kv_all.at[pl.ds(self.near, 4)], kv_out.at[pl.ds(self.near, 4)]),
            (kv_all.at[pl.ds(self.far, 4)], kv_out.at[pl.ds(self.far, 4)]),
            (rows_all, rows_out),
        ]
        self.saves = [pltpu.make_async_copy(*move, sem) for move, sem in zip(moves, sems)]

    def project_queries(self):
        rows = self.rows_all[self.place.block]
        total = jnp.dot(rows, self.weight_of(0), preferred_element_type=F32)
        self.q_ref[...] = (total + self.vectors_ref[6:7, :]).astype(BF16)

    def project(self, first):
        biases = (None, self.vectors_ref[7:8, :])
        project_blocks(
            self.rows_all, first, lambda side: self.weight_of(side + 1), biases, self.kv_all, 2 * D
        )

    def masks(self, far):
        rows = self.rows
        start = self.place.block * rows
        own_segs = own_columns(self.segs_ref, self.place.block)
        first, bias = (self.far, self.far_bias) if far else (self.near, self.near_bias)
        for i in range(4):
            at = slice(i * rows, (i + 1) * rows)
            bias[:, at] = mask_block(own_segs, self.segs_ref, first + i, start, True)

    def lanes(self, pair, side=0):
        return pl.ds(pl.multiple_of(side * D + pair * LANES, LANES), LANES)

    def part(self, first, bias_ref, pair):
        rows = self.rows
        queries = two_heads(self.q_ref[:, self.lanes(pair)] * jnp.asarray(SCALE, BF16))
        keys = self.kv_all[pl.ds(first, 4), :, self.lanes(pair)].reshape(4 * rows, LANES)
        values = self.kv_all[pl.ds(first, 4), :, self.lanes(pair, 1)].reshape(4 * rows, LANES)
        bias = bias_ref[...]
        scores = dot_rows(queries, keys) + jnp.concatenate([bias, bias], axis=0)
        top = jnp.max(scores, axis=1, keepdims=True)
        shares = jnp.exp(scores - top)
        total = jnp.sum(shares, axis=1, keepdims=True)
        return top, total, jnp.dot(shares.astype(BF16), values, preferred_element_type=F32)

    def near_part(self):
        self.project(self.near)
        self.saves[0].start()
        self.lse_ref[...] = jnp.zeros_like(self.lse_ref)

        def visit(pair, carried):
            self.top[pair], self.total[pair], self.mixed[pair] = self.part(
                self.near, self.near_bias, pair
            )
            return carried

        lax.fori_loop(0, PAIRS, visit, 0)

    def far_part(self):
        self.saves[2].start()
        self.project(self.far)
        self.saves[1].start()

        def visit(pair, carried):
            top, total, mixed = self.part(self.far, self.far_bias, pair)
            old_top = self.top[pair]
            new_top = jnp.maximum(top, old_top)
            new, old = jnp.exp(top - new_top), jnp.exp(old_top - new_top)
            self.top[pair] = new_top
            self.total[pair] = total * new + self.total[pair] * old
            self.mixed[pair] = mixed * new + self.mixed[pair] * old
            return carried

        @pl.when(self.place.y == 1)
        def _():
            lax.fori_loop(0, PAIRS, visit, 0)

    def store(self):
        rows = self.rows

        def visit(pair, carried):
            total = self.total[pair]
            self.out_ref[:, self.lanes(pair)] = one_pair(self.mixed[pair] / total).astype(BF16)
            lse = self.top[pair] + jnp.log(total)
            lane = lax.broadcasted_iota(jnp.int32, (rows, LANES), 1)
            kept = jnp.where(lane == 2 * pair, lse[:rows], self.lse_ref[...])
            self.lse_ref[...] = jnp.where(lane == 2 * pair + 1, lse[rows:], kept)
            return carried

        lax.fori_loop(0, PAIRS, visit, 0)
        self.lse_rows_ref[...] = self.lse_ref[...].T[:16]

    def finish(self):
        for save in self.saves:
            save.wait()


def forward_scratch(rows):
    return [
        pltpu.VMEM((8, rows, 2 * D), BF16),
        pltpu.VMEM((8, rows, D), BF16),
        pltpu.VMEM((rows, D), BF16),
        pltpu.VMEM((rows, 4 * rows), F32),
        pltpu.VMEM((rows, 4 * rows), F32),
        pltpu.VMEM((PAIRS, 2 * rows, 1), F32),
        pltpu.VMEM((PAIRS, 2 * rows, 1), F32),
        pltpu.VMEM((PAIRS, 2 * rows, LANES), F32),
    ]


FORWARD_SCRATCH = 8


def forward_shapes(rows):
    return [
        jax.ShapeDtypeStruct((rows, D), BF16),
        jax.ShapeDtypeStruct((rows, LANES), F32),
        jax.ShapeDtypeStruct((16, rows), F32),
        jax.ShapeDtypeStruct((8, rows, 2 * D), BF16),
        jax.ShapeDtypeStruct((8, rows, D), BF16),
    ]


def greet_with_partner(place, others):
    barrier = pltpu.get_barrier_semaphore()
    for device in others:
        pl.semaphore_signal(barrier, inc=1, device_id=device, device_id_type=MESH)

    @pl.when(place.has_partner)
    def _():
        pl.semaphore_signal(barrier, inc=1, device_id=place.partner, device_id_type=MESH)
        pl.semaphore_wait(barrier, len(others) + 1)

    @pl.when(jnp.logical_not(place.has_partner))
    def _():
        pl.semaphore_wait(barrier, len(others))


def attend_kernel(
    rows_ref,
    segs_ref,
    vectors_ref,
    weight_ref,
    cotangent_ref,
    out_ref,
    lse_ref,
    lse_rows_ref,
    kv_out,
    rows_out,
    cotangent_out,
    *scratch,
):
    kv_all, rows_all, q_ref = scratch[:3]
    weight, send_sems, recv_sems, local_sems = scratch[FORWARD_SCRATCH:]
    place = Place()
    load = pltpu.make_async_copy(weight_ref, weight, local_sems.at[3])
    load.start()
    greet_with_partner(place, (place.sibling, place.over_x, place.over_y))
    copies = Copies(send_sems, recv_sems)
    gather = BlockGather(place, copies, [rows_ref], [rows_all])
    swap = copies.make(cotangent_ref, cotangent_out, place.partner)
    keep = pltpu.make_async_copy(cotangent_ref, cotangent_out, local_sems.at[4])
    gather.begin()

    @pl.when(place.has_partner)
    def _():
        swap.start()

    @pl.when(jnp.logical_not(place.has_partner))
    def _():
        keep.start()

    attention = AttentionForward(
        place,
        q_ref,
        segs_ref,
        rows_all,
        kv_all,
        (out_ref, lse_ref, lse_rows_ref, kv_out, rows_out),
        scratch[3:FORWARD_SCRATCH],
        [local_sems.at[i] for i in range(3)],
        lambda side: weight[:, side * D : (side + 1) * D],
        vectors_ref,
    )
    attention.masks(False)
    attention.masks(True)
    load.wait()
    attention.project_queries()
    gather.first_halves()
    gather.second_halves()
    gather.wait_near()
    gather.corners()
    attention.near_part()
    gather.wait_far()
    attention.far_part()
    attention.store()
    attention.finish()
    gather.finish()

    @pl.when(place.has_partner)
    def _():
        swap.wait()

    @pl.when(jnp.logical_not(place.has_partner))
    def _():
        keep.wait()


def attend(normed, segs, vectors, weight, cotangent, collective_id):
    rows = normed.shape[0]
    vmem = pl.BlockSpec(memory_space=pltpu.VMEM)
    anywhere = pl.BlockSpec(memory_space=pl.ANY)
    return pl.pallas_call(
        attend_kernel,
        in_specs=[vmem, vmem, vmem, anywhere, anywhere],
        out_specs=[vmem, vmem, vmem, anywhere, anywhere, vmem],
        out_shape=forward_shapes(rows) + [jax.ShapeDtypeStruct((rows, D), BF16)],
        scratch_shapes=forward_scratch(rows)
        + [
            pltpu.VMEM(weight.shape, BF16),
            pltpu.SemaphoreType.DMA((BLOCK_COPIES + 1,)),
            pltpu.SemaphoreType.DMA((BLOCK_COPIES + 1,)),
            pltpu.SemaphoreType.DMA((5,)),
        ],
        compiler_params=pltpu.CompilerParams(
            collective_id=collective_id, has_side_effects=True, vmem_limit_bytes=36 << 20
        ),
        name="attend",
    )(normed, segs, vectors, weight, cotangent)


def opening_kernel(count, *refs):
    tokens_ref, segs_ref, first_ref = refs[:3]
    vector_refs = refs[3 : 3 + VECTORS]
    shares = refs[3 + VECTORS : 3 + VECTORS + count]
    refs = refs[3 + VECTORS + count :]
    (
        tokens_out,
        segs_out,
        vectors_out,
        normed_out,
        normal_out,
        inverse_out,
        attended_out,
        lse_out,
        lse_rows_out,
        kv_out,
        rows_out,
        first_out,
    ) = refs[:12]
    fulls = refs[12 : 12 + count]
    refs = refs[12 + count :]
    kv_all, rows_all, q_ref = refs[:3]
    forward = refs[3:FORWARD_SCRATCH]
    vectors_own, vectors_all, segs_row, segs_sent, segs_own = refs[FORWARD_SCRATCH : FORWARD_SCRATCH + 5]
    refs = refs[FORWARD_SCRATCH + 5 :]
    first_full, tokens_all, send_sems, recv_sems, local_sems = refs[:5]
    stages, vector_rows = refs[5 : 5 + count], refs[5 + count :]
    place = Place()
    own, other = place.fsdp, 2 * (1 - place.y) + place.core
    loads = [
        pltpu.make_async_copy(src, dst, local_sems.at[count + 8 + i])
        for i, (src, dst) in enumerate(zip((segs_ref, *vector_refs), (segs_row, *vector_rows)))
    ]
    for load in loads:
        load.start()
    for load in loads:
        load.wait()
    vectors_own[...] = jnp.zeros_like(vectors_own)
    for i, row in enumerate(vector_rows):
        size = row.shape[0]
        vectors_own[i : i + 1, :size] = row[...].astype(F32).reshape(1, size)
    segs_sent[...] = jnp.broadcast_to(segs_row[...], segs_sent.shape)
    greet_with_partner(place, (place.sibling, place.over_x, place.over_y, place.over_z))
    copies = Copies(send_sems, recv_sems)
    swap_tokens = copies.make(tokens_ref, tokens_out, place.partner)
    swap_segs = copies.make(segs_sent, segs_own, place.partner)
    vector_copies = [
        copies.make(vectors_own, vectors_all.at[own], place.over_y),
        copies.make(vectors_own, vectors_all.at[own], place.sibling),
        copies.make(vectors_all.at[other], vectors_all.at[other], place.sibling),
    ]
    weights = WeightGather(
        place,
        copies,
        [first_ref, *shares],
        [first_full, *fulls],
        [None, *stages],
        local_sems,
    )
    first_cuts = len(weight_cuts(first_ref.shape))
    gather = BlockGather(place, copies, [tokens_out, segs_own], [tokens_all, segs_out])
    save_first = pltpu.make_async_copy(first_full, first_out, local_sems.at[count + 7])
    attention = AttentionForward(
        place,
        q_ref,
        segs_out,
        rows_all,
        kv_all,
        (attended_out, lse_out, lse_rows_out, kv_out, rows_out),
        forward,
        [local_sems.at[count + i] for i in (2, 3, 5)],
        lambda side: first_full[:, :, side * D : (side + 1) * D].reshape(D, D),
        vectors_out,
    )

    keep_tokens = pltpu.make_async_copy(tokens_ref, tokens_out, local_sems.at[count + 9 + VECTORS])
    vector_copies[0].start()
    vector_copies[1].start()

    @pl.when(place.has_partner)
    def _():
        swap_segs.start()

    @pl.when(place.has_partner)
    def _():
        swap_tokens.start()

    @pl.when(jnp.logical_not(place.has_partner))
    def _():
        keep_tokens.start()

    weights.begin()
    vectors_all[own] = vectors_own[...]

    @pl.when(jnp.logical_not(place.has_partner))
    def _():
        segs_own[...] = segs_sent[...]

    vector_copies[0].wait_recv()
    vector_copies[2].start()
    weights.step(0)
    weights.step(1)
    vector_copies[1].wait_recv()
    vector_copies[2].wait_recv()
    vectors_out[...] = assemble_vectors([vectors_all[i] for i in range(4)])
    weights.step(2)

    @pl.when(place.has_partner)
    def _():
        swap_segs.wait_recv()
        swap_tokens.wait_recv()

    @pl.when(jnp.logical_not(place.has_partner))
    def _():
        keep_tokens.wait()

    gather.begin()
    weights.step(3)

    def norm_block(block):
        return norm_forward(
            tokens_all[block].astype(F32), vectors_out[0:1, :], vectors_out[1:2, :]
        )

    def norm_four(start):
        def visit(index, carried):
            rows_all[start + index] = norm_block(start + index)[0]
            return carried

        lax.fori_loop(0, 4, visit, 0)

    normed, normal, inverse = norm_block(place.block)
    normed_out[...] = normed
    normal_out[...] = normal
    inverse_out[...] = inverse
    weights.step(4)
    gather.first_halves()
    weights.keep_own()
    weights.step(5)
    gather.second_halves()
    gather.wait_near()
    gather.corners()
    norm_four(attention.near)
    attention.masks(False)
    weights.step(6)
    weights.arrive(0, first_cuts)
    save_first.start()
    attention.project_queries()
    weights.step(7)
    attention.near_part()
    weights.step(8)
    gather.wait_far()
    norm_four(attention.far)
    attention.masks(True)
    weights.step(9)
    attention.far_part()
    attention.store()
    save_first.wait()
    attention.finish()
    gather.finish()
    for copy in vector_copies:
        copy.wait_send()

    @pl.when(place.has_partner)
    def _():
        swap_segs.wait_send()
        swap_tokens.wait_send()

    weights.finish()


def opening(tokens, segs_row, vectors, first, shares, collective_id):
    rows, columns = tokens.shape
    count = len(shares)
    cuts = sum(len(weight_cuts(share.shape)) for share in [first, *shares])
    slots = 2 + 3 + cuts * WEIGHT_COPIES + 2 * BLOCK_COPIES
    vmem = pl.BlockSpec(memory_space=pltpu.VMEM)
    anywhere = pl.BlockSpec(memory_space=pl.ANY)
    shape = jax.ShapeDtypeStruct
    segs_shape = (16, segs_row.shape[1])
    return pl.pallas_call(
        partial(opening_kernel, count),
        in_specs=[anywhere] * (3 + VECTORS + count),
        out_specs=[vmem] * 9 + [anywhere] * (3 + count),
        out_shape=[
            shape((rows, columns), tokens.dtype),
            shape((8, *segs_shape), segs_row.dtype),
            shape((16, D), F32),
            shape((rows, D), BF16),
            shape((rows, D), F32),
            shape((rows, 1), F32),
        ]
        + forward_shapes(rows)
        + [shape((4, *share.shape), share.dtype) for share in [first, *shares]],
        scratch_shapes=forward_scratch(rows)
        + [
            pltpu.VMEM((8, D), F32),
            pltpu.VMEM((4, 8, D), F32),
            pltpu.VMEM(segs_row.shape, segs_row.dtype),
            pltpu.VMEM(segs_shape, segs_row.dtype),
            pltpu.VMEM(segs_shape, segs_row.dtype),
            pltpu.VMEM((4, *first.shape), first.dtype),
            pltpu.VMEM((8, rows, D), BF16),
            pltpu.SemaphoreType.DMA((slots,)),
            pltpu.SemaphoreType.DMA((slots,)),
            pltpu.SemaphoreType.DMA((count + 10 + VECTORS,)),
        ]
        + [pltpu.VMEM(share.shape, share.dtype) for share in shares]
        + [pltpu.VMEM(vector.shape, vector.dtype) for vector in vectors],
        compiler_params=pltpu.CompilerParams(
            collective_id=collective_id, has_side_effects=True, vmem_limit_bytes=60 << 20
        ),
        name="opening",
    )(tokens, segs_row, first, *vectors, *shares)


class AttentionGrads:
    def __init__(self, place, grad_ref, lse_ref, delta_ref, segs_ref, kv_all, q_all, grad_all, stats_all, biases, sums):
        self.place = place
        self.grad_ref, self.lse_ref, self.delta_ref = grad_ref, lse_ref, delta_ref
        self.segs_ref, self.kv_all, self.q_all, self.grad_all = segs_ref, kv_all, q_all, grad_all
        self.stats_all = stats_all
        self.query_bias, self.key_bias = biases
        self.query_sum, self.key_sum, self.value_sum = sums
        self.rows = grad_ref.shape[0]

    def masks(self):
        rows, place = self.rows, self.place
        start = place.block * rows
        own_segs = own_columns(self.segs_ref, place.block)
        for i in range(8):
            at = slice(i * rows, (i + 1) * rows)
            self.query_bias[:, at] = mask_block(own_segs, self.segs_ref, i, start, True)
            self.key_bias[:, at] = mask_block(own_segs, self.segs_ref, i, start, False)

    def lanes(self, pair, side=0):
        return pl.ds(pl.multiple_of(side * D + pair * LANES, LANES), LANES)

    def two_blocks(self, ref, index, lanes):
        return ref[pl.ds(2 * index, 2), :, lanes].reshape(2 * self.rows, LANES)

    def bias(self, ref, index):
        step = 2 * self.rows
        bias = ref[:, pl.ds(pl.multiple_of(index * step, step), step)]
        return jnp.concatenate([bias, bias], axis=0)

    def project(self, rows_all, weight, bias):
        for first in (0, 4):
            project_blocks(rows_all, first, lambda side: weight[:, :D], (bias,), self.q_all, D)

    def query_grads(self, first_pair, last_pair):
        scale = jnp.asarray(SCALE, BF16)
        count = self.place.block // 2 + 1

        def visit_pair(pair, carried):
            lanes = self.lanes(pair)
            queries = two_heads(self.q_all[self.place.block, :, lanes] * scale)
            grads = two_heads(self.grad_ref[:, lanes])
            lse = pick_lanes(self.lse_ref[...], pair)
            delta = pick_lanes(self.delta_ref[...], pair)

            def visit(index, total):
                keys = self.two_blocks(self.kv_all, index, lanes)
                values = self.two_blocks(self.kv_all, index, self.lanes(pair, 1))
                scores = dot_rows(queries, keys) + self.bias(self.query_bias, index)
                attention = jnp.exp(scores - lse)
                grad_attention = dot_rows(grads, values)
                grad_scores = (attention * (grad_attention - delta)).astype(BF16)
                return total + jnp.dot(grad_scores, keys, preferred_element_type=F32)

            zeros = jnp.zeros((2 * self.rows, LANES), F32)
            self.query_sum[pair] = lax.fori_loop(0, count, visit, zeros)
            return carried

        lax.fori_loop(first_pair, last_pair, visit_pair, 0)

    def key_grads(self, first, last, fresh):
        rows = self.rows
        scale = jnp.asarray(SCALE, BF16)
        own = self.place.block

        def visit_pair(pair, carried):
            lanes = self.lanes(pair)
            own_keys = two_heads(self.kv_all[own, :, lanes] * scale)
            own_values = two_heads(self.kv_all[own, :, self.lanes(pair, 1)])

            def stat_rows(index, row):
                def spread(block, head):
                    line = self.stats_all[2 * index + block, pl.ds(row + 2 * pair + head, 1), :]
                    return jnp.broadcast_to(line, (rows, rows))

                heads = [
                    jnp.concatenate([spread(0, head), spread(1, head)], axis=1) for head in range(2)
                ]
                return jnp.concatenate(heads, axis=0)

            def visit(index, totals):
                key_total, value_total = totals
                later = self.two_blocks(self.q_all, index, lanes)
                later_grads = self.two_blocks(self.grad_all, index, lanes)
                scores = dot_rows(own_keys, later) + self.bias(self.key_bias, index)
                attention = jnp.exp(scores - stat_rows(index, 0))
                grad_attention = dot_rows(own_values, later_grads)
                grad_scores = attention * (grad_attention - stat_rows(index, 16))
                key_total = key_total + jnp.dot(
                    grad_scores.astype(BF16), later, preferred_element_type=F32
                )
                value_total = value_total + jnp.dot(
                    attention.astype(BF16), later_grads, preferred_element_type=F32
                )
                return key_total, value_total

            if fresh:
                zeros = jnp.zeros((2 * rows, LANES), F32)
                totals = (zeros, zeros)
            else:
                totals = (self.key_sum[pair], self.value_sum[pair])
            self.key_sum[pair], self.value_sum[pair] = lax.fori_loop(first, last, visit, totals)
            return carried

        lax.fori_loop(0, PAIRS, visit_pair, 0)

    def near_keys(self):
        self.key_grads(self.place.block // 2, 2 * self.place.y + 2, True)

    def far_keys(self):
        @pl.when(self.place.y == 0)
        def _():
            self.key_grads(2, 4, False)

    def store(self, out_ref):
        def visit(pair, carried):
            out_ref[:, self.lanes(pair)] = (one_pair(self.query_sum[pair]) * SCALE).astype(BF16)
            out_ref[:, self.lanes(pair, 1)] = (one_pair(self.key_sum[pair]) * SCALE).astype(BF16)
            out_ref[:, self.lanes(pair, 2)] = one_pair(self.value_sum[pair]).astype(BF16)
            return carried

        lax.fori_loop(0, PAIRS, visit, 0)


def attention_scratch(rows):
    return [
        pltpu.VMEM((8, rows, 2 * D), BF16),
        pltpu.VMEM((8, rows, D), BF16),
        pltpu.VMEM((8, rows, D), BF16),
        pltpu.VMEM((8, 32, rows), F32),
        pltpu.VMEM((rows, 8 * rows), F32),
        pltpu.VMEM((rows, 8 * rows), F32),
        pltpu.VMEM((PAIRS, 2 * rows, LANES), F32),
        pltpu.VMEM((PAIRS, 2 * rows, LANES), F32),
        pltpu.VMEM((PAIRS, 2 * rows, LANES), F32),
    ]


ATTENTION_SCRATCH = 9


def attend_back_kernel(
    grad_ref,
    stats_ref,
    lse_ref,
    delta_ref,
    segs_ref,
    vectors_ref,
    kv_ref,
    rows_ref,
    weight_ref,
    out_ref,
    *scratch,
):
    kv_all, q_all, grad_all, stats_all = scratch[:4]
    biases, sums = scratch[4:6], scratch[6:9]
    rows_all, weight, send_sems, recv_sems, local_sems = scratch[ATTENTION_SCRATCH:]
    place = Place()
    loads = [
        pltpu.make_async_copy(src, dst, local_sems.at[i])
        for i, (src, dst) in enumerate(
            ((rows_ref, rows_all), (weight_ref.at[:, pl.ds(0, D)], weight), (kv_ref, kv_all))
        )
    ]
    for load in loads:
        load.start()
    greet((place.sibling, place.over_x, place.over_y))
    copies = Copies(send_sems, recv_sems)
    gather = BlockGather(place, copies, [grad_ref, stats_ref], [grad_all, stats_all])
    gather.begin()
    grads = AttentionGrads(
        place, grad_ref, lse_ref, delta_ref, segs_ref, kv_all, q_all, grad_all, stats_all, biases, sums
    )
    grads.masks()
    loads[0].wait()
    loads[1].wait()
    grads.project(rows_all, weight, vectors_ref[6:7, :])
    gather.first_halves()
    loads[2].wait()
    gather.second_halves()
    grads.query_grads(0, 3)
    gather.corners()
    grads.query_grads(3, PAIRS)
    gather.wait_near()
    grads.near_keys()
    gather.wait_far()
    grads.far_keys()
    grads.store(out_ref)
    gather.finish()


def attend_back(grads, stats, lse, delta, segs, state, weight, vectors, collective_id):
    kv, rows_all = state
    rows = grads.shape[0]
    slots = 2 * BLOCK_COPIES
    vmem = pl.BlockSpec(memory_space=pltpu.VMEM)
    anywhere = pl.BlockSpec(memory_space=pl.ANY)
    return pl.pallas_call(
        attend_back_kernel,
        in_specs=[vmem] * 6 + [anywhere] * 3,
        out_specs=vmem,
        out_shape=jax.ShapeDtypeStruct((rows, 3 * D), BF16),
        scratch_shapes=attention_scratch(rows)
        + [
            pltpu.VMEM((8, rows, D), BF16),
            pltpu.VMEM((D, D), BF16),
            pltpu.SemaphoreType.DMA((slots,)),
            pltpu.SemaphoreType.DMA((slots,)),
            pltpu.SemaphoreType.DMA((3,)),
        ],
        compiler_params=pltpu.CompilerParams(
            collective_id=collective_id, has_side_effects=True, vmem_limit_bytes=36 << 20
        ),
        name="attend_back",
    )(grads, stats, lse, delta, segs, vectors, kv, rows_all, weight)


CHUNK_ROWS, CHUNK_COLUMNS = 192, 768
REDUCE_COPIES = 9
VECTOR_AXES = 5


def chunk_places(shapes):
    places = [
        (which, row, column, CHUNK_COLUMNS)
        for which, (rows, columns) in enumerate(shapes)
        for row in range(0, rows, CHUNK_ROWS)
        for column in range(0, columns, CHUNK_COLUMNS)
    ]
    which, row, column, width = places.pop()
    cut = 2 * width // 3
    return places + [(which, row, column, cut), (which, row, column + cut, width - cut)]


CORE_SLOTS = 4
REDUCE_STAGES = ("core0", "core1", "y", "x", "z", "zz", "zz_back", "z_back", "x_back")


class GradientSum:
    def __init__(self, place, copies, places, sums, buffers):
        self.place = place
        (
            self.own,
            self.got_core,
            self.got_y,
            self.to_x,
            self.got_x,
            self.to_z,
            self.got_z,
            self.to_zz,
            self.got_zz,
            self.to_core,
        ) = buffers
        self.places = places
        self.x_rows, self.z_rows = CHUNK_ROWS // 2, CHUNK_ROWS // 4
        x, y, low, high = place.x, place.y, place.low, place.high
        self.plans = []
        self.finals = []
        for k, (which, row, column, width) in enumerate(places):
            out = sums[which]
            half = width // 2

            def piece(first, rows, start, columns, out=out, row=row, column=column):
                return out.at[
                    pl.ds(pl.multiple_of(row + first, 16), rows),
                    pl.ds(pl.multiple_of(column + start, LANES), columns),
                ]

            def wide_part(ref, *index, columns=width):
                return ref.at[(*index, slice(None), pl.ds(0, columns))]

            final = piece(x * self.x_rows + low * self.z_rows, self.z_rows, high * half, half)
            wide = piece(x * self.x_rows + low * self.z_rows, self.z_rows, 0, width)
            tall = piece(x * self.x_rows, self.x_rows, 0, width)
            slot = k % CORE_SLOTS
            moves = (
                (wide_part(self.to_core, slot, 0), wide_part(self.got_core, k, 0), place.sibling),
                (wide_part(self.to_core, slot, 1), wide_part(self.got_core, k, 1), place.sibling),
                (wide_part(self.own, k, 1 - y), wide_part(self.got_y, k), place.over_y),
                (wide_part(self.to_x, k), wide_part(self.got_x, k), place.over_x),
                (wide_part(self.to_z, k), wide_part(self.got_z, k), place.over_z),
                (
                    wide_part(self.to_zz, k, columns=half),
                    wide_part(self.got_zz, k, columns=half),
                    place.over_zz,
                ),
                (final, final, place.over_zz),
                (wide, wide, place.over_z),
                (tall, tall, place.over_x),
            )
            self.plans.append(
                {name: copies.make(*move) for name, move in zip(REDUCE_STAGES, moves)}
            )
            self.finals.append(final)
        self.stages = (
            self.stage_x,
            self.stage_z,
            self.stage_zz,
            self.stage_final,
            self.stage_z_back,
            self.stage_x_back,
        )

    def make(self, which, left, right):
        core = self.place.core
        for k, (owner, row, column, width) in enumerate(self.places):
            if owner != which:
                continue
            quarter_rows = left.shape[0] // 4

            def term(quarter):
                first = pl.multiple_of(quarter * quarter_rows + row, 16)
                rows = left[pl.ds(first, CHUNK_ROWS), :]
                columns = right[:, column : column + width]
                return jnp.dot(rows, columns, preferred_element_type=F32).astype(BF16)

            if k >= CORE_SLOTS:
                for name in ("core0", "core1"):
                    self.plans[k - CORE_SLOTS][name].wait_send()
            for i in range(2):
                self.to_core[k % CORE_SLOTS, i, :, :width] = term(2 * i + 1 - core)
            self.plans[k]["core0"].start()
            self.plans[k]["core1"].start()
            for i in range(2):
                self.own[k, i, :, :width] = term(2 * i + core)

    def add_up(self, store, loads, rows):
        step = self.z_rows

        def visit(index, carried):
            offset = pl.multiple_of(index * step, 16)
            total = loads[0](offset, step).astype(F32)
            for load in loads[1:]:
                total = total + load(offset, step).astype(F32)
            store(offset, step, total.astype(BF16))
            return carried

        if rows == step:
            visit(0, 0)
        else:
            lax.fori_loop(0, rows // step, visit, 0)

    def slab(self, ref, *index, first=0, start=0, width=None):
        def load(offset, rows):
            place = pl.ds(pl.multiple_of(first + offset, 16), rows)
            return ref[(*index, place, pl.ds(pl.multiple_of(start, LANES), width))]

        return load

    def stage_y(self, k):
        plan, y, width = self.plans[k], self.place.y, self.places[k][3]
        plan["core0"].wait_recv()
        plan["core1"].wait_recv()

        def store(offset, rows, value):
            self.own[k, 1 - y, pl.ds(offset, rows), :width] = value

        loads = [
            self.slab(self.own, k, 1 - y, width=width),
            self.slab(self.got_core, k, 1 - y, width=width),
        ]
        self.add_up(store, loads, CHUNK_ROWS)
        plan["y"].start()

    def terms_at(self, k, first, depth, inner=0, start=0, width=None):
        y = self.place.y
        part = {"start": start, "width": self.places[k][3] if width is None else width}
        loads = [
            self.slab(self.own, k, y, first=first, **part),
            self.slab(self.got_core, k, y, first=first, **part),
            self.slab(self.got_y, k, first=first, **part),
        ]
        if depth > 0:
            loads.append(self.slab(self.got_x, k, first=inner, **part))
        if depth > 1:
            loads.append(self.slab(self.got_z, k, **part))
        return loads

    def stage_x(self, k):
        plan, width = self.plans[k], self.places[k][3]
        plan["y"].wait_recv()

        def store(offset, rows, value):
            self.to_x[k, pl.ds(offset, rows), :width] = value

        self.add_up(store, self.terms_at(k, (1 - self.place.x) * self.x_rows, 0), self.x_rows)
        plan["x"].start()

    def stage_z(self, k):
        plan, width = self.plans[k], self.places[k][3]
        plan["x"].wait_recv()
        inner = (1 - self.place.low) * self.z_rows

        def store(offset, rows, value):
            self.to_z[k, :, :width] = value

        first = self.place.x * self.x_rows + inner
        self.add_up(store, self.terms_at(k, first, 1, inner), self.z_rows)
        plan["z"].start()

    def last_terms(self, k, side):
        inner = self.place.low * self.z_rows
        first = self.place.x * self.x_rows + inner
        half = self.places[k][3] // 2
        return self.terms_at(k, first, 2, inner, side * half, half)

    def stage_zz(self, k):
        plan, half = self.plans[k], self.places[k][3] // 2
        plan["z"].wait_recv()

        def store(offset, rows, value):
            self.to_zz[k, :, :half] = value

        self.add_up(store, self.last_terms(k, 1 - self.place.high), self.z_rows)
        plan["zz"].start()

    def stage_final(self, k):
        plan, half = self.plans[k], self.places[k][3] // 2
        plan["zz"].wait_recv()

        def store(offset, rows, value):
            self.finals[k][...] = value

        terms = self.last_terms(k, self.place.high)
        self.add_up(store, terms + [self.slab(self.got_zz, k, width=half)], self.z_rows)
        plan["zz_back"].start()

    def stage_z_back(self, k):
        self.plans[k]["zz_back"].wait_recv()
        self.plans[k]["z_back"].start()

    def stage_x_back(self, k):
        self.plans[k]["z_back"].wait_recv()
        self.plans[k]["x_back"].start()

    def ticks(self):
        return len(self.plans) + len(self.stages) - 1

    def tick(self, tick):
        for lag, stage in enumerate(self.stages):
            if 0 <= tick - lag < len(self.plans):
                stage(tick - lag)

    def finish(self):
        for k, plan in enumerate(self.plans):
            plan["x_back"].wait_recv()
            waited = k + CORE_SLOTS < len(self.plans)
            for name in REDUCE_STAGES[2:] if waited else REDUCE_STAGES:
                plan[name].wait_send()


def reduce_scratch(chunks):
    rows, columns = CHUNK_ROWS, CHUNK_COLUMNS
    shapes = [
        (chunks, 2, rows, columns),
        (chunks, 2, rows, columns),
        (chunks, rows, columns),
        (chunks, rows // 2, columns),
        (chunks, rows // 2, columns),
        (chunks, rows // 4, columns),
        (chunks, rows // 4, columns),
        (chunks, rows // 4, columns // 2),
        (chunks, rows // 4, columns // 2),
        (CORE_SLOTS, 2, rows, columns),
    ]
    return [pltpu.VMEM(shape, BF16) for shape in shapes]


REDUCE_SCRATCH = 10
CLOSING_INPUTS = 11


def closing_kernel(places, count, *refs):
    (
        grad_ref,
        stats_ref,
        lse_ref,
        delta_ref,
        segs_ref,
        normal_ref,
        inverse_ref,
        gain_ref,
        middle_ref,
        terms_ref,
        vectors_ref,
    ) = refs[:CLOSING_INPUTS]
    refs = refs[CLOSING_INPUTS:]
    factors = refs[: 4 * count - 1]
    rows_ref, kv_ref, weight_ref = refs[4 * count - 1 : 4 * count + 2]
    refs = refs[4 * count + 2 :]
    sums, vector_out, tokens_out = refs[:count], refs[count], refs[count + 1]
    refs = refs[count + 2 :]
    kv_all, q_all, grad_all, stats_all = refs[:4]
    biases, attention_sums = refs[4:6], refs[6:9]
    refs = refs[ATTENTION_SCRATCH:]
    buffers = refs[:REDUCE_SCRATCH]
    (
        grads_ref,
        grad_rows,
        weight,
        left,
        right,
        vector_got,
        tokens_own,
        send_sems,
        recv_sems,
        local_sems,
    ) = refs[REDUCE_SCRATCH:]

    place = Place()
    load_kv = pltpu.make_async_copy(kv_ref, kv_all, local_sems.at[0])
    load_weight = pltpu.make_async_copy(weight_ref, weight, local_sems.at[1])
    load_rows = pltpu.make_async_copy(rows_ref, grad_rows, local_sems.at[2])
    load_kv.start()
    load_rows.start()
    load_weight.start()
    greet_with_partner(
        place, (place.sibling, place.over_x, place.over_y, place.over_z, place.over_zz)
    )
    copies = Copies(send_sems, recv_sems)
    gather = BlockGather(place, copies, [grad_ref, stats_ref], [grad_all, stats_all])
    swap = copies.make(tokens_own, tokens_out, place.partner)
    reduce = GradientSum(place, copies, places, sums, buffers)
    chunks = len(places)
    by_weight = [[k for k in range(chunks) if places[k][0] == which] for which in range(count)]
    vector_devices = (place.over_x, place.over_z, place.over_zz, place.sibling, place.over_y)
    vector_copies = [
        copies.make(vector_out, vector_got.at[i], device)
        for i, device in enumerate(vector_devices)
    ]
    tokens = grad_ref.shape[0]

    def make_terms(which, last_right=None):
        later_left, later_right, first_left = factors[4 * which : 4 * which + 3]
        rows, columns = later_left.shape[1], later_right.shape[1]
        left[:rows, :tokens] = later_left[...].T
        left[:rows, tokens:] = first_left[...].T
        right[:tokens, :columns] = later_right[...]
        if last_right is None:
            right[tokens:, :columns] = factors[4 * which + 3][...]
        else:
            right[tokens:, :columns] = last_right
        reduce.make(which, left.at[pl.ds(0, rows), :], right)

    gather.begin()
    make_terms(0)
    grads = AttentionGrads(
        place,
        grad_ref,
        lse_ref,
        delta_ref,
        segs_ref,
        kv_all,
        q_all,
        grad_all,
        stats_all,
        biases,
        attention_sums,
    )
    gather.first_halves()
    for k in by_weight[0]:
        reduce.stage_y(k)
    gather.second_halves()
    grads.masks()
    load_rows.wait()
    load_weight.wait()
    grads.project(grad_rows, weight, vectors_ref[6:7, :])
    load_kv.wait()
    grads.query_grads(0, PAIRS)
    gather.corners()
    gather.wait_near()
    make_terms(1)
    for k in by_weight[1]:
        reduce.stage_y(k)
    reduce.tick(0)
    grads.near_keys()
    gather.wait_far()
    reduce.tick(1)
    grads.far_keys()
    grads.store(grads_ref)
    reduce.tick(2)
    make_terms(2)
    for k in by_weight[2]:
        reduce.stage_y(k)
    own_grads = grads_ref[...]
    make_terms(3, own_grads)
    reduce.tick(3)
    grad_normed = dot_rows(own_grads, weight[...])
    grad_input, grad_gain, grad_bias = norm_backward(
        grad_normed, normal_ref[...], inverse_ref[...], gain_ref[...]
    )
    swapped = (middle_ref[...] + grad_input).astype(BF16)
    tokens_own[...] = swapped

    @pl.when(place.has_partner)
    def _():
        swap.start()

    @pl.when(jnp.logical_not(place.has_partner))
    def _():
        tokens_out[...] = swapped

    vector_out[...] = terms_ref[...]
    query_bias = jnp.sum(own_grads[:, :D].astype(F32), axis=0, keepdims=True)
    value_bias = jnp.sum(own_grads[:, 2 * D :].astype(F32), axis=0, keepdims=True)
    for row, value in ((0, grad_gain[None]), (1, grad_bias[None]), (6, query_bias), (7, value_bias)):
        vector_out[row : row + 1, :] = vector_out[row : row + 1, :] + value
    vector_copies[0].start()
    for k in by_weight[3]:
        reduce.stage_y(k)

    def vector_step(index):
        vector_copies[index].wait()
        vector_out[...] = vector_out[...] + vector_got[index]
        if index + 1 < VECTOR_AXES:
            vector_copies[index + 1].start()

    for tick in range(4, reduce.ticks()):
        reduce.tick(tick)
        if tick - 4 < VECTOR_AXES - 1:
            vector_step(tick - 4)
    vector_step(VECTOR_AXES - 1)
    reduce.finish()
    gather.finish()

    @pl.when(place.has_partner)
    def _():
        swap.wait_recv()
        swap.wait_send()


def closing(attention, norm, terms, factors, weight, vectors, collective_id):
    grads, stats, lse, delta, segs, (kv, rows_all) = attention
    rows = grads.shape[0]
    count = len(factors)
    shapes = [(group[0].shape[1] // 4, group[1].shape[1]) for group in factors]
    places = chunk_places(shapes)
    chunks = len(places)
    slots = chunks * REDUCE_COPIES + VECTOR_AXES + 2 * BLOCK_COPIES + 1
    flat = [factor for group in factors for factor in group]
    tallest = max(group[0].shape[1] for group in factors)
    widest = max(group[1].shape[1] for group in factors)
    vmem = pl.BlockSpec(memory_space=pltpu.VMEM)
    anywhere = pl.BlockSpec(memory_space=pl.ANY)
    return pl.pallas_call(
        partial(closing_kernel, places, count),
        in_specs=[vmem] * (CLOSING_INPUTS + len(flat)) + [anywhere] * 3,
        out_specs=[vmem] * (count + 2),
        out_shape=[jax.ShapeDtypeStruct(shape, BF16) for shape in shapes]
        + [jax.ShapeDtypeStruct(terms.shape, F32), jax.ShapeDtypeStruct((rows, D), BF16)],
        scratch_shapes=attention_scratch(rows)
        + reduce_scratch(chunks)
        + [
            pltpu.VMEM((rows, 3 * D), BF16),
            pltpu.VMEM((8, rows, D), BF16),
            pltpu.VMEM(weight.shape, BF16),
            pltpu.VMEM((tallest, 2 * rows), BF16),
            pltpu.VMEM((2 * rows, widest), BF16),
            pltpu.VMEM((VECTOR_AXES, *terms.shape), F32),
            pltpu.VMEM((rows, D), BF16),
            pltpu.SemaphoreType.DMA((slots,)),
            pltpu.SemaphoreType.DMA((slots,)),
            pltpu.SemaphoreType.DMA((3,)),
        ],
        compiler_params=pltpu.CompilerParams(
            collective_id=collective_id, has_side_effects=True, vmem_limit_bytes=60 << 20
        ),
        name="closing",
    )(grads, stats, lse, delta, segs, *norm, terms, vectors, *flat, rows_all, kv, weight)


class PlaneLinks:
    def leave(self, value):
        pairs = [(c * 4 + f, (2 * f + c % 2) * 4 + c // 2) for c in range(8) for f in range(4)]
        return lax.ppermute(value, ("ctx", "fsdp"), pairs)

    def open(self, tokens, segs_row, vectors, shares):
        tokens, segs, vectors, *results = opening(tokens, segs_row, vectors, shares[0], shares[1:], 0)
        *first, kv, rows_all = results[:8]
        return tokens.astype(F32), segs, vectors, as_matrices(results[8:]), (*first, (kv, rows_all))

    def attend(self, normed, vectors, weight, segs, cotangent):
        attended, lse, lse_rows, kv, rows_all, cotangent = attend(
            normed, segs, vectors, weight, cotangent, 2
        )
        return (attended, lse, lse_rows, (kv, rows_all)), cotangent

    def attend_back(self, attention, weight, vectors):
        return attend_back(*attention, weight, vectors, 3)

    def close(self, attention, norm, factors, terms, weight, vectors):
        *sums, terms, tokens_grad = closing(attention, norm, terms, factors, weight, vectors, 4)
        return [total.astype(F32) for total in sums], terms, tokens_grad


class PlainLinks:
    def leave(self, value):
        return value

    def open(self, tokens, segs_row, vectors, shares):
        segs = (segs_row, lax.all_gather(segs_row, "ctx", axis=1, tiled=True))
        gathered = lax.all_gather(pack_vectors(*vectors), "fsdp", axis=0)
        vectors = assemble_vectors([gathered[i] for i in range(4)])
        weights = as_matrices([lax.all_gather(share, "fsdp", axis=0) for share in shares])
        resid = tokens.astype(F32)
        first = norm_forward(resid, vectors[0:1], vectors[1:2])
        first = first + self.attend(first[0], vectors, weights[0], segs, None)[0]
        return resid, segs, vectors, weights, first

    def place(self, segs):
        own_segs, all_segs = segs
        rows = own_segs.shape[1]
        start = (lax.axis_index("ctx") * rows).reshape(1).astype(jnp.int32)
        return start, own_segs.reshape(rows, 1), all_segs

    def blocks(self, block):
        return lax.all_gather(block, "ctx", axis=0)

    def attend(self, normed, vectors, weight, segs, cotangent):
        start, own_segs, all_segs = self.place(segs)
        bias = jnp.concatenate([vectors[6:7], jnp.zeros((1, D), F32), vectors[7:8]], axis=1)
        projected = (jnp.dot(normed, weight, preferred_element_type=F32) + bias).astype(BF16)
        queries, kv_own = projected[:, :D], projected[:, D:]
        kv = self.blocks(kv_own).reshape(-1, 2 * D)
        attended, lse, lse_rows = attention_forward(start, queries, kv, own_segs, all_segs)
        return (attended, lse, lse_rows, (queries, kv_own, kv)), cotangent

    def attend_back(self, attention, weight, vectors):
        grads, stats, lse, delta, segs, (queries, kv_own, kv) = attention
        start, own_segs, all_segs = self.place(segs)
        q_all = self.blocks(queries).reshape(-1, D)
        grad_all = self.blocks(grads).reshape(-1, D)
        return attention_backward(
            start,
            queries,
            grads,
            kv_own,
            lse,
            delta,
            kv,
            q_all,
            grad_all,
            self.blocks(stats),
            own_segs,
            all_segs,
        )

    def close(self, attention, norm, factors, terms, weight, vectors):
        grad_projected = self.attend_back(attention, weight, vectors)
        grad_input, more = input_gradient(grad_projected, weight, *norm)
        terms = terms + jnp.concatenate(
            [more[:2], jnp.zeros((4, D), F32), more[2:], jnp.zeros((8, D), F32)], axis=0
        )
        sums = []
        for later_left, later_right, first_left, *first_right in factors:
            left = jnp.concatenate([later_left, first_left], axis=0)
            right = jnp.concatenate([later_right, *(first_right or [grad_projected])], axis=0)
            term = column_products(left, right).astype(BF16)
            share = lax.psum_scatter(term, "fsdp", scatter_dimension=0, tiled=True)
            sums.append(lax.psum(share.astype(F32), "ctx"))
        return sums, lax.psum(terms, ("ctx", "fsdp")), grad_input.astype(BF16)


def as_matrices(fulls):
    return tuple(full.reshape(-1, full.shape[-1]) for full in fulls)


def layer_forward(resid, weights, vectors, first):
    gain_two, bias_two, bias_proj, bias_out = (vectors[i : i + 1] for i in range(2, 6))
    bias_fc = vectors[8:12].reshape(1, 4 * D)
    _, weight_proj, weight_fc, weight_out = weights
    normed_one, normal_one, inverse_one, attended, lse, lse_rows, state = first
    middle = resid + jnp.dot(attended, weight_proj, preferred_element_type=F32) + bias_proj
    normed_two, normal_two, inverse_two = norm_forward(middle, gain_two, bias_two)
    hidden = jnp.dot(normed_two, weight_fc, preferred_element_type=F32) + bias_fc
    activated = jax.nn.gelu(hidden, approximate=True).astype(BF16)
    result_rows = middle + jnp.dot(activated, weight_out, preferred_element_type=F32) + bias_out
    saved = (
        normed_one,
        normal_one,
        inverse_one,
        state,
        attended,
        lse,
        lse_rows,
        normed_two,
        normal_two,
        inverse_two,
        hidden,
        activated,
    )
    return result_rows, saved


def layer_backward(gradient, weights, vectors, saved, links, segs):
    weight_qkv, weight_proj, weight_fc, weight_out = weights
    gain_one, gain_two = vectors[0:1], vectors[2:3]
    (
        normed_one,
        normal_one,
        inverse_one,
        state,
        attended,
        lse,
        lse_rows,
        normed_two,
        normal_two,
        inverse_two,
        hidden,
        activated,
    ) = saved
    total = lambda value: jnp.sum(value.astype(F32), axis=0)
    grad_branch = gradient.astype(BF16)
    grad_activated = dot_rows(grad_branch, weight_out)
    gelu_pull = jax.vjp(partial(jax.nn.gelu, approximate=True), hidden)[1]
    grad_hidden = gelu_pull(grad_activated)[0].astype(BF16)
    grad_normed_two = dot_rows(grad_hidden, weight_fc)
    grad_in_two, grad_gain_two, grad_bias_two = norm_backward(
        grad_normed_two, normal_two, inverse_two, gain_two
    )
    grad_middle = gradient + grad_in_two
    grad_proj = grad_middle.astype(BF16)
    grad_attended = dot_rows(grad_proj, weight_proj).astype(BF16)
    products = grad_attended.astype(F32) * attended.astype(F32)
    head_of = jnp.arange(D, dtype=jnp.int32) // HDIM
    by_lane = (head_of[:, None] == jnp.arange(LANES, dtype=jnp.int32)[None, :]).astype(F32)
    by_row = (jnp.arange(16, dtype=jnp.int32)[:, None] == head_of[None, :]).astype(F32)
    delta = jnp.dot(products, by_lane, precision=lax.Precision.HIGHEST, preferred_element_type=F32)
    delta_rows = lax.dot_general(
        by_row,
        products,
        (((1,), (1,)), ((), ())),
        precision=lax.Precision.HIGHEST,
        preferred_element_type=F32,
    )
    stats = jnp.concatenate([lse_rows, delta_rows], axis=0)
    attention = (grad_attended, stats, lse, delta, segs, state)
    norm = (normal_one, inverse_one, gain_one, grad_middle)
    matrices = ((activated, grad_branch), (normed_two, grad_hidden), (attended, grad_proj))
    upper = jnp.stack([grad_gain_two, grad_bias_two, total(grad_proj), total(grad_branch)])
    lower = total(grad_hidden).reshape(4, D)
    return attention, norm, matrices, (upper, lower)


def input_gradient(grad_projected, weight_qkv, normal, inverse, gain, middle):
    total = lambda value: jnp.sum(value.astype(F32), axis=0)
    grad_normed = dot_rows(grad_projected, weight_qkv)
    grad_in, grad_gain, grad_bias = norm_backward(grad_normed, normal, inverse, gain)
    terms = [
        grad_gain,
        grad_bias,
        total(grad_projected[:, :D]),
        total(grad_projected[:, 2 * D :]),
    ]
    return middle + grad_in, jnp.stack(terms)


def body(
    links,
    tokens,
    segment_ids,
    ln1_gain,
    ln1_bias,
    attn_weight,
    attn_bias,
    proj_weight,
    proj_bias,
    ln2_gain,
    ln2_bias,
    fc_weight,
    fc_bias,
    out_weight,
    out_bias,
    out_cotangent,
):
    vectors = (
        ln1_gain,
        ln1_bias,
        ln2_gain,
        ln2_bias,
        proj_bias,
        out_bias,
        attn_bias,
        fc_bias,
    )
    shares = [attn_weight, proj_weight, fc_weight, out_weight]
    resid, segs, vectors, weights, first = links.open(tokens[0], segment_ids, vectors, shares)
    resid, saved = layer_forward(resid, weights, vectors, first)
    saved_layers = [saved]
    first = norm_forward(resid, vectors[0:1], vectors[1:2])
    attended, gradient = links.attend(first[0], vectors, weights[0], segs, out_cotangent[0])
    resid, saved = layer_forward(resid, weights, vectors, first + attended)
    saved_layers.append(saved)
    output = links.leave(resid.astype(BF16))
    gradient = gradient.astype(F32)
    attention, norm, later, (upper, lower) = layer_backward(
        gradient, weights, vectors, saved_layers[1], links, segs
    )
    later_projected = links.attend_back(attention, weights[0], vectors)
    gradient, terms = input_gradient(later_projected, weights[0], *norm)
    attention, norm, first, (more_upper, more_lower) = layer_backward(
        gradient, weights, vectors, saved_layers[0], links, segs
    )
    factors = [(*a, *b) for a, b in zip(later, first)]
    factors.append((saved_layers[1][0], later_projected, saved_layers[0][0]))
    packed = jnp.concatenate(
        [terms[:2], upper + more_upper, terms[2:], lower + more_lower, jnp.zeros((4, D), F32)], axis=0
    )
    (out_grad, fc_grad, proj_grad, qkv_grad), summed, tokens_grad = links.close(
        attention, norm, factors, packed, weights[0], vectors
    )
    own = lax.axis_index("fsdp")
    pick = lambda value, axis: lax.dynamic_index_in_dim(value, own, axis, keepdims=False)
    small = pick(summed[:6].reshape(6, 4, -1), 1)
    bias_qv = pick(summed[6:8].reshape(4, -1), 0)
    bias_fc = pick(summed[8:12], 0)
    gain_one, bias_one, gain_two, bias_two, bias_proj, bias_out = (small[i] for i in range(6))
    return (
        output[None],
        tokens_grad[None],
        gain_one,
        bias_one,
        qkv_grad,
        bias_qv,
        proj_grad,
        bias_proj,
        gain_two,
        bias_two,
        fc_grad,
        bias_fc,
        out_grad,
        bias_out,
    )


def solution(mesh):
    links = PlaneLinks() if (mesh.shape["ctx"], mesh.shape["fsdp"]) == (8, 4) else PlainLinks()
    rows = P("fsdp", "ctx", None)
    vector, matrix = P("fsdp"), P("fsdp", None)
    in_specs = (
        rows,
        P("fsdp", "ctx"),
        vector,
        vector,
        matrix,
        vector,
        matrix,
        vector,
        vector,
        vector,
        matrix,
        vector,
        matrix,
        vector,
        rows,
    )
    out_specs = (
        rows,
        rows,
        vector,
        vector,
        matrix,
        vector,
        matrix,
        vector,
        vector,
        vector,
        matrix,
        vector,
        matrix,
        vector,
    )
    return jax.shard_map(
        partial(body, links), mesh=mesh, in_specs=in_specs, out_specs=out_specs, check_vma=False
    )
```

```python
from functools import partial

import jax
import jax.numpy as jnp
from jax import lax
from jax.experimental import pallas as pl
from jax.experimental.pallas import tpu as pltpu
from jax.sharding import PartitionSpec as P

D = 768
HEADS = 12
HDIM = 64
PAIRS = HEADS // 2
LANES = 128
EPSILON = 1e-05
NEGATIVE = -1e30
SCALE = HDIM ** (-0.5)
MESH = pl.DeviceIdType.MESH
F32 = jnp.float32
BF16 = jnp.bfloat16


def norm_forward(resid, gain_row, bias_row):
    average = jnp.mean(resid, axis=-1, keepdims=True)
    centred = resid - average
    variance = jnp.mean(centred * centred, axis=-1, keepdims=True)
    inverse = lax.rsqrt(variance + EPSILON)
    normal = centred * inverse
    return ((normal * gain_row + bias_row).astype(BF16), normal, inverse)


def norm_backward(grad_normed, normal, inverse, gain_row):
    scaled = grad_normed * gain_row
    mean_term = jnp.mean(scaled, axis=-1, keepdims=True)
    second = jnp.mean(scaled * normal, axis=-1, keepdims=True)
    grad_input = inverse * (scaled - mean_term - normal * second)
    return (grad_input, jnp.sum(grad_normed * normal, axis=0), jnp.sum(grad_normed, axis=0))


def two_heads(rows):
    lane = lax.broadcasted_iota(jnp.int32, rows.shape, 1)
    zero = jnp.zeros_like(rows)
    first = jnp.where(lane < HDIM, rows, zero)
    second = jnp.where(lane < HDIM, zero, rows)
    return jnp.concatenate([first, second], axis=0)


def one_pair(stacked):
    half = stacked.shape[0] // 2
    lane = lax.broadcasted_iota(jnp.int32, (half, LANES), 1)
    return jnp.where(lane < HDIM, stacked[:half], stacked[half:])


def dot_rows(left, right):
    return lax.dot_general(left, right, (((1,), (1,)), ((), ())), preferred_element_type=F32)


def column_products(left, right):
    return lax.dot_general(left, right, (((0,), (0,)), ((), ())), preferred_element_type=F32)


def pick_lanes(columns, pair):
    lane = lax.broadcasted_iota(jnp.int32, columns.shape, 1)
    first = jnp.sum(jnp.where(lane == 2 * pair, columns, 0.0), axis=1, keepdims=True)
    second = jnp.sum(jnp.where(lane == 2 * pair + 1, columns, 0.0), axis=1, keepdims=True)
    return jnp.concatenate([first, second], axis=0)


def mask_columns(bias_ref, own_segs, all_segs_ref, start, own_is_query):
    rows, columns = bias_ref.shape
    step = min(1024, columns)
    own_place = start + lax.broadcasted_iota(jnp.int32, (rows, step), 0)
    for offset in range(0, columns, step):
        place = offset + lax.broadcasted_iota(jnp.int32, (rows, step), 1)
        causal = (place <= own_place) if own_is_query else (own_place <= place)
        same = own_segs == all_segs_ref[:, offset : offset + step]
        bias_ref[:, offset : offset + step] = jnp.where(causal & same, 0.0, NEGATIVE)


def attention_forward_kernel(
    start_ref, q_ref, k_ref, v_ref, own_segs_ref, all_segs_ref, out_ref, lse_ref, lse_rows_ref, bias_ref
):
    pair = pl.program_id(0)
    rows, keys = bias_ref.shape

    @pl.when(pair == 0)
    def _():
        mask_columns(bias_ref, own_segs_ref[...], all_segs_ref, start_ref[0], True)
        lse_ref[...] = jnp.zeros_like(lse_ref)

    queries = two_heads(q_ref[...] * jnp.asarray(SCALE, BF16))
    step = min(1024, keys)

    def scores_of(offset):
        scores = dot_rows(queries, k_ref[pl.ds(offset, step), :])
        bias = bias_ref[:, pl.ds(offset, step)]
        return scores + jnp.concatenate([bias, bias], axis=0)

    if step == keys:
        scores = scores_of(0)
        top = jnp.max(scores, axis=1, keepdims=True)
        weights = jnp.exp(scores - top)
        total = jnp.sum(weights, axis=1, keepdims=True)
        mixed = jnp.dot(weights.astype(BF16), v_ref[...], preferred_element_type=F32)
    else:

        def visit(index, carried):
            top, total, mixed = carried
            offset = pl.multiple_of(index * step, step)
            scores = scores_of(offset)
            new_top = jnp.maximum(top, jnp.max(scores, axis=1, keepdims=True))
            weights = jnp.exp(scores - new_top)
            factor = jnp.exp(top - new_top)
            total = total * factor + jnp.sum(weights, axis=1, keepdims=True)
            more = jnp.dot(
                weights.astype(BF16), v_ref[pl.ds(offset, step), :], preferred_element_type=F32
            )
            return new_top, total, mixed * factor + more

        top, total, mixed = lax.fori_loop(
            0,
            (start_ref[0] + rows + step - 1) // step,
            visit,
            (
                jnp.full((2 * rows, 1), NEGATIVE, F32),
                jnp.zeros((2 * rows, 1), F32),
                jnp.zeros((2 * rows, LANES), F32),
            ),
        )
    out_ref[...] = one_pair(mixed / total).astype(BF16)
    lse = top + jnp.log(total)
    lane = lax.broadcasted_iota(jnp.int32, (rows, LANES), 1)
    kept = lse_ref[...]
    kept = jnp.where(lane == 2 * pair, lse[:rows], kept)
    kept = jnp.where(lane == 2 * pair + 1, lse[rows:], kept)
    lse_ref[...] = kept

    @pl.when(pair == PAIRS - 1)
    def _():
        lse_rows_ref[...] = kept.T[:16]


def attention_forward(start, queries, kv, own_segs, all_segs):
    rows = queries.shape[0]
    keys = kv.shape[0]
    whole = lambda shape: pl.BlockSpec(shape, lambda p: (0, 0))
    return pl.pallas_call(
        attention_forward_kernel,
        grid=(PAIRS,),
        in_specs=[
            pl.BlockSpec(memory_space=pltpu.SMEM),
            pl.BlockSpec((rows, LANES), lambda p: (0, p)),
            pl.BlockSpec((keys, LANES), lambda p: (0, p)),
            pl.BlockSpec((keys, LANES), lambda p: (0, PAIRS + p)),
            whole((rows, 1)),
            whole((1, keys)),
        ],
        out_specs=[
            pl.BlockSpec((rows, LANES), lambda p: (0, p)),
            whole((rows, LANES)),
            whole((16, rows)),
        ],
        out_shape=[
            jax.ShapeDtypeStruct((rows, D), BF16),
            jax.ShapeDtypeStruct((rows, LANES), F32),
            jax.ShapeDtypeStruct((16, rows), F32),
        ],
        scratch_shapes=[pltpu.VMEM((rows, keys), F32)],
        compiler_params=pltpu.CompilerParams(vmem_limit_bytes=60 << 20),
        cost_estimate=pl.CostEstimate(
            flops=8 * rows * keys * D, bytes_accessed=4 * keys * D, transcendentals=rows * keys * HEADS
        ),
        name="attention_forward",
    )(start, queries, kv, kv, own_segs, all_segs)


def attention_backward_kernel(
    start_ref,
    q_ref,
    grad_ref,
    k_own_ref,
    v_own_ref,
    lse_ref,
    delta_ref,
    k_ref,
    v_ref,
    q_all_ref,
    grad_all_ref,
    stats_ref,
    own_segs_ref,
    all_segs_ref,
    out_ref,
    query_bias_ref,
    key_bias_ref,
):
    pair = pl.program_id(0)
    rows, tokens = query_bias_ref.shape
    start = start_ref[0]

    @pl.when(pair == 0)
    def _():
        mask_columns(query_bias_ref, own_segs_ref[...], all_segs_ref, start, True)
        mask_columns(key_bias_ref, own_segs_ref[...], all_segs_ref, start, False)

    step = min(256, tokens)
    blocks = step // rows
    scale = jnp.asarray(SCALE, BF16)

    def doubled(bias):
        return jnp.concatenate([bias, bias], axis=0)

    queries = two_heads(q_ref[...] * scale)
    grads = two_heads(grad_ref[...])
    lse = pick_lanes(lse_ref[...], pair)
    delta = pick_lanes(delta_ref[...], pair)

    def visit_keys(index, grad_query):
        offset = pl.multiple_of(index * step, step)
        keys = k_ref[pl.ds(offset, step), :]
        values = v_ref[pl.ds(offset, step), :]
        bias = doubled(query_bias_ref[:, pl.ds(offset, step)])
        attention = jnp.exp(dot_rows(queries, keys) + bias - lse)
        grad_attention = dot_rows(grads, values)
        grad_scores = (attention * (grad_attention - delta)).astype(BF16)
        return grad_query + jnp.dot(grad_scores, keys, preferred_element_type=F32)

    zeros = jnp.zeros((2 * rows, LANES), F32)
    grad_query = lax.fori_loop(0, (start + rows + step - 1) // step, visit_keys, zeros)

    own_keys = two_heads(k_own_ref[...] * scale)
    own_values = two_heads(v_own_ref[...])

    def row_of(block, row):
        return jnp.broadcast_to(stats_ref[block, pl.ds(row, 1), :], (rows, rows))

    def stat_rows(index, row):
        first = [row_of(index * blocks + b, row + 2 * pair) for b in range(blocks)]
        second = [row_of(index * blocks + b, row + 2 * pair + 1) for b in range(blocks)]
        return jnp.concatenate(
            [jnp.concatenate(first, axis=1), jnp.concatenate(second, axis=1)], axis=0
        )

    def visit_queries(index, carried):
        grad_keys, grad_values = carried
        offset = pl.multiple_of(index * step, step)
        later = q_all_ref[pl.ds(offset, step), :]
        later_grads = grad_all_ref[pl.ds(offset, step), :]
        bias = doubled(key_bias_ref[:, pl.ds(offset, step)])
        attention = jnp.exp(dot_rows(own_keys, later) + bias - stat_rows(index, 0))
        grad_attention = dot_rows(own_values, later_grads)
        grad_scores = (attention * (grad_attention - stat_rows(index, 16))).astype(BF16)
        grad_keys = grad_keys + jnp.dot(grad_scores, later, preferred_element_type=F32)
        grad_values = grad_values + jnp.dot(
            attention.astype(BF16), later_grads, preferred_element_type=F32
        )
        return grad_keys, grad_values

    grad_keys, grad_values = lax.fori_loop(
        start // step, tokens // step, visit_queries, (zeros, zeros)
    )
    base = pl.multiple_of(pair * LANES, LANES)
    out_ref[:, pl.ds(base, LANES)] = (one_pair(grad_query) * SCALE).astype(BF16)
    out_ref[:, pl.ds(D + base, LANES)] = (one_pair(grad_keys) * SCALE).astype(BF16)
    out_ref[:, pl.ds(2 * D + base, LANES)] = one_pair(grad_values).astype(BF16)


def attention_backward(
    start, queries, grads, kv_own, lse, delta, kv, q_all, grad_all, stats, own_segs, all_segs
):
    rows = queries.shape[0]
    tokens = kv.shape[0]
    whole = lambda shape: pl.BlockSpec(shape, lambda p: (0,) * len(shape))
    own = pl.BlockSpec((rows, LANES), lambda p: (0, p))
    every = pl.BlockSpec((tokens, LANES), lambda p: (0, p))
    return pl.pallas_call(
        attention_backward_kernel,
        grid=(PAIRS,),
        in_specs=[
            pl.BlockSpec(memory_space=pltpu.SMEM),
            own,
            own,
            own,
            pl.BlockSpec((rows, LANES), lambda p: (0, PAIRS + p)),
            whole((rows, LANES)),
            whole((rows, LANES)),
            every,
            pl.BlockSpec((tokens, LANES), lambda p: (0, PAIRS + p)),
            every,
            every,
            whole(stats.shape),
            whole((rows, 1)),
            whole((1, tokens)),
        ],
        out_specs=whole((rows, 3 * D)),
        out_shape=jax.ShapeDtypeStruct((rows, 3 * D), BF16),
        scratch_shapes=[pltpu.VMEM((rows, tokens), F32), pltpu.VMEM((rows, tokens), F32)],
        compiler_params=pltpu.CompilerParams(vmem_limit_bytes=60 << 20),
        cost_estimate=pl.CostEstimate(
            flops=16 * rows * tokens * D,
            bytes_accessed=8 * tokens * D,
            transcendentals=rows * tokens * HEADS,
        ),
        name="attention_backward",
    )(
        start,
        queries,
        grads,
        kv_own,
        kv_own,
        lse,
        delta,
        kv,
        kv,
        q_all,
        grad_all,
        stats,
        own_segs,
        all_segs,
    )


def place_bits():
    ctx, fsdp = lax.axis_index("ctx"), lax.axis_index("fsdp")
    return lax.rem(ctx, 2), ctx // 2, fsdp // 2, lax.rem(fsdp, 2)


class Place:
    def __init__(self):
        self.x, self.z, self.y, self.core = x, z, y, core = place_bits()
        self.low, self.high = low, high = lax.rem(z, 2), z // 2
        self.fsdp = fsdp = 2 * y + core
        self.block = 2 * fsdp + x
        self.sibling = (2 * z + x, 2 * y + 1 - core)
        self.over_y = (2 * z + x, 2 * (1 - y) + core)
        self.over_x = (2 * z + 1 - x, fsdp)
        self.over_z = (2 * (z + 1 - 2 * low) + x, fsdp)
        self.over_zz = (2 * (z + 2 - 4 * high) + x, fsdp)
        self.partner = (2 * fsdp + x, z)
        self.has_partner = fsdp != z


class Copies:
    def __init__(self, send_sems, recv_sems):
        self.send_sems, self.recv_sems = send_sems, recv_sems
        self.used = 0

    def make(self, src, dst, device):
        slot = self.used
        self.used += 1
        return pltpu.make_async_remote_copy(
            src_ref=src,
            dst_ref=dst,
            send_sem=self.send_sems.at[slot],
            recv_sem=self.recv_sems.at[slot],
            device_id=device,
            device_id_type=MESH,
        )


def greet(devices):
    barrier = pltpu.get_barrier_semaphore()
    for device in devices:
        pl.semaphore_signal(barrier, inc=1, device_id=device, device_id_type=MESH)
    pl.semaphore_wait(barrier, len(devices))


WEIGHT_COPIES = 11


def weight_cuts(shape):
    rows, columns = shape
    pieces = 1 if rows * columns <= 192 * 768 else 3 if columns == 3 * D else 2
    width = columns // pieces
    return [(i * width, width) for i in range(pieces)]


class WeightGather:
    def __init__(self, place, copies, shares, fulls, stages, local_sems):
        x, low = place.x, place.low
        own, other = place.fsdp, 2 * (1 - place.y) + place.core
        self.plans = []
        self.locals = []
        self.arrived = set()
        for which, (share, full) in enumerate(zip(shares, fulls)):
            part = share.shape[0] // 4
            for first, width in weight_cuts(share.shape):
                columns = pl.ds(first, width)

                def piece(ref, x_bit, low_bit, part=part, columns=columns):
                    return ref.at[pl.ds((2 * low_bit + x_bit) * part, part), columns]

                def side(ref, x_bit, low_bit, index, part=part, first=first, width=width):
                    start = (2 * low_bit + x_bit) * part
                    if part % 32 == 0:
                        rows = pl.ds(start + index * (part // 2), part // 2)
                        return ref.at[rows, pl.ds(first, width)]
                    half = width // 2
                    return ref.at[pl.ds(start, part), pl.ds(first + index * half, half)]

                theirs = full.at[other]
                same = lambda view, device: copies.make(view, view, device)
                mine = piece(theirs, x, low)
                from_x, from_z = piece(theirs, 1 - x, low), piece(theirs, x, 1 - low)
                self.plans.append(
                    [
                        copies.make(piece(share, x, low), piece(full.at[own], x, low), place.over_y),
                        same(mine, place.over_x),
                        same(mine, place.over_z),
                        same(mine, place.sibling),
                        same(side(theirs, 1 - x, low, 0), place.over_z),
                        same(from_x, place.sibling),
                        same(side(theirs, x, 1 - low, 1), place.over_x),
                        same(from_z, place.sibling),
                        same(side(theirs, 1 - x, 1 - low, 0), place.sibling),
                        same(side(theirs, 1 - x, 1 - low, 1), place.sibling),
                        copies.make(share.at[:, columns], full.at[own, :, columns], place.sibling),
                    ]
                )
            sem = local_sems.at[which]
            if stages[which] is None:
                self.locals.append((pltpu.make_async_copy(share, full.at[own], sem), None))
            else:
                self.locals.append(
                    (
                        pltpu.make_async_copy(share, stages[which], sem),
                        pltpu.make_async_copy(stages[which], full.at[own], sem),
                    )
                )

    def begin(self):
        for plan in self.plans:
            plan[0].start()
        for plan in self.plans:
            plan[10].start()
        for into, _ in self.locals:
            into.start()

    def keep_own(self):
        for into, out in self.locals:
            into.wait()
            if out is not None:
                out.start()

    def arrive(self, first, last):
        for index in range(first, last):
            if index not in self.arrived:
                self.arrived.add(index)
                for copy in (3, 5, 7, 8, 9, 10):
                    self.plans[index][copy].wait_recv()

    def steps(self):
        count = len(self.plans)
        for step in range(count + 2):
            yield step

    def step(self, step):
        count = len(self.plans)
        if step < count:
            plan = self.plans[step]
            plan[0].wait_recv()
            plan[1].start()
            plan[2].start()
            plan[3].start()
        if 0 <= step - 1 < count:
            plan = self.plans[step - 1]
            plan[1].wait_recv()
            plan[4].start()
            plan[5].start()
            plan[2].wait_recv()
            plan[6].start()
            plan[7].start()
        if 0 <= step - 2 < count:
            plan = self.plans[step - 2]
            plan[4].wait_recv()
            plan[8].start()
            plan[6].wait_recv()
            plan[9].start()

    def finish(self):
        self.arrive(0, len(self.plans))
        for plan in self.plans:
            for copy in plan:
                copy.wait_send()
        for _, out in self.locals:
            if out is not None:
                out.wait()


BLOCK_COPIES = 13


class BlockGather:
    def __init__(self, place, copies, blocks, fulls):
        self.own = place.block
        self.pairs = list(zip(blocks, fulls))
        self.plans = []
        for block, full in self.pairs:
            half = block.shape[0] // 2

            def part(ref, side, half=half):
                return ref.at[pl.ds(side * half, half), :]

            def slot_of(x_bit, y_bit, full=full):
                return full.at[4 * y_bit + 2 * place.core + x_bit]

            same = lambda view, device: copies.make(view, view, device)
            x, y = place.x, place.y
            mine, from_x = slot_of(x, y), slot_of(1 - x, y)
            from_y, from_both = slot_of(x, 1 - y), slot_of(1 - x, 1 - y)
            self.plans.append(
                [
                    copies.make(block, mine, place.sibling),
                    copies.make(part(block, 0), part(mine, 0), place.over_x),
                    copies.make(part(block, 1), part(mine, 1), place.over_y),
                    copies.make(part(block, 1), part(mine, 1), place.over_x),
                    copies.make(part(block, 0), part(mine, 0), place.over_y),
                    same(part(from_x, 0), place.over_y),
                    same(part(from_x, 0), place.sibling),
                    same(part(from_y, 1), place.over_x),
                    same(part(from_y, 1), place.sibling),
                    same(part(from_x, 1), place.sibling),
                    same(part(from_y, 0), place.sibling),
                    same(part(from_both, 0), place.sibling),
                    same(part(from_both, 1), place.sibling),
                ]
            )

    def begin(self):
        for index in (1, 2, 3, 4, 0):
            for plan in self.plans:
                plan[index].start()
        for block, full in self.pairs:
            full[self.own] = block[...]

    def relay(self, *pairs):
        for arrived, followers in pairs:
            for plan in self.plans:
                plan[arrived].wait_recv()
                for index in followers:
                    plan[index].start()

    def first_halves(self):
        self.relay((1, (5, 6)), (2, (7, 8)))

    def second_halves(self):
        self.relay((3, (9,)), (4, (10,)))

    def corners(self):
        self.relay((5, (11,)), (7, (12,)))

    def wait(self, *indices):
        for plan in self.plans:
            for index in indices:
                plan[index].wait_recv()

    def wait_near(self):
        self.wait(0, 6, 9)

    def wait_far(self):
        self.wait(8, 10, 11, 12)

    def finish(self):
        for plan in self.plans:
            for copy in plan:
                copy.wait_send()


VECTORS = 8


def pack_vectors(ln1_gain, ln1_bias, ln2_gain, ln2_bias, proj_bias, out_bias, attn_bias, fc_bias):
    rows = (ln1_gain, ln1_bias, ln2_gain, ln2_bias, proj_bias, out_bias, attn_bias, fc_bias)
    return jnp.stack([jnp.pad(row.astype(F32), (0, D - row.shape[0])) for row in rows])


def assemble_vectors(shares):
    quarter = D // 4
    small = jnp.concatenate([share[:6, :quarter] for share in shares], axis=1)
    query = jnp.concatenate([shares[0][6:7, : 2 * quarter], shares[1][6:7, : 2 * quarter]], axis=1)
    value = jnp.concatenate([shares[2][6:7, : 2 * quarter], shares[3][6:7, : 2 * quarter]], axis=1)
    hidden = [share[7:8] for share in shares]
    return jnp.concatenate([small, query, value, *hidden, jnp.zeros((4, D), F32)], axis=0)


def mask_block(own_segs, segs_ref, block, start, own_is_query):
    rows = own_segs.shape[0]
    own_place = start + lax.broadcasted_iota(jnp.int32, (rows, rows), 0)
    place = block * rows + lax.broadcasted_iota(jnp.int32, (rows, rows), 1)
    causal = (place <= own_place) if own_is_query else (own_place <= place)
    same = own_segs == segs_ref[block, 0:1, :]
    return jnp.where(causal & same, 0.0, NEGATIVE)


def own_columns(segs_ref, block):
    rows = segs_ref.shape[2]
    return jnp.broadcast_to(segs_ref[block, 0:1, :], (rows, rows)).T


def project_blocks(rows_all, first, weight_of, bias, out_ref, width):
    rows = rows_all[pl.ds(first, 4)].reshape(4 * rows_all.shape[1], D)
    for side in range(width // D):
        total = jnp.dot(rows, weight_of(side), preferred_element_type=F32)
        if bias[side] is not None:
            total = total + bias[side]
        out_ref[pl.ds(first, 4), :, side * D : (side + 1) * D] = total.astype(BF16).reshape(4, -1, D)


class AttentionForward:
    def __init__(
        self, place, q_ref, segs_ref, rows_all, kv_all, outs, scratch, sems, weight_of, vectors_ref
    ):
        self.place = place
        out_ref, lse_ref, lse_rows_ref, kv_out, rows_out = outs
        self.q_ref, self.segs_ref, self.kv_all = q_ref, segs_ref, kv_all
        self.rows_all, self.weight_of, self.vectors_ref = rows_all, weight_of, vectors_ref
        self.out_ref, self.lse_ref, self.lse_rows_ref = out_ref, lse_ref, lse_rows_ref
        self.near_bias, self.far_bias, self.top, self.total, self.mixed = scratch
        self.rows = q_ref.shape[0]
        self.near, self.far = 4 * place.y, 4 * (1 - place.y)
        moves = [
            (kv_all.at[pl.ds(self.near, 4)], kv_out.at[pl.ds(self.near, 4)]),
            (kv_all.at[pl.ds(self.far, 4)], kv_out.at[pl.ds(self.far, 4)]),
            (rows_all, rows_out),
        ]
        self.saves = [pltpu.make_async_copy(*move, sem) for move, sem in zip(moves, sems)]

    def project_queries(self):
        rows = self.rows_all[self.place.block]
        total = jnp.dot(rows, self.weight_of(0), preferred_element_type=F32)
        self.q_ref[...] = (total + self.vectors_ref[6:7, :]).astype(BF16)

    def project(self, first):
        biases = (None, self.vectors_ref[7:8, :])
        project_blocks(
            self.rows_all, first, lambda side: self.weight_of(side + 1), biases, self.kv_all, 2 * D
        )

    def masks(self, far):
        rows = self.rows
        start = self.place.block * rows
        own_segs = own_columns(self.segs_ref, self.place.block)
        first, bias = (self.far, self.far_bias) if far else (self.near, self.near_bias)
        for i in range(4):
            at = slice(i * rows, (i + 1) * rows)
            bias[:, at] = mask_block(own_segs, self.segs_ref, first + i, start, True)

    def lanes(self, pair, side=0):
        return pl.ds(pl.multiple_of(side * D + pair * LANES, LANES), LANES)

    def part(self, first, bias_ref, pair):
        rows = self.rows
        queries = two_heads(self.q_ref[:, self.lanes(pair)] * jnp.asarray(SCALE, BF16))
        keys = self.kv_all[pl.ds(first, 4), :, self.lanes(pair)].reshape(4 * rows, LANES)
        values = self.kv_all[pl.ds(first, 4), :, self.lanes(pair, 1)].reshape(4 * rows, LANES)
        bias = bias_ref[...]
        scores = dot_rows(queries, keys) + jnp.concatenate([bias, bias], axis=0)
        top = jnp.max(scores, axis=1, keepdims=True)
        shares = jnp.exp(scores - top)
        total = jnp.sum(shares, axis=1, keepdims=True)
        return top, total, jnp.dot(shares.astype(BF16), values, preferred_element_type=F32)

    def near_part(self):
        self.project(self.near)
        self.saves[0].start()
        self.lse_ref[...] = jnp.zeros_like(self.lse_ref)

        def visit(pair, carried):
            self.top[pair], self.total[pair], self.mixed[pair] = self.part(
                self.near, self.near_bias, pair
            )
            return carried

        lax.fori_loop(0, PAIRS, visit, 0, unroll=3)

    def far_part(self):
        self.saves[2].start()
        self.project(self.far)
        self.saves[1].start()

        def visit(pair, carried):
            top, total, mixed = self.part(self.far, self.far_bias, pair)
            old_top = self.top[pair]
            new_top = jnp.maximum(top, old_top)
            new, old = jnp.exp(top - new_top), jnp.exp(old_top - new_top)
            self.top[pair] = new_top
            self.total[pair] = total * new + self.total[pair] * old
            self.mixed[pair] = mixed * new + self.mixed[pair] * old
            return carried

        @pl.when(self.place.y == 1)
        def _():
            lax.fori_loop(0, PAIRS, visit, 0, unroll=3)

    def store(self):
        rows = self.rows

        def visit(pair, carried):
            total = self.total[pair]
            self.out_ref[:, self.lanes(pair)] = one_pair(self.mixed[pair] / total).astype(BF16)
            lse = self.top[pair] + jnp.log(total)
            lane = lax.broadcasted_iota(jnp.int32, (rows, LANES), 1)
            kept = jnp.where(lane == 2 * pair, lse[:rows], self.lse_ref[...])
            self.lse_ref[...] = jnp.where(lane == 2 * pair + 1, lse[rows:], kept)
            return carried

        lax.fori_loop(0, PAIRS, visit, 0, unroll=3)
        self.lse_rows_ref[...] = self.lse_ref[...].T[:16]

    def finish(self):
        for save in self.saves:
            save.wait()


def forward_scratch(rows):
    return [
        pltpu.VMEM((8, rows, 2 * D), BF16),
        pltpu.VMEM((8, rows, D), BF16),
        pltpu.VMEM((rows, D), BF16),
        pltpu.VMEM((rows, 4 * rows), F32),
        pltpu.VMEM((rows, 4 * rows), F32),
        pltpu.VMEM((PAIRS, 2 * rows, 1), F32),
        pltpu.VMEM((PAIRS, 2 * rows, 1), F32),
        pltpu.VMEM((PAIRS, 2 * rows, LANES), F32),
    ]


FORWARD_SCRATCH = 8


def forward_shapes(rows):
    return [
        jax.ShapeDtypeStruct((rows, D), BF16),
        jax.ShapeDtypeStruct((rows, LANES), F32),
        jax.ShapeDtypeStruct((16, rows), F32),
        jax.ShapeDtypeStruct((8, rows, 2 * D), BF16),
        jax.ShapeDtypeStruct((8, rows, D), BF16),
    ]


def greet_with_partner(place, others):
    barrier = pltpu.get_barrier_semaphore()
    for device in others:
        pl.semaphore_signal(barrier, inc=1, device_id=device, device_id_type=MESH)

    @pl.when(place.has_partner)
    def _():
        pl.semaphore_signal(barrier, inc=1, device_id=place.partner, device_id_type=MESH)
        pl.semaphore_wait(barrier, len(others) + 1)

    @pl.when(jnp.logical_not(place.has_partner))
    def _():
        pl.semaphore_wait(barrier, len(others))


def attend_kernel(
    rows_ref,
    segs_ref,
    vectors_ref,
    weight_ref,
    cotangent_ref,
    out_ref,
    lse_ref,
    lse_rows_ref,
    kv_out,
    rows_out,
    cotangent_out,
    *scratch,
):
    kv_all, rows_all, q_ref = scratch[:3]
    weight, send_sems, recv_sems, local_sems = scratch[FORWARD_SCRATCH:]
    place = Place()
    load = pltpu.make_async_copy(weight_ref, weight, local_sems.at[3])
    load.start()
    greet_with_partner(place, (place.sibling, place.over_x, place.over_y))
    copies = Copies(send_sems, recv_sems)
    gather = BlockGather(place, copies, [rows_ref], [rows_all])
    swap = copies.make(cotangent_ref, cotangent_out, place.partner)
    keep = pltpu.make_async_copy(cotangent_ref, cotangent_out, local_sems.at[4])
    gather.begin()

    @pl.when(place.has_partner)
    def _():
        swap.start()

    @pl.when(jnp.logical_not(place.has_partner))
    def _():
        keep.start()

    attention = AttentionForward(
        place,
        q_ref,
        segs_ref,
        rows_all,
        kv_all,
        (out_ref, lse_ref, lse_rows_ref, kv_out, rows_out),
        scratch[3:FORWARD_SCRATCH],
        [local_sems.at[i] for i in range(3)],
        lambda side: weight[:, side * D : (side + 1) * D],
        vectors_ref,
    )
    attention.masks(False)
    attention.masks(True)
    load.wait()
    attention.project_queries()
    gather.first_halves()
    gather.second_halves()
    gather.wait_near()
    gather.corners()
    attention.near_part()
    gather.wait_far()
    attention.far_part()
    attention.store()
    attention.finish()
    gather.finish()

    @pl.when(place.has_partner)
    def _():
        swap.wait()

    @pl.when(jnp.logical_not(place.has_partner))
    def _():
        keep.wait()


def attend(normed, segs, vectors, weight, cotangent, collective_id):
    rows = normed.shape[0]
    vmem = pl.BlockSpec(memory_space=pltpu.VMEM)
    anywhere = pl.BlockSpec(memory_space=pl.ANY)
    return pl.pallas_call(
        attend_kernel,
        in_specs=[vmem, vmem, vmem, anywhere, anywhere],
        out_specs=[vmem, vmem, vmem, anywhere, anywhere, vmem],
        out_shape=forward_shapes(rows) + [jax.ShapeDtypeStruct((rows, D), BF16)],
        scratch_shapes=forward_scratch(rows)
        + [
            pltpu.VMEM(weight.shape, BF16),
            pltpu.SemaphoreType.DMA((BLOCK_COPIES + 1,)),
            pltpu.SemaphoreType.DMA((BLOCK_COPIES + 1,)),
            pltpu.SemaphoreType.DMA((5,)),
        ],
        compiler_params=pltpu.CompilerParams(
            collective_id=collective_id, has_side_effects=True, vmem_limit_bytes=36 << 20
        ),
        name="attend",
    )(normed, segs, vectors, weight, cotangent)


def opening_kernel(count, *refs):
    tokens_ref, segs_ref, first_ref = refs[:3]
    vector_refs = refs[3 : 3 + VECTORS]
    shares = refs[3 + VECTORS : 3 + VECTORS + count]
    refs = refs[3 + VECTORS + count :]
    (
        tokens_out,
        segs_out,
        vectors_out,
        normed_out,
        normal_out,
        inverse_out,
        attended_out,
        lse_out,
        lse_rows_out,
        kv_out,
        rows_out,
        first_out,
    ) = refs[:12]
    fulls = refs[12 : 12 + count]
    refs = refs[12 + count :]
    kv_all, rows_all, q_ref = refs[:3]
    forward = refs[3:FORWARD_SCRATCH]
    vectors_own, vectors_all, segs_row, segs_sent, segs_own = refs[FORWARD_SCRATCH : FORWARD_SCRATCH + 5]
    refs = refs[FORWARD_SCRATCH + 5 :]
    first_full, tokens_all, send_sems, recv_sems, local_sems = refs[:5]
    stages, vector_rows = refs[5 : 5 + count], refs[5 + count :]
    place = Place()
    own, other = place.fsdp, 2 * (1 - place.y) + place.core
    loads = [
        pltpu.make_async_copy(src, dst, local_sems.at[count + 8 + i])
        for i, (src, dst) in enumerate(zip((segs_ref, *vector_refs), (segs_row, *vector_rows)))
    ]
    for load in loads:
        load.start()
    for load in loads:
        load.wait()
    vectors_own[...] = jnp.zeros_like(vectors_own)
    for i, row in enumerate(vector_rows):
        size = row.shape[0]
        vectors_own[i : i + 1, :size] = row[...].astype(F32).reshape(1, size)
    segs_sent[...] = jnp.broadcast_to(segs_row[...], segs_sent.shape)
    greet_with_partner(place, (place.sibling, place.over_x, place.over_y, place.over_z))
    copies = Copies(send_sems, recv_sems)
    swap_tokens = copies.make(tokens_ref, tokens_out, place.partner)
    swap_segs = copies.make(segs_sent, segs_own, place.partner)
    vector_copies = [
        copies.make(vectors_own, vectors_all.at[own], place.over_y),
        copies.make(vectors_own, vectors_all.at[own], place.sibling),
        copies.make(vectors_all.at[other], vectors_all.at[other], place.sibling),
    ]
    weights = WeightGather(
        place,
        copies,
        [first_ref, *shares],
        [first_full, *fulls],
        [None, *stages],
        local_sems,
    )
    first_cuts = len(weight_cuts(first_ref.shape))
    gather = BlockGather(place, copies, [tokens_out, segs_own], [tokens_all, segs_out])
    save_first = pltpu.make_async_copy(first_full, first_out, local_sems.at[count + 7])
    attention = AttentionForward(
        place,
        q_ref,
        segs_out,
        rows_all,
        kv_all,
        (attended_out, lse_out, lse_rows_out, kv_out, rows_out),
        forward,
        [local_sems.at[count + i] for i in (2, 3, 5)],
        lambda side: first_full[:, :, side * D : (side + 1) * D].reshape(D, D),
        vectors_out,
    )

    keep_tokens = pltpu.make_async_copy(tokens_ref, tokens_out, local_sems.at[count + 9 + VECTORS])
    vector_copies[0].start()
    vector_copies[1].start()

    @pl.when(place.has_partner)
    def _():
        swap_segs.start()

    @pl.when(place.has_partner)
    def _():
        swap_tokens.start()

    @pl.when(jnp.logical_not(place.has_partner))
    def _():
        keep_tokens.start()

    weights.begin()
    vectors_all[own] = vectors_own[...]

    @pl.when(jnp.logical_not(place.has_partner))
    def _():
        segs_own[...] = segs_sent[...]

    vector_copies[0].wait_recv()
    vector_copies[2].start()
    weights.step(0)
    weights.step(1)
    vector_copies[1].wait_recv()
    vector_copies[2].wait_recv()
    vectors_out[...] = assemble_vectors([vectors_all[i] for i in range(4)])
    weights.step(2)

    @pl.when(place.has_partner)
    def _():
        swap_segs.wait_recv()
        swap_tokens.wait_recv()

    @pl.when(jnp.logical_not(place.has_partner))
    def _():
        keep_tokens.wait()

    gather.begin()
    weights.step(3)

    def norm_block(block):
        return norm_forward(
            tokens_all[block].astype(F32), vectors_out[0:1, :], vectors_out[1:2, :]
        )

    def norm_four(start):
        def visit(index, carried):
            rows_all[start + index] = norm_block(start + index)[0]
            return carried

        lax.fori_loop(0, 4, visit, 0)

    normed, normal, inverse = norm_block(place.block)
    normed_out[...] = normed
    normal_out[...] = normal
    inverse_out[...] = inverse
    weights.step(4)
    gather.first_halves()
    weights.keep_own()
    weights.step(5)
    gather.second_halves()
    gather.wait_near()
    gather.corners()
    norm_four(attention.near)
    attention.masks(False)
    weights.step(6)
    weights.arrive(0, first_cuts)
    save_first.start()
    attention.project_queries()
    weights.step(7)
    attention.near_part()
    weights.step(8)
    gather.wait_far()
    norm_four(attention.far)
    attention.masks(True)
    weights.step(9)
    attention.far_part()
    attention.store()
    save_first.wait()
    attention.finish()
    gather.finish()
    for copy in vector_copies:
        copy.wait_send()

    @pl.when(place.has_partner)
    def _():
        swap_segs.wait_send()
        swap_tokens.wait_send()

    weights.finish()


def opening(tokens, segs_row, vectors, first, shares, collective_id):
    rows, columns = tokens.shape
    count = len(shares)
    cuts = sum(len(weight_cuts(share.shape)) for share in [first, *shares])
    slots = 2 + 3 + cuts * WEIGHT_COPIES + 2 * BLOCK_COPIES
    vmem = pl.BlockSpec(memory_space=pltpu.VMEM)
    anywhere = pl.BlockSpec(memory_space=pl.ANY)
    shape = jax.ShapeDtypeStruct
    segs_shape = (16, segs_row.shape[1])
    return pl.pallas_call(
        partial(opening_kernel, count),
        in_specs=[anywhere] * (3 + VECTORS + count),
        out_specs=[vmem] * 9 + [anywhere] * (3 + count),
        out_shape=[
            shape((rows, columns), tokens.dtype),
            shape((8, *segs_shape), segs_row.dtype),
            shape((16, D), F32),
            shape((rows, D), BF16),
            shape((rows, D), F32),
            shape((rows, 1), F32),
        ]
        + forward_shapes(rows)
        + [shape((4, *share.shape), share.dtype) for share in [first, *shares]],
        scratch_shapes=forward_scratch(rows)
        + [
            pltpu.VMEM((8, D), F32),
            pltpu.VMEM((4, 8, D), F32),
            pltpu.VMEM(segs_row.shape, segs_row.dtype),
            pltpu.VMEM(segs_shape, segs_row.dtype),
            pltpu.VMEM(segs_shape, segs_row.dtype),
            pltpu.VMEM((4, *first.shape), first.dtype),
            pltpu.VMEM((8, rows, D), BF16),
            pltpu.SemaphoreType.DMA((slots,)),
            pltpu.SemaphoreType.DMA((slots,)),
            pltpu.SemaphoreType.DMA((count + 10 + VECTORS,)),
        ]
        + [pltpu.VMEM(share.shape, share.dtype) for share in shares]
        + [pltpu.VMEM(vector.shape, vector.dtype) for vector in vectors],
        compiler_params=pltpu.CompilerParams(
            collective_id=collective_id, has_side_effects=True, vmem_limit_bytes=60 << 20
        ),
        name="opening",
    )(tokens, segs_row, first, *vectors, *shares)


GROUP = 3


class AttentionGrads:
    def __init__(self, place, grad_ref, lse_ref, delta_ref, segs_ref, kv_all, q_all, grad_all, stats_all, biases, sums):
        self.place = place
        self.grad_ref, self.lse_ref, self.delta_ref = grad_ref, lse_ref, delta_ref
        self.segs_ref, self.kv_all, self.q_all, self.grad_all = segs_ref, kv_all, q_all, grad_all
        self.stats_all = stats_all
        self.query_bias, self.key_bias = biases
        self.query_sum, self.key_sum, self.value_sum = sums
        self.rows = grad_ref.shape[0]

    def masks(self):
        rows, place = self.rows, self.place
        start = place.block * rows
        own_segs = own_columns(self.segs_ref, place.block)
        for i in range(8):
            at = slice(i * rows, (i + 1) * rows)
            self.query_bias[:, at] = mask_block(own_segs, self.segs_ref, i, start, True)
            self.key_bias[:, at] = mask_block(own_segs, self.segs_ref, i, start, False)

    def lanes(self, pair, side=0):
        return pl.ds(pl.multiple_of(side * D + pair * LANES, LANES), LANES)

    def two_blocks(self, ref, index, lanes):
        return ref[pl.ds(2 * index, 2), :, lanes].reshape(2 * self.rows, LANES)

    def bias(self, ref, index):
        step = 2 * self.rows
        bias = ref[:, pl.ds(pl.multiple_of(index * step, step), step)]
        return jnp.concatenate([bias, bias], axis=0)

    def project(self, rows_all, weight, bias):
        for first in (0, 4):
            project_blocks(rows_all, first, lambda side: weight[:, :D], (bias,), self.q_all, D)

    def query_grads(self, first_pair, last_pair):
        scale = jnp.asarray(SCALE, BF16)
        count = self.place.block // 2 + 1

        def visit_pairs(group, carried):
            pairs = [group * GROUP + i for i in range(GROUP)]
            own = []
            for pair in pairs:
                queries = two_heads(self.q_all[self.place.block, :, self.lanes(pair)] * scale)
                grads = two_heads(self.grad_ref[:, self.lanes(pair)])
                lse = pick_lanes(self.lse_ref[...], pair)
                own.append((queries, grads, lse, pick_lanes(self.delta_ref[...], pair)))

            def visit(index, totals):
                bias = self.bias(self.query_bias, index)
                sums = []
                for pair, total, (queries, grads, lse, delta) in zip(pairs, totals, own):
                    keys = self.two_blocks(self.kv_all, index, self.lanes(pair))
                    values = self.two_blocks(self.kv_all, index, self.lanes(pair, 1))
                    attention = jnp.exp(dot_rows(queries, keys) + bias - lse)
                    grad_attention = dot_rows(grads, values)
                    grad_scores = (attention * (grad_attention - delta)).astype(BF16)
                    sums.append(total + jnp.dot(grad_scores, keys, preferred_element_type=F32))
                return tuple(sums)

            zeros = jnp.zeros((2 * self.rows, LANES), F32)
            totals = lax.fori_loop(0, count, visit, (zeros,) * GROUP)
            for pair, total in zip(pairs, totals):
                self.query_sum[pair] = total
            return carried

        lax.fori_loop(first_pair // GROUP, last_pair // GROUP, visit_pairs, 0)

    def key_grads(self, first, last, fresh):
        rows = self.rows
        scale = jnp.asarray(SCALE, BF16)
        own_block = self.place.block

        def stat_rows(index, pair, row):
            def spread(block, head):
                line = self.stats_all[2 * index + block, pl.ds(row + 2 * pair + head, 1), :]
                return jnp.broadcast_to(line, (rows, rows))

            heads = [jnp.concatenate([spread(0, head), spread(1, head)], axis=1) for head in range(2)]
            return jnp.concatenate(heads, axis=0)

        def visit_pairs(group, carried):
            pairs = [group * GROUP + i for i in range(GROUP)]
            own = []
            for pair in pairs:
                keys = two_heads(self.kv_all[own_block, :, self.lanes(pair)] * scale)
                own.append((keys, two_heads(self.kv_all[own_block, :, self.lanes(pair, 1)])))

            def visit(index, totals):
                bias = self.bias(self.key_bias, index)
                sums = []
                for pair, (key_total, value_total), (keys, values) in zip(pairs, totals, own):
                    later = self.two_blocks(self.q_all, index, self.lanes(pair))
                    later_grads = self.two_blocks(self.grad_all, index, self.lanes(pair))
                    scores = dot_rows(keys, later) + bias
                    attention = jnp.exp(scores - stat_rows(index, pair, 0))
                    grad_attention = dot_rows(values, later_grads)
                    grad_scores = attention * (grad_attention - stat_rows(index, pair, 16))
                    key_total = key_total + jnp.dot(
                        grad_scores.astype(BF16), later, preferred_element_type=F32
                    )
                    value_total = value_total + jnp.dot(
                        attention.astype(BF16), later_grads, preferred_element_type=F32
                    )
                    sums.append((key_total, value_total))
                return tuple(sums)

            if fresh:
                zeros = jnp.zeros((2 * rows, LANES), F32)
                totals = ((zeros, zeros),) * GROUP
            else:
                totals = tuple((self.key_sum[pair], self.value_sum[pair]) for pair in pairs)
            totals = lax.fori_loop(first, last, visit, totals)
            for pair, (key_total, value_total) in zip(pairs, totals):
                self.key_sum[pair], self.value_sum[pair] = key_total, value_total
            return carried

        lax.fori_loop(0, PAIRS // GROUP, visit_pairs, 0)

    def near_keys(self):
        self.key_grads(self.place.block // 2, 2 * self.place.y + 2, True)

    def far_keys(self):
        @pl.when(self.place.y == 0)
        def _():
            self.key_grads(2, 4, False)

    def store(self, out_ref):
        def visit(pair, carried):
            out_ref[:, self.lanes(pair)] = (one_pair(self.query_sum[pair]) * SCALE).astype(BF16)
            out_ref[:, self.lanes(pair, 1)] = (one_pair(self.key_sum[pair]) * SCALE).astype(BF16)
            out_ref[:, self.lanes(pair, 2)] = one_pair(self.value_sum[pair]).astype(BF16)
            return carried

        lax.fori_loop(0, PAIRS, visit, 0)


def attention_scratch(rows):
    return [
        pltpu.VMEM((8, rows, 2 * D), BF16),
        pltpu.VMEM((8, rows, D), BF16),
        pltpu.VMEM((8, rows, D), BF16),
        pltpu.VMEM((8, 32, rows), F32),
        pltpu.VMEM((rows, 8 * rows), F32),
        pltpu.VMEM((rows, 8 * rows), F32),
        pltpu.VMEM((PAIRS, 2 * rows, LANES), F32),
        pltpu.VMEM((PAIRS, 2 * rows, LANES), F32),
        pltpu.VMEM((PAIRS, 2 * rows, LANES), F32),
    ]


ATTENTION_SCRATCH = 9


def attend_back_kernel(
    grad_ref,
    stats_ref,
    lse_ref,
    delta_ref,
    segs_ref,
    vectors_ref,
    kv_ref,
    rows_ref,
    weight_ref,
    out_ref,
    *scratch,
):
    kv_all, q_all, grad_all, stats_all = scratch[:4]
    biases, sums = scratch[4:6], scratch[6:9]
    rows_all, weight, send_sems, recv_sems, local_sems = scratch[ATTENTION_SCRATCH:]
    place = Place()
    loads = [
        pltpu.make_async_copy(src, dst, local_sems.at[i])
        for i, (src, dst) in enumerate(
            ((rows_ref, rows_all), (weight_ref.at[:, pl.ds(0, D)], weight), (kv_ref, kv_all))
        )
    ]
    for load in loads:
        load.start()
    greet((place.sibling, place.over_x, place.over_y))
    copies = Copies(send_sems, recv_sems)
    gather = BlockGather(place, copies, [grad_ref, stats_ref], [grad_all, stats_all])
    gather.begin()
    grads = AttentionGrads(
        place, grad_ref, lse_ref, delta_ref, segs_ref, kv_all, q_all, grad_all, stats_all, biases, sums
    )
    grads.masks()
    loads[0].wait()
    loads[1].wait()
    grads.project(rows_all, weight, vectors_ref[6:7, :])
    gather.first_halves()
    loads[2].wait()
    gather.second_halves()
    grads.query_grads(0, GROUP)
    gather.corners()
    grads.query_grads(GROUP, PAIRS)
    gather.wait_near()
    grads.near_keys()
    gather.wait_far()
    grads.far_keys()
    grads.store(out_ref)
    gather.finish()


def attend_back(grads, stats, lse, delta, segs, state, weight, vectors, collective_id):
    kv, rows_all = state
    rows = grads.shape[0]
    slots = 2 * BLOCK_COPIES
    vmem = pl.BlockSpec(memory_space=pltpu.VMEM)
    anywhere = pl.BlockSpec(memory_space=pl.ANY)
    return pl.pallas_call(
        attend_back_kernel,
        in_specs=[vmem] * 6 + [anywhere] * 3,
        out_specs=vmem,
        out_shape=jax.ShapeDtypeStruct((rows, 3 * D), BF16),
        scratch_shapes=attention_scratch(rows)
        + [
            pltpu.VMEM((8, rows, D), BF16),
            pltpu.VMEM((D, D), BF16),
            pltpu.SemaphoreType.DMA((slots,)),
            pltpu.SemaphoreType.DMA((slots,)),
            pltpu.SemaphoreType.DMA((3,)),
        ],
        compiler_params=pltpu.CompilerParams(
            collective_id=collective_id, has_side_effects=True, vmem_limit_bytes=36 << 20
        ),
        name="attend_back",
    )(grads, stats, lse, delta, segs, vectors, kv, rows_all, weight)


CHUNK_ROWS, CHUNK_COLUMNS = 192, 768
REDUCE_COPIES = 9
VECTOR_AXES = 5


def chunk_places(shapes):
    places = [
        (which, row, column, CHUNK_COLUMNS)
        for which, (rows, columns) in enumerate(shapes)
        for row in range(0, rows, CHUNK_ROWS)
        for column in range(0, columns, CHUNK_COLUMNS)
    ]
    which, row, column, width = places.pop()
    cut = 2 * width // 3
    return places + [(which, row, column, cut), (which, row, column + cut, width - cut)]


CORE_SLOTS = 4
REDUCE_STAGES = ("core0", "core1", "y", "x", "z", "zz", "zz_back", "z_back", "x_back")


class GradientSum:
    def __init__(self, place, copies, places, sums, buffers):
        self.place = place
        (
            self.own,
            self.got_core,
            self.got_y,
            self.to_x,
            self.got_x,
            self.to_z,
            self.got_z,
            self.to_zz,
            self.got_zz,
            self.to_core,
        ) = buffers
        self.places = places
        self.x_rows, self.z_rows = CHUNK_ROWS // 2, CHUNK_ROWS // 4
        x, y, low, high = place.x, place.y, place.low, place.high
        self.plans = []
        self.finals = []
        for k, (which, row, column, width) in enumerate(places):
            out = sums[which]
            half = width // 2

            def piece(first, rows, start, columns, out=out, row=row, column=column):
                return out.at[
                    pl.ds(pl.multiple_of(row + first, 16), rows),
                    pl.ds(pl.multiple_of(column + start, LANES), columns),
                ]

            def wide_part(ref, *index, columns=width):
                return ref.at[(*index, slice(None), pl.ds(0, columns))]

            final = piece(x * self.x_rows + low * self.z_rows, self.z_rows, high * half, half)
            wide = piece(x * self.x_rows + low * self.z_rows, self.z_rows, 0, width)
            tall = piece(x * self.x_rows, self.x_rows, 0, width)
            slot = k % CORE_SLOTS
            moves = (
                (wide_part(self.to_core, slot, 0), wide_part(self.got_core, k, 0), place.sibling),
                (wide_part(self.to_core, slot, 1), wide_part(self.got_core, k, 1), place.sibling),
                (wide_part(self.own, k, 1 - y), wide_part(self.got_y, k), place.over_y),
                (wide_part(self.to_x, k), wide_part(self.got_x, k), place.over_x),
                (wide_part(self.to_z, k), wide_part(self.got_z, k), place.over_z),
                (
                    wide_part(self.to_zz, k, columns=half),
                    wide_part(self.got_zz, k, columns=half),
                    place.over_zz,
                ),
                (final, final, place.over_zz),
                (wide, wide, place.over_z),
                (tall, tall, place.over_x),
            )
            self.plans.append(
                {name: copies.make(*move) for name, move in zip(REDUCE_STAGES, moves)}
            )
            self.finals.append(final)
        self.stages = (
            self.stage_x,
            self.stage_z,
            self.stage_zz,
            self.stage_final,
            self.stage_z_back,
            self.stage_x_back,
        )

    def make(self, which, left, right):
        core = self.place.core
        for k, (owner, row, column, width) in enumerate(self.places):
            if owner != which:
                continue
            quarter_rows = left.shape[0] // 4

            def term(quarter):
                first = pl.multiple_of(quarter * quarter_rows + row, 16)
                rows = left[pl.ds(first, CHUNK_ROWS), :]
                columns = right[:, column : column + width]
                return jnp.dot(rows, columns, preferred_element_type=F32).astype(BF16)

            if k >= CORE_SLOTS:
                for name in ("core0", "core1"):
                    self.plans[k - CORE_SLOTS][name].wait_send()
            for i in range(2):
                self.to_core[k % CORE_SLOTS, i, :, :width] = term(2 * i + 1 - core)
            self.plans[k]["core0"].start()
            self.plans[k]["core1"].start()
            for i in range(2):
                self.own[k, i, :, :width] = term(2 * i + core)

    def add_up(self, store, loads, rows):
        step = self.z_rows

        def visit(index, carried):
            offset = pl.multiple_of(index * step, 16)
            total = loads[0](offset, step).astype(F32)
            for load in loads[1:]:
                total = total + load(offset, step).astype(F32)
            store(offset, step, total.astype(BF16))
            return carried

        if rows == step:
            visit(0, 0)
        else:
            lax.fori_loop(0, rows // step, visit, 0)

    def slab(self, ref, *index, first=0, start=0, width=None):
        def load(offset, rows):
            place = pl.ds(pl.multiple_of(first + offset, 16), rows)
            return ref[(*index, place, pl.ds(pl.multiple_of(start, LANES), width))]

        return load

    def stage_y(self, k):
        plan, y, width = self.plans[k], self.place.y, self.places[k][3]
        plan["core0"].wait_recv()
        plan["core1"].wait_recv()

        def store(offset, rows, value):
            self.own[k, 1 - y, pl.ds(offset, rows), :width] = value

        loads = [
            self.slab(self.own, k, 1 - y, width=width),
            self.slab(self.got_core, k, 1 - y, width=width),
        ]
        self.add_up(store, loads, CHUNK_ROWS)
        plan["y"].start()

    def terms_at(self, k, first, depth, inner=0, start=0, width=None):
        y = self.place.y
        part = {"start": start, "width": self.places[k][3] if width is None else width}
        loads = [
            self.slab(self.own, k, y, first=first, **part),
            self.slab(self.got_core, k, y, first=first, **part),
            self.slab(self.got_y, k, first=first, **part),
        ]
        if depth > 0:
            loads.append(self.slab(self.got_x, k, first=inner, **part))
        if depth > 1:
            loads.append(self.slab(self.got_z, k, **part))
        return loads

    def stage_x(self, k):
        plan, width = self.plans[k], self.places[k][3]
        plan["y"].wait_recv()

        def store(offset, rows, value):
            self.to_x[k, pl.ds(offset, rows), :width] = value

        self.add_up(store, self.terms_at(k, (1 - self.place.x) * self.x_rows, 0), self.x_rows)
        plan["x"].start()

    def stage_z(self, k):
        plan, width = self.plans[k], self.places[k][3]
        plan["x"].wait_recv()
        inner = (1 - self.place.low) * self.z_rows

        def store(offset, rows, value):
            self.to_z[k, :, :width] = value

        first = self.place.x * self.x_rows + inner
        self.add_up(store, self.terms_at(k, first, 1, inner), self.z_rows)
        plan["z"].start()

    def last_terms(self, k, side):
        inner = self.place.low * self.z_rows
        first = self.place.x * self.x_rows + inner
        half = self.places[k][3] // 2
        return self.terms_at(k, first, 2, inner, side * half, half)

    def stage_zz(self, k):
        plan, half = self.plans[k], self.places[k][3] // 2
        plan["z"].wait_recv()

        def store(offset, rows, value):
            self.to_zz[k, :, :half] = value

        self.add_up(store, self.last_terms(k, 1 - self.place.high), self.z_rows)
        plan["zz"].start()

    def stage_final(self, k):
        plan, half = self.plans[k], self.places[k][3] // 2
        plan["zz"].wait_recv()

        def store(offset, rows, value):
            self.finals[k][...] = value

        terms = self.last_terms(k, self.place.high)
        self.add_up(store, terms + [self.slab(self.got_zz, k, width=half)], self.z_rows)
        plan["zz_back"].start()

    def stage_z_back(self, k):
        self.plans[k]["zz_back"].wait_recv()
        self.plans[k]["z_back"].start()

    def stage_x_back(self, k):
        self.plans[k]["z_back"].wait_recv()
        self.plans[k]["x_back"].start()

    def ticks(self):
        return len(self.plans) + len(self.stages) - 1

    def tick(self, tick):
        for lag, stage in enumerate(self.stages):
            if 0 <= tick - lag < len(self.plans):
                stage(tick - lag)

    def finish(self):
        for k, plan in enumerate(self.plans):
            plan["x_back"].wait_recv()
            waited = k + CORE_SLOTS < len(self.plans)
            for name in REDUCE_STAGES[2:] if waited else REDUCE_STAGES:
                plan[name].wait_send()


def reduce_scratch(chunks):
    rows, columns = CHUNK_ROWS, CHUNK_COLUMNS
    shapes = [
        (chunks, 2, rows, columns),
        (chunks, 2, rows, columns),
        (chunks, rows, columns),
        (chunks, rows // 2, columns),
        (chunks, rows // 2, columns),
        (chunks, rows // 4, columns),
        (chunks, rows // 4, columns),
        (chunks, rows // 4, columns // 2),
        (chunks, rows // 4, columns // 2),
        (CORE_SLOTS, 2, rows, columns),
    ]
    return [pltpu.VMEM(shape, BF16) for shape in shapes]


REDUCE_SCRATCH = 10
CLOSING_INPUTS = 11


def closing_kernel(places, count, *refs):
    (
        grad_ref,
        stats_ref,
        lse_ref,
        delta_ref,
        segs_ref,
        normal_ref,
        inverse_ref,
        gain_ref,
        middle_ref,
        terms_ref,
        vectors_ref,
    ) = refs[:CLOSING_INPUTS]
    refs = refs[CLOSING_INPUTS:]
    factors = refs[: 4 * count - 1]
    rows_ref, kv_ref, weight_ref = refs[4 * count - 1 : 4 * count + 2]
    refs = refs[4 * count + 2 :]
    sums, (small_out, bias_out, wide_out, tokens_out) = refs[:count], refs[count : count + 4]
    refs = refs[count + 4 :]
    kv_all, q_all, grad_all, stats_all = refs[:4]
    biases, attention_sums = refs[4:6], refs[6:9]
    refs = refs[ATTENTION_SCRATCH:]
    buffers = refs[:REDUCE_SCRATCH]
    (
        grads_ref,
        grad_rows,
        weight,
        left,
        right,
        vector_sum,
        vector_got,
        tokens_own,
        send_sems,
        recv_sems,
        local_sems,
    ) = refs[REDUCE_SCRATCH:]

    place = Place()
    load_kv = pltpu.make_async_copy(kv_ref, kv_all, local_sems.at[0])
    load_weight = pltpu.make_async_copy(weight_ref, weight, local_sems.at[1])
    load_rows = pltpu.make_async_copy(rows_ref, grad_rows, local_sems.at[2])
    load_kv.start()
    load_rows.start()
    load_weight.start()
    greet_with_partner(
        place, (place.sibling, place.over_x, place.over_y, place.over_z, place.over_zz)
    )
    copies = Copies(send_sems, recv_sems)
    gather = BlockGather(place, copies, [grad_ref, stats_ref], [grad_all, stats_all])
    swap = copies.make(tokens_own, tokens_out, place.partner)
    reduce = GradientSum(place, copies, places, sums, buffers)
    chunks = len(places)
    by_weight = [[k for k in range(chunks) if places[k][0] == which] for which in range(count)]
    vector_devices = (place.over_x, place.over_z, place.over_zz, place.sibling, place.over_y)
    vector_copies = [
        copies.make(vector_sum, vector_got.at[i], device)
        for i, device in enumerate(vector_devices)
    ]
    tokens = grad_ref.shape[0]

    def make_terms(which, last_right=None):
        later_left, later_right, first_left = factors[4 * which : 4 * which + 3]
        rows, columns = later_left.shape[1], later_right.shape[1]
        left[:rows, :tokens] = later_left[...].T
        left[:rows, tokens:] = first_left[...].T
        right[:tokens, :columns] = later_right[...]
        if last_right is None:
            right[tokens:, :columns] = factors[4 * which + 3][...]
        else:
            right[tokens:, :columns] = last_right
        reduce.make(which, left.at[pl.ds(0, rows), :], right)

    gather.begin()
    make_terms(0)
    grads = AttentionGrads(
        place,
        grad_ref,
        lse_ref,
        delta_ref,
        segs_ref,
        kv_all,
        q_all,
        grad_all,
        stats_all,
        biases,
        attention_sums,
    )
    gather.first_halves()
    for k in by_weight[0]:
        reduce.stage_y(k)
    gather.second_halves()
    grads.masks()
    load_rows.wait()
    load_weight.wait()
    grads.project(grad_rows, weight, vectors_ref[6:7, :])
    load_kv.wait()
    grads.query_grads(0, PAIRS)
    gather.corners()
    gather.wait_near()
    make_terms(1)
    for k in by_weight[1]:
        reduce.stage_y(k)
    reduce.tick(0)
    grads.near_keys()
    gather.wait_far()
    reduce.tick(1)
    grads.far_keys()
    grads.store(grads_ref)
    reduce.tick(2)
    make_terms(2)
    for k in by_weight[2]:
        reduce.stage_y(k)
    own_grads = grads_ref[...]
    make_terms(3, own_grads)
    reduce.tick(3)
    grad_normed = dot_rows(own_grads, weight[...])
    grad_input, grad_gain, grad_bias = norm_backward(
        grad_normed, normal_ref[...], inverse_ref[...], gain_ref[...]
    )
    swapped = (middle_ref[...] + grad_input).astype(BF16)
    tokens_own[...] = swapped

    @pl.when(place.has_partner)
    def _():
        swap.start()

    @pl.when(jnp.logical_not(place.has_partner))
    def _():
        tokens_out[...] = swapped

    vector_sum[...] = terms_ref[...]
    query_bias = jnp.sum(own_grads[:, :D].astype(F32), axis=0, keepdims=True)
    value_bias = jnp.sum(own_grads[:, 2 * D :].astype(F32), axis=0, keepdims=True)
    for row, value in ((0, grad_gain[None]), (1, grad_bias[None]), (6, query_bias), (7, value_bias)):
        vector_sum[row : row + 1, :] = vector_sum[row : row + 1, :] + value
    vector_copies[0].start()
    for k in by_weight[3]:
        reduce.stage_y(k)

    def vector_step(index):
        vector_copies[index].wait()
        vector_sum[...] = vector_sum[...] + vector_got[index]
        if index + 1 < VECTOR_AXES:
            vector_copies[index + 1].start()

    for tick in range(4, reduce.ticks()):
        reduce.tick(tick)
        if tick - 4 < VECTOR_AXES - 1:
            vector_step(tick - 4)
    vector_step(VECTOR_AXES - 1)
    small_out[...] = vector_sum[:6, :]
    bias_out[...] = vector_sum[6:8, :]
    wide_out[...] = vector_sum[8:12, :]
    reduce.finish()
    gather.finish()

    @pl.when(place.has_partner)
    def _():
        swap.wait_recv()
        swap.wait_send()


def closing(attention, norm, terms, factors, weight, vectors, collective_id):
    grads, stats, lse, delta, segs, (kv, rows_all) = attention
    rows = grads.shape[0]
    count = len(factors)
    shapes = [(group[0].shape[1] // 4, group[1].shape[1]) for group in factors]
    places = chunk_places(shapes)
    chunks = len(places)
    slots = chunks * REDUCE_COPIES + VECTOR_AXES + 2 * BLOCK_COPIES + 1
    flat = [factor for group in factors for factor in group]
    tallest = max(group[0].shape[1] for group in factors)
    widest = max(group[1].shape[1] for group in factors)
    vmem = pl.BlockSpec(memory_space=pltpu.VMEM)
    anywhere = pl.BlockSpec(memory_space=pl.ANY)
    return pl.pallas_call(
        partial(closing_kernel, places, count),
        in_specs=[vmem] * (CLOSING_INPUTS + len(flat)) + [anywhere] * 3,
        out_specs=[vmem] * (count + 4),
        out_shape=[jax.ShapeDtypeStruct(shape, BF16) for shape in shapes]
        + [jax.ShapeDtypeStruct((size, D), F32) for size in (6, 2, 4)]
        + [jax.ShapeDtypeStruct((rows, D), BF16)],
        scratch_shapes=attention_scratch(rows)
        + reduce_scratch(chunks)
        + [
            pltpu.VMEM((rows, 3 * D), BF16),
            pltpu.VMEM((8, rows, D), BF16),
            pltpu.VMEM(weight.shape, BF16),
            pltpu.VMEM((tallest, 2 * rows), BF16),
            pltpu.VMEM((2 * rows, widest), BF16),
            pltpu.VMEM(terms.shape, F32),
            pltpu.VMEM((VECTOR_AXES, *terms.shape), F32),
            pltpu.VMEM((rows, D), BF16),
            pltpu.SemaphoreType.DMA((slots,)),
            pltpu.SemaphoreType.DMA((slots,)),
            pltpu.SemaphoreType.DMA((3,)),
        ],
        compiler_params=pltpu.CompilerParams(
            collective_id=collective_id, has_side_effects=True, vmem_limit_bytes=60 << 20
        ),
        name="closing",
    )(grads, stats, lse, delta, segs, *norm, terms, vectors, *flat, rows_all, kv, weight)


class PlaneLinks:
    def leave(self, value):
        pairs = [(c * 4 + f, (2 * f + c % 2) * 4 + c // 2) for c in range(8) for f in range(4)]
        return lax.ppermute(value, ("ctx", "fsdp"), pairs)

    def open(self, tokens, segs_row, vectors, shares):
        tokens, segs, vectors, *results = opening(tokens, segs_row, vectors, shares[0], shares[1:], 0)
        *first, kv, rows_all = results[:8]
        return tokens.astype(F32), segs, vectors, as_matrices(results[8:]), (*first, (kv, rows_all))

    def attend(self, normed, vectors, weight, segs, cotangent):
        attended, lse, lse_rows, kv, rows_all, cotangent = attend(
            normed, segs, vectors, weight, cotangent, 2
        )
        return (attended, lse, lse_rows, (kv, rows_all)), cotangent

    def attend_back(self, attention, weight, vectors):
        return attend_back(*attention, weight, vectors, 3)

    def close(self, attention, norm, factors, terms, weight, vectors):
        *sums, small, bias, wide, tokens_grad = closing(
            attention, norm, terms, factors, weight, vectors, 4
        )
        return [total.astype(F32) for total in sums], (small, bias, wide), tokens_grad


class PlainLinks:
    def leave(self, value):
        return value

    def open(self, tokens, segs_row, vectors, shares):
        segs = (segs_row, lax.all_gather(segs_row, "ctx", axis=1, tiled=True))
        gathered = lax.all_gather(pack_vectors(*vectors), "fsdp", axis=0)
        vectors = assemble_vectors([gathered[i] for i in range(4)])
        weights = as_matrices([lax.all_gather(share, "fsdp", axis=0) for share in shares])
        resid = tokens.astype(F32)
        first = norm_forward(resid, vectors[0:1], vectors[1:2])
        first = first + self.attend(first[0], vectors, weights[0], segs, None)[0]
        return resid, segs, vectors, weights, first

    def place(self, segs):
        own_segs, all_segs = segs
        rows = own_segs.shape[1]
        start = (lax.axis_index("ctx") * rows).reshape(1).astype(jnp.int32)
        return start, own_segs.reshape(rows, 1), all_segs

    def blocks(self, block):
        return lax.all_gather(block, "ctx", axis=0)

    def attend(self, normed, vectors, weight, segs, cotangent):
        start, own_segs, all_segs = self.place(segs)
        bias = jnp.concatenate([vectors[6:7], jnp.zeros((1, D), F32), vectors[7:8]], axis=1)
        projected = (jnp.dot(normed, weight, preferred_element_type=F32) + bias).astype(BF16)
        queries, kv_own = projected[:, :D], projected[:, D:]
        kv = self.blocks(kv_own).reshape(-1, 2 * D)
        attended, lse, lse_rows = attention_forward(start, queries, kv, own_segs, all_segs)
        return (attended, lse, lse_rows, (queries, kv_own, kv)), cotangent

    def attend_back(self, attention, weight, vectors):
        grads, stats, lse, delta, segs, (queries, kv_own, kv) = attention
        start, own_segs, all_segs = self.place(segs)
        q_all = self.blocks(queries).reshape(-1, D)
        grad_all = self.blocks(grads).reshape(-1, D)
        return attention_backward(
            start,
            queries,
            grads,
            kv_own,
            lse,
            delta,
            kv,
            q_all,
            grad_all,
            self.blocks(stats),
            own_segs,
            all_segs,
        )

    def close(self, attention, norm, factors, terms, weight, vectors):
        grad_projected = self.attend_back(attention, weight, vectors)
        grad_input, more = input_gradient(grad_projected, weight, *norm)
        terms = terms + jnp.concatenate(
            [more[:2], jnp.zeros((4, D), F32), more[2:], jnp.zeros((8, D), F32)], axis=0
        )
        sums = []
        for later_left, later_right, first_left, *first_right in factors:
            left = jnp.concatenate([later_left, first_left], axis=0)
            right = jnp.concatenate([later_right, *(first_right or [grad_projected])], axis=0)
            term = column_products(left, right).astype(BF16)
            share = lax.psum_scatter(term, "fsdp", scatter_dimension=0, tiled=True)
            sums.append(lax.psum(share.astype(F32), "ctx"))
        terms = lax.psum(terms, ("ctx", "fsdp"))
        return sums, (terms[:6], terms[6:8], terms[8:12]), grad_input.astype(BF16)


def as_matrices(fulls):
    return tuple(full.reshape(-1, full.shape[-1]) for full in fulls)


def layer_forward(resid, weights, vectors, first):
    gain_two, bias_two, bias_proj, bias_out = (vectors[i : i + 1] for i in range(2, 6))
    bias_fc = vectors[8:12].reshape(1, 4 * D)
    _, weight_proj, weight_fc, weight_out = weights
    normed_one, normal_one, inverse_one, attended, lse, lse_rows, state = first
    middle = resid + jnp.dot(attended, weight_proj, preferred_element_type=F32) + bias_proj
    normed_two, normal_two, inverse_two = norm_forward(middle, gain_two, bias_two)
    hidden = jnp.dot(normed_two, weight_fc, preferred_element_type=F32) + bias_fc
    activated = jax.nn.gelu(hidden, approximate=True).astype(BF16)
    result_rows = middle + jnp.dot(activated, weight_out, preferred_element_type=F32) + bias_out
    saved = (
        normed_one,
        normal_one,
        inverse_one,
        state,
        attended,
        lse,
        lse_rows,
        normed_two,
        normal_two,
        inverse_two,
        hidden,
        activated,
    )
    return result_rows, saved


def layer_backward(gradient, weights, vectors, saved, links, segs):
    weight_qkv, weight_proj, weight_fc, weight_out = weights
    gain_one, gain_two = vectors[0:1], vectors[2:3]
    (
        normed_one,
        normal_one,
        inverse_one,
        state,
        attended,
        lse,
        lse_rows,
        normed_two,
        normal_two,
        inverse_two,
        hidden,
        activated,
    ) = saved
    total = lambda value: jnp.sum(value.astype(F32), axis=0)
    grad_branch = gradient.astype(BF16)
    grad_activated = dot_rows(grad_branch, weight_out)
    gelu_pull = jax.vjp(partial(jax.nn.gelu, approximate=True), hidden)[1]
    grad_hidden = gelu_pull(grad_activated)[0].astype(BF16)
    grad_normed_two = dot_rows(grad_hidden, weight_fc)
    grad_in_two, grad_gain_two, grad_bias_two = norm_backward(
        grad_normed_two, normal_two, inverse_two, gain_two
    )
    grad_middle = gradient + grad_in_two
    grad_proj = grad_middle.astype(BF16)
    grad_attended = dot_rows(grad_proj, weight_proj).astype(BF16)
    products = grad_attended.astype(F32) * attended.astype(F32)
    head_of = jnp.arange(D, dtype=jnp.int32) // HDIM
    by_lane = (head_of[:, None] == jnp.arange(LANES, dtype=jnp.int32)[None, :]).astype(F32)
    by_row = (jnp.arange(16, dtype=jnp.int32)[:, None] == head_of[None, :]).astype(F32)
    delta = jnp.dot(products, by_lane, precision=lax.Precision.HIGHEST, preferred_element_type=F32)
    delta_rows = lax.dot_general(
        by_row,
        products,
        (((1,), (1,)), ((), ())),
        precision=lax.Precision.HIGHEST,
        preferred_element_type=F32,
    )
    stats = jnp.concatenate([lse_rows, delta_rows], axis=0)
    attention = (grad_attended, stats, lse, delta, segs, state)
    norm = (normal_one, inverse_one, gain_one, grad_middle)
    matrices = ((activated, grad_branch), (normed_two, grad_hidden), (attended, grad_proj))
    upper = jnp.stack([grad_gain_two, grad_bias_two, total(grad_proj), total(grad_branch)])
    lower = total(grad_hidden).reshape(4, D)
    return attention, norm, matrices, (upper, lower)


def input_gradient(grad_projected, weight_qkv, normal, inverse, gain, middle):
    total = lambda value: jnp.sum(value.astype(F32), axis=0)
    grad_normed = dot_rows(grad_projected, weight_qkv)
    grad_in, grad_gain, grad_bias = norm_backward(grad_normed, normal, inverse, gain)
    terms = [
        grad_gain,
        grad_bias,
        total(grad_projected[:, :D]),
        total(grad_projected[:, 2 * D :]),
    ]
    return middle + grad_in, jnp.stack(terms)


def body(
    links,
    tokens,
    segment_ids,
    ln1_gain,
    ln1_bias,
    attn_weight,
    attn_bias,
    proj_weight,
    proj_bias,
    ln2_gain,
    ln2_bias,
    fc_weight,
    fc_bias,
    out_weight,
    out_bias,
    out_cotangent,
):
    vectors = (
        ln1_gain,
        ln1_bias,
        ln2_gain,
        ln2_bias,
        proj_bias,
        out_bias,
        attn_bias,
        fc_bias,
    )
    shares = [attn_weight, proj_weight, fc_weight, out_weight]
    resid, segs, vectors, weights, first = links.open(tokens[0], segment_ids, vectors, shares)
    resid, saved = layer_forward(resid, weights, vectors, first)
    saved_layers = [saved]
    first = norm_forward(resid, vectors[0:1], vectors[1:2])
    attended, gradient = links.attend(first[0], vectors, weights[0], segs, out_cotangent[0])
    resid, saved = layer_forward(resid, weights, vectors, first + attended)
    saved_layers.append(saved)
    output = links.leave(resid.astype(BF16))
    gradient = gradient.astype(F32)
    attention, norm, later, (upper, lower) = layer_backward(
        gradient, weights, vectors, saved_layers[1], links, segs
    )
    later_projected = links.attend_back(attention, weights[0], vectors)
    gradient, terms = input_gradient(later_projected, weights[0], *norm)
    attention, norm, first, (more_upper, more_lower) = layer_backward(
        gradient, weights, vectors, saved_layers[0], links, segs
    )
    factors = [(*a, *b) for a, b in zip(later, first)]
    factors.append((saved_layers[1][0], later_projected, saved_layers[0][0]))
    packed = jnp.concatenate(
        [terms[:2], upper + more_upper, terms[2:], lower + more_lower, jnp.zeros((4, D), F32)], axis=0
    )
    (out_grad, fc_grad, proj_grad, qkv_grad), (small, bias_qv, bias_fc), tokens_grad = links.close(
        attention, norm, factors, packed, weights[0], vectors
    )
    own = lax.axis_index("fsdp")
    pick = lambda value, axis: lax.dynamic_index_in_dim(value, own, axis, keepdims=False)
    small = pick(small.reshape(6, 4, -1), 1)
    bias_qv = pick(bias_qv.reshape(4, -1), 0)
    bias_fc = pick(bias_fc, 0)
    gain_one, bias_one, gain_two, bias_two, bias_proj, bias_out = (small[i] for i in range(6))
    return (
        output[None],
        tokens_grad[None],
        gain_one,
        bias_one,
        qkv_grad,
        bias_qv,
        proj_grad,
        bias_proj,
        gain_two,
        bias_two,
        fc_grad,
        bias_fc,
        out_grad,
        bias_out,
    )


def solution(mesh):
    links = PlaneLinks() if (mesh.shape["ctx"], mesh.shape["fsdp"]) == (8, 4) else PlainLinks()
    rows = P("fsdp", "ctx", None)
    vector, matrix = P("fsdp"), P("fsdp", None)
    in_specs = (
        rows,
        P("fsdp", "ctx"),
        vector,
        vector,
        matrix,
        vector,
        matrix,
        vector,
        vector,
        vector,
        matrix,
        vector,
        matrix,
        vector,
        rows,
    )
    out_specs = (
        rows,
        rows,
        vector,
        vector,
        matrix,
        vector,
        matrix,
        vector,
        vector,
        vector,
        matrix,
        vector,
        matrix,
        vector,
    )
    return jax.shard_map(
        partial(body, links), mesh=mesh, in_specs=in_specs, out_specs=out_specs, check_vma=False
    )
```

```python
from functools import partial

import jax
import jax.numpy as jnp
from jax import lax
from jax.experimental import pallas as pl
from jax.experimental.pallas import tpu as pltpu
from jax.sharding import PartitionSpec as P

D = 768
HEADS = 12
HDIM = 64
PAIRS = HEADS // 2
LANES = 128
EPSILON = 1e-05
NEGATIVE = -1e30
SCALE = HDIM ** (-0.5)
MESH = pl.DeviceIdType.MESH
F32 = jnp.float32
BF16 = jnp.bfloat16


def norm_forward(resid, gain_row, bias_row):
    average = jnp.mean(resid, axis=-1, keepdims=True)
    centred = resid - average
    variance = jnp.mean(centred * centred, axis=-1, keepdims=True)
    inverse = lax.rsqrt(variance + EPSILON)
    normal = centred * inverse
    return ((normal * gain_row + bias_row).astype(BF16), normal, inverse)


def norm_backward(grad_normed, normal, inverse, gain_row):
    scaled = grad_normed * gain_row
    mean_term = jnp.mean(scaled, axis=-1, keepdims=True)
    second = jnp.mean(scaled * normal, axis=-1, keepdims=True)
    grad_input = inverse * (scaled - mean_term - normal * second)
    return (grad_input, jnp.sum(grad_normed * normal, axis=0), jnp.sum(grad_normed, axis=0))


def two_heads(rows):
    lane = lax.broadcasted_iota(jnp.int32, rows.shape, 1)
    zero = jnp.zeros_like(rows)
    first = jnp.where(lane < HDIM, rows, zero)
    second = jnp.where(lane < HDIM, zero, rows)
    return jnp.concatenate([first, second], axis=0)


def one_pair(stacked):
    half = stacked.shape[0] // 2
    lane = lax.broadcasted_iota(jnp.int32, (half, LANES), 1)
    return jnp.where(lane < HDIM, stacked[:half], stacked[half:])


def dot_rows(left, right):
    return lax.dot_general(left, right, (((1,), (1,)), ((), ())), preferred_element_type=F32)


def column_products(left, right):
    return lax.dot_general(left, right, (((0,), (0,)), ((), ())), preferred_element_type=F32)


def pick_lanes(columns, pair):
    lane = lax.broadcasted_iota(jnp.int32, columns.shape, 1)
    first = jnp.sum(jnp.where(lane == 2 * pair, columns, 0.0), axis=1, keepdims=True)
    second = jnp.sum(jnp.where(lane == 2 * pair + 1, columns, 0.0), axis=1, keepdims=True)
    return jnp.concatenate([first, second], axis=0)


def mask_columns(bias_ref, own_segs, all_segs_ref, start, own_is_query):
    rows, columns = bias_ref.shape
    step = min(1024, columns)
    own_place = start + lax.broadcasted_iota(jnp.int32, (rows, step), 0)
    for offset in range(0, columns, step):
        place = offset + lax.broadcasted_iota(jnp.int32, (rows, step), 1)
        causal = (place <= own_place) if own_is_query else (own_place <= place)
        same = own_segs == all_segs_ref[:, offset : offset + step]
        bias_ref[:, offset : offset + step] = jnp.where(causal & same, 0.0, NEGATIVE)


def attention_forward_kernel(
    start_ref, q_ref, k_ref, v_ref, own_segs_ref, all_segs_ref, out_ref, lse_ref, lse_rows_ref, bias_ref
):
    pair = pl.program_id(0)
    rows, keys = bias_ref.shape

    @pl.when(pair == 0)
    def _():
        mask_columns(bias_ref, own_segs_ref[...], all_segs_ref, start_ref[0], True)
        lse_ref[...] = jnp.zeros_like(lse_ref)

    queries = two_heads(q_ref[...] * jnp.asarray(SCALE, BF16))
    step = min(1024, keys)

    def scores_of(offset):
        scores = dot_rows(queries, k_ref[pl.ds(offset, step), :])
        bias = bias_ref[:, pl.ds(offset, step)]
        return scores + jnp.concatenate([bias, bias], axis=0)

    if step == keys:
        scores = scores_of(0)
        top = jnp.max(scores, axis=1, keepdims=True)
        weights = jnp.exp(scores - top)
        total = jnp.sum(weights, axis=1, keepdims=True)
        mixed = jnp.dot(weights.astype(BF16), v_ref[...], preferred_element_type=F32)
    else:

        def visit(index, carried):
            top, total, mixed = carried
            offset = pl.multiple_of(index * step, step)
            scores = scores_of(offset)
            new_top = jnp.maximum(top, jnp.max(scores, axis=1, keepdims=True))
            weights = jnp.exp(scores - new_top)
            factor = jnp.exp(top - new_top)
            total = total * factor + jnp.sum(weights, axis=1, keepdims=True)
            more = jnp.dot(
                weights.astype(BF16), v_ref[pl.ds(offset, step), :], preferred_element_type=F32
            )
            return new_top, total, mixed * factor + more

        top, total, mixed = lax.fori_loop(
            0,
            (start_ref[0] + rows + step - 1) // step,
            visit,
            (
                jnp.full((2 * rows, 1), NEGATIVE, F32),
                jnp.zeros((2 * rows, 1), F32),
                jnp.zeros((2 * rows, LANES), F32),
            ),
        )
    out_ref[...] = one_pair(mixed / total).astype(BF16)
    lse = top + jnp.log(total)
    lane = lax.broadcasted_iota(jnp.int32, (rows, LANES), 1)
    kept = lse_ref[...]
    kept = jnp.where(lane == 2 * pair, lse[:rows], kept)
    kept = jnp.where(lane == 2 * pair + 1, lse[rows:], kept)
    lse_ref[...] = kept

    @pl.when(pair == PAIRS - 1)
    def _():
        lse_rows_ref[...] = kept.T[:16]


def attention_forward(start, queries, kv, own_segs, all_segs):
    rows = queries.shape[0]
    keys = kv.shape[0]
    whole = lambda shape: pl.BlockSpec(shape, lambda p: (0, 0))
    return pl.pallas_call(
        attention_forward_kernel,
        grid=(PAIRS,),
        in_specs=[
            pl.BlockSpec(memory_space=pltpu.SMEM),
            pl.BlockSpec((rows, LANES), lambda p: (0, p)),
            pl.BlockSpec((keys, LANES), lambda p: (0, p)),
            pl.BlockSpec((keys, LANES), lambda p: (0, PAIRS + p)),
            whole((rows, 1)),
            whole((1, keys)),
        ],
        out_specs=[
            pl.BlockSpec((rows, LANES), lambda p: (0, p)),
            whole((rows, LANES)),
            whole((16, rows)),
        ],
        out_shape=[
            jax.ShapeDtypeStruct((rows, D), BF16),
            jax.ShapeDtypeStruct((rows, LANES), F32),
            jax.ShapeDtypeStruct((16, rows), F32),
        ],
        scratch_shapes=[pltpu.VMEM((rows, keys), F32)],
        compiler_params=pltpu.CompilerParams(vmem_limit_bytes=60 << 20),
        cost_estimate=pl.CostEstimate(
            flops=8 * rows * keys * D, bytes_accessed=4 * keys * D, transcendentals=rows * keys * HEADS
        ),
        name="attention_forward",
    )(start, queries, kv, kv, own_segs, all_segs)


def attention_backward_kernel(
    start_ref,
    q_ref,
    grad_ref,
    k_own_ref,
    v_own_ref,
    lse_ref,
    delta_ref,
    k_ref,
    v_ref,
    q_all_ref,
    grad_all_ref,
    stats_ref,
    own_segs_ref,
    all_segs_ref,
    out_ref,
    query_bias_ref,
    key_bias_ref,
):
    pair = pl.program_id(0)
    rows, tokens = query_bias_ref.shape
    start = start_ref[0]

    @pl.when(pair == 0)
    def _():
        mask_columns(query_bias_ref, own_segs_ref[...], all_segs_ref, start, True)
        mask_columns(key_bias_ref, own_segs_ref[...], all_segs_ref, start, False)

    step = min(256, tokens)
    blocks = step // rows
    scale = jnp.asarray(SCALE, BF16)

    def doubled(bias):
        return jnp.concatenate([bias, bias], axis=0)

    queries = two_heads(q_ref[...] * scale)
    grads = two_heads(grad_ref[...])
    lse = pick_lanes(lse_ref[...], pair)
    delta = pick_lanes(delta_ref[...], pair)

    def visit_keys(index, grad_query):
        offset = pl.multiple_of(index * step, step)
        keys = k_ref[pl.ds(offset, step), :]
        values = v_ref[pl.ds(offset, step), :]
        bias = doubled(query_bias_ref[:, pl.ds(offset, step)])
        attention = jnp.exp(dot_rows(queries, keys) + bias - lse)
        grad_attention = dot_rows(grads, values)
        grad_scores = (attention * (grad_attention - delta)).astype(BF16)
        return grad_query + jnp.dot(grad_scores, keys, preferred_element_type=F32)

    zeros = jnp.zeros((2 * rows, LANES), F32)
    grad_query = lax.fori_loop(0, (start + rows + step - 1) // step, visit_keys, zeros)

    own_keys = two_heads(k_own_ref[...] * scale)
    own_values = two_heads(v_own_ref[...])

    def row_of(block, row):
        return jnp.broadcast_to(stats_ref[block, pl.ds(row, 1), :], (rows, rows))

    def stat_rows(index, row):
        first = [row_of(index * blocks + b, row + 2 * pair) for b in range(blocks)]
        second = [row_of(index * blocks + b, row + 2 * pair + 1) for b in range(blocks)]
        return jnp.concatenate(
            [jnp.concatenate(first, axis=1), jnp.concatenate(second, axis=1)], axis=0
        )

    def visit_queries(index, carried):
        grad_keys, grad_values = carried
        offset = pl.multiple_of(index * step, step)
        later = q_all_ref[pl.ds(offset, step), :]
        later_grads = grad_all_ref[pl.ds(offset, step), :]
        bias = doubled(key_bias_ref[:, pl.ds(offset, step)])
        attention = jnp.exp(dot_rows(own_keys, later) + bias - stat_rows(index, 0))
        grad_attention = dot_rows(own_values, later_grads)
        grad_scores = (attention * (grad_attention - stat_rows(index, 16))).astype(BF16)
        grad_keys = grad_keys + jnp.dot(grad_scores, later, preferred_element_type=F32)
        grad_values = grad_values + jnp.dot(
            attention.astype(BF16), later_grads, preferred_element_type=F32
        )
        return grad_keys, grad_values

    grad_keys, grad_values = lax.fori_loop(
        start // step, tokens // step, visit_queries, (zeros, zeros)
    )
    base = pl.multiple_of(pair * LANES, LANES)
    out_ref[:, pl.ds(base, LANES)] = (one_pair(grad_query) * SCALE).astype(BF16)
    out_ref[:, pl.ds(D + base, LANES)] = (one_pair(grad_keys) * SCALE).astype(BF16)
    out_ref[:, pl.ds(2 * D + base, LANES)] = one_pair(grad_values).astype(BF16)


def attention_backward(
    start, queries, grads, kv_own, lse, delta, kv, q_all, grad_all, stats, own_segs, all_segs
):
    rows = queries.shape[0]
    tokens = kv.shape[0]
    whole = lambda shape: pl.BlockSpec(shape, lambda p: (0,) * len(shape))
    own = pl.BlockSpec((rows, LANES), lambda p: (0, p))
    every = pl.BlockSpec((tokens, LANES), lambda p: (0, p))
    return pl.pallas_call(
        attention_backward_kernel,
        grid=(PAIRS,),
        in_specs=[
            pl.BlockSpec(memory_space=pltpu.SMEM),
            own,
            own,
            own,
            pl.BlockSpec((rows, LANES), lambda p: (0, PAIRS + p)),
            whole((rows, LANES)),
            whole((rows, LANES)),
            every,
            pl.BlockSpec((tokens, LANES), lambda p: (0, PAIRS + p)),
            every,
            every,
            whole(stats.shape),
            whole((rows, 1)),
            whole((1, tokens)),
        ],
        out_specs=whole((rows, 3 * D)),
        out_shape=jax.ShapeDtypeStruct((rows, 3 * D), BF16),
        scratch_shapes=[pltpu.VMEM((rows, tokens), F32), pltpu.VMEM((rows, tokens), F32)],
        compiler_params=pltpu.CompilerParams(vmem_limit_bytes=60 << 20),
        cost_estimate=pl.CostEstimate(
            flops=16 * rows * tokens * D,
            bytes_accessed=8 * tokens * D,
            transcendentals=rows * tokens * HEADS,
        ),
        name="attention_backward",
    )(
        start,
        queries,
        grads,
        kv_own,
        kv_own,
        lse,
        delta,
        kv,
        kv,
        q_all,
        grad_all,
        stats,
        own_segs,
        all_segs,
    )


def place_bits():
    ctx, fsdp = lax.axis_index("ctx"), lax.axis_index("fsdp")
    return lax.rem(ctx, 2), ctx // 2, fsdp // 2, lax.rem(fsdp, 2)


class Place:
    def __init__(self):
        self.x, self.z, self.y, self.core = x, z, y, core = place_bits()
        self.low, self.high = low, high = lax.rem(z, 2), z // 2
        self.fsdp = fsdp = 2 * y + core
        self.block = 2 * fsdp + x
        self.sibling = (2 * z + x, 2 * y + 1 - core)
        self.over_y = (2 * z + x, 2 * (1 - y) + core)
        self.over_x = (2 * z + 1 - x, fsdp)
        self.over_z = (2 * (z + 1 - 2 * low) + x, fsdp)
        self.over_zz = (2 * (z + 2 - 4 * high) + x, fsdp)
        self.partner = (2 * fsdp + x, z)
        self.has_partner = fsdp != z


class Copies:
    def __init__(self, send_sems, recv_sems):
        self.send_sems, self.recv_sems = send_sems, recv_sems
        self.used = 0

    def make(self, src, dst, device):
        slot = self.used
        self.used += 1
        return pltpu.make_async_remote_copy(
            src_ref=src,
            dst_ref=dst,
            send_sem=self.send_sems.at[slot],
            recv_sem=self.recv_sems.at[slot],
            device_id=device,
            device_id_type=MESH,
        )


def greet(devices):
    barrier = pltpu.get_barrier_semaphore()
    for device in devices:
        pl.semaphore_signal(barrier, inc=1, device_id=device, device_id_type=MESH)
    pl.semaphore_wait(barrier, len(devices))


WEIGHT_COPIES = 11


def weight_cuts(shape):
    rows, columns = shape
    pieces = 1 if rows * columns <= 192 * 768 else 3 if columns == 3 * D else 2
    width = columns // pieces
    return [(i * width, width) for i in range(pieces)]


class WeightGather:
    def __init__(self, place, copies, shares, fulls, stages, local_sems):
        x, low = place.x, place.low
        own, other = place.fsdp, 2 * (1 - place.y) + place.core
        self.plans = []
        self.locals = []
        self.arrived = set()
        for which, (share, full) in enumerate(zip(shares, fulls)):
            part = share.shape[0] // 4
            for first, width in weight_cuts(share.shape):
                columns = pl.ds(first, width)

                def piece(ref, x_bit, low_bit, part=part, columns=columns):
                    return ref.at[pl.ds((2 * low_bit + x_bit) * part, part), columns]

                def side(ref, x_bit, low_bit, index, part=part, first=first, width=width):
                    start = (2 * low_bit + x_bit) * part
                    if part % 32 == 0:
                        rows = pl.ds(start + index * (part // 2), part // 2)
                        return ref.at[rows, pl.ds(first, width)]
                    half = width // 2
                    return ref.at[pl.ds(start, part), pl.ds(first + index * half, half)]

                theirs = full.at[other]
                same = lambda view, device: copies.make(view, view, device)
                mine = piece(theirs, x, low)
                from_x, from_z = piece(theirs, 1 - x, low), piece(theirs, x, 1 - low)
                self.plans.append(
                    [
                        copies.make(piece(share, x, low), piece(full.at[own], x, low), place.over_y),
                        same(mine, place.over_x),
                        same(mine, place.over_z),
                        same(mine, place.sibling),
                        same(side(theirs, 1 - x, low, 0), place.over_z),
                        same(from_x, place.sibling),
                        same(side(theirs, x, 1 - low, 1), place.over_x),
                        same(from_z, place.sibling),
                        same(side(theirs, 1 - x, 1 - low, 0), place.sibling),
                        same(side(theirs, 1 - x, 1 - low, 1), place.sibling),
                        copies.make(share.at[:, columns], full.at[own, :, columns], place.sibling),
                    ]
                )
            sem = local_sems.at[which]
            if stages[which] is None:
                self.locals.append((pltpu.make_async_copy(share, full.at[own], sem), None))
            else:
                self.locals.append(
                    (
                        pltpu.make_async_copy(share, stages[which], sem),
                        pltpu.make_async_copy(stages[which], full.at[own], sem),
                    )
                )

    def begin(self):
        for plan in self.plans:
            plan[0].start()
        for plan in self.plans:
            plan[10].start()
        for into, _ in self.locals:
            into.start()

    def keep_own(self):
        for into, out in self.locals:
            into.wait()
            if out is not None:
                out.start()

    def arrive(self, first, last):
        for index in range(first, last):
            if index not in self.arrived:
                self.arrived.add(index)
                for copy in (3, 5, 7, 8, 9, 10):
                    self.plans[index][copy].wait_recv()

    def steps(self):
        count = len(self.plans)
        for step in range(count + 2):
            yield step

    def step(self, step):
        count = len(self.plans)
        if step < count:
            plan = self.plans[step]
            plan[0].wait_recv()
            plan[1].start()
            plan[2].start()
            plan[3].start()
        if 0 <= step - 1 < count:
            plan = self.plans[step - 1]
            plan[1].wait_recv()
            plan[4].start()
            plan[5].start()
            plan[2].wait_recv()
            plan[6].start()
            plan[7].start()
        if 0 <= step - 2 < count:
            plan = self.plans[step - 2]
            plan[4].wait_recv()
            plan[8].start()
            plan[6].wait_recv()
            plan[9].start()

    def finish(self):
        self.arrive(0, len(self.plans))
        for plan in self.plans:
            for copy in plan:
                copy.wait_send()
        for _, out in self.locals:
            if out is not None:
                out.wait()


BLOCK_COPIES = 13


class BlockGather:
    def __init__(self, place, copies, blocks, fulls):
        self.own = place.block
        self.pairs = list(zip(blocks, fulls))
        self.plans = []
        for block, full in self.pairs:
            half = block.shape[0] // 2

            def part(ref, side, half=half):
                return ref.at[pl.ds(side * half, half), :]

            def slot_of(x_bit, y_bit, full=full):
                return full.at[4 * y_bit + 2 * place.core + x_bit]

            same = lambda view, device: copies.make(view, view, device)
            x, y = place.x, place.y
            mine, from_x = slot_of(x, y), slot_of(1 - x, y)
            from_y, from_both = slot_of(x, 1 - y), slot_of(1 - x, 1 - y)
            self.plans.append(
                [
                    copies.make(block, mine, place.sibling),
                    copies.make(part(block, 0), part(mine, 0), place.over_x),
                    copies.make(part(block, 1), part(mine, 1), place.over_y),
                    copies.make(part(block, 1), part(mine, 1), place.over_x),
                    copies.make(part(block, 0), part(mine, 0), place.over_y),
                    same(part(from_x, 0), place.over_y),
                    same(part(from_x, 0), place.sibling),
                    same(part(from_y, 1), place.over_x),
                    same(part(from_y, 1), place.sibling),
                    same(part(from_x, 1), place.sibling),
                    same(part(from_y, 0), place.sibling),
                    same(part(from_both, 0), place.sibling),
                    same(part(from_both, 1), place.sibling),
                ]
            )

    def begin(self):
        for index in (1, 2, 3, 4, 0):
            for plan in self.plans:
                plan[index].start()
        for block, full in self.pairs:
            full[self.own] = block[...]

    def relay(self, *pairs):
        for arrived, followers in pairs:
            for plan in self.plans:
                plan[arrived].wait_recv()
                for index in followers:
                    plan[index].start()

    def first_halves(self):
        self.relay((1, (5, 6)), (2, (7, 8)))

    def second_halves(self):
        self.relay((3, (9,)), (4, (10,)))

    def corners(self):
        self.relay((5, (11,)), (7, (12,)))

    def wait(self, *indices):
        for plan in self.plans:
            for index in indices:
                plan[index].wait_recv()

    def wait_near(self):
        self.wait(0, 6, 9)

    def wait_far(self):
        self.wait(8, 10, 11, 12)

    def finish(self):
        for plan in self.plans:
            for copy in plan:
                copy.wait_send()


VECTORS = 8


def pack_vectors(ln1_gain, ln1_bias, ln2_gain, ln2_bias, proj_bias, out_bias, attn_bias, fc_bias):
    rows = (ln1_gain, ln1_bias, ln2_gain, ln2_bias, proj_bias, out_bias, attn_bias, fc_bias)
    return jnp.stack([jnp.pad(row.astype(F32), (0, D - row.shape[0])) for row in rows])


def assemble_vectors(shares):
    quarter = D // 4
    small = jnp.concatenate([share[:6, :quarter] for share in shares], axis=1)
    query = jnp.concatenate([shares[0][6:7, : 2 * quarter], shares[1][6:7, : 2 * quarter]], axis=1)
    value = jnp.concatenate([shares[2][6:7, : 2 * quarter], shares[3][6:7, : 2 * quarter]], axis=1)
    hidden = [share[7:8] for share in shares]
    return jnp.concatenate([small, query, value, *hidden, jnp.zeros((4, D), F32)], axis=0)


def mask_block(own_segs, segs_ref, block, start, own_is_query):
    rows = own_segs.shape[0]
    own_place = start + lax.broadcasted_iota(jnp.int32, (rows, rows), 0)
    place = block * rows + lax.broadcasted_iota(jnp.int32, (rows, rows), 1)
    causal = (place <= own_place) if own_is_query else (own_place <= place)
    same = own_segs == segs_ref[block, 0:1, :]
    return jnp.where(causal & same, 0.0, NEGATIVE)


def own_columns(segs_ref, block):
    rows = segs_ref.shape[2]
    return jnp.broadcast_to(segs_ref[block, 0:1, :], (rows, rows)).T


def project_blocks(rows_all, first, weight_of, bias, out_ref, width):
    rows = rows_all[pl.ds(first, 4)].reshape(4 * rows_all.shape[1], D)
    for side in range(width // D):
        total = jnp.dot(rows, weight_of(side), preferred_element_type=F32)
        if bias[side] is not None:
            total = total + bias[side]
        out_ref[pl.ds(first, 4), :, side * D : (side + 1) * D] = total.astype(BF16).reshape(4, -1, D)


class AttentionForward:
    def __init__(
        self, place, q_ref, segs_ref, rows_all, kv_all, outs, scratch, sems, weight_of, vectors_ref
    ):
        self.place = place
        out_ref, lse_ref, lse_rows_ref, kv_out, rows_out = outs
        self.q_ref, self.segs_ref, self.kv_all = q_ref, segs_ref, kv_all
        self.rows_all, self.weight_of, self.vectors_ref = rows_all, weight_of, vectors_ref
        self.out_ref, self.lse_ref, self.lse_rows_ref = out_ref, lse_ref, lse_rows_ref
        self.near_bias, self.far_bias, self.top, self.total, self.mixed = scratch
        self.rows = q_ref.shape[0]
        self.near, self.far = 4 * place.y, 4 * (1 - place.y)
        moves = [
            (kv_all.at[pl.ds(self.near, 4)], kv_out.at[pl.ds(self.near, 4)]),
            (kv_all.at[pl.ds(self.far, 4)], kv_out.at[pl.ds(self.far, 4)]),
            (rows_all, rows_out),
        ]
        self.saves = [pltpu.make_async_copy(*move, sem) for move, sem in zip(moves, sems)]

    def project_queries(self):
        rows = self.rows_all[self.place.block]
        total = jnp.dot(rows, self.weight_of(0), preferred_element_type=F32)
        self.q_ref[...] = (total + self.vectors_ref[6:7, :]).astype(BF16)

    def project(self, first):
        biases = (None, self.vectors_ref[7:8, :])
        project_blocks(
            self.rows_all, first, lambda side: self.weight_of(side + 1), biases, self.kv_all, 2 * D
        )

    def masks(self, far):
        rows = self.rows
        start = self.place.block * rows
        own_segs = own_columns(self.segs_ref, self.place.block)
        first, bias = (self.far, self.far_bias) if far else (self.near, self.near_bias)
        for i in range(4):
            at = slice(i * rows, (i + 1) * rows)
            bias[:, at] = mask_block(own_segs, self.segs_ref, first + i, start, True)

    def lanes(self, pair, side=0):
        return pl.ds(pl.multiple_of(side * D + pair * LANES, LANES), LANES)

    def part(self, first, bias_ref, pair):
        rows = self.rows
        queries = two_heads(self.q_ref[:, self.lanes(pair)] * jnp.asarray(SCALE, BF16))
        keys = self.kv_all[pl.ds(first, 4), :, self.lanes(pair)].reshape(4 * rows, LANES)
        values = self.kv_all[pl.ds(first, 4), :, self.lanes(pair, 1)].reshape(4 * rows, LANES)
        bias = bias_ref[...]
        scores = dot_rows(queries, keys) + jnp.concatenate([bias, bias], axis=0)
        top = jnp.max(scores, axis=1, keepdims=True)
        shares = jnp.exp(scores - top)
        total = jnp.sum(shares, axis=1, keepdims=True)
        return top, total, jnp.dot(shares.astype(BF16), values, preferred_element_type=F32)

    def near_part(self):
        self.project(self.near)
        self.saves[0].start()
        self.lse_ref[...] = jnp.zeros_like(self.lse_ref)

        def visit(pair, carried):
            self.top[pair], self.total[pair], self.mixed[pair] = self.part(
                self.near, self.near_bias, pair
            )
            return carried

        lax.fori_loop(0, PAIRS, visit, 0, unroll=3)

    def far_part(self):
        self.saves[2].start()
        self.project(self.far)
        self.saves[1].start()

        def visit(pair, carried):
            top, total, mixed = self.part(self.far, self.far_bias, pair)
            old_top = self.top[pair]
            new_top = jnp.maximum(top, old_top)
            new, old = jnp.exp(top - new_top), jnp.exp(old_top - new_top)
            self.top[pair] = new_top
            self.total[pair] = total * new + self.total[pair] * old
            self.mixed[pair] = mixed * new + self.mixed[pair] * old
            return carried

        @pl.when(self.place.y == 1)
        def _():
            lax.fori_loop(0, PAIRS, visit, 0, unroll=3)

    def store(self):
        rows = self.rows

        def visit(pair, carried):
            total = self.total[pair]
            self.out_ref[:, self.lanes(pair)] = one_pair(self.mixed[pair] / total).astype(BF16)
            lse = self.top[pair] + jnp.log(total)
            lane = lax.broadcasted_iota(jnp.int32, (rows, LANES), 1)
            kept = jnp.where(lane == 2 * pair, lse[:rows], self.lse_ref[...])
            self.lse_ref[...] = jnp.where(lane == 2 * pair + 1, lse[rows:], kept)
            return carried

        lax.fori_loop(0, PAIRS, visit, 0, unroll=3)
        self.lse_rows_ref[...] = self.lse_ref[...].T[:16]

    def finish(self):
        for save in self.saves:
            save.wait()


def forward_scratch(rows):
    return [
        pltpu.VMEM((8, rows, 2 * D), BF16),
        pltpu.VMEM((8, rows, D), BF16),
        pltpu.VMEM((rows, D), BF16),
        pltpu.VMEM((rows, 4 * rows), F32),
        pltpu.VMEM((rows, 4 * rows), F32),
        pltpu.VMEM((PAIRS, 2 * rows, 1), F32),
        pltpu.VMEM((PAIRS, 2 * rows, 1), F32),
        pltpu.VMEM((PAIRS, 2 * rows, LANES), F32),
    ]


FORWARD_SCRATCH = 8


def forward_shapes(rows):
    return [
        jax.ShapeDtypeStruct((rows, D), BF16),
        jax.ShapeDtypeStruct((rows, LANES), F32),
        jax.ShapeDtypeStruct((16, rows), F32),
        jax.ShapeDtypeStruct((8, rows, 2 * D), BF16),
        jax.ShapeDtypeStruct((8, rows, D), BF16),
    ]


def greet_with_partner(place, others):
    barrier = pltpu.get_barrier_semaphore()
    for device in others:
        pl.semaphore_signal(barrier, inc=1, device_id=device, device_id_type=MESH)

    @pl.when(place.has_partner)
    def _():
        pl.semaphore_signal(barrier, inc=1, device_id=place.partner, device_id_type=MESH)
        pl.semaphore_wait(barrier, len(others) + 1)

    @pl.when(jnp.logical_not(place.has_partner))
    def _():
        pl.semaphore_wait(barrier, len(others))


def attend_kernel(
    rows_ref,
    segs_ref,
    vectors_ref,
    weight_ref,
    cotangent_ref,
    out_ref,
    lse_ref,
    lse_rows_ref,
    kv_out,
    rows_out,
    cotangent_out,
    *scratch,
):
    kv_all, rows_all, q_ref = scratch[:3]
    weight, send_sems, recv_sems, local_sems = scratch[FORWARD_SCRATCH:]
    place = Place()
    load = pltpu.make_async_copy(weight_ref, weight, local_sems.at[3])
    load.start()
    greet_with_partner(place, (place.sibling, place.over_x, place.over_y))
    copies = Copies(send_sems, recv_sems)
    gather = BlockGather(place, copies, [rows_ref], [rows_all])
    swap = copies.make(cotangent_ref, cotangent_out, place.partner)
    keep = pltpu.make_async_copy(cotangent_ref, cotangent_out, local_sems.at[4])
    gather.begin()

    @pl.when(place.has_partner)
    def _():
        swap.start()

    @pl.when(jnp.logical_not(place.has_partner))
    def _():
        keep.start()

    attention = AttentionForward(
        place,
        q_ref,
        segs_ref,
        rows_all,
        kv_all,
        (out_ref, lse_ref, lse_rows_ref, kv_out, rows_out),
        scratch[3:FORWARD_SCRATCH],
        [local_sems.at[i] for i in range(3)],
        lambda side: weight[:, side * D : (side + 1) * D],
        vectors_ref,
    )
    attention.masks(False)
    attention.masks(True)
    load.wait()
    attention.project_queries()
    gather.first_halves()
    gather.second_halves()
    gather.wait_near()
    gather.corners()
    attention.near_part()
    gather.wait_far()
    attention.far_part()
    attention.store()
    attention.finish()
    gather.finish()

    @pl.when(place.has_partner)
    def _():
        swap.wait()

    @pl.when(jnp.logical_not(place.has_partner))
    def _():
        keep.wait()


def attend(normed, segs, vectors, weight, cotangent, collective_id):
    rows = normed.shape[0]
    vmem = pl.BlockSpec(memory_space=pltpu.VMEM)
    anywhere = pl.BlockSpec(memory_space=pl.ANY)
    return pl.pallas_call(
        attend_kernel,
        in_specs=[vmem, vmem, vmem, anywhere, anywhere],
        out_specs=[vmem, vmem, vmem, anywhere, anywhere, vmem],
        out_shape=forward_shapes(rows) + [jax.ShapeDtypeStruct((rows, D), BF16)],
        scratch_shapes=forward_scratch(rows)
        + [
            pltpu.VMEM(weight.shape, BF16),
            pltpu.SemaphoreType.DMA((BLOCK_COPIES + 1,)),
            pltpu.SemaphoreType.DMA((BLOCK_COPIES + 1,)),
            pltpu.SemaphoreType.DMA((5,)),
        ],
        compiler_params=pltpu.CompilerParams(
            collective_id=collective_id, has_side_effects=True, vmem_limit_bytes=36 << 20
        ),
        name="attend",
    )(normed, segs, vectors, weight, cotangent)


def opening_kernel(count, *refs):
    tokens_ref, segs_ref, first_ref = refs[:3]
    vector_refs = refs[3 : 3 + VECTORS]
    shares = refs[3 + VECTORS : 3 + VECTORS + count]
    refs = refs[3 + VECTORS + count :]
    (
        tokens_out,
        segs_out,
        vectors_out,
        normed_out,
        normal_out,
        inverse_out,
        attended_out,
        lse_out,
        lse_rows_out,
        kv_out,
        rows_out,
        first_out,
    ) = refs[:12]
    fulls = refs[12 : 12 + count]
    refs = refs[12 + count :]
    kv_all, rows_all, q_ref = refs[:3]
    forward = refs[3:FORWARD_SCRATCH]
    vectors_own, vectors_all, segs_row, segs_sent, segs_own = refs[FORWARD_SCRATCH : FORWARD_SCRATCH + 5]
    refs = refs[FORWARD_SCRATCH + 5 :]
    first_full, tokens_all, send_sems, recv_sems, local_sems = refs[:5]
    stages, vector_rows = refs[5 : 5 + count], refs[5 + count :]
    place = Place()
    own, other = place.fsdp, 2 * (1 - place.y) + place.core
    loads = [
        pltpu.make_async_copy(src, dst, local_sems.at[count + 8 + i])
        for i, (src, dst) in enumerate(zip((segs_ref, *vector_refs), (segs_row, *vector_rows)))
    ]
    for load in loads:
        load.start()
    for load in loads:
        load.wait()
    vectors_own[...] = jnp.zeros_like(vectors_own)
    for i, row in enumerate(vector_rows):
        size = row.shape[0]
        vectors_own[i : i + 1, :size] = row[...].astype(F32).reshape(1, size)
    segs_sent[...] = jnp.broadcast_to(segs_row[...], segs_sent.shape)
    greet_with_partner(place, (place.sibling, place.over_x, place.over_y, place.over_z))
    copies = Copies(send_sems, recv_sems)
    swap_tokens = copies.make(tokens_ref, tokens_out, place.partner)
    swap_segs = copies.make(segs_sent, segs_own, place.partner)
    vector_copies = [
        copies.make(vectors_own, vectors_all.at[own], place.over_y),
        copies.make(vectors_own, vectors_all.at[own], place.sibling),
        copies.make(vectors_all.at[other], vectors_all.at[other], place.sibling),
    ]
    weights = WeightGather(
        place,
        copies,
        [first_ref, *shares],
        [first_full, *fulls],
        [None, *stages],
        local_sems,
    )
    first_cuts = len(weight_cuts(first_ref.shape))
    gather = BlockGather(place, copies, [tokens_out, segs_own], [tokens_all, segs_out])
    save_first = pltpu.make_async_copy(first_full, first_out, local_sems.at[count + 7])
    attention = AttentionForward(
        place,
        q_ref,
        segs_out,
        rows_all,
        kv_all,
        (attended_out, lse_out, lse_rows_out, kv_out, rows_out),
        forward,
        [local_sems.at[count + i] for i in (2, 3, 5)],
        lambda side: first_full[:, :, side * D : (side + 1) * D].reshape(D, D),
        vectors_out,
    )

    keep_tokens = pltpu.make_async_copy(tokens_ref, tokens_out, local_sems.at[count + 9 + VECTORS])
    vector_copies[0].start()
    vector_copies[1].start()

    @pl.when(place.has_partner)
    def _():
        swap_segs.start()

    @pl.when(place.has_partner)
    def _():
        swap_tokens.start()

    @pl.when(jnp.logical_not(place.has_partner))
    def _():
        keep_tokens.start()

    weights.begin()
    vectors_all[own] = vectors_own[...]

    @pl.when(jnp.logical_not(place.has_partner))
    def _():
        segs_own[...] = segs_sent[...]

    vector_copies[0].wait_recv()
    vector_copies[2].start()
    weights.step(0)
    weights.step(1)
    vector_copies[1].wait_recv()
    vector_copies[2].wait_recv()
    vectors_out[...] = assemble_vectors([vectors_all[i] for i in range(4)])
    weights.step(2)

    @pl.when(place.has_partner)
    def _():
        swap_segs.wait_recv()
        swap_tokens.wait_recv()

    @pl.when(jnp.logical_not(place.has_partner))
    def _():
        keep_tokens.wait()

    gather.begin()
    weights.step(3)

    def norm_block(block):
        return norm_forward(
            tokens_all[block].astype(F32), vectors_out[0:1, :], vectors_out[1:2, :]
        )

    def norm_four(start):
        def visit(index, carried):
            rows_all[start + index] = norm_block(start + index)[0]
            return carried

        lax.fori_loop(0, 4, visit, 0)

    normed, normal, inverse = norm_block(place.block)
    normed_out[...] = normed
    normal_out[...] = normal
    inverse_out[...] = inverse
    weights.step(4)
    gather.first_halves()
    weights.keep_own()
    weights.step(5)
    gather.second_halves()
    gather.wait_near()
    gather.corners()
    norm_four(attention.near)
    attention.masks(False)
    weights.step(6)
    weights.arrive(0, first_cuts)
    save_first.start()
    attention.project_queries()
    weights.step(7)
    attention.near_part()
    weights.step(8)
    gather.wait_far()
    norm_four(attention.far)
    attention.masks(True)
    weights.step(9)
    attention.far_part()
    attention.store()
    save_first.wait()
    attention.finish()
    gather.finish()
    for copy in vector_copies:
        copy.wait_send()

    @pl.when(place.has_partner)
    def _():
        swap_segs.wait_send()
        swap_tokens.wait_send()

    weights.finish()


def opening(tokens, segs_row, vectors, first, shares, collective_id):
    rows, columns = tokens.shape
    count = len(shares)
    cuts = sum(len(weight_cuts(share.shape)) for share in [first, *shares])
    slots = 2 + 3 + cuts * WEIGHT_COPIES + 2 * BLOCK_COPIES
    vmem = pl.BlockSpec(memory_space=pltpu.VMEM)
    anywhere = pl.BlockSpec(memory_space=pl.ANY)
    shape = jax.ShapeDtypeStruct
    segs_shape = (16, segs_row.shape[1])
    return pl.pallas_call(
        partial(opening_kernel, count),
        in_specs=[anywhere] * (3 + VECTORS + count),
        out_specs=[vmem] * 9 + [anywhere] * (3 + count),
        out_shape=[
            shape((rows, columns), tokens.dtype),
            shape((8, *segs_shape), segs_row.dtype),
            shape((16, D), F32),
            shape((rows, D), BF16),
            shape((rows, D), F32),
            shape((rows, 1), F32),
        ]
        + forward_shapes(rows)
        + [shape((4, *share.shape), share.dtype) for share in [first, *shares]],
        scratch_shapes=forward_scratch(rows)
        + [
            pltpu.VMEM((8, D), F32),
            pltpu.VMEM((4, 8, D), F32),
            pltpu.VMEM(segs_row.shape, segs_row.dtype),
            pltpu.VMEM(segs_shape, segs_row.dtype),
            pltpu.VMEM(segs_shape, segs_row.dtype),
            pltpu.VMEM((4, *first.shape), first.dtype),
            pltpu.VMEM((8, rows, D), BF16),
            pltpu.SemaphoreType.DMA((slots,)),
            pltpu.SemaphoreType.DMA((slots,)),
            pltpu.SemaphoreType.DMA((count + 10 + VECTORS,)),
        ]
        + [pltpu.VMEM(share.shape, share.dtype) for share in shares]
        + [pltpu.VMEM(vector.shape, vector.dtype) for vector in vectors],
        compiler_params=pltpu.CompilerParams(
            collective_id=collective_id, has_side_effects=True, vmem_limit_bytes=60 << 20
        ),
        name="opening",
    )(tokens, segs_row, first, *vectors, *shares)


GROUP = 3


class AttentionGrads:
    def __init__(self, place, grad_ref, lse_ref, delta_ref, segs_ref, kv_all, q_all, grad_all, stats_all, biases, sums):
        self.place = place
        self.grad_ref, self.lse_ref, self.delta_ref = grad_ref, lse_ref, delta_ref
        self.segs_ref, self.kv_all, self.q_all, self.grad_all = segs_ref, kv_all, q_all, grad_all
        self.stats_all = stats_all
        self.query_bias, self.key_bias = biases
        self.query_sum, self.key_sum, self.value_sum = sums
        self.rows = grad_ref.shape[0]

    def masks(self):
        rows, place = self.rows, self.place
        start = place.block * rows
        own_segs = own_columns(self.segs_ref, place.block)
        for i in range(8):
            at = slice(i * rows, (i + 1) * rows)
            self.query_bias[:, at] = mask_block(own_segs, self.segs_ref, i, start, True)
            self.key_bias[:, at] = mask_block(own_segs, self.segs_ref, i, start, False)

    def lanes(self, pair, side=0):
        return pl.ds(pl.multiple_of(side * D + pair * LANES, LANES), LANES)

    def two_blocks(self, ref, index, lanes):
        return ref[pl.ds(2 * index, 2), :, lanes].reshape(2 * self.rows, LANES)

    def bias(self, ref, index):
        step = 2 * self.rows
        bias = ref[:, pl.ds(pl.multiple_of(index * step, step), step)]
        return jnp.concatenate([bias, bias], axis=0)

    def project(self, rows_all, weight, bias):
        for first in (0, 4):
            project_blocks(rows_all, first, lambda side: weight[:, :D], (bias,), self.q_all, D)

    def query_grads(self, first_pair, last_pair):
        scale = jnp.asarray(SCALE, BF16)
        count = self.place.block // 2 + 1

        def visit_pairs(group, carried):
            pairs = [group * GROUP + i for i in range(GROUP)]
            own = []
            for pair in pairs:
                queries = two_heads(self.q_all[self.place.block, :, self.lanes(pair)] * scale)
                grads = two_heads(self.grad_ref[:, self.lanes(pair)])
                lse = pick_lanes(self.lse_ref[...], pair)
                own.append((queries, grads, lse, pick_lanes(self.delta_ref[...], pair)))

            def visit(index, totals):
                bias = self.bias(self.query_bias, index)
                sums = []
                for pair, total, (queries, grads, lse, delta) in zip(pairs, totals, own):
                    keys = self.two_blocks(self.kv_all, index, self.lanes(pair))
                    values = self.two_blocks(self.kv_all, index, self.lanes(pair, 1))
                    attention = jnp.exp(dot_rows(queries, keys) + bias - lse)
                    grad_attention = dot_rows(grads, values)
                    grad_scores = (attention * (grad_attention - delta)).astype(BF16)
                    sums.append(total + jnp.dot(grad_scores, keys, preferred_element_type=F32))
                return tuple(sums)

            zeros = jnp.zeros((2 * self.rows, LANES), F32)
            totals = lax.fori_loop(0, count, visit, (zeros,) * GROUP)
            for pair, total in zip(pairs, totals):
                self.query_sum[pair] = total
            return carried

        lax.fori_loop(first_pair // GROUP, last_pair // GROUP, visit_pairs, 0)

    def key_grads(self, first, last, fresh):
        rows = self.rows
        scale = jnp.asarray(SCALE, BF16)
        own_block = self.place.block

        def stat_rows(index, pair, row):
            def spread(block, head):
                line = self.stats_all[2 * index + block, pl.ds(row + 2 * pair + head, 1), :]
                return jnp.broadcast_to(line, (rows, rows))

            heads = [jnp.concatenate([spread(0, head), spread(1, head)], axis=1) for head in range(2)]
            return jnp.concatenate(heads, axis=0)

        def visit_pairs(group, carried):
            pairs = [group * GROUP + i for i in range(GROUP)]
            own = []
            for pair in pairs:
                keys = two_heads(self.kv_all[own_block, :, self.lanes(pair)] * scale)
                own.append((keys, two_heads(self.kv_all[own_block, :, self.lanes(pair, 1)])))

            def visit(index, totals):
                bias = self.bias(self.key_bias, index)
                sums = []
                for pair, (key_total, value_total), (keys, values) in zip(pairs, totals, own):
                    later = self.two_blocks(self.q_all, index, self.lanes(pair))
                    later_grads = self.two_blocks(self.grad_all, index, self.lanes(pair))
                    scores = dot_rows(keys, later) + bias
                    attention = jnp.exp(scores - stat_rows(index, pair, 0))
                    grad_attention = dot_rows(values, later_grads)
                    grad_scores = attention * (grad_attention - stat_rows(index, pair, 16))
                    key_total = key_total + jnp.dot(
                        grad_scores.astype(BF16), later, preferred_element_type=F32
                    )
                    value_total = value_total + jnp.dot(
                        attention.astype(BF16), later_grads, preferred_element_type=F32
                    )
                    sums.append((key_total, value_total))
                return tuple(sums)

            if fresh:
                zeros = jnp.zeros((2 * rows, LANES), F32)
                totals = ((zeros, zeros),) * GROUP
            else:
                totals = tuple((self.key_sum[pair], self.value_sum[pair]) for pair in pairs)
            totals = lax.fori_loop(first, last, visit, totals)
            for pair, (key_total, value_total) in zip(pairs, totals):
                self.key_sum[pair], self.value_sum[pair] = key_total, value_total
            return carried

        lax.fori_loop(0, PAIRS // GROUP, visit_pairs, 0)

    def near_keys(self):
        self.key_grads(self.place.block // 2, 2 * self.place.y + 2, True)

    def far_keys(self):
        @pl.when(self.place.y == 0)
        def _():
            self.key_grads(2, 4, False)

    def store(self, out_ref):
        def visit(pair, carried):
            out_ref[:, self.lanes(pair)] = (one_pair(self.query_sum[pair]) * SCALE).astype(BF16)
            out_ref[:, self.lanes(pair, 1)] = (one_pair(self.key_sum[pair]) * SCALE).astype(BF16)
            out_ref[:, self.lanes(pair, 2)] = one_pair(self.value_sum[pair]).astype(BF16)
            return carried

        lax.fori_loop(0, PAIRS, visit, 0)


def attention_scratch(rows):
    return [
        pltpu.VMEM((8, rows, 2 * D), BF16),
        pltpu.VMEM((8, rows, D), BF16),
        pltpu.VMEM((8, rows, D), BF16),
        pltpu.VMEM((8, 32, rows), F32),
        pltpu.VMEM((rows, 8 * rows), F32),
        pltpu.VMEM((rows, 8 * rows), F32),
        pltpu.VMEM((PAIRS, 2 * rows, LANES), F32),
        pltpu.VMEM((PAIRS, 2 * rows, LANES), F32),
        pltpu.VMEM((PAIRS, 2 * rows, LANES), F32),
    ]


ATTENTION_SCRATCH = 9


def attend_back_kernel(
    grad_ref,
    stats_ref,
    lse_ref,
    delta_ref,
    segs_ref,
    vectors_ref,
    kv_ref,
    rows_ref,
    weight_ref,
    out_ref,
    *scratch,
):
    kv_all, q_all, grad_all, stats_all = scratch[:4]
    biases, sums = scratch[4:6], scratch[6:9]
    rows_all, weight, send_sems, recv_sems, local_sems = scratch[ATTENTION_SCRATCH:]
    place = Place()
    loads = [
        pltpu.make_async_copy(src, dst, local_sems.at[i])
        for i, (src, dst) in enumerate(
            ((rows_ref, rows_all), (weight_ref.at[:, pl.ds(0, D)], weight), (kv_ref, kv_all))
        )
    ]
    for load in loads:
        load.start()
    greet((place.sibling, place.over_x, place.over_y))
    copies = Copies(send_sems, recv_sems)
    gather = BlockGather(place, copies, [grad_ref, stats_ref], [grad_all, stats_all])
    gather.begin()
    grads = AttentionGrads(
        place, grad_ref, lse_ref, delta_ref, segs_ref, kv_all, q_all, grad_all, stats_all, biases, sums
    )
    grads.masks()
    loads[0].wait()
    loads[1].wait()
    grads.project(rows_all, weight, vectors_ref[6:7, :])
    gather.first_halves()
    loads[2].wait()
    gather.second_halves()
    grads.query_grads(0, GROUP)
    gather.corners()
    grads.query_grads(GROUP, PAIRS)
    gather.wait_near()
    grads.near_keys()
    gather.wait_far()
    grads.far_keys()
    grads.store(out_ref)
    gather.finish()


def attend_back(grads, stats, lse, delta, segs, state, weight, vectors, collective_id):
    kv, rows_all = state
    rows = grads.shape[0]
    slots = 2 * BLOCK_COPIES
    vmem = pl.BlockSpec(memory_space=pltpu.VMEM)
    anywhere = pl.BlockSpec(memory_space=pl.ANY)
    return pl.pallas_call(
        attend_back_kernel,
        in_specs=[vmem] * 6 + [anywhere] * 3,
        out_specs=vmem,
        out_shape=jax.ShapeDtypeStruct((rows, 3 * D), BF16),
        scratch_shapes=attention_scratch(rows)
        + [
            pltpu.VMEM((8, rows, D), BF16),
            pltpu.VMEM((D, D), BF16),
            pltpu.SemaphoreType.DMA((slots,)),
            pltpu.SemaphoreType.DMA((slots,)),
            pltpu.SemaphoreType.DMA((3,)),
        ],
        compiler_params=pltpu.CompilerParams(
            collective_id=collective_id, has_side_effects=True, vmem_limit_bytes=36 << 20
        ),
        name="attend_back",
    )(grads, stats, lse, delta, segs, vectors, kv, rows_all, weight)


CHUNK_ROWS, CHUNK_COLUMNS = 192, 768
REDUCE_COPIES = 9
VECTOR_AXES = 5


def chunk_places(shapes):
    places = [
        (which, row, column, CHUNK_COLUMNS)
        for which, (rows, columns) in enumerate(shapes)
        for row in range(0, rows, CHUNK_ROWS)
        for column in range(0, columns, CHUNK_COLUMNS)
    ]
    which, row, column, width = places.pop()
    cut = 2 * width // 3
    return places + [(which, row, column, cut), (which, row, column + cut, width - cut)]


CORE_SLOTS = 6
REDUCE_STAGES = ("core0", "core1", "y", "x", "z", "zz", "zz_back", "z_back", "x_back")


class GradientSum:
    def __init__(self, place, copies, places, sums, buffers):
        self.place = place
        (
            self.own,
            self.got_core,
            self.got_y,
            self.to_x,
            self.got_x,
            self.to_z,
            self.got_z,
            self.to_zz,
            self.got_zz,
            self.to_core,
        ) = buffers
        self.places = places
        self.x_rows, self.z_rows = CHUNK_ROWS // 2, CHUNK_ROWS // 4
        x, y, low, high = place.x, place.y, place.low, place.high
        self.plans = []
        self.finals = []
        for k, (which, row, column, width) in enumerate(places):
            out = sums[which]
            half = width // 2

            def piece(first, rows, start, columns, out=out, row=row, column=column):
                return out.at[
                    pl.ds(pl.multiple_of(row + first, 16), rows),
                    pl.ds(pl.multiple_of(column + start, LANES), columns),
                ]

            def wide_part(ref, *index, columns=width):
                return ref.at[(*index, slice(None), pl.ds(0, columns))]

            final = piece(x * self.x_rows + low * self.z_rows, self.z_rows, high * half, half)
            wide = piece(x * self.x_rows + low * self.z_rows, self.z_rows, 0, width)
            tall = piece(x * self.x_rows, self.x_rows, 0, width)
            slot = k % CORE_SLOTS
            moves = (
                (wide_part(self.to_core, slot, 0), wide_part(self.got_core, k, 0), place.sibling),
                (wide_part(self.to_core, slot, 1), wide_part(self.got_core, k, 1), place.sibling),
                (wide_part(self.own, k, 1 - y), wide_part(self.got_y, k), place.over_y),
                (wide_part(self.to_x, k), wide_part(self.got_x, k), place.over_x),
                (wide_part(self.to_z, k), wide_part(self.got_z, k), place.over_z),
                (
                    wide_part(self.to_zz, k, columns=half),
                    wide_part(self.got_zz, k, columns=half),
                    place.over_zz,
                ),
                (final, final, place.over_zz),
                (wide, wide, place.over_z),
                (tall, tall, place.over_x),
            )
            self.plans.append(
                {name: copies.make(*move) for name, move in zip(REDUCE_STAGES, moves)}
            )
            self.finals.append(final)
        self.stages = (
            self.stage_x,
            self.stage_z,
            self.stage_zz,
            self.stage_final,
            self.stage_z_back,
            self.stage_x_back,
        )

    def make(self, which, left, right):
        core = self.place.core
        for k, (owner, row, column, width) in enumerate(self.places):
            if owner != which:
                continue
            quarter_rows = left.shape[0] // 4

            def term(quarter):
                first = pl.multiple_of(quarter * quarter_rows + row, 16)
                rows = left[pl.ds(first, CHUNK_ROWS), :]
                columns = right[:, column : column + width]
                return jnp.dot(rows, columns, preferred_element_type=F32).astype(BF16)

            if k >= CORE_SLOTS:
                for name in ("core0", "core1"):
                    self.plans[k - CORE_SLOTS][name].wait_send()
            for i in range(2):
                self.to_core[k % CORE_SLOTS, i, :, :width] = term(2 * i + 1 - core)
            self.plans[k]["core0"].start()
            self.plans[k]["core1"].start()
            for i in range(2):
                self.own[k, i, :, :width] = term(2 * i + core)

    def add_up(self, store, loads, rows):
        step = self.z_rows

        def visit(index, carried):
            offset = pl.multiple_of(index * step, 16)
            total = loads[0](offset, step).astype(F32)
            for load in loads[1:]:
                total = total + load(offset, step).astype(F32)
            store(offset, step, total.astype(BF16))
            return carried

        if rows == step:
            visit(0, 0)
        else:
            lax.fori_loop(0, rows // step, visit, 0)

    def slab(self, ref, *index, first=0, start=0, width=None):
        def load(offset, rows):
            place = pl.ds(pl.multiple_of(first + offset, 16), rows)
            return ref[(*index, place, pl.ds(pl.multiple_of(start, LANES), width))]

        return load

    def stage_y(self, k):
        plan, y, width = self.plans[k], self.place.y, self.places[k][3]
        plan["core0"].wait_recv()
        plan["core1"].wait_recv()

        def store(offset, rows, value):
            self.own[k, 1 - y, pl.ds(offset, rows), :width] = value

        loads = [
            self.slab(self.own, k, 1 - y, width=width),
            self.slab(self.got_core, k, 1 - y, width=width),
        ]
        self.add_up(store, loads, CHUNK_ROWS)
        plan["y"].start()

    def terms_at(self, k, first, depth, inner=0, start=0, width=None):
        y = self.place.y
        part = {"start": start, "width": self.places[k][3] if width is None else width}
        loads = [
            self.slab(self.own, k, y, first=first, **part),
            self.slab(self.got_core, k, y, first=first, **part),
            self.slab(self.got_y, k, first=first, **part),
        ]
        if depth > 0:
            loads.append(self.slab(self.got_x, k, first=inner, **part))
        if depth > 1:
            loads.append(self.slab(self.got_z, k, **part))
        return loads

    def stage_x(self, k):
        plan, width = self.plans[k], self.places[k][3]
        plan["y"].wait_recv()

        def store(offset, rows, value):
            self.to_x[k, pl.ds(offset, rows), :width] = value

        self.add_up(store, self.terms_at(k, (1 - self.place.x) * self.x_rows, 0), self.x_rows)
        plan["x"].start()

    def stage_z(self, k):
        plan, width = self.plans[k], self.places[k][3]
        plan["x"].wait_recv()
        inner = (1 - self.place.low) * self.z_rows

        def store(offset, rows, value):
            self.to_z[k, :, :width] = value

        first = self.place.x * self.x_rows + inner
        self.add_up(store, self.terms_at(k, first, 1, inner), self.z_rows)
        plan["z"].start()

    def last_terms(self, k, side):
        inner = self.place.low * self.z_rows
        first = self.place.x * self.x_rows + inner
        half = self.places[k][3] // 2
        return self.terms_at(k, first, 2, inner, side * half, half)

    def stage_zz(self, k):
        plan, half = self.plans[k], self.places[k][3] // 2
        plan["z"].wait_recv()

        def store(offset, rows, value):
            self.to_zz[k, :, :half] = value

        self.add_up(store, self.last_terms(k, 1 - self.place.high), self.z_rows)
        plan["zz"].start()

    def stage_final(self, k):
        plan, half = self.plans[k], self.places[k][3] // 2
        plan["zz"].wait_recv()

        def store(offset, rows, value):
            self.finals[k][...] = value

        terms = self.last_terms(k, self.place.high)
        self.add_up(store, terms + [self.slab(self.got_zz, k, width=half)], self.z_rows)
        plan["zz_back"].start()

    def stage_z_back(self, k):
        self.plans[k]["zz_back"].wait_recv()
        self.plans[k]["z_back"].start()

    def stage_x_back(self, k):
        self.plans[k]["z_back"].wait_recv()
        self.plans[k]["x_back"].start()

    def ticks(self):
        return len(self.plans) + len(self.stages) - 1

    def tick(self, tick):
        for lag, stage in enumerate(self.stages):
            if 0 <= tick - lag < len(self.plans):
                stage(tick - lag)

    def finish(self):
        for k, plan in enumerate(self.plans):
            plan["x_back"].wait_recv()
            waited = k + CORE_SLOTS < len(self.plans)
            for name in REDUCE_STAGES[2:] if waited else REDUCE_STAGES:
                plan[name].wait_send()


def reduce_scratch(chunks):
    rows, columns = CHUNK_ROWS, CHUNK_COLUMNS
    shapes = [
        (chunks, 2, rows, columns),
        (chunks, 2, rows, columns),
        (chunks, rows, columns),
        (chunks, rows // 2, columns),
        (chunks, rows // 2, columns),
        (chunks, rows // 4, columns),
        (chunks, rows // 4, columns),
        (chunks, rows // 4, columns // 2),
        (chunks, rows // 4, columns // 2),
        (CORE_SLOTS, 2, rows, columns),
    ]
    return [pltpu.VMEM(shape, BF16) for shape in shapes]


REDUCE_SCRATCH = 10
CLOSING_INPUTS = 11


def closing_kernel(places, count, *refs):
    (
        grad_ref,
        stats_ref,
        lse_ref,
        delta_ref,
        segs_ref,
        normal_ref,
        inverse_ref,
        gain_ref,
        middle_ref,
        terms_ref,
        vectors_ref,
    ) = refs[:CLOSING_INPUTS]
    refs = refs[CLOSING_INPUTS:]
    factors = refs[: 4 * count - 1]
    rows_ref, kv_ref, weight_ref = refs[4 * count - 1 : 4 * count + 2]
    refs = refs[4 * count + 2 :]
    sums, (small_out, bias_out, wide_out, tokens_out) = refs[:count], refs[count : count + 4]
    refs = refs[count + 4 :]
    kv_all, q_all, grad_all, stats_all = refs[:4]
    biases, attention_sums = refs[4:6], refs[6:9]
    refs = refs[ATTENTION_SCRATCH:]
    buffers = refs[:REDUCE_SCRATCH]
    (
        grads_ref,
        grad_rows,
        weight,
        left,
        right,
        vector_sum,
        vector_got,
        tokens_own,
        send_sems,
        recv_sems,
        local_sems,
    ) = refs[REDUCE_SCRATCH:]

    place = Place()
    load_kv = pltpu.make_async_copy(kv_ref, kv_all, local_sems.at[0])
    load_weight = pltpu.make_async_copy(weight_ref, weight, local_sems.at[1])
    load_rows = pltpu.make_async_copy(rows_ref, grad_rows, local_sems.at[2])
    load_kv.start()
    load_rows.start()
    load_weight.start()
    greet_with_partner(
        place, (place.sibling, place.over_x, place.over_y, place.over_z, place.over_zz)
    )
    copies = Copies(send_sems, recv_sems)
    gather = BlockGather(place, copies, [grad_ref, stats_ref], [grad_all, stats_all])
    swap = copies.make(tokens_own, tokens_out, place.partner)
    reduce = GradientSum(place, copies, places, sums, buffers)
    chunks = len(places)
    by_weight = [[k for k in range(chunks) if places[k][0] == which] for which in range(count)]
    vector_devices = (place.over_x, place.over_z, place.over_zz, place.sibling, place.over_y)
    vector_copies = [
        copies.make(vector_sum, vector_got.at[i], device)
        for i, device in enumerate(vector_devices)
    ]
    tokens = grad_ref.shape[0]

    def make_terms(which, last_right=None):
        later_left, later_right, first_left = factors[4 * which : 4 * which + 3]
        rows, columns = later_left.shape[1], later_right.shape[1]
        left[:rows, :tokens] = later_left[...].T
        left[:rows, tokens:] = first_left[...].T
        right[:tokens, :columns] = later_right[...]
        if last_right is None:
            right[tokens:, :columns] = factors[4 * which + 3][...]
        else:
            right[tokens:, :columns] = last_right
        reduce.make(which, left.at[pl.ds(0, rows), :], right)

    gather.begin()
    make_terms(0)
    grads = AttentionGrads(
        place,
        grad_ref,
        lse_ref,
        delta_ref,
        segs_ref,
        kv_all,
        q_all,
        grad_all,
        stats_all,
        biases,
        attention_sums,
    )
    gather.first_halves()
    for k in by_weight[0]:
        reduce.stage_y(k)
    gather.second_halves()
    grads.masks()
    load_rows.wait()
    load_weight.wait()
    grads.project(grad_rows, weight, vectors_ref[6:7, :])
    load_kv.wait()
    grads.query_grads(0, PAIRS)
    gather.corners()
    gather.wait_near()
    make_terms(1)
    for k in by_weight[1]:
        reduce.stage_y(k)
    reduce.tick(0)
    grads.near_keys()
    gather.wait_far()
    reduce.tick(1)
    grads.far_keys()
    grads.store(grads_ref)
    reduce.tick(2)
    make_terms(2)
    for k in by_weight[2]:
        reduce.stage_y(k)
    own_grads = grads_ref[...]
    make_terms(3, own_grads)
    reduce.tick(3)
    grad_normed = dot_rows(own_grads, weight[...])
    grad_input, grad_gain, grad_bias = norm_backward(
        grad_normed, normal_ref[...], inverse_ref[...], gain_ref[...]
    )
    swapped = (middle_ref[...] + grad_input).astype(BF16)
    tokens_own[...] = swapped

    @pl.when(place.has_partner)
    def _():
        swap.start()

    @pl.when(jnp.logical_not(place.has_partner))
    def _():
        tokens_out[...] = swapped

    vector_sum[...] = terms_ref[...]
    query_bias = jnp.sum(own_grads[:, :D].astype(F32), axis=0, keepdims=True)
    value_bias = jnp.sum(own_grads[:, 2 * D :].astype(F32), axis=0, keepdims=True)
    for row, value in ((0, grad_gain[None]), (1, grad_bias[None]), (6, query_bias), (7, value_bias)):
        vector_sum[row : row + 1, :] = vector_sum[row : row + 1, :] + value
    vector_copies[0].start()
    for k in by_weight[3]:
        reduce.stage_y(k)

    def vector_step(index):
        vector_copies[index].wait()
        vector_sum[...] = vector_sum[...] + vector_got[index]
        if index + 1 < VECTOR_AXES:
            vector_copies[index + 1].start()

    for tick in range(4, reduce.ticks()):
        reduce.tick(tick)
        if tick - 4 < VECTOR_AXES - 1:
            vector_step(tick - 4)
    vector_step(VECTOR_AXES - 1)
    small_out[...] = vector_sum[:6, :]
    bias_out[...] = vector_sum[6:8, :]
    wide_out[...] = vector_sum[8:12, :]
    reduce.finish()
    gather.finish()

    @pl.when(place.has_partner)
    def _():
        swap.wait_recv()
        swap.wait_send()


def closing(attention, norm, terms, factors, weight, vectors, collective_id):
    grads, stats, lse, delta, segs, (kv, rows_all) = attention
    rows = grads.shape[0]
    count = len(factors)
    shapes = [(group[0].shape[1] // 4, group[1].shape[1]) for group in factors]
    places = chunk_places(shapes)
    chunks = len(places)
    slots = chunks * REDUCE_COPIES + VECTOR_AXES + 2 * BLOCK_COPIES + 1
    flat = [factor for group in factors for factor in group]
    tallest = max(group[0].shape[1] for group in factors)
    widest = max(group[1].shape[1] for group in factors)
    vmem = pl.BlockSpec(memory_space=pltpu.VMEM)
    anywhere = pl.BlockSpec(memory_space=pl.ANY)
    return pl.pallas_call(
        partial(closing_kernel, places, count),
        in_specs=[vmem] * (CLOSING_INPUTS + len(flat)) + [anywhere] * 3,
        out_specs=[vmem] * (count + 4),
        out_shape=[jax.ShapeDtypeStruct(shape, BF16) for shape in shapes]
        + [jax.ShapeDtypeStruct((size, D), F32) for size in (6, 2, 4)]
        + [jax.ShapeDtypeStruct((rows, D), BF16)],
        scratch_shapes=attention_scratch(rows)
        + reduce_scratch(chunks)
        + [
            pltpu.VMEM((rows, 3 * D), BF16),
            pltpu.VMEM((8, rows, D), BF16),
            pltpu.VMEM(weight.shape, BF16),
            pltpu.VMEM((tallest, 2 * rows), BF16),
            pltpu.VMEM((2 * rows, widest), BF16),
            pltpu.VMEM(terms.shape, F32),
            pltpu.VMEM((VECTOR_AXES, *terms.shape), F32),
            pltpu.VMEM((rows, D), BF16),
            pltpu.SemaphoreType.DMA((slots,)),
            pltpu.SemaphoreType.DMA((slots,)),
            pltpu.SemaphoreType.DMA((3,)),
        ],
        compiler_params=pltpu.CompilerParams(
            collective_id=collective_id, has_side_effects=True, vmem_limit_bytes=60 << 20
        ),
        name="closing",
    )(grads, stats, lse, delta, segs, *norm, terms, vectors, *flat, rows_all, kv, weight)


class PlaneLinks:
    def leave(self, value):
        pairs = [(c * 4 + f, (2 * f + c % 2) * 4 + c // 2) for c in range(8) for f in range(4)]
        return lax.ppermute(value, ("ctx", "fsdp"), pairs)

    def open(self, tokens, segs_row, vectors, shares):
        tokens, segs, vectors, *results = opening(tokens, segs_row, vectors, shares[0], shares[1:], 0)
        *first, kv, rows_all = results[:8]
        return tokens.astype(F32), segs, vectors, as_matrices(results[8:]), (*first, (kv, rows_all))

    def attend(self, normed, vectors, weight, segs, cotangent):
        attended, lse, lse_rows, kv, rows_all, cotangent = attend(
            normed, segs, vectors, weight, cotangent, 2
        )
        return (attended, lse, lse_rows, (kv, rows_all)), cotangent

    def attend_back(self, attention, weight, vectors):
        return attend_back(*attention, weight, vectors, 3)

    def close(self, attention, norm, factors, terms, weight, vectors):
        *sums, small, bias, wide, tokens_grad = closing(
            attention, norm, terms, factors, weight, vectors, 4
        )
        return [total.astype(F32) for total in sums], (small, bias, wide), tokens_grad


class PlainLinks:
    def leave(self, value):
        return value

    def open(self, tokens, segs_row, vectors, shares):
        segs = (segs_row, lax.all_gather(segs_row, "ctx", axis=1, tiled=True))
        gathered = lax.all_gather(pack_vectors(*vectors), "fsdp", axis=0)
        vectors = assemble_vectors([gathered[i] for i in range(4)])
        weights = as_matrices([lax.all_gather(share, "fsdp", axis=0) for share in shares])
        resid = tokens.astype(F32)
        first = norm_forward(resid, vectors[0:1], vectors[1:2])
        first = first + self.attend(first[0], vectors, weights[0], segs, None)[0]
        return resid, segs, vectors, weights, first

    def place(self, segs):
        own_segs, all_segs = segs
        rows = own_segs.shape[1]
        start = (lax.axis_index("ctx") * rows).reshape(1).astype(jnp.int32)
        return start, own_segs.reshape(rows, 1), all_segs

    def blocks(self, block):
        return lax.all_gather(block, "ctx", axis=0)

    def attend(self, normed, vectors, weight, segs, cotangent):
        start, own_segs, all_segs = self.place(segs)
        bias = jnp.concatenate([vectors[6:7], jnp.zeros((1, D), F32), vectors[7:8]], axis=1)
        projected = (jnp.dot(normed, weight, preferred_element_type=F32) + bias).astype(BF16)
        queries, kv_own = projected[:, :D], projected[:, D:]
        kv = self.blocks(kv_own).reshape(-1, 2 * D)
        attended, lse, lse_rows = attention_forward(start, queries, kv, own_segs, all_segs)
        return (attended, lse, lse_rows, (queries, kv_own, kv)), cotangent

    def attend_back(self, attention, weight, vectors):
        grads, stats, lse, delta, segs, (queries, kv_own, kv) = attention
        start, own_segs, all_segs = self.place(segs)
        q_all = self.blocks(queries).reshape(-1, D)
        grad_all = self.blocks(grads).reshape(-1, D)
        return attention_backward(
            start,
            queries,
            grads,
            kv_own,
            lse,
            delta,
            kv,
            q_all,
            grad_all,
            self.blocks(stats),
            own_segs,
            all_segs,
        )

    def close(self, attention, norm, factors, terms, weight, vectors):
        grad_projected = self.attend_back(attention, weight, vectors)
        grad_input, more = input_gradient(grad_projected, weight, *norm)
        terms = terms + jnp.concatenate(
            [more[:2], jnp.zeros((4, D), F32), more[2:], jnp.zeros((8, D), F32)], axis=0
        )
        sums = []
        for later_left, later_right, first_left, *first_right in factors:
            left = jnp.concatenate([later_left, first_left], axis=0)
            right = jnp.concatenate([later_right, *(first_right or [grad_projected])], axis=0)
            term = column_products(left, right).astype(BF16)
            share = lax.psum_scatter(term, "fsdp", scatter_dimension=0, tiled=True)
            sums.append(lax.psum(share.astype(F32), "ctx"))
        terms = lax.psum(terms, ("ctx", "fsdp"))
        return sums, (terms[:6], terms[6:8], terms[8:12]), grad_input.astype(BF16)


def as_matrices(fulls):
    return tuple(full.reshape(-1, full.shape[-1]) for full in fulls)


def layer_forward(resid, weights, vectors, first):
    gain_two, bias_two, bias_proj, bias_out = (vectors[i : i + 1] for i in range(2, 6))
    bias_fc = vectors[8:12].reshape(1, 4 * D)
    _, weight_proj, weight_fc, weight_out = weights
    normed_one, normal_one, inverse_one, attended, lse, lse_rows, state = first
    middle = resid + jnp.dot(attended, weight_proj, preferred_element_type=F32) + bias_proj
    normed_two, normal_two, inverse_two = norm_forward(middle, gain_two, bias_two)
    hidden = jnp.dot(normed_two, weight_fc, preferred_element_type=F32) + bias_fc
    activated = jax.nn.gelu(hidden, approximate=True).astype(BF16)
    result_rows = middle + jnp.dot(activated, weight_out, preferred_element_type=F32) + bias_out
    saved = (
        normed_one,
        normal_one,
        inverse_one,
        state,
        attended,
        lse,
        lse_rows,
        normed_two,
        normal_two,
        inverse_two,
        hidden,
        activated,
    )
    return result_rows, saved


def layer_backward(gradient, weights, vectors, saved, links, segs):
    weight_qkv, weight_proj, weight_fc, weight_out = weights
    gain_one, gain_two = vectors[0:1], vectors[2:3]
    (
        normed_one,
        normal_one,
        inverse_one,
        state,
        attended,
        lse,
        lse_rows,
        normed_two,
        normal_two,
        inverse_two,
        hidden,
        activated,
    ) = saved
    total = lambda value: jnp.sum(value.astype(F32), axis=0)
    grad_branch = gradient.astype(BF16)
    grad_activated = dot_rows(grad_branch, weight_out)
    gelu_pull = jax.vjp(partial(jax.nn.gelu, approximate=True), hidden)[1]
    grad_hidden = gelu_pull(grad_activated)[0].astype(BF16)
    grad_normed_two = dot_rows(grad_hidden, weight_fc)
    grad_in_two, grad_gain_two, grad_bias_two = norm_backward(
        grad_normed_two, normal_two, inverse_two, gain_two
    )
    grad_middle = gradient + grad_in_two
    grad_proj = grad_middle.astype(BF16)
    grad_attended = dot_rows(grad_proj, weight_proj).astype(BF16)
    products = grad_attended.astype(F32) * attended.astype(F32)
    head_of = jnp.arange(D, dtype=jnp.int32) // HDIM
    by_lane = (head_of[:, None] == jnp.arange(LANES, dtype=jnp.int32)[None, :]).astype(F32)
    by_row = (jnp.arange(16, dtype=jnp.int32)[:, None] == head_of[None, :]).astype(F32)
    delta = jnp.dot(products, by_lane, precision=lax.Precision.HIGHEST, preferred_element_type=F32)
    delta_rows = lax.dot_general(
        by_row,
        products,
        (((1,), (1,)), ((), ())),
        precision=lax.Precision.HIGHEST,
        preferred_element_type=F32,
    )
    stats = jnp.concatenate([lse_rows, delta_rows], axis=0)
    attention = (grad_attended, stats, lse, delta, segs, state)
    norm = (normal_one, inverse_one, gain_one, grad_middle)
    matrices = ((activated, grad_branch), (normed_two, grad_hidden), (attended, grad_proj))
    upper = jnp.stack([grad_gain_two, grad_bias_two, total(grad_proj), total(grad_branch)])
    lower = total(grad_hidden).reshape(4, D)
    return attention, norm, matrices, (upper, lower)


def input_gradient(grad_projected, weight_qkv, normal, inverse, gain, middle):
    total = lambda value: jnp.sum(value.astype(F32), axis=0)
    grad_normed = dot_rows(grad_projected, weight_qkv)
    grad_in, grad_gain, grad_bias = norm_backward(grad_normed, normal, inverse, gain)
    terms = [
        grad_gain,
        grad_bias,
        total(grad_projected[:, :D]),
        total(grad_projected[:, 2 * D :]),
    ]
    return middle + grad_in, jnp.stack(terms)


def body(
    links,
    tokens,
    segment_ids,
    ln1_gain,
    ln1_bias,
    attn_weight,
    attn_bias,
    proj_weight,
    proj_bias,
    ln2_gain,
    ln2_bias,
    fc_weight,
    fc_bias,
    out_weight,
    out_bias,
    out_cotangent,
):
    vectors = (
        ln1_gain,
        ln1_bias,
        ln2_gain,
        ln2_bias,
        proj_bias,
        out_bias,
        attn_bias,
        fc_bias,
    )
    shares = [attn_weight, proj_weight, fc_weight, out_weight]
    resid, segs, vectors, weights, first = links.open(tokens[0], segment_ids, vectors, shares)
    resid, saved = layer_forward(resid, weights, vectors, first)
    saved_layers = [saved]
    first = norm_forward(resid, vectors[0:1], vectors[1:2])
    attended, gradient = links.attend(first[0], vectors, weights[0], segs, out_cotangent[0])
    resid, saved = layer_forward(resid, weights, vectors, first + attended)
    saved_layers.append(saved)
    output = links.leave(resid.astype(BF16))
    gradient = gradient.astype(F32)
    attention, norm, later, (upper, lower) = layer_backward(
        gradient, weights, vectors, saved_layers[1], links, segs
    )
    later_projected = links.attend_back(attention, weights[0], vectors)
    gradient, terms = input_gradient(later_projected, weights[0], *norm)
    attention, norm, first, (more_upper, more_lower) = layer_backward(
        gradient, weights, vectors, saved_layers[0], links, segs
    )
    factors = [(*a, *b) for a, b in zip(later, first)]
    factors.append((saved_layers[1][0], later_projected, saved_layers[0][0]))
    packed = jnp.concatenate(
        [terms[:2], upper + more_upper, terms[2:], lower + more_lower, jnp.zeros((4, D), F32)], axis=0
    )
    (out_grad, fc_grad, proj_grad, qkv_grad), (small, bias_qv, bias_fc), tokens_grad = links.close(
        attention, norm, factors, packed, weights[0], vectors
    )
    own = lax.axis_index("fsdp")
    pick = lambda value, axis: lax.dynamic_index_in_dim(value, own, axis, keepdims=False)
    small = pick(small.reshape(6, 4, -1), 1)
    bias_qv = pick(bias_qv.reshape(4, -1), 0)
    bias_fc = pick(bias_fc, 0)
    gain_one, bias_one, gain_two, bias_two, bias_proj, bias_out = (small[i] for i in range(6))
    return (
        output[None],
        tokens_grad[None],
        gain_one,
        bias_one,
        qkv_grad,
        bias_qv,
        proj_grad,
        bias_proj,
        gain_two,
        bias_two,
        fc_grad,
        bias_fc,
        out_grad,
        bias_out,
    )


def solution(mesh):
    links = PlaneLinks() if (mesh.shape["ctx"], mesh.shape["fsdp"]) == (8, 4) else PlainLinks()
    rows = P("fsdp", "ctx", None)
    vector, matrix = P("fsdp"), P("fsdp", None)
    in_specs = (
        rows,
        P("fsdp", "ctx"),
        vector,
        vector,
        matrix,
        vector,
        matrix,
        vector,
        vector,
        vector,
        matrix,
        vector,
        matrix,
        vector,
        rows,
    )
    out_specs = (
        rows,
        rows,
        vector,
        vector,
        matrix,
        vector,
        matrix,
        vector,
        vector,
        vector,
        matrix,
        vector,
        matrix,
        vector,
    )
    return jax.shard_map(
        partial(body, links), mesh=mesh, in_specs=in_specs, out_specs=out_specs, check_vma=False
    )
```
